32 devices in a mesh: dp: 8 (over y, x, core), mp: 4 (over z).
Axes of the slice: x: 2, y: 2, z: 4, core: 2. Of those that a mesh axis runs over, the one named last changes fastest.
Arguments:
- tokens: bfloat16 [12288, 1024], P(('dp', 'mp')), may hold values from -6 to 6
- seg_ids: int32 [8, 1536], P('dp'), may hold values from 0 to 1, as said below
- bucket_of: int32 [128], replicated, may hold values from 0 to 31, as said below
- ln1_gain: float32 [1024], replicated, may hold values from 0.5 to 1.5
- ln1_bias: float32 [1024], replicated, may hold values from -1.2 to 1.2
- w_qkv: bfloat16 [3, 1024, 1024], P(None, None, 'mp'), may hold values from -0.1875 to 0.1875
- rel_table: float32 [32, 16], P(None, 'mp'), may hold values from -4 to 4
- w_out: bfloat16 [1024, 1024], P('mp'), may hold values from -2 to 2
- ln2_gain: float32 [1024], replicated, may hold values from 0.5 to 1.5
- ln2_bias: float32 [1024], replicated, may hold values from -1.2 to 1.2
- w_up: bfloat16 [1024, 4096], P(None, 'mp'), may hold values from -0.1875 to 0.1875
- up_bias: float32 [4096], P('mp'), may hold values from -1.2 to 1.2
- w_down: bfloat16 [4096, 1024], P('mp'), may hold values from -0.09375 to 0.09375
- down_bias: float32 [1024], replicated, may hold values from -1.2 to 1.2
- out_grad: bfloat16 [12288, 1024], P(('dp', 'mp')), may hold values from -6 to 6
Outputs:
- layer_out: bfloat16 [12288, 1024], P(('dp', 'mp'))
- grad_tokens: bfloat16 [12288, 1024], P(('dp', 'mp'))
- grad_ln1_gain: float32 [1024], replicated
- grad_ln1_bias: float32 [1024], replicated
- grad_qkv: float32 [3, 1024, 1024], P(None, None, 'mp')
- grad_table: float32 [32, 16], P(None, 'mp')
- grad_wout: float32 [1024, 1024], P('mp')
- grad_ln2_gain: float32 [1024], replicated
- grad_ln2_bias: float32 [1024], replicated
- grad_up: float32 [1024, 4096], P(None, 'mp')
- grad_up_bias: float32 [4096], P('mp')
- grad_down: float32 [4096, 1024], P('mp')
- grad_down_bias: float32 [1024], replicated
The draws below stay inside these ranges and needn't reach their ends.
Inputs may be any that keep to these rules, and one draw needn't show every extreme that they name: `seg_ids`: each row holds 2 sequences: ids 0 then 1, never falling; each sequence has 512 to 1024 tokens, and some row has one of exactly 1024 tokens. bucket_of[d] = d for d < 16; beyond, it never falls, rises by at most one from one distance to the next, and its last entry is 31.
All inputs are finite; a program needn't handle non-finite values.
Results may differ from the reference program's by a relative error of at most 0.02.
Values may be sent and summed in bfloat16 or wider, within the bound.
No kernel may reach another device: no remote copies, remote signals or barrier semaphores. Data moves between devices by JAX's collectives and lax.ppermute only.
A program may use at most 192 MiB of HBM per device.

```python
import jax
import jax.numpy as jnp
from jax import lax

D = 1024
HEADS = 16
HEAD = 64
FF = 4096
NB = 32
MAXD = 128
BLOCK = 512
TOK_DEV = 1536
SEQ_MOST = 1024
TOKENS = 12288
N_DP = 8


def draw_bucket_of(key, part):
    half_buckets = NB // 2
    places = jax.random.permutation(key, MAXD - half_buckets - 1) + half_buckets + 1
    bounds = places[:NB - half_buckets - 1]
    distance = jnp.arange(MAXD, dtype=jnp.int32)
    passed = jnp.sum((bounds[None, :] <= distance[:, None]).astype(jnp.int32), axis=1)
    return jnp.where(distance < half_buckets, distance, half_buckets + passed).astype(jnp.int32)


def draw_seg_ids(key, part):
    least_len = TOK_DEV - SEQ_MOST
    cuts = jax.random.randint(jax.random.fold_in(key, 11), (N_DP,), least_len, SEQ_MOST + 1)
    forced_row = jax.random.randint(jax.random.fold_in(key, 12), (), 0, N_DP)
    forced_side = jax.random.randint(jax.random.fold_in(key, 13), (), 0, 2)
    forced_cut = jnp.where(forced_side == 0, SEQ_MOST, least_len).astype(jnp.int32)
    cuts = jnp.where(jnp.arange(N_DP, dtype=jnp.int32) == forced_row, forced_cut, cuts.astype(jnp.int32))
    position = jnp.arange(TOK_DEV, dtype=jnp.int32)
    return (position[None, :] >= cuts[:, None]).astype(jnp.int32)


def steps_of(own_key, shape, cuts, low, high):
    gain = 1.0
    for axis_at, shards_of in cuts:
        steps = jax.random.uniform(jax.random.fold_in(jax.random.fold_in(own_key, 6), axis_at), (shards_of,), jnp.float32, low / len(cuts), high / len(cuts))
        gain = gain * jnp.repeat(jnp.exp(steps), shape[axis_at] // shards_of).reshape((-1,) + (1,) * (len(shape) - 1 - axis_at))
    return gain


def normal_values(own_key, dims, scale, reach, cuts=(), kind=jnp.bfloat16):
    factor_of = steps_of(own_key, dims, cuts, -0.22, 0.18) if cuts else 1.0
    entries = jax.random.normal(own_key, dims, jnp.float32) * scale * factor_of
    return jnp.minimum(jnp.maximum(entries, -reach), reach).astype(kind)


def setup_inputs(seed: int = 0) -> dict:
    seeds = jax.random.split(jax.random.key(seed), 16)
    tokens = normal_values(seeds[0], (TOKENS, D), 1.0, 6.0, ((0, 32),))
    seg_ids = draw_seg_ids(jax.random.fold_in(seeds[15], 71), 0)
    bucket_of = draw_bucket_of(jax.random.fold_in(seeds[15], 71), 0)
    ln1_gain = jnp.clip(1.0 + 0.1 * jax.random.normal(seeds[3], (D,), jnp.float32), 0.5, 1.5)
    ln1_bias = normal_values(seeds[4], (D,), 0.2, 1.2, (), jnp.float32)
    w_qkv = normal_values(seeds[5], (3, D, HEADS * HEAD), D ** -0.5, 0.1875, ((2, 4),))
    rel_table = normal_values(seeds[6], (NB, HEADS), 1.0, 4.0, ((1, 4),), jnp.float32)
    w_out = normal_values(seeds[7], (HEADS * HEAD, D), (max(HEADS * HEAD // 128, 1)) ** -0.5, 2.0, ((0, 4),))
    ln2_gain = jnp.clip(1.0 + 0.1 * jax.random.normal(seeds[8], (D,), jnp.float32), 0.5, 1.5)
    ln2_bias = normal_values(seeds[9], (D,), 0.2, 1.2, (), jnp.float32)
    w_up = normal_values(seeds[10], (D, FF), D ** -0.5, 0.1875, ((1, 4),))
    up_bias = normal_values(seeds[11], (FF,), 0.2, 1.2, ((0, 4),), jnp.float32)
    w_down = normal_values(seeds[12], (FF, D), FF ** -0.5, 0.09375, ((0, 4),))
    down_bias = normal_values(seeds[13], (D,), 0.2, 1.2, (), jnp.float32)
    out_grad = normal_values(seeds[14], (TOKENS, D), 1.0, 6.0, ((0, 32),))
    return {"tokens": tokens, "seg_ids": seg_ids, "bucket_of": bucket_of, "ln1_gain": ln1_gain, "ln1_bias": ln1_bias, "w_qkv": w_qkv, "rel_table": rel_table, "w_out": w_out, "ln2_gain": ln2_gain, "ln2_bias": ln2_bias, "w_up": w_up, "up_bias": up_bias, "w_down": w_down, "down_bias": down_bias, "out_grad": out_grad}


@jax.custom_vjp
def low(v):
    return lax.optimization_barrier(v.astype(jnp.bfloat16)).astype(jnp.float32)

@jax.custom_vjp
def low_back(v):
    return v

def low_keep(v):
    return (low(v), None)

def low_pass(kept, grad):
    return (grad,)

def back_keep(v):
    return (v, None)

def back_low(kept, grad):
    return (low(grad),)
low.defvjp(low_keep, low_pass)
low_back.defvjp(back_keep, back_low)
EPSILON = 1e-05
HIGHEST_PRECISION = lax.Precision.HIGHEST
MASKED_SCORE = -1e+30

def layer_norm(inputs, norm_gain, norm_bias):
    center = inputs - lax.optimization_barrier(jnp.mean(inputs, axis=-1, keepdims=True))
    spread = lax.optimization_barrier(jnp.mean(center * center, axis=-1, keepdims=True))
    return center * lax.rsqrt(spread + EPSILON) * norm_gain + norm_bias

def matmul(left, right):
    return jnp.dot(left, right, precision=HIGHEST_PRECISION, preferred_element_type=jnp.float32)

def attention(queries, keys_all, values_all, rel_table, seg_row, bucket_of):
    key_index = jnp.arange(TOK_DEV, dtype=jnp.int32)
    score_scale = HEAD ** (-0.5)

    def one_block(block_index):
        row_start = block_index * BLOCK
        query_block = lax.dynamic_slice_in_dim(queries, row_start, BLOCK, 0)
        row_index = row_start + jnp.arange(BLOCK, dtype=jnp.int32)
        distance = row_index[:, None] - key_index[None, :]
        bucket = bucket_of[jnp.clip(distance, 0, MAXD - 1)]
        pos_bias = jnp.transpose(rel_table[bucket], (2, 0, 1))
        seg_block = lax.dynamic_slice_in_dim(seg_row, row_start, BLOCK, 0)
        allowed = (seg_block[:, None] == seg_row[None, :]) & (distance >= 0)
        raw_scores = jnp.einsum('qhd,khd->hqk', query_block, keys_all, precision=HIGHEST_PRECISION)
        scores = low_back(raw_scores * score_scale + pos_bias)
        masked = jnp.where(allowed[None], scores, MASKED_SCORE)
        row_max = lax.optimization_barrier(jnp.max(masked, axis=-1, keepdims=True))
        log_total = row_max + jnp.log(lax.optimization_barrier(jnp.sum(jnp.exp(masked - row_max), axis=-1, keepdims=True)))
        soft_low = low(jnp.exp(masked - log_total))
        return jnp.einsum('hqk,khd->qhd', soft_low, values_all, precision=HIGHEST_PRECISION)
    pieces = lax.map(jax.checkpoint(one_block), jnp.arange(TOK_DEV // BLOCK, dtype=jnp.int32))
    return pieces.reshape(TOK_DEV, HEADS * HEAD)

def layer(inputs, ln1_gain, ln1_bias, w_qkv, rel_table, w_out, ln2_gain, ln2_bias, w_up, up_bias, w_down, down_bias, seg_row, bucket_of):
    normed = low(layer_norm(inputs, ln1_gain, ln1_bias))
    queries = low_back(low(matmul(normed, w_qkv[0]))).reshape(TOK_DEV, HEADS, HEAD)
    keys_all = low_back(low(matmul(normed, w_qkv[1]))).reshape(TOK_DEV, HEADS, HEAD)
    values_all = low_back(low(matmul(normed, w_qkv[2]))).reshape(TOK_DEV, HEADS, HEAD)
    attended = low_back(low(attention(queries, keys_all, values_all, rel_table, seg_row, bucket_of)))
    branch = low_back(matmul(attended, w_out))
    hidden_in = inputs + branch
    second = low(layer_norm(hidden_in, ln2_gain, ln2_bias))
    pre_act = low_back(matmul(second, w_up) + up_bias)
    activated = low(jax.nn.gelu(pre_act, approximate=False))
    return hidden_in + (matmul(activated, w_down) + down_bias)

def reference(tokens, seg_ids, bucket_of, ln1_gain, ln1_bias, w_qkv, rel_table, w_out, ln2_gain, ln2_bias, w_up, up_bias, w_down, down_bias, out_grad):
    params = (ln1_gain, ln1_bias, w_qkv.astype(jnp.float32), rel_table, w_out.astype(jnp.float32), ln2_gain, ln2_bias, w_up.astype(jnp.float32), up_bias, w_down.astype(jnp.float32), down_bias)
    group_tokens = tokens.astype(jnp.float32).reshape(N_DP, TOK_DEV, D)
    group_grads = out_grad.astype(jnp.float32).reshape(N_DP, TOK_DEV, D)

    def group_step(running, group_item):
        inputs, cotangent, seg_row = group_item

        def forward(layer_in, layer_params):
            return layer(layer_in, *layer_params, seg_row, bucket_of)
        layer_out, pullback = jax.vjp(forward, inputs, params)
        token_grad, param_grads = pullback(cotangent)
        running = jax.tree.map(lambda left, right: left + right, running, param_grads)
        return (running, (layer_out.astype(jnp.bfloat16), token_grad.astype(jnp.bfloat16)))
    empty_grads = jax.tree.map(jnp.zeros_like, params)
    summed, (outputs, input_grads) = lax.scan(group_step, empty_grads, (group_tokens, group_grads, seg_ids))
    return (outputs.reshape(TOKENS, D), input_grads.reshape(TOKENS, D), summed[0], summed[1], summed[2], summed[3], summed[4], summed[5], summed[6], summed[7], summed[8], summed[9], summed[10])
```

```python
import jax
import jax.numpy as jnp
from jax import lax
from jax.experimental import pallas as pl
from jax.experimental.pallas import tpu as pltpu
from jax.sharding import PartitionSpec as P


EPSILON = 1e-05
HIGHEST_PRECISION = lax.Precision.HIGHEST


def layer_norm(inputs, norm_gain, norm_bias):
    center = inputs - jnp.mean(inputs, axis=-1, keepdims=True)
    spread = jnp.mean(center * center, axis=-1, keepdims=True)
    return center * lax.rsqrt(spread + EPSILON) * norm_gain + norm_bias


def gelu_exact(inputs):
    return jax.nn.gelu(inputs, approximate=False)


BLK = 256
HEAD_LANES = 64
NEAR = 128


def head_mask(rows, width, head, axis):
    place = lax.broadcasted_iota(jnp.int32, (rows, width), axis)
    return (place >= head * HEAD_LANES) & (place < (head + 1) * HEAD_LANES)


def one_head(value, head):
    keep = head_mask(value.shape[0], value.shape[1], head, 1)
    return jnp.where(keep, value, jnp.zeros_like(value))


def dot_nt(left, right):
    return lax.dot_general(
        left, right, (((1,), (1,)), ((), ())), preferred_element_type=jnp.float32
    )


def dot_nn(left, right):
    return lax.dot_general(
        left, right, (((1,), (0,)), ((), ())), preferred_element_type=jnp.float32
    )


def attention_forward_kernel(
    cut_ref, q_ref, k_ref, v_ref, bias_ref, out_ref, lse_ref, tile_ref, masked_v, score_ref
):
    heads = masked_v.shape[0]
    block = pl.program_id(0)
    cut = cut_ref[0]

    @pl.when(block == 0)
    def _():
        for head in range(heads):
            wide = jnp.broadcast_to(bias_ref[head : head + 1, :], (BLK, 2 * BLK))
            tile_ref[head] = pltpu.roll(wide, 0, 1, stride=1, stride_axis=0)
            masked_v[head] = one_head(v_ref[...], head)

    row_start = block * BLK
    first = jnp.where(row_start >= cut, cut // BLK, 0)
    rows = row_start + lax.broadcasted_iota(jnp.int32, (BLK, BLK), 0)
    seg_start = jnp.where(rows >= cut, cut, 0)
    columns = lax.broadcasted_iota(jnp.int32, (BLK, BLK), 1)
    q_block = q_ref[...]
    q_heads = [one_head(q_block, head) for head in range(heads)]

    def scores_of(key_block, tops):
        key_start = pl.multiple_of(key_block * BLK, BLK)
        keys = k_ref[pl.ds(key_start, BLK), :]
        places = key_start + columns
        allowed = (places <= rows) & (places >= seg_start)
        offset = pl.multiple_of(jnp.maximum(key_block - block + 1, 0) * BLK, BLK)
        near = key_block - block + 1 >= 0
        new_tops = []
        for head in range(heads):
            raw = dot_nt(q_heads[head], keys)
            far = bias_ref[head : head + 1, 2 * BLK - 1 : 2 * BLK]
            bias = jnp.where(near, tile_ref[head, :, pl.ds(offset, BLK)], far)
            scores = jnp.where(allowed, raw + bias, -1e30)
            score_ref[head, :, pl.ds(key_start, BLK)] = scores
            top = tops[head]
            for lane in range(0, BLK, 128):
                top = jnp.maximum(top, scores[:, lane : lane + 128])
            new_tops.append(top)
        return tuple(new_tops)

    start = tuple(jnp.full((BLK, 128), -1e30, jnp.float32) for _ in range(heads))
    tops = lax.fori_loop(first, block + 1, scores_of, start)
    tops = [jnp.max(top, axis=1, keepdims=True) for top in tops]

    def weighted(key_block, carry):
        total, sums = carry
        key_start = pl.multiple_of(key_block * BLK, BLK)
        new_sums = []
        pieces = []
        values = []
        for head in range(heads):
            soft = jnp.exp(score_ref[head, :, pl.ds(key_start, BLK)] - tops[head])
            part = sums[head]
            for lane in range(0, BLK, 128):
                part = part + soft[:, lane : lane + 128]
            new_sums.append(part)
            pieces.append(soft.astype(jnp.bfloat16))
            values.append(masked_v[head, pl.ds(key_start, BLK), :])
        total = total + dot_nn(
            jnp.concatenate(pieces, axis=1), jnp.concatenate(values, axis=0)
        )
        return total, tuple(new_sums)

    total, sums = lax.fori_loop(
        first,
        block + 1,
        weighted,
        (
            jnp.zeros((BLK, heads * HEAD_LANES), jnp.float32),
            tuple(jnp.zeros((BLK, 128), jnp.float32) for _ in range(heads)),
        ),
    )
    lanes = lax.broadcasted_iota(jnp.int32, (BLK, heads * HEAD_LANES), 1)
    narrow = lax.broadcasted_iota(jnp.int32, (BLK, 128), 1)
    scale = jnp.zeros((BLK, heads * HEAD_LANES), jnp.float32)
    logs = jnp.zeros((BLK, 128), jnp.float32)
    for head in range(heads):
        sum_one = jnp.sum(sums[head], axis=1, keepdims=True)
        scale = jnp.where(lanes // HEAD_LANES == head, 1.0 / sum_one, scale)
        logs = jnp.where(narrow == head, tops[head] + jnp.log(sum_one), logs)
    out_ref[...] = (total * scale).astype(jnp.bfloat16)
    lse_ref[...] = jnp.transpose(logs)[0:8, :]


def attention_forward(cut, queries, keys, values, near_bias):
    length, width = queries.shape
    heads = width // HEAD_LANES
    whole = lambda block, cut: (0, 0)
    return pl.pallas_call(
        attention_forward_kernel,
        grid_spec=pltpu.PrefetchScalarGridSpec(
            num_scalar_prefetch=1,
            grid=(length // BLK,),
            in_specs=[
                pl.BlockSpec((BLK, width), lambda block, cut: (block, 0)),
                pl.BlockSpec((length, width), whole),
                pl.BlockSpec((length, width), whole),
                pl.BlockSpec((8, 2 * BLK), whole),
            ],
            out_specs=[
                pl.BlockSpec((BLK, width), lambda block, cut: (block, 0)),
                pl.BlockSpec((8, BLK), lambda block, cut: (0, block)),
            ],
            scratch_shapes=[
                pltpu.VMEM((heads, BLK, 2 * BLK), jnp.float32),
                pltpu.VMEM((heads, length, width), jnp.bfloat16),
                pltpu.VMEM((heads, BLK, length), jnp.float32),
            ],
        ),
        out_shape=[
            jax.ShapeDtypeStruct((length, width), jnp.bfloat16),
            jax.ShapeDtypeStruct((8, length), jnp.float32),
        ],
        compiler_params=pltpu.CompilerParams(
            dimension_semantics=("arbitrary",), vmem_limit_bytes=48 * 1024 * 1024
        ),
        cost_estimate=pl.CostEstimate(
            flops=8 * length * length * width, bytes_accessed=8 * length * width,
            transcendentals=heads * length * length // 2,
        ),
        name="attention_forward",
    )(cut, queries, keys, values, near_bias)


def attention_backward_kernel(
    cut_ref, q_ref, k_ref, v_ref, grad_ref, att_ref, lse_ref, bias_ref,
    dq_ref, dk_ref, dv_ref, table_ref,
    tile_ref, q_masked, grad_masked, delta_ref, dq_sum, near_sum, far_sum,
):
    heads = q_masked.shape[0]
    block = pl.program_id(0)
    n_blocks = pl.num_programs(0)
    length, width = q_ref.shape
    cut = cut_ref[0]

    @pl.when(block == 0)
    def _():
        product = grad_ref[...].astype(jnp.float32) * att_ref[...].astype(jnp.float32)
        high = product.astype(jnp.bfloat16)
        rest = (product - high.astype(jnp.float32)).astype(jnp.bfloat16)
        row = lax.broadcasted_iota(jnp.int32, (16, width), 0)
        lane = lax.broadcasted_iota(jnp.int32, (16, width), 1)
        pick = jnp.where(lane // HEAD_LANES == row, 1.0, 0.0).astype(jnp.bfloat16)
        delta_ref[...] = (dot_nt(pick, high) + dot_nt(pick, rest))[0:8, :]
        for head in range(heads):
            wide = jnp.broadcast_to(bias_ref[head : head + 1, :], (BLK, 2 * BLK))
            tile_ref[head] = pltpu.roll(wide, 0, 1, stride=1, stride_axis=0)
            q_masked[head] = one_head(q_ref[...], head)
            grad_masked[head] = one_head(grad_ref[...], head)
        dq_sum[...] = jnp.zeros_like(dq_sum)
        near_sum[...] = jnp.zeros_like(near_sum)
        far_sum[...] = jnp.zeros_like(far_sum)

    key_start = pl.multiple_of(block * BLK, BLK)
    keys = k_ref[pl.ds(key_start, BLK), :]
    values = v_ref[pl.ds(key_start, BLK), :]
    keys_t = jnp.transpose(keys)
    places = key_start + lax.broadcasted_iota(jnp.int32, (BLK, BLK), 0)
    columns = lax.broadcasted_iota(jnp.int32, (BLK, BLK), 1)
    last = jnp.where(key_start + BLK <= cut, (cut + BLK - 1) // BLK, n_blocks)

    def one_block(query_block, carry):
        dk, dv = carry
        row_start = pl.multiple_of(query_block * BLK, BLK)
        rows = row_start + columns
        allowed = (places <= rows) & (places >= jnp.where(rows >= cut, cut, 0))
        distance = query_block - block
        near = distance <= 1
        offset = pl.multiple_of(jnp.minimum(distance, 1) * BLK, BLK)
        soft_pieces, grad_pieces, q_pieces, out_pieces = [], [], [], []
        for head in range(heads):
            q_head = q_masked[head, pl.ds(row_start, BLK), :]
            grad_head = grad_masked[head, pl.ds(row_start, BLK), :]
            far = bias_ref[head : head + 1, BLK - 1 : BLK]
            bias = jnp.where(near, tile_ref[head, :, pl.ds(offset, BLK)], far)
            scores = dot_nt(keys, q_head) + bias
            log_total = lse_ref[head : head + 1, pl.ds(row_start, BLK)]
            soft = jnp.exp(jnp.where(allowed, scores - log_total, -1e30))
            grad_soft = dot_nt(values, grad_head)
            delta = delta_ref[head : head + 1, pl.ds(row_start, BLK)]
            grad_scores = soft * (grad_soft - delta)
            grad_low = grad_scores.astype(jnp.bfloat16)

            @pl.when(near)
            def _():
                near_sum[head, :, pl.ds(offset, BLK)] += grad_scores

            @pl.when(jnp.logical_not(near))
            def _():
                far_sum[head] += jnp.sum(
                    grad_scores.reshape(BLK // 8, 8, BLK), axis=0
                )

            spot = slice(head * HEAD_LANES, (head + 1) * HEAD_LANES)
            dq_sum[spot, pl.ds(row_start, BLK)] += dot_nn(keys_t[spot, :], grad_low)
            soft_pieces.append(soft.astype(jnp.bfloat16))
            grad_pieces.append(grad_low)
            q_pieces.append(q_head)
            out_pieces.append(grad_head)
        dv = dv + dot_nn(
            jnp.concatenate(soft_pieces, axis=1), jnp.concatenate(out_pieces, axis=0)
        )
        dk = dk + dot_nn(
            jnp.concatenate(grad_pieces, axis=1), jnp.concatenate(q_pieces, axis=0)
        )
        return dk, dv

    empty = jnp.zeros((BLK, width), jnp.float32)
    dk, dv = lax.fori_loop(block, last, one_block, (empty, empty))
    dk_ref[...] = dk.astype(jnp.bfloat16)
    dv_ref[...] = dv.astype(jnp.bfloat16)

    @pl.when(block == n_blocks - 1)
    def _():
        for query_block in range(length // BLK):
            spot = slice(query_block * BLK, (query_block + 1) * BLK)
            dq_ref[spot, :] = (
                jnp.transpose(dq_sum[:, spot]) * (HEAD_LANES ** -0.5)
            ).astype(jnp.bfloat16)
        for head in range(heads):
            lined = jnp.zeros((8, 2 * BLK), jnp.float32)
            for group in range(BLK // 8):
                piece = near_sum[head, group * 8 : group * 8 + 8, :]
                shift = (2 * BLK - group * 8) % (2 * BLK)
                lined = lined + (pltpu.roll(piece, shift, 1) if shift else piece)
            total = lined[0:1, :]
            for row in range(1, 8):
                total = total + pltpu.roll(lined, 2 * BLK - row, 1)[row : row + 1, :]
            table_ref[head : head + 1, :] = total
            rest = jnp.sum(far_sum[head], axis=0, keepdims=True)
            table_ref[heads + head : heads + head + 1, :] = jnp.concatenate(
                [rest, jnp.zeros_like(rest)], axis=1
            )


def attention_backward(cut, queries, keys, values, grad_att, attended, logs, near_bias):
    length, width = queries.shape
    heads = width // HEAD_LANES
    whole = lambda block, cut: (0, 0)
    full = pl.BlockSpec((length, width), whole)
    return pl.pallas_call(
        attention_backward_kernel,
        grid_spec=pltpu.PrefetchScalarGridSpec(
            num_scalar_prefetch=1,
            grid=(length // BLK,),
            in_specs=[
                full, full, full, full, full,
                pl.BlockSpec((8, length), whole),
                pl.BlockSpec((8, 2 * BLK), whole),
            ],
            out_specs=[
                full,
                pl.BlockSpec((BLK, width), lambda block, cut: (block, 0)),
                pl.BlockSpec((BLK, width), lambda block, cut: (block, 0)),
                pl.BlockSpec((8, 2 * BLK), whole),
            ],
            scratch_shapes=[
                pltpu.VMEM((heads, BLK, 2 * BLK), jnp.float32),
                pltpu.VMEM((heads, length, width), jnp.bfloat16),
                pltpu.VMEM((heads, length, width), jnp.bfloat16),
                pltpu.VMEM((8, length), jnp.float32),
                pltpu.VMEM((width, length), jnp.float32),
                pltpu.VMEM((heads, BLK, 2 * BLK), jnp.float32),
                pltpu.VMEM((heads, 8, BLK), jnp.float32),
            ],
        ),
        out_shape=[
            jax.ShapeDtypeStruct((length, width), jnp.bfloat16),
            jax.ShapeDtypeStruct((length, width), jnp.bfloat16),
            jax.ShapeDtypeStruct((length, width), jnp.bfloat16),
            jax.ShapeDtypeStruct((8, 2 * BLK), jnp.float32),
        ],
        compiler_params=pltpu.CompilerParams(
            dimension_semantics=("arbitrary",), vmem_limit_bytes=56 * 1024 * 1024
        ),
        cost_estimate=pl.CostEstimate(
            flops=20 * length * length * width, bytes_accessed=16 * length * width,
            transcendentals=heads * length * length // 2,
        ),
        name="attention_backward",
    )(cut, queries, keys, values, grad_att, attended, logs, near_bias)


def distance_bias(rel_table, bucket_of):
    hot = (
        bucket_of[:, None] == jnp.arange(rel_table.shape[0], dtype=jnp.int32)[None, :]
    ).astype(jnp.float32)
    by_distance = jnp.einsum(
        "dn,nh->hd", hot, rel_table, precision=HIGHEST_PRECISION,
        preferred_element_type=jnp.float32,
    )
    return hot, by_distance


def near_tables(by_distance):
    heads, reach = by_distance.shape
    far = by_distance[:, reach - 1 :]
    forward = jnp.concatenate(
        [
            jnp.broadcast_to(far, (heads, BLK - reach + 1)),
            by_distance[:, ::-1],
            jnp.broadcast_to(far, (heads, BLK - 1)),
        ],
        axis=1,
    )
    backward = jnp.concatenate(
        [by_distance, jnp.broadcast_to(far, (heads, 2 * BLK - reach))], axis=1
    )
    rows = ((0, 8 - heads), (0, 0))
    return jnp.pad(forward, rows), jnp.pad(backward, rows)


def table_gradient(hot, table_sums, heads):
    reach = hot.shape[0]
    near = table_sums[:heads, : reach - 1]
    far = jnp.sum(table_sums[:heads, reach - 1 :], axis=1) + jnp.sum(
        table_sums[heads : 2 * heads], axis=1
    )
    by_distance = jnp.concatenate([near, far[:, None]], axis=1)
    return jnp.einsum(
        "dn,hd->nh", hot, by_distance, precision=HIGHEST_PRECISION,
        preferred_element_type=jnp.float32,
    )


def body(
    tokens,
    seg_ids,
    bucket_of,
    ln1_gain,
    ln1_bias,
    w_qkv,
    rel_table,
    w_out,
    ln2_gain,
    ln2_bias,
    w_up,
    up_bias,
    w_down,
    down_bias,
    out_grad,
):
    seg_row = seg_ids[0]
    group_len = seg_row.shape[0]
    part_rows = tokens.shape[0]
    model_width = tokens.shape[1]
    local_heads = rel_table.shape[1]
    head_size = w_out.shape[0] // local_heads
    score_scale = head_size ** (-0.5)
    x_part = tokens.astype(jnp.float32)
    normed = lax.all_gather(
        layer_norm(x_part, ln1_gain, ln1_bias).astype(jnp.bfloat16), "mp", axis=0, tiled=True
    )
    queries, keys_all, values_all = [
        jnp.dot(normed, w_qkv[slot_index], preferred_element_type=jnp.float32).astype(jnp.bfloat16)
        for slot_index in range(3)
    ]
    queries = queries * jnp.asarray(score_scale, jnp.bfloat16)
    hot, by_distance = distance_bias(rel_table, bucket_of)
    forward_bias, backward_bias = near_tables(by_distance)
    cut = jnp.sum((seg_row == seg_row[0]).astype(jnp.int32)).reshape(1)
    attended, logs = attention_forward(cut, queries, keys_all, values_all, forward_bias)
    branch = lax.psum_scatter(
        jnp.dot(attended, w_out, preferred_element_type=jnp.float32).astype(jnp.bfloat16),
        "mp",
        scatter_dimension=0,
        tiled=True,
    ).astype(jnp.float32)
    hidden_in = x_part + branch
    second = lax.all_gather(
        layer_norm(hidden_in, ln2_gain, ln2_bias).astype(jnp.bfloat16), "mp", axis=0, tiled=True
    )
    pre_act = jnp.dot(second, w_up, preferred_element_type=jnp.float32) + up_bias
    activated, gelu_pull = jax.vjp(gelu_exact, pre_act)
    activated_low = activated.astype(jnp.bfloat16)
    ff_part = lax.psum_scatter(
        jnp.dot(activated_low, w_down, preferred_element_type=jnp.float32).astype(jnp.bfloat16),
        "mp",
        scatter_dimension=0,
        tiled=True,
    ).astype(jnp.float32)
    layer_out = (hidden_in + ff_part + down_bias).astype(jnp.bfloat16)
    grad_part = out_grad.astype(jnp.float32)
    grad_rows = lax.all_gather(out_grad, "mp", axis=0, tiled=True)
    grad_down = jnp.einsum(
        "tf,td->fd", activated_low, grad_rows, preferred_element_type=jnp.float32
    )
    grad_act = jnp.einsum("td,fd->tf", grad_rows, w_down, preferred_element_type=jnp.float32)
    grad_pre = gelu_pull(grad_act)[0].astype(jnp.bfloat16)
    second_back = lax.all_gather(
        layer_norm(hidden_in, ln2_gain, ln2_bias).astype(jnp.bfloat16), "mp", axis=0, tiled=True
    )
    grad_up = jnp.einsum("td,tf->df", second_back, grad_pre, preferred_element_type=jnp.float32)
    grad_up_bias = jnp.sum(grad_pre, axis=0, dtype=jnp.float32)
    grad_second = lax.psum_scatter(
        jnp.einsum("tf,df->td", grad_pre, w_up, preferred_element_type=jnp.float32).astype(
            jnp.bfloat16
        ),
        "mp",
        scatter_dimension=0,
        tiled=True,
    ).astype(jnp.float32)
    norm2_value, norm2_pull = jax.vjp(layer_norm, hidden_in, ln2_gain, ln2_bias)
    grad_from_norm, grad_ln2_gain, grad_ln2_bias = norm2_pull(grad_second)
    grad_hidden = grad_part + grad_from_norm
    grad_branch = lax.all_gather(grad_hidden.astype(jnp.bfloat16), "mp", axis=0, tiled=True)
    grad_wout = jnp.einsum("tc,td->cd", attended, grad_branch, preferred_element_type=jnp.float32)
    grad_att = jnp.einsum(
        "td,cd->tc", grad_branch, w_out, preferred_element_type=jnp.float32
    ).astype(jnp.bfloat16)
    grad_queries, grad_keys, grad_values, table_sums = attention_backward(
        cut, queries, keys_all, values_all, grad_att, attended, logs, backward_bias
    )
    grad_table = table_gradient(hot, table_sums, local_heads)
    grad_proj = [grad_queries, grad_keys, grad_values]
    normed_back = lax.all_gather(
        layer_norm(x_part, ln1_gain, ln1_bias).astype(jnp.bfloat16), "mp", axis=0, tiled=True
    )
    grad_qkv = jnp.stack(
        [
            jnp.einsum("tc,td->cd", normed_back, grad_one, preferred_element_type=jnp.float32)
            for grad_one in grad_proj
        ]
    )
    running = jnp.zeros((part_rows * lax.axis_size("mp"), model_width), jnp.float32)
    for slot_index in range(3):
        running = running + jnp.einsum(
            "td,cd->tc",
            grad_proj[slot_index],
            w_qkv[slot_index],
            preferred_element_type=jnp.float32,
        )
    grad_first = lax.psum_scatter(
        running.astype(jnp.bfloat16), "mp", scatter_dimension=0, tiled=True
    ).astype(jnp.float32)
    norm1_value, norm1_pull = jax.vjp(layer_norm, x_part, ln1_gain, ln1_bias)
    grad_from_first, grad_ln1_gain, grad_ln1_bias = norm1_pull(grad_first)
    grad_tokens = (grad_hidden + grad_from_first).astype(jnp.bfloat16)
    grad_down_bias = jnp.sum(grad_part, axis=0)
    grad_qkv, grad_table, grad_wout, grad_up, grad_up_bias, grad_down = lax.psum(
        (grad_qkv, grad_table, grad_wout, grad_up, grad_up_bias, grad_down), "dp"
    )
    grad_ln1_gain, grad_ln1_bias, grad_ln2_gain, grad_ln2_bias, grad_down_bias = lax.psum(
        (grad_ln1_gain, grad_ln1_bias, grad_ln2_gain, grad_ln2_bias, grad_down_bias), ("dp", "mp")
    )
    return (
        layer_out,
        grad_tokens,
        grad_ln1_gain,
        grad_ln1_bias,
        grad_qkv,
        grad_table,
        grad_wout,
        grad_ln2_gain,
        grad_ln2_bias,
        grad_up,
        grad_up_bias,
        grad_down,
        grad_down_bias,
    )


def solution(mesh):
    return jax.shard_map(
        body,
        mesh=mesh,
        in_specs=(
            P(("dp", "mp"), None),
            P("dp", None),
            P(),
            P(),
            P(),
            P(None, None, "mp"),
            P(None, "mp"),
            P("mp", None),
            P(),
            P(),
            P(None, "mp"),
            P("mp"),
            P("mp", None),
            P(),
            P(("dp", "mp"), None),
        ),
        out_specs=(
            P(("dp", "mp"), None),
            P(("dp", "mp"), None),
            P(),
            P(),
            P(None, None, "mp"),
            P(None, "mp"),
            P("mp", None),
            P(),
            P(),
            P(None, "mp"),
            P("mp"),
            P("mp", None),
            P(),
        ),
        check_vma=False,
    )
```

```python
import functools

import jax
import jax.numpy as jnp
from jax import lax
from jax.experimental import pallas as pl
from jax.experimental.pallas import tpu as pltpu
from jax.sharding import Mesh, PartitionSpec as P

EPSILON = 1e-05
HIGHEST_PRECISION = lax.Precision.HIGHEST
TIE = 1
BLK = 256
HEAD_LANES = 64
NEAR = 128


def head_mask(rows, width, head, axis):
    place = lax.broadcasted_iota(jnp.int32, (rows, width), axis)
    return (place >= head * HEAD_LANES) & (place < (head + 1) * HEAD_LANES)


def one_head(value, head):
    keep = head_mask(value.shape[0], value.shape[1], head, 1)
    return jnp.where(keep, value, jnp.zeros_like(value))


def scaled(queries):
    return queries * jnp.asarray(HEAD_LANES ** -0.5, queries.dtype)


def dot_nt(left, right):
    return lax.dot_general(
        left, right, (((1,), (1,)), ((), ())), preferred_element_type=jnp.float32
    )


def dot_nn(left, right):
    return lax.dot_general(
        left, right, (((1,), (0,)), ((), ())), preferred_element_type=jnp.float32
    )


def attention_forward_kernel(
    cut_ref, qkv_ref, bias_ref, out_ref, lse_ref, tile_ref, masked_v, score_ref
):
    heads = masked_v.shape[0]
    width = out_ref.shape[1]
    block = pl.program_id(0)
    cut = cut_ref[0]

    @pl.when(block == 0)
    def _():
        for head in range(heads):
            wide = jnp.broadcast_to(bias_ref[head : head + 1, :], (BLK, 2 * BLK))
            tile_ref[head] = pltpu.roll(wide, 0, 1, stride=1, stride_axis=0)
            masked_v[head] = one_head(qkv_ref[:, 2 * width :], head)

    row_start = block * BLK
    first = jnp.where(row_start >= cut, cut // BLK, 0)
    rows = row_start + lax.broadcasted_iota(jnp.int32, (BLK, BLK), 0)
    seg_start = jnp.where(rows >= cut, cut, 0)
    columns = lax.broadcasted_iota(jnp.int32, (BLK, BLK), 1)
    q_block = scaled(qkv_ref[pl.ds(pl.multiple_of(row_start, BLK), BLK), 0:width])
    q_heads = [one_head(q_block, head) for head in range(heads)]

    def scores_of(key_block, tops):
        key_start = pl.multiple_of(key_block * BLK, BLK)
        keys = qkv_ref[pl.ds(key_start, BLK), width : 2 * width]
        places = key_start + columns
        allowed = (places <= rows) & (places >= seg_start)
        offset = pl.multiple_of(jnp.maximum(key_block - block + 1, 0) * BLK, BLK)
        near = key_block - block + 1 >= 0
        new_tops = []
        for head in range(heads):
            raw = dot_nt(q_heads[head], keys)
            far = bias_ref[head : head + 1, 2 * BLK - 1 : 2 * BLK]
            bias = jnp.where(near, tile_ref[head, :, pl.ds(offset, BLK)], far)
            scores = jnp.where(allowed, raw + bias, -1e30)
            score_ref[head, :, pl.ds(key_start, BLK)] = scores
            top = tops[head]
            for lane in range(0, BLK, 128):
                top = jnp.maximum(top, scores[:, lane : lane + 128])
            new_tops.append(top)
        return tuple(new_tops)

    start = tuple(jnp.full((BLK, 128), -1e30, jnp.float32) for _ in range(heads))
    tops = lax.fori_loop(first, block + 1, scores_of, start)
    tops = [jnp.max(top, axis=1, keepdims=True) for top in tops]

    def weighted(key_block, carry):
        total, sums = carry
        key_start = pl.multiple_of(key_block * BLK, BLK)
        new_sums = []
        pieces = []
        values = []
        for head in range(heads):
            soft = jnp.exp(score_ref[head, :, pl.ds(key_start, BLK)] - tops[head])
            part = sums[head]
            for lane in range(0, BLK, 128):
                part = part + soft[:, lane : lane + 128]
            new_sums.append(part)
            pieces.append(soft.astype(jnp.bfloat16))
            values.append(masked_v[head, pl.ds(key_start, BLK), :])
        total = total + dot_nn(
            jnp.concatenate(pieces, axis=1), jnp.concatenate(values, axis=0)
        )
        return total, tuple(new_sums)

    total, sums = lax.fori_loop(
        first,
        block + 1,
        weighted,
        (
            jnp.zeros((BLK, heads * HEAD_LANES), jnp.float32),
            tuple(jnp.zeros((BLK, 128), jnp.float32) for _ in range(heads)),
        ),
    )
    lanes = lax.broadcasted_iota(jnp.int32, (BLK, heads * HEAD_LANES), 1)
    narrow = lax.broadcasted_iota(jnp.int32, (BLK, 128), 1)
    scale = jnp.zeros((BLK, heads * HEAD_LANES), jnp.float32)
    logs = jnp.zeros((BLK, 128), jnp.float32)
    for head in range(heads):
        sum_one = jnp.sum(sums[head], axis=1, keepdims=True)
        scale = jnp.where(lanes // HEAD_LANES == head, 1.0 / sum_one, scale)
        logs = jnp.where(narrow == head, tops[head] + jnp.log(sum_one), logs)
    out_ref[...] = (total * scale).astype(jnp.bfloat16)
    lse_ref[...] = jnp.transpose(logs)[0:8, :]


def attention_forward(cut, projected, near_bias):
    length, width = projected.shape[0], projected.shape[1] // 3
    heads = width // HEAD_LANES
    whole = lambda block, cut: (0, 0)
    return pl.pallas_call(
        attention_forward_kernel,
        grid_spec=pltpu.PrefetchScalarGridSpec(
            num_scalar_prefetch=1,
            grid=(length // BLK,),
            in_specs=[
                pl.BlockSpec((length, 3 * width), whole),
                pl.BlockSpec((8, 2 * BLK), whole),
            ],
            out_specs=[
                pl.BlockSpec((BLK, width), lambda block, cut: (block, 0)),
                pl.BlockSpec((8, BLK), lambda block, cut: (0, block)),
            ],
            scratch_shapes=[
                pltpu.VMEM((heads, BLK, 2 * BLK), jnp.float32),
                pltpu.VMEM((heads, length, width), jnp.bfloat16),
                pltpu.VMEM((heads, BLK, length), jnp.float32),
            ],
        ),
        out_shape=[
            jax.ShapeDtypeStruct((length, width), jnp.bfloat16),
            jax.ShapeDtypeStruct((8, length), jnp.float32),
        ],
        compiler_params=pltpu.CompilerParams(
            dimension_semantics=("arbitrary",), vmem_limit_bytes=48 * 1024 * 1024
        ),
        cost_estimate=pl.CostEstimate(
            flops=8 * length * length * width, bytes_accessed=8 * length * width,
            transcendentals=heads * length * length // 2,
        ),
        name="attention_forward",
    )(cut, projected, near_bias)


def attention_backward_kernel(
    cut_ref, qkv_ref, grad_ref, att_ref, lse_ref, bias_ref, dqkv_ref, table_ref,
    tile_ref, q_masked, grad_masked, delta_ref, dq_sum, near_sum, far_sum,
):
    heads = q_masked.shape[0]
    block = pl.program_id(0)
    n_blocks = pl.num_programs(0)
    length, width = grad_ref.shape
    cut = cut_ref[0]

    @pl.when(block == 0)
    def _():
        product = grad_ref[...].astype(jnp.float32) * att_ref[...].astype(jnp.float32)
        high = product.astype(jnp.bfloat16)
        rest = (product - high.astype(jnp.float32)).astype(jnp.bfloat16)
        row = lax.broadcasted_iota(jnp.int32, (16, width), 0)
        lane = lax.broadcasted_iota(jnp.int32, (16, width), 1)
        pick = jnp.where(lane // HEAD_LANES == row, 1.0, 0.0).astype(jnp.bfloat16)
        delta_ref[...] = (dot_nt(pick, high) + dot_nt(pick, rest))[0:8, :]
        for head in range(heads):
            wide = jnp.broadcast_to(bias_ref[head : head + 1, :], (BLK, 2 * BLK))
            tile_ref[head] = pltpu.roll(wide, 0, 1, stride=1, stride_axis=0)
            q_masked[head] = one_head(scaled(qkv_ref[:, 0:width]), head)
            grad_masked[head] = one_head(grad_ref[...], head)
        dq_sum[...] = jnp.zeros_like(dq_sum)
        near_sum[...] = jnp.zeros_like(near_sum)
        far_sum[...] = jnp.zeros_like(far_sum)

    key_start = pl.multiple_of(block * BLK, BLK)
    keys = qkv_ref[pl.ds(key_start, BLK), width : 2 * width]
    values = qkv_ref[pl.ds(key_start, BLK), 2 * width :]
    keys_t = jnp.transpose(keys)
    places = key_start + lax.broadcasted_iota(jnp.int32, (BLK, BLK), 0)
    columns = lax.broadcasted_iota(jnp.int32, (BLK, BLK), 1)
    last = jnp.where(key_start + BLK <= cut, (cut + BLK - 1) // BLK, n_blocks)

    def one_block(query_block, carry):
        dk, dv = carry
        row_start = pl.multiple_of(query_block * BLK, BLK)
        rows = row_start + columns
        allowed = (places <= rows) & (places >= jnp.where(rows >= cut, cut, 0))
        distance = query_block - block
        near = distance <= 1
        offset = pl.multiple_of(jnp.minimum(distance, 1) * BLK, BLK)
        soft_pieces, grad_pieces, q_pieces, out_pieces = [], [], [], []
        for head in range(heads):
            q_head = q_masked[head, pl.ds(row_start, BLK), :]
            grad_head = grad_masked[head, pl.ds(row_start, BLK), :]
            far = bias_ref[head : head + 1, BLK - 1 : BLK]
            bias = jnp.where(near, tile_ref[head, :, pl.ds(offset, BLK)], far)
            scores = dot_nt(keys, q_head) + bias
            log_total = lse_ref[head : head + 1, pl.ds(row_start, BLK)]
            soft = jnp.exp(jnp.where(allowed, scores - log_total, -1e30))
            grad_soft = dot_nt(values, grad_head)
            delta = delta_ref[head : head + 1, pl.ds(row_start, BLK)]
            grad_scores = soft * (grad_soft - delta)
            grad_low = grad_scores.astype(jnp.bfloat16)

            @pl.when(near)
            def _():
                near_sum[head, :, pl.ds(offset, BLK)] += grad_scores

            @pl.when(jnp.logical_not(near))
            def _():
                far_sum[head] += jnp.sum(
                    grad_scores.reshape(BLK // 8, 8, BLK), axis=0
                )

            spot = slice(head * HEAD_LANES, (head + 1) * HEAD_LANES)
            dq_sum[spot, pl.ds(row_start, BLK)] += dot_nn(keys_t[spot, :], grad_low)
            soft_pieces.append(soft.astype(jnp.bfloat16))
            grad_pieces.append(grad_low)
            q_pieces.append(q_head)
            out_pieces.append(grad_head)
        dv = dv + dot_nn(
            jnp.concatenate(soft_pieces, axis=1), jnp.concatenate(out_pieces, axis=0)
        )
        dk = dk + dot_nn(
            jnp.concatenate(grad_pieces, axis=1), jnp.concatenate(q_pieces, axis=0)
        )
        return dk, dv

    empty = jnp.zeros((BLK, width), jnp.float32)
    dk, dv = lax.fori_loop(block, last, one_block, (empty, empty))
    dqkv_ref[pl.ds(key_start, BLK), width : 2 * width] = dk.astype(jnp.bfloat16)
    dqkv_ref[pl.ds(key_start, BLK), 2 * width :] = dv.astype(jnp.bfloat16)

    @pl.when(block == n_blocks - 1)
    def _():
        for query_block in range(length // BLK):
            spot = slice(query_block * BLK, (query_block + 1) * BLK)
            dqkv_ref[spot, 0:width] = (
                jnp.transpose(dq_sum[:, spot]) * (HEAD_LANES ** -0.5)
            ).astype(jnp.bfloat16)
        for head in range(heads):
            lined = jnp.zeros((8, 2 * BLK), jnp.float32)
            for group in range(BLK // 8):
                piece = near_sum[head, group * 8 : group * 8 + 8, :]
                shift = (2 * BLK - group * 8) % (2 * BLK)
                lined = lined + (pltpu.roll(piece, shift, 1) if shift else piece)
            total = lined[0:1, :]
            for row in range(1, 8):
                total = total + pltpu.roll(lined, 2 * BLK - row, 1)[row : row + 1, :]
            table_ref[head : head + 1, :] = total
            rest = jnp.sum(far_sum[head], axis=0, keepdims=True)
            table_ref[heads + head : heads + head + 1, :] = jnp.concatenate(
                [rest, jnp.zeros_like(rest)], axis=1
            )


def attention_backward(cut, projected, grad_att, attended, logs, near_bias):
    length, width = attended.shape
    heads = width // HEAD_LANES
    whole = lambda block, cut: (0, 0)
    full = pl.BlockSpec((length, width), whole)
    return pl.pallas_call(
        attention_backward_kernel,
        grid_spec=pltpu.PrefetchScalarGridSpec(
            num_scalar_prefetch=1,
            grid=(length // BLK,),
            in_specs=[
                pl.BlockSpec((length, 3 * width), whole), full, full,
                pl.BlockSpec((8, length), whole),
                pl.BlockSpec((8, 2 * BLK), whole),
            ],
            out_specs=[
                pl.BlockSpec((length, 3 * width), whole),
                pl.BlockSpec((8, 2 * BLK), whole),
            ],
            scratch_shapes=[
                pltpu.VMEM((heads, BLK, 2 * BLK), jnp.float32),
                pltpu.VMEM((heads, length, width), jnp.bfloat16),
                pltpu.VMEM((heads, length, width), jnp.bfloat16),
                pltpu.VMEM((8, length), jnp.float32),
                pltpu.VMEM((width, length), jnp.float32),
                pltpu.VMEM((heads, BLK, 2 * BLK), jnp.float32),
                pltpu.VMEM((heads, 8, BLK), jnp.float32),
            ],
        ),
        out_shape=[
            jax.ShapeDtypeStruct((length, 3 * width), jnp.bfloat16),
            jax.ShapeDtypeStruct((8, 2 * BLK), jnp.float32),
        ],
        compiler_params=pltpu.CompilerParams(
            dimension_semantics=("arbitrary",), vmem_limit_bytes=56 * 1024 * 1024
        ),
        cost_estimate=pl.CostEstimate(
            flops=20 * length * length * width, bytes_accessed=16 * length * width,
            transcendentals=heads * length * length // 2,
        ),
        name="attention_backward",
    )(cut, projected, grad_att, attended, logs, near_bias)


def distance_bias(rel_table, bucket_of):
    hot = (
        bucket_of[:, None] == jnp.arange(rel_table.shape[0], dtype=jnp.int32)[None, :]
    ).astype(jnp.float32)
    by_distance = jnp.einsum(
        "dn,nh->hd", hot, rel_table, precision=HIGHEST_PRECISION,
        preferred_element_type=jnp.float32,
    )
    return hot, by_distance


def near_tables(by_distance):
    heads, reach = by_distance.shape
    far = by_distance[:, reach - 1 :]
    forward = jnp.concatenate(
        [
            jnp.broadcast_to(far, (heads, BLK - reach + 1)),
            by_distance[:, ::-1],
            jnp.broadcast_to(far, (heads, BLK - 1)),
        ],
        axis=1,
    )
    backward = jnp.concatenate(
        [by_distance, jnp.broadcast_to(far, (heads, 2 * BLK - reach))], axis=1
    )
    rows = ((0, 8 - heads), (0, 0))
    return jnp.pad(forward, rows), jnp.pad(backward, rows)


def table_gradient(hot, table_sums, heads):
    reach = hot.shape[0]
    near = table_sums[:heads, : reach - 1]
    far = jnp.sum(table_sums[:heads, reach - 1 :], axis=1) + jnp.sum(
        table_sums[heads : 2 * heads], axis=1
    )
    by_distance = jnp.concatenate([near, far[:, None]], axis=1)
    return jnp.einsum(
        "dn,hd->nh", hot, by_distance, precision=HIGHEST_PRECISION,
        preferred_element_type=jnp.float32,
    )


TEAM = 4


def place_of(axis):
    return lax.axis_index(axis)


def flip(value, axis, bit):
    size = lax.axis_size(axis)
    return lax.ppermute(value, axis, [(i, i ^ bit) for i in range(size)])


def halve(value, dim, axis, bit):
    mine = (lax.axis_index(axis) // bit) % 2
    keep = lax.dynamic_index_in_dim(value, mine, dim, keepdims=False)
    send = lax.dynamic_index_in_dim(value, 1 - mine, dim, keepdims=False)
    received = flip(send.astype(jnp.bfloat16), axis, bit)
    return (keep.astype(jnp.float32) + received.astype(jnp.float32)).astype(jnp.bfloat16)


def double(value, axis, bit):
    mine = (lax.axis_index(axis) // bit) % 2
    other = flip(value, axis, bit)
    pair = jnp.zeros((2,) + value.shape, value.dtype)
    pair = lax.dynamic_update_index_in_dim(pair, value, mine, 0)
    return lax.dynamic_update_index_in_dim(pair, other, 1 - mine, 0)


def bits_of(size):
    bits = []
    bit = 1
    while bit < size:
        bits.append(bit)
        bit *= 2
    return bits


def chain_gather(own):
    size = lax.axis_size("mp")
    spot = lax.axis_index("mp")
    rows = own.shape[0]
    right = left = own
    rights, lefts = {}, {}
    for step in range(1, size):
        right = lax.ppermute(right, "mp", [(i, i + 1) for i in range(step - 1, size - 1)])
        left = lax.ppermute(left, "mp", [(i, i - 1) for i in range(1, size - step + 1)])
        rights[step], lefts[step] = right, left
    whole = jnp.zeros((size * rows,) + own.shape[1:], own.dtype)
    whole = lax.dynamic_update_slice_in_dim(whole, own, spot * rows, 0)
    for step in range(1, size):
        block = rights[step] + lefts[size - step]
        source = lax.rem(spot + size - step, size)
        whole = lax.dynamic_update_slice_in_dim(whole, block, source * rows, 0)
    return whole, rights


def chain_scatter(value):
    size = lax.axis_size("mp")
    spot = lax.axis_index("mp")
    rows = value.shape[0] // size

    def block(place):
        return lax.dynamic_slice_in_dim(value, place * rows, rows, 0).astype(jnp.float32)

    from_left = from_right = None
    for step in range(1, size):
        reach = size - step
        to_right = block(jnp.minimum(spot + reach, size - 1))
        to_left = block(jnp.maximum(spot - reach, 0))
        if from_left is not None:
            to_right = to_right + from_left.astype(jnp.float32)
            to_left = to_left + from_right.astype(jnp.float32)
        from_left = lax.ppermute(
            to_right.astype(jnp.bfloat16), "mp", [(i, i + 1) for i in range(step)]
        )
        from_right = lax.ppermute(
            to_left.astype(jnp.bfloat16), "mp", [(i, i - 1) for i in range(size - step, size)]
        )
    return block(spot) + from_left.astype(jnp.float32) + from_right.astype(jnp.float32)


def swap_over_chain(stack):
    size = lax.axis_size("mp")
    spot = lax.axis_index("mp")
    own = lax.dynamic_index_in_dim(stack, spot, 0, keepdims=True)
    result = lax.dynamic_update_slice_in_dim(jnp.zeros_like(stack), own, spot, 0)
    for step in [2, 1, 3] if size == 4 else range(1, size):
        send = lax.dynamic_index_in_dim(stack, lax.rem(spot + step, size), 0, keepdims=True)
        received = lax.ppermute(send, "mp", [(i, (i + step) % size) for i in range(size)])
        result = lax.dynamic_update_slice_in_dim(
            result, received, lax.rem(spot + size - step, size), 0
        )
    return result


def team_gather(own):
    core = flip(own, "team", 1)
    across = flip(own, "team", 2)
    return jnp.concatenate([own, core], axis=0), jnp.concatenate(
        [across, flip(across, "team", 1)], axis=0
    )


def normalize(inputs):
    center = inputs - jnp.mean(inputs, axis=-1, keepdims=True)
    spread = jnp.mean(center * center, axis=-1, keepdims=True)
    inverse = lax.rsqrt(spread + EPSILON)
    return center * inverse, inverse


def normalize_backward(grad, gain, unit, inverse):
    scaled_grad = grad * gain
    middle = jnp.mean(scaled_grad, axis=-1, keepdims=True)
    along = jnp.mean(scaled_grad * unit, axis=-1, keepdims=True)
    return (scaled_grad - middle - unit * along) * inverse


def dot_tn(left, right):
    return lax.dot_general(
        left, right, (((0,), (0,)), ((), ())), preferred_element_type=jnp.float32
    )


def feed_kernel(
    weight_ref, bias_ref, second_ref, grad_ref,
    act_ref, pre_ref, back_ref, out_ref, sum_ref, back_sum, out_sum, *, unit,
):
    step = pl.program_id(0)
    parts, copies, _, depth = weight_ref.shape
    hidden = parts * copies * unit
    w_up = weight_ref[:, :, 0:unit, :].reshape(hidden, depth)
    w_down = weight_ref[:, :, unit : 2 * unit, :].reshape(hidden, depth)
    pre = dot_nt(second_ref[...], w_up) + bias_ref[...]
    grad_act = dot_nt(grad_ref[...], w_down)
    cdf = 0.5 + 0.5 * lax.erf(pre * 0.7071067811865476)
    pdf = jnp.exp(pre * pre * -0.5) * 0.3989422804014327
    active = (pre * cdf).astype(jnp.bfloat16)
    grad_pre = ((cdf + pre * pdf) * grad_act).astype(jnp.bfloat16)
    act_ref[...] = active
    pre_ref[...] = grad_pre
    sum_ref[...] = jnp.sum(grad_pre.astype(jnp.float32), axis=0, keepdims=True)
    back = dot_nn(grad_pre, w_up)
    out = dot_nn(active, w_down)

    @pl.when(step == 0)
    def _():
        back_sum[...] = back
        out_sum[...] = out

    @pl.when(step > 0)
    def _():
        back_sum[...] += back
        out_sum[...] += out

    @pl.when(step == pl.num_programs(0) - 1)
    def _():
        back_ref[...] = back_sum[...].astype(jnp.bfloat16)
        out_ref[...] = out_sum[...].astype(jnp.bfloat16)


def feed_forward(weights, bias_row, second, grad, unit):
    parts, copies, per, depth = weights.shape
    rows = second.shape[0]
    width = parts * copies * unit
    take = 2 if parts % 2 == 0 else 1
    hidden = take * copies * unit
    whole = pl.BlockSpec((rows, depth), lambda step: (0, 0))
    column = pl.BlockSpec((rows, hidden), lambda step: (0, step))
    line = pl.BlockSpec((1, hidden), lambda step: (0, step))
    return pl.pallas_call(
        functools.partial(feed_kernel, unit=unit),
        grid=(parts // take,),
        in_specs=[
            pl.BlockSpec((take, copies, per, depth), lambda step: (step, 0, 0, 0)),
            line, whole, whole,
        ],
        out_specs=[column, column, whole, whole, line],
        out_shape=[
            jax.ShapeDtypeStruct((rows, width), jnp.bfloat16),
            jax.ShapeDtypeStruct((rows, width), jnp.bfloat16),
            jax.ShapeDtypeStruct((rows, depth), jnp.bfloat16),
            jax.ShapeDtypeStruct((rows, depth), jnp.bfloat16),
            jax.ShapeDtypeStruct((1, width), jnp.float32),
        ],
        scratch_shapes=[
            pltpu.VMEM((rows, depth), jnp.float32),
            pltpu.VMEM((rows, depth), jnp.float32),
        ],
        compiler_params=pltpu.CompilerParams(
            dimension_semantics=("arbitrary",), vmem_limit_bytes=56 * 1024 * 1024
        ),
        cost_estimate=pl.CostEstimate(
            flops=8 * rows * width * depth, bytes_accessed=8 * rows * depth + 4 * width * depth,
            transcendentals=2 * rows * width,
        ),
        name="feed_forward",
    )(weights, bias_row, second, grad)


def weight_grad_kernel(
    act_a, act_b, pre_a, pre_b, second_a, second_b, grad_a, grad_b, out_ref
):
    _, copies, _, unit, depth = out_ref.shape
    up = dot_tn(pre_a[...], second_a[...]) + dot_tn(pre_b[...], second_b[...])
    out_ref[0, :, 0] = up.astype(jnp.bfloat16).reshape(copies, unit, depth)
    down = dot_tn(act_a[...], grad_a[...]) + dot_tn(act_b[...], grad_b[...])
    out_ref[0, :, 1] = down.astype(jnp.bfloat16).reshape(copies, unit, depth)


def weight_grads(acts, pres, seconds, grads, parts, copies):
    rows, width = acts[0].shape
    depth = seconds[0].shape[1]
    unit = width // (parts * copies)
    column = pl.BlockSpec((rows, width // parts), lambda step: (0, step))
    whole = pl.BlockSpec((rows, depth), lambda step: (0, 0))
    return pl.pallas_call(
        weight_grad_kernel,
        grid=(parts,),
        in_specs=[column] * 4 + [whole] * 4,
        out_specs=pl.BlockSpec((1, copies, 2, unit, depth), lambda step: (step, 0, 0, 0, 0)),
        out_shape=jax.ShapeDtypeStruct((parts, copies, 2, unit, depth), jnp.bfloat16),
        compiler_params=pltpu.CompilerParams(
            dimension_semantics=("arbitrary",), vmem_limit_bytes=56 * 1024 * 1024
        ),
        cost_estimate=pl.CostEstimate(
            flops=8 * rows * width * depth, bytes_accessed=16 * rows * depth + 4 * width * depth,
            transcendentals=0,
        ),
        name="weight_grads",
    )(*acts, *pres, *seconds, *grads)


def body(
    tokens, seg_ids, bucket_of, ln1_gain, ln1_bias, w_qkv, rel_table, w_out,
    ln2_gain, ln2_bias, w_up, up_bias, w_down, down_bias, out_grad,
):
    low = jnp.bfloat16
    wide = jnp.float32
    copies = lax.axis_size("copy")
    parts = lax.axis_size("mp")
    copy = lax.axis_index("copy")
    member = lax.axis_index("team")
    part = lax.axis_index("mp")
    core = member % 2
    rows, depth = tokens.shape
    heads = rel_table.shape[1]
    head_width = w_out.shape[0]
    team_units = w_up.shape[1] // TEAM
    unit = team_units // copies
    seg_row = seg_ids[0]

    x_part = tokens.astype(wide)
    unit1, inverse1 = normalize(x_part)
    normed, rights = chain_gather((unit1 * ln1_gain + ln1_bias).astype(low))

    spot = member * team_units + copy * unit
    out_rows = head_width // (2 * copies)
    piece = jnp.concatenate(
        [
            jnp.transpose(lax.dynamic_slice_in_dim(w_up, spot, unit, 1)),
            lax.dynamic_slice_in_dim(w_down, spot, unit, 0),
            lax.dynamic_slice_in_dim(w_out, (copy * 2 + core) * out_rows, out_rows, 0),
        ],
        axis=0,
    )
    piece = lax.optimization_barrier((piece, rights[TIE]))[0]
    weights = lax.all_gather(piece, ("mp", "copy"), axis=0, tiled=False).reshape(
        parts, copies, piece.shape[0], depth
    )
    own_out = weights[:, :, 2 * unit :, :]
    other_out = flip(own_out, "team", 1)
    is_first = core == 0
    w_out_full = jnp.stack(
        [jnp.where(is_first, own_out, other_out), jnp.where(is_first, other_out, own_out)], axis=2
    ).reshape(parts, head_width, depth)
    bias_all = up_bias[None]
    for bit in bits_of(parts):
        bias_all = double(bias_all, "mp", bit).reshape(-1, up_bias.shape[0])
    bias_row = lax.dynamic_slice_in_dim(bias_all, member * team_units, team_units, 1).reshape(1, -1)
    grad_near, grad_far = team_gather(out_grad)

    w_cat = jnp.transpose(w_qkv, (1, 0, 2)).reshape(depth, -1)
    projected = jnp.dot(normed, w_cat, preferred_element_type=wide).astype(low)
    hot, by_distance = distance_bias(rel_table, bucket_of)
    forward_bias, backward_bias = near_tables(by_distance)
    cut = jnp.sum((seg_row == seg_row[0]).astype(jnp.int32)).reshape(1)
    attended, logs = attention_forward(cut, projected, forward_bias)
    own_rows = swap_over_chain(attended.reshape(parts, rows, head_width))
    branch = jnp.einsum("jtc,jcd->td", own_rows, w_out_full, preferred_element_type=wide)
    hidden_in = x_part + branch
    unit2, inverse2 = normalize(hidden_in)
    second = (unit2 * ln2_gain + ln2_bias).astype(low)
    second_near, second_far = team_gather(second)

    act_near, pre_near, back_near, feed_near, sums_near = feed_forward(
        weights, bias_row, second_near, grad_near, unit
    )
    act_far, pre_far, back_far, feed_far, sums_far = feed_forward(
        weights, bias_row, second_far, grad_far, unit
    )
    beside = flip(back_near[rows:], "team", 1)
    onward = back_far[:rows].astype(wide) + flip(back_far[rows:], "team", 1).astype(wide)
    across = flip(onward.astype(low), "team", 2)
    grad_second = back_near[:rows].astype(wide) + beside.astype(wide) + across.astype(wide)
    grad_part = out_grad.astype(wide)
    grad_hidden = grad_part + normalize_backward(grad_second, ln2_gain, unit2, inverse2)
    grad_branch = grad_hidden.astype(low)
    grad_stack = jnp.einsum("td,jcd->jtc", grad_branch, w_out_full, preferred_element_type=wide)
    grad_att = swap_over_chain(grad_stack.astype(low)).reshape(parts * rows, head_width)

    ff_grads = weight_grads(
        (act_near, act_far), (pre_near, pre_far), (second_near, second_far),
        (grad_near, grad_far), parts, copies,
    )
    ff_piece = lax.psum_scatter(
        ff_grads.reshape(parts * copies, 2 * unit, depth), ("mp", "copy"),
        scatter_dimension=0, tiled=False,
    )
    ff_all = lax.all_gather(ff_piece, ("team", "copy"), axis=0, tiled=False).reshape(
        TEAM * copies, 2, unit, depth
    )
    grad_up = jnp.transpose(ff_all[:, 0].reshape(TEAM * team_units, depth)).astype(wide)
    grad_down = ff_all[:, 1].reshape(TEAM * team_units, depth).astype(wide)

    beside = flip(jnp.stack([feed_far[rows:], feed_near[rows:]]), "team", 1)
    onward = feed_far[:rows].astype(wide) + beside[0].astype(wide)
    feed_own = (
        feed_near[:rows].astype(wide) + beside[1].astype(wide)
        + flip(onward.astype(low), "team", 2).astype(wide)
    )
    layer_out = (hidden_in + feed_own + down_bias).astype(low)

    wout_grad = jnp.einsum("jtc,td->jcd", own_rows, grad_branch, preferred_element_type=wide)
    wout_grad = wout_grad.astype(low).reshape(parts, 2, 2, copies, -1, depth)
    wout_grad = halve(halve(wout_grad, 1, "team", 1), 1, "team", 2)
    for bit in reversed(bits_of(copies)):
        wout_grad = halve(
            wout_grad.reshape((parts, 2, -1) + wout_grad.shape[2:]), 1, "copy", bit
        )
    wout_grad = wout_grad.reshape(parts, -1, depth)
    for bit in reversed(bits_of(parts)):
        wout_grad = halve(wout_grad.reshape((2, -1) + wout_grad.shape[1:]), 0, "mp", bit)
    wout_grad = wout_grad.reshape(-1, depth)

    dqkv, table_sums = attention_backward(
        cut, projected, grad_att, attended, logs, backward_bias
    )
    running = lax.dot_general(
        dqkv, w_cat, (((1,), (1,)), ((), ())), preferred_element_type=wide
    ).astype(low)
    grad_first = chain_scatter(running)
    grad_first_norm = normalize_backward(grad_first, ln1_gain, unit1, inverse1)
    grad_tokens = (grad_hidden + grad_first_norm).astype(low)

    qkv_grad = dot_tn(normed, dqkv).astype(low)
    qkv_grad = qkv_grad.reshape(2, 2, copies, -1, qkv_grad.shape[1])
    qkv_grad = halve(halve(qkv_grad, 0, "team", 1), 0, "team", 2)
    for bit in reversed(bits_of(copies)):
        qkv_grad = halve(qkv_grad.reshape((2, -1) + qkv_grad.shape[1:]), 0, "copy", bit)
    qkv_grad = qkv_grad.reshape(-1, 3 * head_width)
    flat = jnp.concatenate([qkv_grad.reshape(-1, head_width), wout_grad.reshape(-1, head_width)])
    for bit in bits_of(copies):
        flat = double(flat, "copy", bit)
    flat = double(double(flat, "team", 2), "team", 1)
    flat = flat.reshape(TEAM * copies, -1, head_width)
    qkv_rows = qkv_grad.shape[0] * 3
    grad_qkv = jnp.transpose(
        flat[:, :qkv_rows].reshape(depth, 3, head_width), (1, 0, 2)
    ).astype(wide)
    grad_wout = flat[:, qkv_rows:].reshape(head_width, depth).astype(wide)

    running_wide = running.astype(wide)
    unit_all = (normed.astype(wide) - ln1_bias) / ln1_gain
    sums = (sums_near + sums_far).reshape(parts, team_units)
    up_sums = lax.dynamic_update_slice_in_dim(
        jnp.zeros((parts, TEAM * team_units), wide), sums, member * team_units, 1
    )
    table_line = table_gradient(hot, table_sums, heads).reshape(1, -1)
    table_all = lax.dynamic_update_slice_in_dim(
        jnp.zeros((parts, table_line.shape[1]), wide), table_line, part, 0
    )
    lines = [
        jnp.sum(running_wide * unit_all, axis=0), jnp.sum(running_wide, axis=0),
        jnp.sum(grad_second * unit2, axis=0), jnp.sum(grad_second, axis=0),
        jnp.sum(grad_part, axis=0),
    ]
    small = jnp.concatenate(lines + [up_sums.reshape(-1), table_all.reshape(-1)])
    small = jnp.pad(small, (0, -small.shape[0] % 1024)).reshape(-1, 1024)
    for axis, size in (("team", TEAM), ("copy", copies), ("mp", parts)):
        for bit in bits_of(size):
            small = small + flip(small, axis, bit)
    small = small.reshape(-1)
    lines = [small[index * depth : (index + 1) * depth] for index in range(5)]
    start = 5 * depth
    count = TEAM * team_units
    up_sums = small[start : start + parts * count].reshape(parts, count)
    grad_up_bias = lax.dynamic_index_in_dim(up_sums, part, 0, keepdims=False)
    start = start + parts * count
    count = rel_table.size
    table_all = small[start : start + parts * count].reshape(parts, count)
    grad_table = lax.dynamic_index_in_dim(table_all, part, 0, keepdims=False).reshape(
        rel_table.shape
    )
    return (
        layer_out, grad_tokens, lines[0], lines[1], grad_qkv, grad_table, grad_wout,
        lines[2], lines[3], grad_up, grad_up_bias, grad_down, lines[4],
    )


def solution(mesh):
    groups, parts = mesh.shape["dp"], mesh.shape["mp"]
    split = Mesh(
        mesh.devices.reshape(groups // TEAM, TEAM, parts), ("copy", "team", "mp")
    )
    every = ("copy", "team", "mp")
    return jax.shard_map(
        body,
        mesh=split,
        in_specs=(
            P(every, None), P(("copy", "team"), None), P(), P(), P(), P(None, None, "mp"),
            P(None, "mp"), P("mp", None), P(), P(), P(None, "mp"), P("mp"), P("mp", None), P(),
            P(every, None),
        ),
        out_specs=(
            P(every, None), P(every, None), P(), P(), P(None, None, "mp"), P(None, "mp"),
            P("mp", None), P(), P(), P(None, "mp"), P("mp"), P("mp", None), P(),
        ),
        check_vma=False,
    )
```

```python
import functools

import jax
import jax.numpy as jnp
from jax import lax
from jax.experimental import pallas as pl
from jax.experimental.pallas import tpu as pltpu
from jax.sharding import Mesh, PartitionSpec as P

EPSILON = 1e-05
HIGHEST_PRECISION = lax.Precision.HIGHEST
FEED_STEPS = 2
EARLY = True
BLK = 256
HEAD_LANES = 64
NEAR = 128


def head_mask(rows, width, head, axis):
    place = lax.broadcasted_iota(jnp.int32, (rows, width), axis)
    return (place >= head * HEAD_LANES) & (place < (head + 1) * HEAD_LANES)


def one_head(value, head):
    keep = head_mask(value.shape[0], value.shape[1], head, 1)
    return jnp.where(keep, value, jnp.zeros_like(value))


def scaled(queries):
    return queries * jnp.asarray(HEAD_LANES ** -0.5, queries.dtype)


def dot_nt(left, right):
    return lax.dot_general(
        left, right, (((1,), (1,)), ((), ())), preferred_element_type=jnp.float32
    )


def dot_nn(left, right):
    return lax.dot_general(
        left, right, (((1,), (0,)), ((), ())), preferred_element_type=jnp.float32
    )


def attention_forward_kernel(
    cut_ref, qkv_ref, bias_ref, out_ref, lse_ref, tile_ref, masked_v, score_ref, *, first_head
):
    heads = masked_v.shape[0]
    width = out_ref.shape[1]
    block = pl.program_id(0)
    cut = cut_ref[0]

    @pl.when(block == 0)
    def _():
        for head in range(heads):
            wide = jnp.broadcast_to(bias_ref[first_head + head : first_head + head + 1, :], (BLK, 2 * BLK))
            tile_ref[head] = pltpu.roll(wide, 0, 1, stride=1, stride_axis=0)
            masked_v[head] = one_head(qkv_ref[:, 2 * width :], head)

    row_start = block * BLK
    first = jnp.where(row_start >= cut, cut // BLK, 0)
    rows = row_start + lax.broadcasted_iota(jnp.int32, (BLK, BLK), 0)
    seg_start = jnp.where(rows >= cut, cut, 0)
    columns = lax.broadcasted_iota(jnp.int32, (BLK, BLK), 1)
    q_block = scaled(qkv_ref[pl.ds(pl.multiple_of(row_start, BLK), BLK), 0:width])
    q_heads = [one_head(q_block, head) for head in range(heads)]

    def scores_of(key_block, tops):
        key_start = pl.multiple_of(key_block * BLK, BLK)
        keys = qkv_ref[pl.ds(key_start, BLK), width : 2 * width]
        places = key_start + columns
        allowed = (places <= rows) & (places >= seg_start)
        offset = pl.multiple_of(jnp.maximum(key_block - block + 1, 0) * BLK, BLK)
        near = key_block - block + 1 >= 0
        new_tops = []
        for head in range(heads):
            raw = dot_nt(q_heads[head], keys)
            far = bias_ref[first_head + head : first_head + head + 1, 2 * BLK - 1 : 2 * BLK]
            bias = jnp.where(near, tile_ref[head, :, pl.ds(offset, BLK)], far)
            scores = jnp.where(allowed, raw + bias, -1e30)
            score_ref[head, :, pl.ds(key_start, BLK)] = scores
            top = tops[head]
            for lane in range(0, BLK, 128):
                top = jnp.maximum(top, scores[:, lane : lane + 128])
            new_tops.append(top)
        return tuple(new_tops)

    start = tuple(jnp.full((BLK, 128), -1e30, jnp.float32) for _ in range(heads))
    tops = lax.fori_loop(first, block + 1, scores_of, start)
    tops = [jnp.max(top, axis=1, keepdims=True) for top in tops]

    def weighted(key_block, carry):
        total, sums = carry
        key_start = pl.multiple_of(key_block * BLK, BLK)
        new_sums = []
        pieces = []
        values = []
        for head in range(heads):
            soft = jnp.exp(score_ref[head, :, pl.ds(key_start, BLK)] - tops[head])
            part = sums[head]
            for lane in range(0, BLK, 128):
                part = part + soft[:, lane : lane + 128]
            new_sums.append(part)
            pieces.append(soft.astype(jnp.bfloat16))
            values.append(masked_v[head, pl.ds(key_start, BLK), :])
        total = total + dot_nn(
            jnp.concatenate(pieces, axis=1), jnp.concatenate(values, axis=0)
        )
        return total, tuple(new_sums)

    total, sums = lax.fori_loop(
        first,
        block + 1,
        weighted,
        (
            jnp.zeros((BLK, heads * HEAD_LANES), jnp.float32),
            tuple(jnp.zeros((BLK, 128), jnp.float32) for _ in range(heads)),
        ),
    )
    lanes = lax.broadcasted_iota(jnp.int32, (BLK, heads * HEAD_LANES), 1)
    narrow = lax.broadcasted_iota(jnp.int32, (BLK, 128), 1)
    scale = jnp.zeros((BLK, heads * HEAD_LANES), jnp.float32)
    logs = jnp.zeros((BLK, 128), jnp.float32)
    for head in range(heads):
        sum_one = jnp.sum(sums[head], axis=1, keepdims=True)
        scale = jnp.where(lanes // HEAD_LANES == head, 1.0 / sum_one, scale)
        logs = jnp.where(narrow == head, tops[head] + jnp.log(sum_one), logs)
    out_ref[...] = (total * scale).astype(jnp.bfloat16)
    lse_ref[...] = jnp.transpose(logs)[0:8, :]


def attention_forward(cut, projected, near_bias, first_head):
    length, width = projected.shape[0], projected.shape[1] // 3
    heads = width // HEAD_LANES
    whole = lambda block, cut: (0, 0)
    return pl.pallas_call(
        functools.partial(attention_forward_kernel, first_head=first_head),
        grid_spec=pltpu.PrefetchScalarGridSpec(
            num_scalar_prefetch=1,
            grid=(length // BLK,),
            in_specs=[
                pl.BlockSpec((length, 3 * width), whole),
                pl.BlockSpec((8, 2 * BLK), whole),
            ],
            out_specs=[
                pl.BlockSpec((BLK, width), lambda block, cut: (block, 0)),
                pl.BlockSpec((8, BLK), lambda block, cut: (0, block)),
            ],
            scratch_shapes=[
                pltpu.VMEM((heads, BLK, 2 * BLK), jnp.float32),
                pltpu.VMEM((heads, length, width), jnp.bfloat16),
                pltpu.VMEM((heads, BLK, length), jnp.float32),
            ],
        ),
        out_shape=[
            jax.ShapeDtypeStruct((length, width), jnp.bfloat16),
            jax.ShapeDtypeStruct((8, length), jnp.float32),
        ],
        compiler_params=pltpu.CompilerParams(
            dimension_semantics=("arbitrary",), vmem_limit_bytes=48 * 1024 * 1024
        ),
        cost_estimate=pl.CostEstimate(
            flops=8 * length * length * width, bytes_accessed=8 * length * width,
            transcendentals=heads * length * length // 2,
        ),
        name="attention_forward",
    )(cut, projected, near_bias)


def attention_backward_kernel(
    cut_ref, qkv_ref, grad_ref, att_ref, lse_ref, bias_ref, dqkv_ref, table_ref,
    tile_ref, q_masked, grad_masked, delta_ref, dq_sum, near_sum, far_sum,
    *, first_head,
):
    heads = q_masked.shape[0]
    block = pl.program_id(0)
    n_blocks = pl.num_programs(0)
    length, width = grad_ref.shape
    cut = cut_ref[0]

    @pl.when(block == 0)
    def _():
        product = grad_ref[...].astype(jnp.float32) * att_ref[...].astype(jnp.float32)
        high = product.astype(jnp.bfloat16)
        rest = (product - high.astype(jnp.float32)).astype(jnp.bfloat16)
        row = lax.broadcasted_iota(jnp.int32, (16, width), 0)
        lane = lax.broadcasted_iota(jnp.int32, (16, width), 1)
        pick = jnp.where(lane // HEAD_LANES == row, 1.0, 0.0).astype(jnp.bfloat16)
        delta_ref[...] = (dot_nt(pick, high) + dot_nt(pick, rest))[0:8, :]
        for head in range(heads):
            wide = jnp.broadcast_to(bias_ref[first_head + head : first_head + head + 1, :], (BLK, 2 * BLK))
            tile_ref[head] = pltpu.roll(wide, 0, 1, stride=1, stride_axis=0)
            q_masked[head] = one_head(scaled(qkv_ref[:, 0:width]), head)
            grad_masked[head] = one_head(grad_ref[...], head)
        dq_sum[...] = jnp.zeros_like(dq_sum)
        near_sum[...] = jnp.zeros_like(near_sum)
        far_sum[...] = jnp.zeros_like(far_sum)

    key_start = pl.multiple_of(block * BLK, BLK)
    keys = qkv_ref[pl.ds(key_start, BLK), width : 2 * width]
    values = qkv_ref[pl.ds(key_start, BLK), 2 * width :]
    keys_t = jnp.transpose(keys)
    places = key_start + lax.broadcasted_iota(jnp.int32, (BLK, BLK), 0)
    columns = lax.broadcasted_iota(jnp.int32, (BLK, BLK), 1)
    last = jnp.where(key_start + BLK <= cut, (cut + BLK - 1) // BLK, n_blocks)

    def one_block(query_block, carry):
        dk, dv = carry
        row_start = pl.multiple_of(query_block * BLK, BLK)
        rows = row_start + columns
        allowed = (places <= rows) & (places >= jnp.where(rows >= cut, cut, 0))
        distance = query_block - block
        near = distance <= 1
        offset = pl.multiple_of(jnp.minimum(distance, 1) * BLK, BLK)
        soft_pieces, grad_pieces, q_pieces, out_pieces = [], [], [], []
        for head in range(heads):
            q_head = q_masked[head, pl.ds(row_start, BLK), :]
            grad_head = grad_masked[head, pl.ds(row_start, BLK), :]
            far = bias_ref[first_head + head : first_head + head + 1, BLK - 1 : BLK]
            bias = jnp.where(near, tile_ref[head, :, pl.ds(offset, BLK)], far)
            scores = dot_nt(keys, q_head) + bias
            log_total = lse_ref[head : head + 1, pl.ds(row_start, BLK)]
            soft = jnp.exp(jnp.where(allowed, scores - log_total, -1e30))
            grad_soft = dot_nt(values, grad_head)
            delta = delta_ref[head : head + 1, pl.ds(row_start, BLK)]
            grad_scores = soft * (grad_soft - delta)
            grad_low = grad_scores.astype(jnp.bfloat16)

            @pl.when(near)
            def _():
                near_sum[head, :, pl.ds(offset, BLK)] += grad_scores

            @pl.when(jnp.logical_not(near))
            def _():
                far_sum[head] += jnp.sum(
                    grad_scores.reshape(BLK // 8, 8, BLK), axis=0
                )

            spot = slice(head * HEAD_LANES, (head + 1) * HEAD_LANES)
            dq_sum[spot, pl.ds(row_start, BLK)] += dot_nn(keys_t[spot, :], grad_low)
            soft_pieces.append(soft.astype(jnp.bfloat16))
            grad_pieces.append(grad_low)
            q_pieces.append(q_head)
            out_pieces.append(grad_head)
        dv = dv + dot_nn(
            jnp.concatenate(soft_pieces, axis=1), jnp.concatenate(out_pieces, axis=0)
        )
        dk = dk + dot_nn(
            jnp.concatenate(grad_pieces, axis=1), jnp.concatenate(q_pieces, axis=0)
        )
        return dk, dv

    empty = jnp.zeros((BLK, width), jnp.float32)
    dk, dv = lax.fori_loop(block, last, one_block, (empty, empty))
    dqkv_ref[pl.ds(key_start, BLK), width : 2 * width] = dk.astype(jnp.bfloat16)
    dqkv_ref[pl.ds(key_start, BLK), 2 * width :] = dv.astype(jnp.bfloat16)

    @pl.when(block == n_blocks - 1)
    def _():
        for query_block in range(length // BLK):
            spot = slice(query_block * BLK, (query_block + 1) * BLK)
            dqkv_ref[spot, 0:width] = (
                jnp.transpose(dq_sum[:, spot]) * (HEAD_LANES ** -0.5)
            ).astype(jnp.bfloat16)
        for head in range(heads):
            lined = jnp.zeros((8, 2 * BLK), jnp.float32)
            for group in range(BLK // 8):
                piece = near_sum[head, group * 8 : group * 8 + 8, :]
                shift = (2 * BLK - group * 8) % (2 * BLK)
                lined = lined + (pltpu.roll(piece, shift, 1) if shift else piece)
            total = lined[0:1, :]
            for row in range(1, 8):
                total = total + pltpu.roll(lined, 2 * BLK - row, 1)[row : row + 1, :]
            table_ref[head : head + 1, :] = total
            rest = jnp.sum(far_sum[head], axis=0, keepdims=True)
            table_ref[heads + head : heads + head + 1, :] = jnp.concatenate(
                [rest, jnp.zeros_like(rest)], axis=1
            )


def attention_backward(cut, projected, grad_att, attended, logs, near_bias, first_head):
    length, width = attended.shape
    heads = width // HEAD_LANES
    whole = lambda block, cut: (0, 0)
    full = pl.BlockSpec((length, width), whole)
    return pl.pallas_call(
        functools.partial(attention_backward_kernel, first_head=first_head),
        grid_spec=pltpu.PrefetchScalarGridSpec(
            num_scalar_prefetch=1,
            grid=(length // BLK,),
            in_specs=[
                pl.BlockSpec((length, 3 * width), whole), full, full,
                pl.BlockSpec((8, length), whole),
                pl.BlockSpec((8, 2 * BLK), whole),
            ],
            out_specs=[
                pl.BlockSpec((length, 3 * width), whole),
                pl.BlockSpec((8, 2 * BLK), whole),
            ],
            scratch_shapes=[
                pltpu.VMEM((heads, BLK, 2 * BLK), jnp.float32),
                pltpu.VMEM((heads, length, width), jnp.bfloat16),
                pltpu.VMEM((heads, length, width), jnp.bfloat16),
                pltpu.VMEM((8, length), jnp.float32),
                pltpu.VMEM((width, length), jnp.float32),
                pltpu.VMEM((heads, BLK, 2 * BLK), jnp.float32),
                pltpu.VMEM((heads, 8, BLK), jnp.float32),
            ],
        ),
        out_shape=[
            jax.ShapeDtypeStruct((length, 3 * width), jnp.bfloat16),
            jax.ShapeDtypeStruct((8, 2 * BLK), jnp.float32),
        ],
        compiler_params=pltpu.CompilerParams(
            dimension_semantics=("arbitrary",), vmem_limit_bytes=56 * 1024 * 1024
        ),
        cost_estimate=pl.CostEstimate(
            flops=20 * length * length * width, bytes_accessed=16 * length * width,
            transcendentals=heads * length * length // 2,
        ),
        name="attention_backward",
    )(cut, projected, grad_att, attended, logs, near_bias)


def distance_bias(rel_table, bucket_of):
    hot = (
        bucket_of[:, None] == jnp.arange(rel_table.shape[0], dtype=jnp.int32)[None, :]
    ).astype(jnp.float32)
    by_distance = jnp.einsum(
        "dn,nh->hd", hot, rel_table, precision=HIGHEST_PRECISION,
        preferred_element_type=jnp.float32,
    )
    return hot, by_distance


def near_tables(by_distance):
    heads, reach = by_distance.shape
    far = by_distance[:, reach - 1 :]
    forward = jnp.concatenate(
        [
            jnp.broadcast_to(far, (heads, BLK - reach + 1)),
            by_distance[:, ::-1],
            jnp.broadcast_to(far, (heads, BLK - 1)),
        ],
        axis=1,
    )
    backward = jnp.concatenate(
        [by_distance, jnp.broadcast_to(far, (heads, 2 * BLK - reach))], axis=1
    )
    rows = ((0, 8 - heads), (0, 0))
    return jnp.pad(forward, rows), jnp.pad(backward, rows)


def table_gradient(hot, near_sums, far_sums):
    reach = hot.shape[0]
    near = near_sums[:, : reach - 1]
    far = jnp.sum(near_sums[:, reach - 1 :], axis=1) + jnp.sum(far_sums, axis=1)
    by_distance = jnp.concatenate([near, far[:, None]], axis=1)
    return jnp.einsum(
        "dn,hd->nh", hot, by_distance, precision=HIGHEST_PRECISION,
        preferred_element_type=jnp.float32,
    )


TEAM = 4


def after(value, *gates):
    return lax.optimization_barrier((value,) + gates)[0]


def flip(value, axis, bit):
    size = lax.axis_size(axis)
    return lax.ppermute(value, axis, [(i, i ^ bit) for i in range(size)])


def halve(value, dim, axis, bit):
    mine = (lax.axis_index(axis) // bit) % 2
    keep = lax.dynamic_index_in_dim(value, mine, dim, keepdims=False)
    send = lax.dynamic_index_in_dim(value, 1 - mine, dim, keepdims=False)
    received = flip(send.astype(jnp.bfloat16), axis, bit)
    return (keep.astype(jnp.float32) + received.astype(jnp.float32)).astype(jnp.bfloat16)


def double(value, axis, bit):
    mine = (lax.axis_index(axis) // bit) % 2
    other = flip(value, axis, bit)
    return jnp.where(mine == 0, jnp.stack([value, other]), jnp.stack([other, value]))


def bits_of(size):
    bits = []
    bit = 1
    while bit < size:
        bits.append(bit)
        bit *= 2
    return bits


def with_partner(own):
    return jnp.concatenate([own, flip(own, "team", 1)], axis=0)


def feed_grads_kernel(piece_ref, up_ref, down_ref):
    up_ref[...] = jnp.transpose(piece_ref[0, 0].astype(jnp.float32))
    down_ref[...] = piece_ref[0, 1].astype(jnp.float32)


def feed_grads_out(pieces, copies):
    count, _, unit, depth = pieces.shape
    merge = max(1, 128 // unit)
    if merge > 1:
        pieces = jnp.transpose(
            pieces.reshape(count // merge, merge, 2, unit, depth), (0, 2, 1, 3, 4)
        ).reshape(count // merge, 2, merge * unit, depth)
    count, _, unit, depth = pieces.shape
    each = copies // merge

    def spot(step):
        core, side, place = step // (2 * each), (step // each) % 2, step % each
        return (side * 2 + core) * each + place

    return pl.pallas_call(
        feed_grads_kernel,
        grid=(count,),
        in_specs=[pl.BlockSpec((1, 2, unit, depth), lambda step: (step, 0, 0, 0))],
        out_specs=[
            pl.BlockSpec((depth, unit), lambda step: (0, spot(step))),
            pl.BlockSpec((unit, depth), lambda step: (spot(step), 0)),
        ],
        out_shape=[
            jax.ShapeDtypeStruct((depth, count * unit), jnp.float32),
            jax.ShapeDtypeStruct((count * unit, depth), jnp.float32),
        ],
        compiler_params=pltpu.CompilerParams(dimension_semantics=("arbitrary",)),
        cost_estimate=pl.CostEstimate(
            flops=0, bytes_accessed=12 * count * unit * depth, transcendentals=0
        ),
        name="feed_grads_out",
    )(pieces)


def attention_grads_kernel(piece_ref, qkv_ref, out_ref):
    group = piece_ref.shape[0]
    rows, width = qkv_ref.shape[1] // group, qkv_ref.shape[2]
    few = out_ref.shape[0] // group
    for item in range(group):
        for slot in range(3):
            qkv_ref[slot, item * rows : (item + 1) * rows, :] = piece_ref[
                item, slot * rows : (slot + 1) * rows, :
            ].astype(jnp.float32)
        for place in range(out_ref.shape[1] // width):
            start = 3 * rows + place * few
            out_ref[item * few : (item + 1) * few, place * width : (place + 1) * width] = (
                piece_ref[item, start : start + few, :].astype(jnp.float32)
            )


def attention_grads_out(pieces, depth, head_width):
    count = pieces.shape[0]
    rows, few = depth // count, head_width // count
    group = max(1, 8 // few)
    return pl.pallas_call(
        attention_grads_kernel,
        grid=(count // group,),
        in_specs=[
            pl.BlockSpec((group,) + pieces.shape[1:], lambda step: (step, 0, 0)),
        ],
        out_specs=[
            pl.BlockSpec((3, group * rows, head_width), lambda step: (0, step, 0)),
            pl.BlockSpec((group * few, depth), lambda step: (step, 0)),
        ],
        out_shape=[
            jax.ShapeDtypeStruct((3, depth, head_width), jnp.float32),
            jax.ShapeDtypeStruct((head_width, depth), jnp.float32),
        ],
        compiler_params=pltpu.CompilerParams(dimension_semantics=("arbitrary",)),
        cost_estimate=pl.CostEstimate(
            flops=0, bytes_accessed=24 * depth * head_width, transcendentals=0
        ),
        name="attention_grads_out",
    )(pieces)


def normalize(inputs):
    center = inputs - jnp.mean(inputs, axis=-1, keepdims=True)
    spread = jnp.mean(center * center, axis=-1, keepdims=True)
    inverse = lax.rsqrt(spread + EPSILON)
    return center * inverse, inverse


def normalize_backward(grad, gain, unit, inverse):
    scaled_grad = grad * gain
    middle = jnp.mean(scaled_grad, axis=-1, keepdims=True)
    along = jnp.mean(scaled_grad * unit, axis=-1, keepdims=True)
    return (scaled_grad - middle - unit * along) * inverse


def dot_tn(left, right):
    return lax.dot_general(
        left, right, (((0,), (0,)), ((), ())), preferred_element_type=jnp.float32
    )


def spread(value, axis, size):
    value = value[None]
    for bit in bits_of(size):
        value = double(value, axis, bit)
        value = value.reshape((-1,) + value.shape[2:])
    return value


def exchange(blocks):
    return [blocks[0]] + [flip(blocks[k], "mp", k) for k in range(1, len(blocks))]


def cotangent_kernel(grad_a, grad_b, weight_a, weight_b, normed_ref, line_ref, out_ref, sum_ref):
    grad = dot_nt(grad_a[...], weight_a[...]) + dot_nt(grad_b[...], weight_b[...])
    unit = (normed_ref[...].astype(jnp.float32) - line_ref[0:1, :]) * line_ref[1:2, :]
    out_ref[...] = grad.astype(jnp.bfloat16)
    rows, depth = grad.shape
    both = jnp.concatenate(
        [
            jnp.sum((grad * unit).reshape(rows // 8, 8, depth), axis=0),
            jnp.sum(grad.reshape(rows // 8, 8, depth), axis=0),
        ],
        axis=0,
    )

    @pl.when(pl.program_id(0) == 0)
    def _():
        sum_ref[...] = both

    @pl.when(pl.program_id(0) > 0)
    def _():
        sum_ref[...] += both


def input_cotangent(grads, weights, normed, lines):
    length, width = grads[0].shape
    depth = weights[0].shape[0]
    row = pl.BlockSpec((BLK, width), lambda step: (step, 0))
    whole = pl.BlockSpec((depth, width), lambda step: (0, 0))
    return pl.pallas_call(
        cotangent_kernel,
        grid=(length // BLK,),
        in_specs=[
            row, row, whole, whole,
            pl.BlockSpec((BLK, depth), lambda step: (step, 0)),
            pl.BlockSpec((2, depth), lambda step: (0, 0)),
        ],
        out_specs=[
            pl.BlockSpec((BLK, depth), lambda step: (step, 0)),
            pl.BlockSpec((16, depth), lambda step: (0, 0)),
        ],
        out_shape=[
            jax.ShapeDtypeStruct((length, depth), jnp.bfloat16),
            jax.ShapeDtypeStruct((16, depth), jnp.float32),
        ],
        compiler_params=pltpu.CompilerParams(dimension_semantics=("arbitrary",)),
        cost_estimate=pl.CostEstimate(
            flops=4 * length * width * depth,
            bytes_accessed=4 * (length * width + depth * width + length * depth),
            transcendentals=0,
        ),
        name="input_cotangent",
    )(*grads, *weights, normed, lines)


def feed_kernel(
    own_ref, beside_ref, across_ref, corner_ref, bias_ref, second_ref, grad_ref,
    act_ref, pre_ref, back_ref, out_ref, sum_ref, *, unit,
):
    copies, _, depth = own_ref.shape
    hidden = copies * unit
    second = second_ref[...]
    grad = grad_ref[...]
    back = out = None
    sums = []
    for slot, ref in enumerate((own_ref, beside_ref, across_ref, corner_ref)):
        spot = slice(slot * hidden, (slot + 1) * hidden)
        w_up = ref[:, 0:unit, :].reshape(hidden, depth)
        w_down = ref[:, unit : 2 * unit, :].reshape(hidden, depth)
        pre = dot_nt(second, w_up) + bias_ref[0:1, spot]
        grad_act = dot_nt(grad, w_down)
        cdf = 0.5 + 0.5 * lax.erf(pre * 0.7071067811865476)
        pdf = jnp.exp(pre * pre * -0.5) * 0.3989422804014327
        active = (pre * cdf).astype(jnp.bfloat16)
        grad_pre = ((cdf + pre * pdf) * grad_act).astype(jnp.bfloat16)
        act_ref[:, spot] = active
        pre_ref[:, spot] = grad_pre
        sums.append(jnp.sum(grad_pre.astype(jnp.float32), axis=0, keepdims=True))
        one_back = dot_nn(grad_pre, w_up)
        one_out = dot_nn(active, w_down)
        back = one_back if back is None else back + one_back
        out = one_out if out is None else out + one_out
    back_ref[...] = back.astype(jnp.bfloat16)
    out_ref[...] = out.astype(jnp.bfloat16)
    line = jnp.concatenate(sums, axis=1)

    @pl.when(pl.program_id(0) == 0)
    def _():
        sum_ref[...] = line

    @pl.when(pl.program_id(0) > 0)
    def _():
        sum_ref[...] += line


def feed_forward(slots, bias_row, second, grad, unit):
    copies, _, depth = slots[0].shape
    rows = second.shape[0]
    width = len(slots) * copies * unit
    take = rows // FEED_STEPS
    whole = lambda step: (0, 0, 0)
    row = pl.BlockSpec((take, depth), lambda step: (step, 0))
    wide = pl.BlockSpec((take, width), lambda step: (step, 0))
    line = pl.BlockSpec((1, width), lambda step: (0, 0))
    return pl.pallas_call(
        functools.partial(feed_kernel, unit=unit),
        grid=(FEED_STEPS,),
        in_specs=[pl.BlockSpec(slot.shape, whole) for slot in slots] + [line, row, row],
        out_specs=[wide, wide, row, row, line],
        out_shape=[
            jax.ShapeDtypeStruct((rows, width), jnp.bfloat16),
            jax.ShapeDtypeStruct((rows, width), jnp.bfloat16),
            jax.ShapeDtypeStruct((rows, depth), jnp.bfloat16),
            jax.ShapeDtypeStruct((rows, depth), jnp.bfloat16),
            jax.ShapeDtypeStruct((1, width), jnp.float32),
        ],
        compiler_params=pltpu.CompilerParams(
            dimension_semantics=("arbitrary",), vmem_limit_bytes=56 * 1024 * 1024
        ),
        cost_estimate=pl.CostEstimate(
            flops=8 * rows * width * depth, bytes_accessed=8 * rows * depth + 4 * width * depth,
            transcendentals=2 * rows * width,
        ),
        name="feed_forward",
    )(*slots, bias_row, second, grad)


def weight_grad_kernel(
    part_ref, act_a, act_b, pre_a, pre_b, second_a, second_b, grad_a, grad_b, out_ref
):
    _, copies, _, unit, depth = out_ref.shape
    up = dot_tn(pre_a[...], second_a[...]) + dot_tn(pre_b[...], second_b[...])
    out_ref[0, :, 0] = up.astype(jnp.bfloat16).reshape(copies, unit, depth)
    down = dot_tn(act_a[...], grad_a[...]) + dot_tn(act_b[...], grad_b[...])
    out_ref[0, :, 1] = down.astype(jnp.bfloat16).reshape(copies, unit, depth)


def weight_grads(part, acts, pres, seconds, grads, parts, copies):
    rows, width = acts[0].shape
    depth = seconds[0].shape[1]
    unit = width // (parts * copies)
    column = pl.BlockSpec((rows, width // parts), lambda step, part: (0, step))
    whole = pl.BlockSpec((rows, depth), lambda step, part: (0, 0))
    return pl.pallas_call(
        weight_grad_kernel,
        grid_spec=pltpu.PrefetchScalarGridSpec(
            num_scalar_prefetch=1,
            grid=(parts,),
            in_specs=[column] * 4 + [whole] * 4,
            out_specs=pl.BlockSpec(
                (1, copies, 2, unit, depth), lambda step, part: (part[0] ^ step, 0, 0, 0, 0)
            ),
        ),
        out_shape=jax.ShapeDtypeStruct((parts, copies, 2, unit, depth), jnp.bfloat16),
        compiler_params=pltpu.CompilerParams(
            dimension_semantics=("arbitrary",), vmem_limit_bytes=56 * 1024 * 1024
        ),
        cost_estimate=pl.CostEstimate(
            flops=8 * rows * width * depth, bytes_accessed=16 * rows * depth + 4 * width * depth,
            transcendentals=0,
        ),
        name="weight_grads",
    )(part, *acts, *pres, *seconds, *grads)


def sync(*values):
    return lax.optimization_barrier(values)


def body(
    tokens, seg_ids, bucket_of, ln1_gain, ln1_bias, w_qkv, rel_table, w_out,
    ln2_gain, ln2_bias, w_up, up_bias, w_down, down_bias, out_grad,
):
    low = jnp.bfloat16
    wide = jnp.float32
    copies = lax.axis_size("copy")
    parts = lax.axis_size("mp")
    copy = lax.axis_index("copy")
    member = lax.axis_index("team")
    part = lax.axis_index("mp")
    core = member % 2
    rows, depth = tokens.shape
    head_width = w_out.shape[0]
    pair_width = 2 * HEAD_LANES
    pairs = head_width // pair_width
    team_units = w_up.shape[1] // TEAM
    unit = team_units // copies
    out_rows = head_width // (2 * copies)
    seg_row = seg_ids[0]
    to_right = [(i, i + 1) for i in range(parts - 1)]
    to_left = [(i + 1, i) for i in range(parts - 1)]

    x_part = tokens.astype(wide)
    unit1, inverse1 = normalize(x_part)
    normed = lax.all_gather(
        (unit1 * ln1_gain + ln1_bias).astype(low), "mp", axis=0, tiled=True
    )

    up_own = jnp.transpose(
        lax.dynamic_slice_in_dim(w_up, member * team_units, team_units, 1)
    ).reshape(copies, unit, depth)
    down_own = lax.dynamic_slice_in_dim(w_down, member * team_units, team_units, 0).reshape(
        copies, unit, depth
    )
    out_own = lax.dynamic_index_in_dim(
        w_out.reshape(copies, 2, out_rows, depth), core, 1, keepdims=False
    )
    own_slot = jnp.concatenate([up_own, down_own, out_own], axis=1)
    piece = lax.dynamic_index_in_dim(own_slot, copy, 0, keepdims=False)
    if not EARLY:
        piece = after(piece, normed)
    right1 = lax.ppermute(piece, "mp", to_right)
    left1 = lax.ppermute(piece, "mp", to_left)
    grad_across = flip(out_grad, "team", 2)
    grad_near = with_partner(out_grad)
    grad_far = with_partner(grad_across)
    biases = [up_bias] + [flip(up_bias, "mp", k) for k in range(1, parts)]
    bias_row = jnp.concatenate(
        [lax.dynamic_slice_in_dim(one, member * team_units, team_units, 0) for one in biases]
    )[None]
    w_cat = [
        jnp.transpose(
            w_qkv[:, :, pair * pair_width : (pair + 1) * pair_width], (1, 0, 2)
        ).reshape(depth, -1)
        for pair in range(pairs)
    ]
    hot, by_distance = distance_bias(rel_table, bucket_of)
    forward_bias, backward_bias = near_tables(by_distance)
    cut = jnp.sum((seg_row == seg_row[0]).astype(jnp.int32)).reshape(1)
    normed, grad_near, grad_far, bias_row, own_slot, w_first, w_last, forward_bias, cut = sync(
        normed, grad_near, grad_far, bias_row, own_slot, w_cat[0], w_cat[1], forward_bias, cut
    )
    w_cat = [w_first, w_last]
    if EARLY:
        right1, left1, normed = sync(right1, left1, normed)

    def attend(pair, projected):
        return attention_forward(cut, projected, forward_bias, 2 * pair)

    def send_rows(att_one):
        blocks = att_one.reshape(parts, rows, pair_width)
        return exchange(
            [
                lax.dynamic_index_in_dim(blocks, part ^ k, 0, keepdims=False)
                for k in range(parts)
            ]
        )

    def whole_out(mine):
        other = flip(mine, "team", 1)
        return jnp.where(
            core == 0, jnp.stack([mine, other], axis=2), jnp.stack([other, mine], axis=2)
        )

    projected = [
        jnp.dot(normed, w_one, preferred_element_type=wide).astype(low) for w_one in w_cat
    ]
    attended, logs = [None, None], [None, None]
    attended[0], logs[0] = attend(0, projected[0])
    if not EARLY:
        right1, left1, attended[0] = sync(right1, left1, attended[0])
    right2 = lax.ppermute(right1, "mp", to_right[1:])
    left2 = lax.ppermute(left1, "mp", to_left[:-1])
    beside_slot = spread(jnp.where(part % 2 == 0, left1, right1), "copy", copies)
    if EARLY:
        right2, left2, beside_slot, attended[0], projected[1] = sync(
            right2, left2, beside_slot, attended[0], projected[1]
        )
    moved = [send_rows(attended[0]), None]
    attended[1], logs[1] = attend(1, projected[1])
    if not EARLY:
        right2, left2, beside_slot, attended[1] = sync(right2, left2, beside_slot, attended[1])
    right3 = lax.ppermute(right2, "mp", to_right[2:])
    left3 = lax.ppermute(left2, "mp", to_left[:-2])
    across_slot = spread(right2 + left2, "copy", copies)
    if EARLY:
        results = sync(right3, left3, across_slot, attended[1], *moved[0])
        right3, left3, across_slot, attended[1] = results[:4]
        moved[0] = list(results[4:])
    corner = jnp.where(
        (part == 0) | (part == parts - 1), right3 + left3, jnp.where(part == 1, left1, right1)
    )
    corner_slot = spread(corner, "copy", copies)
    moved[1] = send_rows(attended[1])
    slots = [own_slot, beside_slot, across_slot, corner_slot]
    w_out_full = jnp.concatenate(
        [
            w_out.reshape(1, copies, 2, out_rows, depth),
            whole_out(jnp.stack([slot[:, 2 * unit :] for slot in slots[1:3]])),
            whole_out(corner_slot[None, :, 2 * unit :]),
        ]
    ).reshape(parts * head_width, depth)

    own_rows = jnp.concatenate(
        [moved[pair][k] for k in range(parts) for pair in range(pairs)], axis=1
    )
    branch = jnp.dot(own_rows, w_out_full, preferred_element_type=wide)
    hidden_in = x_part + branch
    unit2, inverse2 = normalize(hidden_in)
    second = (unit2 * ln2_gain + ln2_bias).astype(low)
    second_across = flip(second, "team", 2)
    second_near = with_partner(second)
    act_near, pre_near, back_near, feed_near, sums_near = feed_forward(
        slots, bias_row, second_near, grad_near, unit
    )
    second_across, back_near = sync(second_across, back_near)
    beside = flip(back_near[rows:], "team", 1)
    second_far = with_partner(second_across)
    act_far, pre_far, back_far, feed_far, sums_far = feed_forward(
        slots, bias_row, second_far, grad_far, unit
    )
    onward = (
        back_far[:rows].astype(wide) + flip(back_far[rows:], "team", 1).astype(wide)
    ).astype(low)
    across = flip(onward, "team", 2)
    ff_grads = weight_grads(
        part.reshape(1), (act_near, after(act_far, onward)), (pre_near, pre_far),
        (second_near, second_far), (grad_near, grad_far), parts, copies,
    )
    ff_grads, across, beside = sync(ff_grads, across, beside)
    ff_piece = lax.psum_scatter(
        ff_grads.reshape(parts * copies, 2 * unit, depth), ("mp", "copy"),
        scatter_dimension=0, tiled=False,
    )
    grad_second = back_near[:rows].astype(wide) + beside.astype(wide) + across.astype(wide)
    grad_part = out_grad.astype(wide)
    grad_hidden = grad_part + normalize_backward(grad_second, ln2_gain, unit2, inverse2)
    grad_branch = grad_hidden.astype(low)
    grad_rows = dot_nt(grad_branch, w_out_full).astype(low)
    received = [
        exchange(
            [
                grad_rows[
                    :, k * head_width + pair * pair_width : k * head_width + (pair + 1) * pair_width
                ]
                for k in range(parts)
            ]
        )
        for pair in range(pairs)
    ]

    def in_order(blocks):
        natural = jnp.zeros((parts, rows, pair_width), low)
        for k in range(parts):
            natural = lax.dynamic_update_index_in_dim(natural, blocks[k], part ^ k, 0)
        return natural.reshape(parts * rows, pair_width)

    def attend_back(pair, grad_att):
        return attention_backward(
            cut, projected[pair], grad_att, attended[pair], logs[pair], backward_bias, 2 * pair
        )

    wout_grad = dot_tn(own_rows, after(grad_branch, grad_rows)).astype(low)
    wout_grad = wout_grad.reshape(parts, 2, 2, copies, -1, depth)
    wout_grad = halve(wout_grad, 1, "team", 1)
    feed_far = after(feed_far, grad_rows)
    feed_beside = flip(jnp.stack([feed_far[rows:], feed_near[rows:]]), "team", 1)
    results = sync(wout_grad, feed_beside, *received[0])
    wout_grad, feed_beside = results[:2]
    received[0] = results[2:]
    wout_grad = halve(wout_grad, 1, "team", 2)
    feed_across = flip(
        (feed_far[:rows].astype(wide) + feed_beside[0].astype(wide)).astype(low), "team", 2
    )
    dqkv, table_sums = [None, None], [None, None]
    dqkv[0], table_sums[0] = attend_back(0, in_order(received[0]))
    results = sync(dqkv[0], wout_grad, feed_across, normed, *received[1])
    dqkv[0], wout_grad, feed_across, late_normed = results[:4]
    received[1] = results[4:]
    half = depth // 2
    normed_keep = lax.dynamic_slice_in_dim(late_normed, core * half, half, 1)
    normed_send = lax.dynamic_slice_in_dim(late_normed, (1 - core) * half, half, 1)
    for bit in reversed(bits_of(copies)):
        wout_grad = halve(
            wout_grad.reshape((parts, 2, -1) + wout_grad.shape[2:]), 1, "copy", bit
        )
    wout_grad = wout_grad.reshape(parts, -1, depth)
    dqkv[1], table_sums[1] = attend_back(1, in_order(received[1]))
    feed_own = (
        feed_near[:rows].astype(wide) + feed_beside[1].astype(wide) + feed_across.astype(wide)
    )
    layer_out = (hidden_in + feed_own + down_bias).astype(low)
    sums = (sums_near + sums_far).reshape(parts, team_units)
    up_sums = jnp.zeros((parts, TEAM * team_units), wide)
    for k in range(parts):
        up_sums = lax.dynamic_update_slice(
            up_sums, sums[k : k + 1], (part ^ k, member * team_units)
        )
    lines = [
        jnp.sum(grad_second * unit2, axis=0), jnp.sum(grad_second, axis=0),
        jnp.sum(grad_part, axis=0),
    ]
    early_lines = jnp.concatenate(lines + [up_sums.reshape(-1)])
    dqkv[1], wout_grad, layer_out, early_lines, normed_keep, normed_send = sync(
        dqkv[1], wout_grad, layer_out, early_lines, normed_keep, normed_send
    )

    running, line_sums = input_cotangent(
        dqkv, w_cat, normed, jnp.stack([ln1_bias, 1.0 / ln1_gain])
    )
    grad_first = lax.psum_scatter(running, "mp", scatter_dimension=0, tiled=True).astype(wide)

    late = [after(one, running) for one in dqkv]
    qkv_send = jnp.concatenate([dot_tn(normed_send, one).astype(low) for one in late], axis=1)
    qkv_keep = jnp.concatenate([dot_tn(normed_keep, one) for one in late], axis=1)
    table_line = table_gradient(
        hot, jnp.concatenate([one[0:2] for one in table_sums]),
        jnp.concatenate([one[2:4] for one in table_sums]),
    ).reshape(1, -1)
    table_all = lax.dynamic_update_slice_in_dim(
        jnp.zeros((parts, table_line.shape[1]), wide), table_line, part, 0
    )
    small = jnp.concatenate(
        [
            jnp.sum(line_sums[0:8], axis=0), jnp.sum(line_sums[8:16], axis=0),
            early_lines, table_all.reshape(-1),
        ]
    )
    small = jnp.pad(small, (0, -small.shape[0] % 1024)).reshape(-1, 1024)

    qkv_got = flip(qkv_send, "team", 1)
    small_got = flip(small, "team", 1)
    wout_got = flip(wout_grad[2:], "mp", 2)
    qkv_grad = (qkv_keep + qkv_got.astype(wide)).astype(low)
    small = small + small_got
    wout_grad = (wout_grad[:2].astype(wide) + wout_got.astype(wide)).astype(low)
    qkv_grad, small, wout_grad, ff_piece = sync(qkv_grad, small, wout_grad, ff_piece)

    qkv_grad = halve(qkv_grad.reshape(2, copies, -1, qkv_grad.shape[1]), 0, "team", 2)
    small_got = flip(small, "team", 2)
    wout_got = flip(wout_grad[1:], "mp", 1)
    ff_all = spread(ff_piece, "copy", copies)
    small = small + small_got
    wout_grad = (wout_grad[:1].astype(wide) + wout_got.astype(wide)).astype(low)
    qkv_grad, small, wout_grad, ff_all = sync(qkv_grad, small, wout_grad, ff_all)

    for bit in reversed(bits_of(copies)):
        qkv_grad = halve(qkv_grad.reshape((2, -1) + qkv_grad.shape[1:]), 0, "copy", bit)
    for bit in bits_of(copies):
        small = small + flip(small, "copy", bit)
    ff_all = double(ff_all, "team", 2)
    wout_grad = wout_grad.reshape(-1, depth)
    qkv_grad = qkv_grad.reshape(-1, 3 * head_width)
    columns = [
        jnp.concatenate(
            [
                qkv_grad[:, (3 * pair + slot) * pair_width : (3 * pair + slot + 1) * pair_width]
                for pair in range(pairs)
            ],
            axis=1,
        )
        for slot in range(3)
    ] + [wout_grad[:, start : start + head_width] for start in range(0, depth, head_width)]
    flat, small, ff_all = sync(jnp.concatenate(columns), small, ff_all)

    flat = spread(flat, "copy", copies)
    small = small + flip(small, "mp", 1)
    ff_all = double(ff_all, "team", 1)
    flat, small, ff_all = sync(flat, small, ff_all)
    flat = double(flat, "team", 2)
    small = small + flip(small, "mp", 2)
    grad_up, grad_down = feed_grads_out(
        ff_all.reshape(TEAM * copies, 2, unit, depth), copies
    )
    flat, small, grad_up, grad_down = sync(flat, small, grad_up, grad_down)
    flat = double(flat, "team", 1)
    grad_qkv, grad_wout = attention_grads_out(
        flat.reshape(TEAM * copies, -1, head_width), depth, head_width
    )

    small = small.reshape(-1)
    lines = [small[index * depth : (index + 1) * depth] for index in range(5)]
    start = 5 * depth
    count = TEAM * team_units
    up_sums = small[start : start + parts * count].reshape(parts, count)
    grad_up_bias = lax.dynamic_index_in_dim(up_sums, part, 0, keepdims=False)
    start = start + parts * count
    count = rel_table.size
    table_all = small[start : start + parts * count].reshape(parts, count)
    grad_table = lax.dynamic_index_in_dim(table_all, part, 0, keepdims=False).reshape(
        rel_table.shape
    )

    grad_first = after(grad_first, grad_qkv, grad_wout)
    grad_first_norm = normalize_backward(grad_first, ln1_gain, unit1, inverse1)
    grad_tokens = (grad_hidden + grad_first_norm).astype(low)
    return (
        layer_out, grad_tokens, lines[0], lines[1], grad_qkv, grad_table, grad_wout,
        lines[2], lines[3], grad_up, grad_up_bias, grad_down, lines[4],
    )


def solution(mesh):
    groups, parts = mesh.shape["dp"], mesh.shape["mp"]
    split = Mesh(
        mesh.devices.reshape(groups // TEAM, TEAM, parts), ("copy", "team", "mp")
    )
    every = ("copy", "team", "mp")
    return jax.shard_map(
        body,
        mesh=split,
        in_specs=(
            P(every, None), P(("copy", "team"), None), P(), P(), P(), P(None, None, "mp"),
            P(None, "mp"), P("mp", None), P(), P(), P(None, "mp"), P("mp"), P("mp", None), P(),
            P(every, None),
        ),
        out_specs=(
            P(every, None), P(every, None), P(), P(), P(None, None, "mp"), P(None, "mp"),
            P("mp", None), P(), P(), P(None, "mp"), P("mp"), P("mp", None), P(),
        ),
        check_vma=False,
    )
```

```python
import functools

import jax
import jax.numpy as jnp
from jax import lax
from jax.experimental import pallas as pl
from jax.experimental.pallas import tpu as pltpu
from jax.sharding import Mesh, PartitionSpec as P

EPSILON = 1e-05
HIGHEST_PRECISION = lax.Precision.HIGHEST
LIGHT = pl.CostEstimate(flops=1, bytes_accessed=1, transcendentals=0)
BLK = 256
HEAD_LANES = 64
NEAR = 128


def head_mask(rows, width, head, axis):
    place = lax.broadcasted_iota(jnp.int32, (rows, width), axis)
    return (place >= head * HEAD_LANES) & (place < (head + 1) * HEAD_LANES)


def one_head(value, head):
    keep = head_mask(value.shape[0], value.shape[1], head, 1)
    return jnp.where(keep, value, jnp.zeros_like(value))


def scaled(queries):
    return queries * jnp.asarray(HEAD_LANES ** -0.5, queries.dtype)


def dot_nt(left, right):
    return lax.dot_general(
        left, right, (((1,), (1,)), ((), ())), preferred_element_type=jnp.float32
    )


def dot_nn(left, right):
    return lax.dot_general(
        left, right, (((1,), (0,)), ((), ())), preferred_element_type=jnp.float32
    )


def attention_forward_kernel(
    cut_ref, qkv_ref, bias_ref, out_ref, lse_ref, tile_ref, masked_v, score_ref, *, first_head
):
    heads = masked_v.shape[0]
    width = out_ref.shape[1]
    block = pl.program_id(0)
    cut = cut_ref[0]

    @pl.when(block == 0)
    def _():
        for head in range(heads):
            wide = jnp.broadcast_to(bias_ref[first_head + head : first_head + head + 1, :], (BLK, 2 * BLK))
            tile_ref[head] = pltpu.roll(wide, 0, 1, stride=1, stride_axis=0)
            masked_v[head] = one_head(qkv_ref[:, 2 * width :], head)

    row_start = block * BLK
    first = jnp.where(row_start >= cut, cut // BLK, 0)
    rows = row_start + lax.broadcasted_iota(jnp.int32, (BLK, BLK), 0)
    seg_start = jnp.where(rows >= cut, cut, 0)
    columns = lax.broadcasted_iota(jnp.int32, (BLK, BLK), 1)
    q_block = scaled(qkv_ref[pl.ds(pl.multiple_of(row_start, BLK), BLK), 0:width])
    q_heads = [one_head(q_block, head) for head in range(heads)]

    def scores_of(key_block, tops):
        key_start = pl.multiple_of(key_block * BLK, BLK)
        keys = qkv_ref[pl.ds(key_start, BLK), width : 2 * width]
        places = key_start + columns
        allowed = (places <= rows) & (places >= seg_start)
        offset = pl.multiple_of(jnp.maximum(key_block - block + 1, 0) * BLK, BLK)
        near = key_block - block + 1 >= 0
        new_tops = []
        for head in range(heads):
            raw = dot_nt(q_heads[head], keys)
            far = bias_ref[first_head + head : first_head + head + 1, 2 * BLK - 1 : 2 * BLK]
            bias = jnp.where(near, tile_ref[head, :, pl.ds(offset, BLK)], far)
            scores = jnp.where(allowed, raw + bias, -1e30)
            score_ref[head, :, pl.ds(key_start, BLK)] = scores
            top = tops[head]
            for lane in range(0, BLK, 128):
                top = jnp.maximum(top, scores[:, lane : lane + 128])
            new_tops.append(top)
        return tuple(new_tops)

    start = tuple(jnp.full((BLK, 128), -1e30, jnp.float32) for _ in range(heads))
    tops = lax.fori_loop(first, block + 1, scores_of, start)
    tops = [jnp.max(top, axis=1, keepdims=True) for top in tops]

    def weighted(key_block, carry):
        total, sums = carry
        key_start = pl.multiple_of(key_block * BLK, BLK)
        new_sums = []
        pieces = []
        values = []
        for head in range(heads):
            soft = jnp.exp(score_ref[head, :, pl.ds(key_start, BLK)] - tops[head])
            part = sums[head]
            for lane in range(0, BLK, 128):
                part = part + soft[:, lane : lane + 128]
            new_sums.append(part)
            pieces.append(soft.astype(jnp.bfloat16))
            values.append(masked_v[head, pl.ds(key_start, BLK), :])
        total = total + dot_nn(
            jnp.concatenate(pieces, axis=1), jnp.concatenate(values, axis=0)
        )
        return total, tuple(new_sums)

    total, sums = lax.fori_loop(
        first,
        block + 1,
        weighted,
        (
            jnp.zeros((BLK, heads * HEAD_LANES), jnp.float32),
            tuple(jnp.zeros((BLK, 128), jnp.float32) for _ in range(heads)),
        ),
    )
    lanes = lax.broadcasted_iota(jnp.int32, (BLK, heads * HEAD_LANES), 1)
    narrow = lax.broadcasted_iota(jnp.int32, (BLK, 128), 1)
    scale = jnp.zeros((BLK, heads * HEAD_LANES), jnp.float32)
    logs = jnp.zeros((BLK, 128), jnp.float32)
    for head in range(heads):
        sum_one = jnp.sum(sums[head], axis=1, keepdims=True)
        scale = jnp.where(lanes // HEAD_LANES == head, 1.0 / sum_one, scale)
        logs = jnp.where(narrow == head, tops[head] + jnp.log(sum_one), logs)
    out_ref[...] = (total * scale).astype(jnp.bfloat16)
    lse_ref[...] = jnp.transpose(logs)[0:8, :]


def attention_forward(cut, projected, near_bias, first_head):
    length, width = projected.shape[0], projected.shape[1] // 3
    heads = width // HEAD_LANES
    whole = lambda block, cut: (0, 0)
    return pl.pallas_call(
        functools.partial(attention_forward_kernel, first_head=first_head),
        grid_spec=pltpu.PrefetchScalarGridSpec(
            num_scalar_prefetch=1,
            grid=(length // BLK,),
            in_specs=[
                pl.BlockSpec((length, 3 * width), whole),
                pl.BlockSpec((8, 2 * BLK), whole),
            ],
            out_specs=[
                pl.BlockSpec((BLK, width), lambda block, cut: (block, 0)),
                pl.BlockSpec((8, BLK), lambda block, cut: (0, block)),
            ],
            scratch_shapes=[
                pltpu.VMEM((heads, BLK, 2 * BLK), jnp.float32),
                pltpu.VMEM((heads, length, width), jnp.bfloat16),
                pltpu.VMEM((heads, BLK, length), jnp.float32),
            ],
        ),
        out_shape=[
            jax.ShapeDtypeStruct((length, width), jnp.bfloat16),
            jax.ShapeDtypeStruct((8, length), jnp.float32),
        ],
        compiler_params=pltpu.CompilerParams(
            dimension_semantics=("arbitrary",), vmem_limit_bytes=48 * 1024 * 1024
        ),
        cost_estimate=LIGHT,
        name="attention_forward",
    )(cut, projected, near_bias)


def attention_backward_kernel(
    cut_ref, qkv_a, qkv_b, grad_ref, att_a, att_b, lse_a, lse_b, bias_ref,
    dqkv_a, dqkv_b, table_ref,
    tile_ref, q_masked, grad_masked, delta_ref, dq_sum, near_sum, far_sum,
):
    heads = q_masked.shape[0]
    block = pl.program_id(0)
    n_blocks = pl.num_programs(0)
    length = grad_ref.shape[0]
    width = att_a.shape[1]
    cut = cut_ref[0]
    qkv_refs, att_refs, lse_refs, out_refs = (
        (qkv_a, qkv_b), (att_a, att_b), (lse_a, lse_b), (dqkv_a, dqkv_b)
    )

    @pl.when(block == 0)
    def _():
        row = lax.broadcasted_iota(jnp.int32, (16, width), 0)
        lane = lax.broadcasted_iota(jnp.int32, (16, width), 1)
        pick = jnp.where(lane // HEAD_LANES == row, 1.0, 0.0).astype(jnp.bfloat16)
        for pair in range(2):
            grad_pair = grad_ref[:, pair * width : (pair + 1) * width]
            product = grad_pair.astype(jnp.float32) * att_refs[pair][...].astype(jnp.float32)
            high = product.astype(jnp.bfloat16)
            rest = (product - high.astype(jnp.float32)).astype(jnp.bfloat16)
            delta_ref[pair] = (dot_nt(pick, high) + dot_nt(pick, rest))[0:8, :]
            queries = scaled(qkv_refs[pair][:, 0:width])
            for place in range(2):
                head = 2 * pair + place
                q_masked[head] = one_head(queries, place)
                grad_masked[head] = one_head(grad_pair, place)
        for head in range(heads):
            wide = jnp.broadcast_to(bias_ref[head : head + 1, :], (BLK, 2 * BLK))
            tile_ref[head] = pltpu.roll(wide, 0, 1, stride=1, stride_axis=0)
        dq_sum[...] = jnp.zeros_like(dq_sum)
        near_sum[...] = jnp.zeros_like(near_sum)
        far_sum[...] = jnp.zeros_like(far_sum)

    key_start = pl.multiple_of(block * BLK, BLK)
    keys = [ref[pl.ds(key_start, BLK), width : 2 * width] for ref in qkv_refs]
    values = [ref[pl.ds(key_start, BLK), 2 * width :] for ref in qkv_refs]
    keys_t = [jnp.transpose(one) for one in keys]
    places = key_start + lax.broadcasted_iota(jnp.int32, (BLK, BLK), 0)
    columns = lax.broadcasted_iota(jnp.int32, (BLK, BLK), 1)
    last = jnp.where(key_start + BLK <= cut, (cut + BLK - 1) // BLK, n_blocks)

    def one_block(query_block, carry):
        row_start = pl.multiple_of(query_block * BLK, BLK)
        rows = row_start + columns
        allowed = (places <= rows) & (places >= jnp.where(rows >= cut, cut, 0))
        distance = query_block - block
        near = distance <= 1
        offset = pl.multiple_of(jnp.minimum(distance, 1) * BLK, BLK)
        results = []
        for pair in range(2):
            soft_pieces, grad_pieces, q_pieces, out_pieces = [], [], [], []
            for place in range(2):
                head = 2 * pair + place
                q_head = q_masked[head, pl.ds(row_start, BLK), :]
                grad_head = grad_masked[head, pl.ds(row_start, BLK), :]
                far = bias_ref[head : head + 1, BLK - 1 : BLK]
                bias = jnp.where(near, tile_ref[head, :, pl.ds(offset, BLK)], far)
                scores = dot_nt(keys[pair], q_head) + bias
                log_total = lse_refs[pair][place : place + 1, pl.ds(row_start, BLK)]
                soft = jnp.exp(jnp.where(allowed, scores - log_total, -1e30))
                grad_soft = dot_nt(values[pair], grad_head)
                delta = delta_ref[pair, place : place + 1, pl.ds(row_start, BLK)]
                grad_scores = soft * (grad_soft - delta)
                grad_low = grad_scores.astype(jnp.bfloat16)

                @pl.when(near)
                def _():
                    near_sum[head, :, pl.ds(offset, BLK)] += grad_scores

                @pl.when(jnp.logical_not(near))
                def _():
                    far_sum[head] += jnp.sum(
                        grad_scores.reshape(BLK // 8, 8, BLK), axis=0
                    )

                own = slice(place * HEAD_LANES, (place + 1) * HEAD_LANES)
                spot = slice(head * HEAD_LANES, (head + 1) * HEAD_LANES)
                dq_sum[spot, pl.ds(row_start, BLK)] += dot_nn(keys_t[pair][own, :], grad_low)
                soft_pieces.append(soft.astype(jnp.bfloat16))
                grad_pieces.append(grad_low)
                q_pieces.append(q_head)
                out_pieces.append(grad_head)
            dk, dv = carry[pair]
            dv = dv + dot_nn(
                jnp.concatenate(soft_pieces, axis=1), jnp.concatenate(out_pieces, axis=0)
            )
            dk = dk + dot_nn(
                jnp.concatenate(grad_pieces, axis=1), jnp.concatenate(q_pieces, axis=0)
            )
            results.append((dk, dv))
        return tuple(results)

    empty = jnp.zeros((BLK, width), jnp.float32)
    results = lax.fori_loop(block, last, one_block, ((empty, empty), (empty, empty)))
    for pair in range(2):
        dk, dv = results[pair]
        out_refs[pair][pl.ds(key_start, BLK), width : 2 * width] = dk.astype(jnp.bfloat16)
        out_refs[pair][pl.ds(key_start, BLK), 2 * width :] = dv.astype(jnp.bfloat16)

    @pl.when(block == n_blocks - 1)
    def _():
        for query_block in range(length // BLK):
            spot = slice(query_block * BLK, (query_block + 1) * BLK)
            turned = (jnp.transpose(dq_sum[:, spot]) * (HEAD_LANES ** -0.5)).astype(jnp.bfloat16)
            for pair in range(2):
                out_refs[pair][spot, 0:width] = turned[:, pair * width : (pair + 1) * width]
        for head in range(heads):
            lined = jnp.zeros((8, 2 * BLK), jnp.float32)
            for group in range(BLK // 8):
                piece = near_sum[head, group * 8 : group * 8 + 8, :]
                shift = (2 * BLK - group * 8) % (2 * BLK)
                lined = lined + (pltpu.roll(piece, shift, 1) if shift else piece)
            total = lined[0:1, :]
            for row in range(1, 8):
                total = total + pltpu.roll(lined, 2 * BLK - row, 1)[row : row + 1, :]
            table_ref[head : head + 1, :] = total
            rest = jnp.sum(far_sum[head], axis=0, keepdims=True)
            table_ref[heads + head : heads + head + 1, :] = jnp.concatenate(
                [rest, jnp.zeros_like(rest)], axis=1
            )


def attention_backward(cut, projected, grad_att, attended, logs, near_bias):
    length, width = attended[0].shape
    heads = 2 * width // HEAD_LANES
    whole = lambda block, cut: (0, 0)
    full = lambda columns: pl.BlockSpec((length, columns), whole)
    lse = pl.BlockSpec((8, length), whole)
    return pl.pallas_call(
        attention_backward_kernel,
        grid_spec=pltpu.PrefetchScalarGridSpec(
            num_scalar_prefetch=1,
            grid=(length // BLK,),
            in_specs=[
                full(3 * width), full(3 * width), full(2 * width), full(width), full(width),
                lse, lse, pl.BlockSpec((8, 2 * BLK), whole),
            ],
            out_specs=[
                full(3 * width), full(3 * width), pl.BlockSpec((8, 2 * BLK), whole),
            ],
            scratch_shapes=[
                pltpu.VMEM((heads, BLK, 2 * BLK), jnp.float32),
                pltpu.VMEM((heads, length, width), jnp.bfloat16),
                pltpu.VMEM((heads, length, width), jnp.bfloat16),
                pltpu.VMEM((2, 8, length), jnp.float32),
                pltpu.VMEM((2 * width, length), jnp.float32),
                pltpu.VMEM((heads, BLK, 2 * BLK), jnp.float32),
                pltpu.VMEM((heads, 8, BLK), jnp.float32),
            ],
        ),
        out_shape=[
            jax.ShapeDtypeStruct((length, 3 * width), jnp.bfloat16),
            jax.ShapeDtypeStruct((length, 3 * width), jnp.bfloat16),
            jax.ShapeDtypeStruct((8, 2 * BLK), jnp.float32),
        ],
        compiler_params=pltpu.CompilerParams(
            dimension_semantics=("arbitrary",), vmem_limit_bytes=48 * 1024 * 1024
        ),
        cost_estimate=LIGHT,
        name="attention_backward",
    )(cut, *projected, grad_att, *attended, *logs, near_bias)


def distance_bias(rel_table, bucket_of):
    hot = (
        bucket_of[:, None] == jnp.arange(rel_table.shape[0], dtype=jnp.int32)[None, :]
    ).astype(jnp.float32)
    by_distance = jnp.einsum(
        "dn,nh->hd", hot, rel_table, precision=HIGHEST_PRECISION,
        preferred_element_type=jnp.float32,
    )
    return hot, by_distance


def near_tables(by_distance):
    heads, reach = by_distance.shape
    far = by_distance[:, reach - 1 :]
    forward = jnp.concatenate(
        [
            jnp.broadcast_to(far, (heads, BLK - reach + 1)),
            by_distance[:, ::-1],
            jnp.broadcast_to(far, (heads, BLK - 1)),
        ],
        axis=1,
    )
    backward = jnp.concatenate(
        [by_distance, jnp.broadcast_to(far, (heads, 2 * BLK - reach))], axis=1
    )
    rows = ((0, 8 - heads), (0, 0))
    return jnp.pad(forward, rows), jnp.pad(backward, rows)


def table_gradient(hot, near_sums, far_sums):
    reach = hot.shape[0]
    near = near_sums[:, : reach - 1]
    far = jnp.sum(near_sums[:, reach - 1 :], axis=1) + jnp.sum(far_sums, axis=1)
    by_distance = jnp.concatenate([near, far[:, None]], axis=1)
    return jnp.einsum(
        "dn,hd->nh", hot, by_distance, precision=HIGHEST_PRECISION,
        preferred_element_type=jnp.float32,
    )


TEAM = 4


def after(value, *gates):
    return lax.optimization_barrier((value,) + gates)[0]


def flip(value, axis, bit):
    size = lax.axis_size(axis)
    return lax.ppermute(value, axis, [(i, i ^ bit) for i in range(size)])


def halve(value, dim, axis, bit):
    mine = (lax.axis_index(axis) // bit) % 2
    keep = lax.dynamic_index_in_dim(value, mine, dim, keepdims=False)
    send = lax.dynamic_index_in_dim(value, 1 - mine, dim, keepdims=False)
    received = flip(send.astype(jnp.bfloat16), axis, bit)
    return (keep.astype(jnp.float32) + received.astype(jnp.float32)).astype(jnp.bfloat16)


def halve_start(value, dim, axis, bit):
    mine = (lax.axis_index(axis) // bit) % 2
    keep = lax.dynamic_index_in_dim(value, mine, dim, keepdims=False)
    send = lax.dynamic_index_in_dim(value, 1 - mine, dim, keepdims=False)
    return keep, flip(send, axis, bit)


def halve_end(pair):
    return (pair[0].astype(jnp.float32) + pair[1].astype(jnp.float32)).astype(jnp.bfloat16)


def double(value, axis, bit):
    mine = (lax.axis_index(axis) // bit) % 2
    other = flip(value, axis, bit)
    return jnp.where(mine == 0, jnp.stack([value, other]), jnp.stack([other, value]))


def bits_of(size):
    bits = []
    bit = 1
    while bit < size:
        bits.append(bit)
        bit *= 2
    return bits


def with_partner(own):
    return jnp.concatenate([own, flip(own, "team", 1)], axis=0)


def feed_grads_kernel(piece_ref, up_ref, down_ref):
    up_ref[...] = jnp.transpose(piece_ref[0, 0].astype(jnp.float32))
    down_ref[...] = piece_ref[0, 1].astype(jnp.float32)


def feed_grads_out(pieces, copies):
    count, _, unit, depth = pieces.shape
    merge = max(1, 128 // unit)
    if merge > 1:
        pieces = jnp.transpose(
            pieces.reshape(count // merge, merge, 2, unit, depth), (0, 2, 1, 3, 4)
        ).reshape(count // merge, 2, merge * unit, depth)
    count, _, unit, depth = pieces.shape
    each = copies // merge

    def spot(step):
        core, side, place = place_in_group(step, each)
        return (side * 2 + core) * each + place

    return pl.pallas_call(
        feed_grads_kernel,
        grid=(count,),
        in_specs=[pl.BlockSpec((1, 2, unit, depth), lambda step: (step, 0, 0, 0))],
        out_specs=[
            pl.BlockSpec((depth, unit), lambda step: (0, spot(step))),
            pl.BlockSpec((unit, depth), lambda step: (spot(step), 0)),
        ],
        out_shape=[
            jax.ShapeDtypeStruct((depth, count * unit), jnp.float32),
            jax.ShapeDtypeStruct((count * unit, depth), jnp.float32),
        ],
        compiler_params=pltpu.CompilerParams(dimension_semantics=("arbitrary",)),
        cost_estimate=LIGHT,
        name="feed_grads_out",
    )(pieces)


def attention_grads_kernel(piece_ref, qkv_ref, out_ref):
    group = piece_ref.shape[0]
    rows, width = qkv_ref.shape[1] // group, qkv_ref.shape[2]
    few = out_ref.shape[0] // group
    for item in range(group):
        for slot in range(3):
            qkv_ref[slot, item * rows : (item + 1) * rows, :] = piece_ref[
                item, slot * rows : (slot + 1) * rows, :
            ].astype(jnp.float32)
        for place in range(out_ref.shape[1] // width):
            start = 3 * rows + place * few
            out_ref[item * few : (item + 1) * few, place * width : (place + 1) * width] = (
                piece_ref[item, start : start + few, :].astype(jnp.float32)
            )


def attention_grads_out(pieces, depth, head_width):
    count = pieces.shape[0]
    rows, few = depth // count, head_width // count
    group = max(1, 8 // few)
    copies = count // TEAM

    def spot(step):
        if copies != 2:
            return step
        core, side, place = place_in_group(step, copies)
        return (core * 2 + side) * copies + place

    return pl.pallas_call(
        attention_grads_kernel,
        grid=(count // group,),
        in_specs=[
            pl.BlockSpec((group,) + pieces.shape[1:], lambda step: (step, 0, 0)),
        ],
        out_specs=[
            pl.BlockSpec((3, group * rows, head_width), lambda step: (0, spot(step), 0)),
            pl.BlockSpec((group * few, depth), lambda step: (spot(step), 0)),
        ],
        out_shape=[
            jax.ShapeDtypeStruct((3, depth, head_width), jnp.float32),
            jax.ShapeDtypeStruct((head_width, depth), jnp.float32),
        ],
        compiler_params=pltpu.CompilerParams(dimension_semantics=("arbitrary",)),
        cost_estimate=LIGHT,
        name="attention_grads_out",
    )(pieces)


def normalize(inputs):
    center = inputs - jnp.mean(inputs, axis=-1, keepdims=True)
    spread = jnp.mean(center * center, axis=-1, keepdims=True)
    inverse = lax.rsqrt(spread + EPSILON)
    return center * inverse, inverse


def normalize_backward(grad, gain, unit, inverse):
    scaled_grad = grad * gain
    middle = jnp.mean(scaled_grad, axis=-1, keepdims=True)
    along = jnp.mean(scaled_grad * unit, axis=-1, keepdims=True)
    return (scaled_grad - middle - unit * along) * inverse


def dot_tn(left, right):
    return lax.dot_general(
        left, right, (((0,), (0,)), ((), ())), preferred_element_type=jnp.float32
    )


def copies_of(value, size):
    halves = [value[None]]
    for bit in bits_of(size):
        value = halves[0] if len(halves) == 1 else jnp.concatenate(halves)
        halves = [value, flip(value, "copy", bit)]
    return halves


def untangle(value, axis, index, size):
    for bit in bits_of(size):
        shape = value.shape
        split = value.reshape(
            shape[:axis] + (size // (2 * bit), 2, bit) + shape[axis + 1 :]
        )
        split = jnp.where((index // bit) % 2 == 1, jnp.flip(split, axis + 1), split)
        value = split.reshape(shape)
    return value


def orders(copies):
    first = [("copy", bit) for bit in bits_of(copies)] + [("team", 2)]
    return first, first[::-1] if copies == 2 else first


def spread_group(value, step, copies):
    choices = [order[step] for order in orders(copies)]
    moves = []
    for place in range(copies * TEAM):
        axis, bit = choices[place % 2]
        moves.append((place, place ^ (bit if axis == "team" else bit * TEAM)))
    got = lax.ppermute(value, ("copy", "team"), moves)
    mine = [(lax.axis_index(axis) // bit) % 2 for axis, bit in choices]
    mine = jnp.where(lax.axis_index("team") % 2 == 0, mine[0], mine[1])
    return jnp.where(mine == 0, jnp.stack([value, got]), jnp.stack([got, value]))


def place_in_group(step, copies):
    core, index = step // (2 * copies), step % (2 * copies)
    if copies != 2:
        return core, index // copies, index % copies
    outer, inner = index // 2, index % 2
    return core, outer + core * (inner - outer), inner + core * (outer - inner)


def exchange(blocks):
    return [blocks[0]] + [flip(blocks[k], "mp", k) for k in range(1, len(blocks))]


def cotangent_kernel(grad_a, grad_b, weight_a, weight_b, normed_ref, line_ref, out_ref, sum_ref):
    grad = sum(
        dot_nt(grad_ref[...], jnp.concatenate([weight_ref[slot] for slot in range(3)], axis=1))
        for grad_ref, weight_ref in ((grad_a, weight_a), (grad_b, weight_b))
    )
    unit = (normed_ref[...].astype(jnp.float32) - line_ref[0:1, :]) * line_ref[1:2, :]
    out_ref[...] = grad.astype(jnp.bfloat16)
    rows, depth = grad.shape
    both = jnp.concatenate(
        [
            jnp.sum((grad * unit).reshape(rows // 8, 8, depth), axis=0),
            jnp.sum(grad.reshape(rows // 8, 8, depth), axis=0),
        ],
        axis=0,
    )

    @pl.when(pl.program_id(0) == 0)
    def _():
        sum_ref[...] = both

    @pl.when(pl.program_id(0) > 0)
    def _():
        sum_ref[...] += both


def input_cotangent(grads, weights, normed, lines):
    length, width = grads[0].shape
    depth = weights.shape[1]
    row = pl.BlockSpec((BLK, width), lambda step: (step, 0))
    part_a = pl.BlockSpec((3, depth, width // 3), lambda step: (0, 0, 0))
    part_b = pl.BlockSpec((3, depth, width // 3), lambda step: (0, 0, 1))
    return pl.pallas_call(
        cotangent_kernel,
        grid=(length // BLK,),
        in_specs=[
            row, row, part_a, part_b,
            pl.BlockSpec((BLK, depth), lambda step: (step, 0)),
            pl.BlockSpec((2, depth), lambda step: (0, 0)),
        ],
        out_specs=[
            pl.BlockSpec((BLK, depth), lambda step: (step, 0)),
            pl.BlockSpec((16, depth), lambda step: (0, 0)),
        ],
        out_shape=[
            jax.ShapeDtypeStruct((length, depth), jnp.bfloat16),
            jax.ShapeDtypeStruct((16, depth), jnp.float32),
        ],
        compiler_params=pltpu.CompilerParams(dimension_semantics=("arbitrary",)),
        cost_estimate=LIGHT,
        name="input_cotangent",
    )(*grads, weights, weights, normed, lines)


def feed_kernel(*refs, unit, count):
    weight_refs = refs[:count]
    (
        bias_ref, second_ref, grad_ref,
        act_ref, pre_ref, back_own, back_other, out_own, out_other, sum_ref,
    ) = refs[count:]
    w_up, w_down = (
        jnp.concatenate(
            [
                ref[:, start : start + unit, :].reshape(ref.shape[0] * unit, ref.shape[2])
                for ref in weight_refs
            ]
        )
        for start in (0, unit)
    )
    pre = dot_nt(second_ref[...], w_up) + bias_ref[...]
    grad_act = dot_nt(grad_ref[...], w_down)
    cdf = 0.5 + 0.5 * lax.erf(pre * 0.7071067811865476)
    pdf = jnp.exp(pre * pre * -0.5) * 0.3989422804014327
    active = (pre * cdf).astype(jnp.bfloat16)
    grad_pre = ((cdf + pre * pdf) * grad_act).astype(jnp.bfloat16)
    act_ref[...] = active
    pre_ref[...] = grad_pre
    line = jnp.sum(grad_pre.astype(jnp.float32), axis=0, keepdims=True)
    back = dot_nn(grad_pre, w_up).astype(jnp.bfloat16)
    out = dot_nn(active, w_down).astype(jnp.bfloat16)

    @pl.when(pl.program_id(0) == 0)
    def _():
        back_own[...] = back
        out_own[...] = out
        sum_ref[...] = line

    @pl.when(pl.program_id(0) == 1)
    def _():
        back_other[...] = back
        out_other[...] = out
        sum_ref[...] += line


def feed_forward(weights, bias_row, second, grad, unit):
    depth = weights[0].shape[2]
    rows = second.shape[0]
    width = unit * sum(one.shape[0] for one in weights)
    take = rows // 2
    row = pl.BlockSpec((take, depth), lambda step: (step, 0))
    one = pl.BlockSpec((take, depth), lambda step: (0, 0))
    wide = pl.BlockSpec((take, width), lambda step: (step, 0))
    line = pl.BlockSpec((1, width), lambda step: (0, 0))
    part = jax.ShapeDtypeStruct((take, depth), jnp.bfloat16)
    return pl.pallas_call(
        functools.partial(feed_kernel, unit=unit, count=len(weights)),
        grid=(2,),
        in_specs=[pl.BlockSpec(each.shape, lambda step: (0, 0, 0)) for each in weights]
        + [line, row, row],
        out_specs=[wide, wide, one, one, one, one, line],
        out_shape=[
            jax.ShapeDtypeStruct((rows, width), jnp.bfloat16),
            jax.ShapeDtypeStruct((rows, width), jnp.bfloat16),
            part, part, part, part,
            jax.ShapeDtypeStruct((1, width), jnp.float32),
        ],
        compiler_params=pltpu.CompilerParams(
            dimension_semantics=("arbitrary",), vmem_limit_bytes=48 * 1024 * 1024
        ),
        cost_estimate=LIGHT,
        name="feed_forward",
    )(*weights, bias_row, second, grad)


def weight_grad_kernel(
    spot_ref, act_a, act_b, pre_a, pre_b, second_a, second_b, grad_a, grad_b, out_ref
):
    _, copies, _, unit, _ = out_ref.shape
    up = dot_tn(pre_a[...], second_a[...]) + dot_tn(pre_b[...], second_b[...])
    down = dot_tn(act_a[...], grad_a[...]) + dot_tn(act_b[...], grad_b[...])
    for place in range(copies):
        rows = slice(place * unit, (place + 1) * unit)
        out_ref[0, spot_ref[1] ^ place, 0] = up[rows].astype(jnp.bfloat16)
        out_ref[0, spot_ref[1] ^ place, 1] = down[rows].astype(jnp.bfloat16)


def weight_grads(spot, acts, pres, seconds, grads, parts, copies):
    rows, width = acts[0].shape
    depth = seconds[0].shape[1]
    unit = width // (parts * copies)
    column = pl.BlockSpec((rows, width // parts), lambda step, part: (0, step))
    whole = pl.BlockSpec((rows, depth), lambda step, part: (0, 0))
    return pl.pallas_call(
        weight_grad_kernel,
        grid_spec=pltpu.PrefetchScalarGridSpec(
            num_scalar_prefetch=1,
            grid=(parts,),
            in_specs=[column] * 4 + [whole] * 4,
            out_specs=pl.BlockSpec(
                (1, copies, 2, unit, depth), lambda step, part: (part[0] ^ step, 0, 0, 0, 0)
            ),
        ),
        out_shape=jax.ShapeDtypeStruct((parts, copies, 2, unit, depth), jnp.bfloat16),
        compiler_params=pltpu.CompilerParams(
            dimension_semantics=("arbitrary",), vmem_limit_bytes=56 * 1024 * 1024
        ),
        cost_estimate=LIGHT,
        name="weight_grads",
    )(spot, *acts, *pres, *seconds, *grads)


def sync(*values):
    return lax.optimization_barrier(values)


def body(
    tokens, seg_ids, bucket_of, ln1_gain, ln1_bias, w_qkv, rel_table, w_out,
    ln2_gain, ln2_bias, w_up, up_bias, w_down, down_bias, out_grad,
):
    low = jnp.bfloat16
    wide = jnp.float32
    copies = lax.axis_size("copy")
    parts = lax.axis_size("mp")
    copy = lax.axis_index("copy")
    member = lax.axis_index("team")
    part = lax.axis_index("mp")
    core = member % 2
    rows, depth = tokens.shape
    head_width = w_out.shape[0]
    pair_width = 2 * HEAD_LANES
    pairs = head_width // pair_width
    team_units = w_up.shape[1] // TEAM
    unit = team_units // copies
    out_rows = head_width // (2 * copies)
    seg_row = seg_ids[0]
    to_right = [(i, i + 1) for i in range(parts - 1)]
    to_left = [(i + 1, i) for i in range(parts - 1)]

    def relay(right, left, step):
        return (
            lax.ppermute(right, "mp", to_right[step - 1 :]),
            lax.ppermute(left, "mp", to_left[: parts - step]),
        )

    def corner_of(right1, left1, right3, left3):
        return jnp.where(
            (part == 0) | (part == parts - 1), right3 + left3, jnp.where(part == 1, left1, right1)
        )

    x_part = tokens.astype(wide)
    unit1, inverse1 = normalize(x_part)
    normed = lax.all_gather(
        (unit1 * ln1_gain + ln1_bias).astype(low), "mp", axis=0, tiled=True
    )
    def own_units(place):
        first = member * team_units + (copy ^ place) * unit
        return jnp.concatenate(
            [
                jnp.transpose(lax.dynamic_slice_in_dim(w_up, first, unit, 1)),
                lax.dynamic_slice_in_dim(w_down, first, unit, 0),
            ]
        )

    own_slot = jnp.stack([own_units(place) for place in range(copies)])
    out_own = lax.dynamic_slice_in_dim(w_out, (copy * 2 + core) * out_rows, out_rows, 0)
    piece = jnp.concatenate([own_slot[0], out_own])
    w_right1, w_left1 = relay(piece, piece, 1)
    grad_across = flip(out_grad, "team", 2)
    grad_near = with_partner(out_grad)
    grad_far = with_partner(grad_across)
    biases = [up_bias] + [flip(up_bias, "mp", k) for k in range(1, parts)]
    bias_row = jnp.concatenate(
        [
            lax.dynamic_slice_in_dim(one, member * team_units + (copy ^ place) * unit, unit, 0)
            for one in biases
            for place in range(copies)
        ]
    )[None]
    w_cat = [
        jnp.transpose(
            w_qkv[:, :, pair * pair_width : (pair + 1) * pair_width], (1, 0, 2)
        ).reshape(depth, -1)
        for pair in range(pairs)
    ]
    hot, by_distance = distance_bias(rel_table, bucket_of)
    forward_bias, backward_bias = near_tables(by_distance)
    cut = jnp.sum((seg_row == seg_row[0]).astype(jnp.int32)).reshape(1)
    normed = after(
        normed, grad_near, grad_far, bias_row, own_slot, w_cat[0], w_cat[1], forward_bias,
        backward_bias, cut, w_right1, w_left1,
    )

    def attend(pair, projected):
        return attention_forward(cut, projected, forward_bias, 2 * pair)

    def send_rows(att_one):
        blocks = att_one.reshape(parts, rows, pair_width)
        return exchange(
            [
                lax.dynamic_index_in_dim(blocks, part ^ k, 0, keepdims=False)
                for k in range(parts)
            ]
        )

    def whole_out(halves):
        mine = jnp.concatenate([half[:, 2 * unit :] for half in halves])
        mine = untangle(mine, 0, copy, copies)
        other = flip(mine, "team", 1)
        return jnp.where(
            core == 0, jnp.stack([mine, other], axis=1), jnp.stack([other, mine], axis=1)
        ).reshape(head_width, depth)

    projected, attended, logs = [None, None], [None, None], [None, None]
    w_right1, w_left1 = after(w_right1, normed), after(w_left1, normed)
    w_right2, w_left2 = relay(w_right1, w_left1, 2)
    beside = copies_of(jnp.where(part % 2 == 0, w_left1, w_right1), copies)
    projected = [
        jnp.dot(normed, w_one, preferred_element_type=wide).astype(low) for w_one in w_cat
    ]
    attended[0], logs[0] = attend(0, after(projected[0], projected[1]))
    w_right2, w_left2, beside[1], attended[0] = sync(w_right2, w_left2, beside[1], attended[0])
    w_right3, w_left3 = relay(w_right2, w_left2, 3)
    across = copies_of(w_right2 + w_left2, copies)
    moved = [send_rows(attended[0]), None]
    attended[1], logs[1] = attend(1, after(projected[1], across[0]))
    results = sync(w_right3, w_left3, across[1], attended[1], *moved[0])
    w_right3, w_left3, across[1], attended[1] = results[:4]
    moved[0] = list(results[4:])
    corner = copies_of(corner_of(w_right1, w_left1, w_right3, w_left3), copies)
    moved[1] = send_rows(attended[1])
    w_out_full = jnp.concatenate(
        [w_out] + [whole_out(halves) for halves in (beside, across, corner)]
    )
    weights = [own_slot] + beside + across + corner

    own_rows = jnp.concatenate(
        [moved[pair][k] for k in range(parts) for pair in range(pairs)], axis=1
    )
    branch = jnp.dot(own_rows, w_out_full, preferred_element_type=wide)
    hidden_in = x_part + branch
    unit2, inverse2 = normalize(hidden_in)
    second = (unit2 * ln2_gain + ln2_bias).astype(low)
    second_across = flip(second, "team", 2)
    second_near = with_partner(second)
    act_near, pre_near, back_own, back_core, feed_own, feed_core, sums_near = feed_forward(
        weights, bias_row, second_near, grad_near, unit
    )
    second_across = after(second_across, back_own)
    back_core = flip(back_core, "team", 1)
    second_far = with_partner(second_across)
    act_far, pre_far, back_side, back_corner, feed_side, feed_corner, sums_far = feed_forward(
        weights, bias_row, second_far, grad_far, unit
    )
    onward = (
        back_side.astype(wide) + flip(back_corner, "team", 1).astype(wide)
    ).astype(low)
    back_across = flip(onward, "team", 2)
    half = depth // 2
    late_normed = after(normed, onward)
    normed_keep = lax.dynamic_slice_in_dim(late_normed, core * half, half, 1)
    normed_send = lax.dynamic_slice_in_dim(late_normed, (1 - core) * half, half, 1)
    feed_stack = jnp.stack([after(feed_corner, onward), feed_core])
    feed_beside = flip(feed_stack, "team", 1)
    ff_grads = weight_grads(
        jnp.stack([part, copy]),
        (act_near, after(act_far, onward, normed_keep, normed_send, feed_stack)),
        (pre_near, pre_far), (second_near, second_far), (grad_near, grad_far), parts, copies,
    )
    ff_piece = lax.psum_scatter(
        ff_grads.reshape(parts * copies, 2 * unit, depth), ("mp", "copy"),
        scatter_dimension=0, tiled=False,
    )
    back_across = after(back_across, ff_grads)
    grad_second = back_own.astype(wide) + back_core.astype(wide) + back_across.astype(wide)
    grad_part = out_grad.astype(wide)
    grad_hidden = grad_part + normalize_backward(grad_second, ln2_gain, unit2, inverse2)
    grad_branch = grad_hidden.astype(low)
    grad_rows = dot_nt(grad_branch, w_out_full).astype(low)
    received = exchange(
        [grad_rows[:, k * head_width : (k + 1) * head_width] for k in range(parts)]
    )
    wout_grad = dot_tn(own_rows, after(grad_branch, grad_rows)).astype(low)
    wout_grad = wout_grad.reshape(parts, 2, 2, copies, -1, depth)
    wout_grad = halve(wout_grad, 1, "team", 1)
    results = sync(wout_grad, feed_beside, *received)
    wout_grad, feed_beside = results[:2]
    received = results[2:]
    wout_pair = halve_start(wout_grad, 1, "team", 2)
    feed_sum = (feed_side.astype(wide) + feed_beside[0].astype(wide)).astype(low)
    feed_across = flip(feed_sum, "team", 2)
    natural = jnp.zeros((parts, rows, head_width), low)
    for k in range(parts):
        natural = lax.dynamic_update_index_in_dim(natural, received[k], part ^ k, 0)
    grad_att = after(natural.reshape(parts * rows, head_width), wout_pair[0], feed_sum)
    first_grads, last_grads, table_sums = attention_backward(
        cut, projected, grad_att, attended, logs, backward_bias
    )
    first_grads, last_grads, wout_last, feed_across, ff_piece = sync(
        first_grads, last_grads, wout_pair[1], feed_across, ff_piece
    )
    dqkv = [first_grads, last_grads]
    wout_grad = halve_end((wout_pair[0], wout_last))
    for bit in reversed(bits_of(copies)):
        wout_grad = wout_grad.reshape((parts, 2, -1) + wout_grad.shape[2:])
        wout_pair = halve_start(wout_grad, 1, "copy", bit)
        if bit > 1:
            wout_grad = halve_end(wout_pair)
    dqkv[0] = after(dqkv[0], wout_pair[0])
    running, line_sums = input_cotangent(
        dqkv, w_qkv, normed, jnp.stack([ln1_bias, 1.0 / ln1_gain])
    )
    grad_first = lax.psum_scatter(running, "mp", scatter_dimension=0, tiled=True).astype(wide)

    wout_last, running = sync(wout_pair[1], running)
    wout_grad = halve_end((wout_pair[0], wout_last)).reshape(parts, -1, depth)
    late = [after(one, running) for one in dqkv]
    qkv_send = jnp.concatenate([dot_tn(normed_send, one).astype(low) for one in late], axis=1)
    qkv_keep = jnp.concatenate([dot_tn(normed_keep, one) for one in late], axis=1)
    table_line = table_gradient(
        hot, table_sums[: table_sums.shape[0] // 2], table_sums[table_sums.shape[0] // 2 :]
    ).reshape(1, -1)
    table_all = lax.dynamic_update_slice_in_dim(
        jnp.zeros((parts, table_line.shape[1]), wide), table_line, part, 0
    )
    grad_second, grad_part, feed_own, sums_near = sync(
        grad_second, grad_part, feed_own, sums_near, running
    )[:4]
    sums = (sums_near + sums_far).reshape(parts, copies, unit)
    sums = untangle(untangle(sums, 0, part, parts), 1, copy, copies)
    up_sums = lax.dynamic_update_slice_in_dim(
        jnp.zeros((parts, TEAM * team_units), wide), sums.reshape(parts, team_units),
        member * team_units, 1,
    )
    lines = [
        jnp.sum(grad_second * unit2, axis=0), jnp.sum(grad_second, axis=0),
        jnp.sum(grad_part, axis=0),
    ]
    early_lines = jnp.concatenate(lines + [up_sums.reshape(-1)])
    small = jnp.concatenate(
        [
            jnp.sum(line_sums[0:8], axis=0), jnp.sum(line_sums[8:16], axis=0),
            early_lines, table_all.reshape(-1),
        ]
    )
    small = jnp.pad(small, (0, -small.shape[0] % 1024)).reshape(-1, 1024)

    qkv_got = flip(qkv_send, "team", 1)
    small_got = flip(small, "team", 1)
    wout_got = flip(wout_grad[2:], "mp", 2)
    wout_grad = (wout_grad[:2].astype(wide) + wout_got.astype(wide)).astype(low)
    qkv_grad = (qkv_keep + qkv_got.astype(wide)).astype(low)
    small = small + small_got
    qkv_grad, small, wout_grad = sync(qkv_grad, small, wout_grad)

    qkv_grad = halve(qkv_grad.reshape(2, copies, -1, qkv_grad.shape[1]), 0, "team", 2)
    small_got = flip(small, "team", 2)
    wout_got = flip(wout_grad[1:], "mp", 1)
    ff_all = spread_group(after(ff_piece, running), 0, copies)
    small = small + small_got
    wout_grad = (wout_grad[:1].astype(wide) + wout_got.astype(wide)).astype(low)
    feed_own = feed_own.astype(wide) + feed_beside[1].astype(wide) + feed_across.astype(wide)
    layer_out = (hidden_in + feed_own + down_bias).astype(low)
    qkv_grad, small, wout_grad, ff_all = sync(qkv_grad, small, wout_grad, ff_all)

    for bit in reversed(bits_of(copies)):
        qkv_grad = halve(qkv_grad.reshape((2, -1) + qkv_grad.shape[1:]), 0, "copy", bit)
    for bit in bits_of(copies):
        small = small + flip(small, "copy", bit)
    for step in range(1, len(orders(copies)[0])):
        ff_all = spread_group(ff_all, step, copies)
    wout_grad = wout_grad.reshape(-1, depth)
    qkv_grad = qkv_grad.reshape(-1, 3 * head_width)
    columns = [
        jnp.concatenate(
            [
                qkv_grad[:, (3 * pair + slot) * pair_width : (3 * pair + slot + 1) * pair_width]
                for pair in range(pairs)
            ],
            axis=1,
        )
        for slot in range(3)
    ] + [wout_grad[:, start : start + head_width] for start in range(0, depth, head_width)]
    flat, small, ff_all = sync(jnp.concatenate(columns), small, ff_all)

    flat = spread_group(flat, 0, copies)
    small = small + flip(small, "mp", 1)
    ff_all = double(ff_all, "team", 1)
    flat, small, ff_all, grad_first = sync(flat, small, ff_all, grad_first)
    for step in range(1, len(orders(copies)[0])):
        flat = spread_group(flat, step, copies)
    small = small + flip(small, "mp", 2)
    grad_up, grad_down = feed_grads_out(
        ff_all.reshape(TEAM * copies, 2, unit, depth), copies
    )
    flat, small, grad_up, grad_down = sync(flat, small, grad_up, grad_down)
    flat = double(flat, "team", 1)
    grad_qkv, grad_wout = attention_grads_out(
        flat.reshape(TEAM * copies, -1, head_width), depth, head_width
    )

    small = small.reshape(-1)
    lines = [small[index * depth : (index + 1) * depth] for index in range(5)]
    start = 5 * depth
    count = TEAM * team_units
    up_sums = small[start : start + parts * count].reshape(parts, count)
    grad_up_bias = lax.dynamic_index_in_dim(up_sums, part, 0, keepdims=False)
    start = start + parts * count
    count = rel_table.size
    table_all = small[start : start + parts * count].reshape(parts, count)
    grad_table = lax.dynamic_index_in_dim(table_all, part, 0, keepdims=False).reshape(
        rel_table.shape
    )

    grad_first = after(grad_first, grad_qkv, grad_wout)
    grad_first_norm = normalize_backward(grad_first, ln1_gain, unit1, inverse1)
    grad_tokens = (grad_hidden + grad_first_norm).astype(low)
    return (
        layer_out, grad_tokens, lines[0], lines[1], grad_qkv, grad_table, grad_wout,
        lines[2], lines[3], grad_up, grad_up_bias, grad_down, lines[4],
    )


def solution(mesh):
    groups, parts = mesh.shape["dp"], mesh.shape["mp"]
    split = Mesh(
        mesh.devices.reshape(groups // TEAM, TEAM, parts), ("copy", "team", "mp")
    )
    every = ("copy", "team", "mp")
    return jax.shard_map(
        body,
        mesh=split,
        in_specs=(
            P(every, None), P(("copy", "team"), None), P(), P(), P(), P(None, None, "mp"),
            P(None, "mp"), P("mp", None), P(), P(), P(None, "mp"), P("mp"), P("mp", None), P(),
            P(every, None),
        ),
        out_specs=(
            P(every, None), P(every, None), P(), P(), P(None, None, "mp"), P(None, "mp"),
            P("mp", None), P(), P(), P(None, "mp"), P("mp"), P("mp", None), P(),
        ),
        check_vma=False,
    )
```

```python
import functools

import jax
import jax.numpy as jnp
from jax import lax
from jax.experimental import pallas as pl
from jax.experimental.pallas import tpu as pltpu
from jax.sharding import Mesh, PartitionSpec as P

EPSILON = 1e-05
HIGHEST_PRECISION = lax.Precision.HIGHEST
LIGHT = pl.CostEstimate(flops=1, bytes_accessed=1, transcendentals=0)
MIDDLE = pl.CostEstimate(flops=2 * 10**10, bytes_accessed=1, transcendentals=0)
SMALL = pl.CostEstimate(flops=1, bytes_accessed=1, transcendentals=0)
COVER = pl.CostEstimate(flops=16 * 10**9, bytes_accessed=1, transcendentals=0)
HEAVY = pl.CostEstimate(flops=10**11, bytes_accessed=1, transcendentals=0)
FEED_STEPS = 4
BLK = 256
HEAD_LANES = 64
NEAR = 128


def head_mask(rows, width, head, axis):
    place = lax.broadcasted_iota(jnp.int32, (rows, width), axis)
    return (place >= head * HEAD_LANES) & (place < (head + 1) * HEAD_LANES)


def one_head(value, head):
    keep = head_mask(value.shape[0], value.shape[1], head, 1)
    return jnp.where(keep, value, jnp.zeros_like(value))


def scaled(queries):
    return queries * jnp.asarray(HEAD_LANES ** -0.5, queries.dtype)


def dot_nt(left, right):
    return lax.dot_general(
        left, right, (((1,), (1,)), ((), ())), preferred_element_type=jnp.float32
    )


def dot_nn(left, right):
    return lax.dot_general(
        left, right, (((1,), (0,)), ((), ())), preferred_element_type=jnp.float32
    )


def attention_forward_kernel(
    cut_ref, rows_ref, weight_ref, bias_ref,
    qkv_a, qkv_b, out_ref, lse_a, lse_b, tile_ref, masked_v, score_ref,
):
    heads = masked_v.shape[0]
    width = out_ref.shape[1] // 2
    block = pl.program_id(0)
    cut = cut_ref[0]
    qkv_refs, lse_refs = (qkv_a, qkv_b), (lse_a, lse_b)

    @pl.when(block == 0)
    def _():
        weights = [
            jnp.concatenate(
                [weight_ref[slot, :, pair * width : (pair + 1) * width] for slot in range(3)],
                axis=1,
            )
            for pair in range(2)
        ]

        def one_chunk(chunk, carry):
            spot = pl.ds(pl.multiple_of(chunk * BLK, BLK), BLK)
            for pair in range(2):
                qkv_refs[pair][spot, :] = dot_nn(rows_ref[spot, :], weights[pair]).astype(
                    jnp.bfloat16
                )
            return carry

        lax.fori_loop(0, rows_ref.shape[0] // BLK, one_chunk, 0)
        for head in range(heads):
            wide = jnp.broadcast_to(bias_ref[head : head + 1, :], (BLK, 2 * BLK))
            tile_ref[head] = pltpu.roll(wide, 0, 1, stride=1, stride_axis=0)
            masked_v[head] = one_head(qkv_refs[head // 2][:, 2 * width :], head % 2)

    row_start = block * BLK
    first = jnp.where(row_start >= cut, cut // BLK, 0)
    rows = row_start + lax.broadcasted_iota(jnp.int32, (BLK, BLK), 0)
    seg_start = jnp.where(rows >= cut, cut, 0)
    columns = lax.broadcasted_iota(jnp.int32, (BLK, BLK), 1)
    own = pl.ds(pl.multiple_of(row_start, BLK), BLK)
    q_heads = [
        one_head(scaled(qkv_refs[head // 2][own, 0:width]), head % 2) for head in range(heads)
    ]

    def scores_of(key_block, tops):
        key_start = pl.multiple_of(key_block * BLK, BLK)
        keys = [ref[pl.ds(key_start, BLK), width : 2 * width] for ref in qkv_refs]
        places = key_start + columns
        allowed = (places <= rows) & (places >= seg_start)
        offset = pl.multiple_of(jnp.maximum(key_block - block + 1, 0) * BLK, BLK)
        near = key_block - block + 1 >= 0
        new_tops = []
        for head in range(heads):
            raw = dot_nt(q_heads[head], keys[head // 2])
            far = bias_ref[head : head + 1, 2 * BLK - 1 : 2 * BLK]
            bias = jnp.where(near, tile_ref[head, :, pl.ds(offset, BLK)], far)
            scores = jnp.where(allowed, raw + bias, -1e30)
            score_ref[head, :, pl.ds(key_start, BLK)] = scores
            top = tops[head]
            for lane in range(0, BLK, 128):
                top = jnp.maximum(top, scores[:, lane : lane + 128])
            new_tops.append(top)
        return tuple(new_tops)

    start = tuple(jnp.full((BLK, 128), -1e30, jnp.float32) for _ in range(heads))
    tops = lax.fori_loop(first, block + 1, scores_of, start)
    tops = [jnp.max(top, axis=1, keepdims=True) for top in tops]

    def weighted(key_block, carry):
        totals, sums = carry
        key_start = pl.multiple_of(key_block * BLK, BLK)
        new_totals, new_sums = [], []
        for pair in range(2):
            pieces, values = [], []
            for head in (2 * pair, 2 * pair + 1):
                soft = jnp.exp(score_ref[head, :, pl.ds(key_start, BLK)] - tops[head])
                part = sums[head]
                for lane in range(0, BLK, 128):
                    part = part + soft[:, lane : lane + 128]
                new_sums.append(part)
                pieces.append(soft.astype(jnp.bfloat16))
                values.append(masked_v[head, pl.ds(key_start, BLK), :])
            new_totals.append(
                totals[pair]
                + dot_nn(jnp.concatenate(pieces, axis=1), jnp.concatenate(values, axis=0))
            )
        return tuple(new_totals), tuple(new_sums)

    totals, sums = lax.fori_loop(
        first,
        block + 1,
        weighted,
        (
            tuple(jnp.zeros((BLK, width), jnp.float32) for _ in range(2)),
            tuple(jnp.zeros((BLK, 128), jnp.float32) for _ in range(heads)),
        ),
    )
    lanes = lax.broadcasted_iota(jnp.int32, (BLK, width), 1)
    for pair in range(2):
        scale = jnp.zeros((BLK, width), jnp.float32)
        logs = jnp.zeros((BLK, width), jnp.float32)
        for place in range(2):
            head = 2 * pair + place
            sum_one = jnp.sum(sums[head], axis=1, keepdims=True)
            scale = jnp.where(lanes // HEAD_LANES == place, 1.0 / sum_one, scale)
            logs = jnp.where(lanes == place, tops[head] + jnp.log(sum_one), logs)
        out_ref[:, pair * width : (pair + 1) * width] = (totals[pair] * scale).astype(jnp.bfloat16)
        lse_refs[pair][...] = jnp.transpose(logs)[0:8, :]


def attention_forward(cut, normed, weights, near_bias):
    length, depth = normed.shape
    width = weights.shape[2] // 2
    heads = 2 * width // HEAD_LANES
    whole = lambda block, cut: (0, 0)
    full = pl.BlockSpec((length, 3 * width), whole)
    row = pl.BlockSpec((BLK, 2 * width), lambda block, cut: (block, 0))
    line = pl.BlockSpec((8, BLK), lambda block, cut: (0, block))
    return pl.pallas_call(
        attention_forward_kernel,
        grid_spec=pltpu.PrefetchScalarGridSpec(
            num_scalar_prefetch=1,
            grid=(length // BLK,),
            in_specs=[
                pl.BlockSpec((length, depth), whole, pipeline_mode=pl.Buffered(1)),
                pl.BlockSpec(
                    weights.shape, lambda block, cut: (0, 0, 0), pipeline_mode=pl.Buffered(1)
                ),
                pl.BlockSpec((8, 2 * BLK), whole),
            ],
            out_specs=[full, full, row, line, line],
            scratch_shapes=[
                pltpu.VMEM((heads, BLK, 2 * BLK), jnp.float32),
                pltpu.VMEM((heads, length, width), jnp.bfloat16),
                pltpu.VMEM((heads, BLK, length), jnp.float32),
            ],
        ),
        out_shape=[jax.ShapeDtypeStruct((length, 3 * width), jnp.bfloat16)] * 2
        + [jax.ShapeDtypeStruct((length, 2 * width), jnp.bfloat16)]
        + [jax.ShapeDtypeStruct((8, length), jnp.float32)] * 2,
        compiler_params=pltpu.CompilerParams(
            dimension_semantics=("arbitrary",), vmem_limit_bytes=48 * 1024 * 1024
        ),
        cost_estimate=LIGHT,
        name="attention_forward",
    )(cut, normed, weights, near_bias)


def attention_backward_kernel(
    cut_ref, qkv_a, qkv_b, grad_ref, att_ref, lse_a, lse_b, bias_ref,
    dqkv_a, dqkv_b, table_ref,
    tile_ref, q_masked, grad_masked, delta_ref, dq_sum, near_sum, far_sum,
):
    heads = q_masked.shape[0]
    block = pl.program_id(0)
    n_blocks = pl.num_programs(0)
    length = grad_ref.shape[0]
    width = att_ref.shape[1] // 2
    cut = cut_ref[0]
    qkv_refs, lse_refs, out_refs = (qkv_a, qkv_b), (lse_a, lse_b), (dqkv_a, dqkv_b)

    @pl.when(block == 0)
    def _():
        row = lax.broadcasted_iota(jnp.int32, (16, width), 0)
        lane = lax.broadcasted_iota(jnp.int32, (16, width), 1)
        pick = jnp.where(lane // HEAD_LANES == row, 1.0, 0.0).astype(jnp.bfloat16)
        for pair in range(2):
            lanes = slice(pair * width, (pair + 1) * width)
            grad_pair = grad_ref[:, lanes]
            product = grad_pair.astype(jnp.float32) * att_ref[:, lanes].astype(jnp.float32)
            high = product.astype(jnp.bfloat16)
            rest = (product - high.astype(jnp.float32)).astype(jnp.bfloat16)
            delta_ref[pair] = (dot_nt(pick, high) + dot_nt(pick, rest))[0:8, :]
            queries = scaled(qkv_refs[pair][:, 0:width])
            for place in range(2):
                head = 2 * pair + place
                q_masked[head] = one_head(queries, place)
                grad_masked[head] = one_head(grad_pair, place)
        for head in range(heads):
            wide = jnp.broadcast_to(bias_ref[head : head + 1, :], (BLK, 2 * BLK))
            tile_ref[head] = pltpu.roll(wide, 0, 1, stride=1, stride_axis=0)
        dq_sum[...] = jnp.zeros_like(dq_sum)
        near_sum[...] = jnp.zeros_like(near_sum)
        far_sum[...] = jnp.zeros_like(far_sum)

    key_start = pl.multiple_of(block * BLK, BLK)
    keys = [ref[pl.ds(key_start, BLK), width : 2 * width] for ref in qkv_refs]
    values = [ref[pl.ds(key_start, BLK), 2 * width :] for ref in qkv_refs]
    keys_t = [jnp.transpose(one) for one in keys]
    places = key_start + lax.broadcasted_iota(jnp.int32, (BLK, BLK), 0)
    columns = lax.broadcasted_iota(jnp.int32, (BLK, BLK), 1)
    last = jnp.where(key_start + BLK <= cut, (cut + BLK - 1) // BLK, n_blocks)

    def one_block(query_block, carry):
        row_start = pl.multiple_of(query_block * BLK, BLK)
        rows = row_start + columns
        allowed = (places <= rows) & (places >= jnp.where(rows >= cut, cut, 0))
        distance = query_block - block
        near = distance <= 1
        offset = pl.multiple_of(jnp.minimum(distance, 1) * BLK, BLK)
        results = []
        for pair in range(2):
            soft_pieces, grad_pieces, q_pieces, out_pieces = [], [], [], []
            for place in range(2):
                head = 2 * pair + place
                q_head = q_masked[head, pl.ds(row_start, BLK), :]
                grad_head = grad_masked[head, pl.ds(row_start, BLK), :]
                far = bias_ref[head : head + 1, BLK - 1 : BLK]
                bias = jnp.where(near, tile_ref[head, :, pl.ds(offset, BLK)], far)
                scores = dot_nt(keys[pair], q_head) + bias
                log_total = lse_refs[pair][place : place + 1, pl.ds(row_start, BLK)]
                soft = jnp.exp(jnp.where(allowed, scores - log_total, -1e30))
                grad_soft = dot_nt(values[pair], grad_head)
                delta = delta_ref[pair, place : place + 1, pl.ds(row_start, BLK)]
                grad_scores = soft * (grad_soft - delta)
                grad_low = grad_scores.astype(jnp.bfloat16)

                @pl.when(near)
                def _():
                    near_sum[head, :, pl.ds(offset, BLK)] += grad_scores

                @pl.when(jnp.logical_not(near))
                def _():
                    far_sum[head] += jnp.sum(
                        grad_scores.reshape(BLK // 8, 8, BLK), axis=0
                    )

                own = slice(place * HEAD_LANES, (place + 1) * HEAD_LANES)
                spot = slice(head * HEAD_LANES, (head + 1) * HEAD_LANES)
                dq_sum[spot, pl.ds(row_start, BLK)] += dot_nn(keys_t[pair][own, :], grad_low)
                soft_pieces.append(soft.astype(jnp.bfloat16))
                grad_pieces.append(grad_low)
                q_pieces.append(q_head)
                out_pieces.append(grad_head)
            dk, dv = carry[pair]
            dv = dv + dot_nn(
                jnp.concatenate(soft_pieces, axis=1), jnp.concatenate(out_pieces, axis=0)
            )
            dk = dk + dot_nn(
                jnp.concatenate(grad_pieces, axis=1), jnp.concatenate(q_pieces, axis=0)
            )
            results.append((dk, dv))
        return tuple(results)

    empty = jnp.zeros((BLK, width), jnp.float32)
    results = lax.fori_loop(block, last, one_block, ((empty, empty), (empty, empty)))
    for pair in range(2):
        dk, dv = results[pair]
        out_refs[pair][pl.ds(key_start, BLK), width : 2 * width] = dk.astype(jnp.bfloat16)
        out_refs[pair][pl.ds(key_start, BLK), 2 * width :] = dv.astype(jnp.bfloat16)

    @pl.when(block == n_blocks - 1)
    def _():
        for query_block in range(length // BLK):
            spot = slice(query_block * BLK, (query_block + 1) * BLK)
            turned = (jnp.transpose(dq_sum[:, spot]) * (HEAD_LANES ** -0.5)).astype(jnp.bfloat16)
            for pair in range(2):
                out_refs[pair][spot, 0:width] = turned[:, pair * width : (pair + 1) * width]
        for head in range(heads):
            lined = jnp.zeros((8, 2 * BLK), jnp.float32)
            for group in range(BLK // 8):
                piece = near_sum[head, group * 8 : group * 8 + 8, :]
                shift = (2 * BLK - group * 8) % (2 * BLK)
                lined = lined + (pltpu.roll(piece, shift, 1) if shift else piece)
            total = lined[0:1, :]
            for row in range(1, 8):
                total = total + pltpu.roll(lined, 2 * BLK - row, 1)[row : row + 1, :]
            table_ref[head : head + 1, :] = total
            rest = jnp.sum(far_sum[head], axis=0, keepdims=True)
            table_ref[heads + head : heads + head + 1, :] = jnp.concatenate(
                [rest, jnp.zeros_like(rest)], axis=1
            )


def attention_backward(cut, projected, grad_att, attended, logs, near_bias):
    length, width = attended.shape[0], attended.shape[1] // 2
    heads = 2 * width // HEAD_LANES
    whole = lambda block, cut: (0, 0)
    full = lambda columns: pl.BlockSpec((length, columns), whole)
    lse = pl.BlockSpec((8, length), whole)
    return pl.pallas_call(
        attention_backward_kernel,
        grid_spec=pltpu.PrefetchScalarGridSpec(
            num_scalar_prefetch=1,
            grid=(length // BLK,),
            in_specs=[
                full(3 * width), full(3 * width), full(2 * width), full(2 * width),
                lse, lse, pl.BlockSpec((8, 2 * BLK), whole),
            ],
            out_specs=[
                full(3 * width), full(3 * width), pl.BlockSpec((8, 2 * BLK), whole),
            ],
            scratch_shapes=[
                pltpu.VMEM((heads, BLK, 2 * BLK), jnp.float32),
                pltpu.VMEM((heads, length, width), jnp.bfloat16),
                pltpu.VMEM((heads, length, width), jnp.bfloat16),
                pltpu.VMEM((2, 8, length), jnp.float32),
                pltpu.VMEM((2 * width, length), jnp.float32),
                pltpu.VMEM((heads, BLK, 2 * BLK), jnp.float32),
                pltpu.VMEM((heads, 8, BLK), jnp.float32),
            ],
        ),
        out_shape=[
            jax.ShapeDtypeStruct((length, 3 * width), jnp.bfloat16),
            jax.ShapeDtypeStruct((length, 3 * width), jnp.bfloat16),
            jax.ShapeDtypeStruct((8, 2 * BLK), jnp.float32),
        ],
        compiler_params=pltpu.CompilerParams(
            dimension_semantics=("arbitrary",), vmem_limit_bytes=48 * 1024 * 1024
        ),
        cost_estimate=MIDDLE,
        name="attention_backward",
    )(cut, *projected, grad_att, attended, *logs, near_bias)


def distance_bias(rel_table, bucket_of):
    hot = (
        bucket_of[:, None] == jnp.arange(rel_table.shape[0], dtype=jnp.int32)[None, :]
    ).astype(jnp.float32)
    by_distance = jnp.einsum(
        "dn,nh->hd", hot, rel_table, precision=HIGHEST_PRECISION,
        preferred_element_type=jnp.float32,
    )
    return hot, by_distance


def near_tables(by_distance):
    heads, reach = by_distance.shape
    far = by_distance[:, reach - 1 :]
    forward = jnp.concatenate(
        [
            jnp.broadcast_to(far, (heads, BLK - reach + 1)),
            by_distance[:, ::-1],
            jnp.broadcast_to(far, (heads, BLK - 1)),
        ],
        axis=1,
    )
    backward = jnp.concatenate(
        [by_distance, jnp.broadcast_to(far, (heads, 2 * BLK - reach))], axis=1
    )
    rows = ((0, 8 - heads), (0, 0))
    return jnp.pad(forward, rows), jnp.pad(backward, rows)


def table_gradient(hot, near_sums, far_sums):
    reach = hot.shape[0]
    near = near_sums[:, : reach - 1]
    far = jnp.sum(near_sums[:, reach - 1 :], axis=1) + jnp.sum(far_sums, axis=1)
    by_distance = jnp.concatenate([near, far[:, None]], axis=1)
    return jnp.einsum(
        "dn,hd->nh", hot, by_distance, precision=HIGHEST_PRECISION,
        preferred_element_type=jnp.float32,
    )


TEAM = 4


def after(value, *gates):
    return lax.optimization_barrier((value,) + gates)[0]


def flip(value, axis, bit):
    size = lax.axis_size(axis)
    return lax.ppermute(value, axis, [(i, i ^ bit) for i in range(size)])


def halve(value, dim, axis, bit):
    mine = (lax.axis_index(axis) // bit) % 2
    keep = lax.dynamic_index_in_dim(value, mine, dim, keepdims=False)
    send = lax.dynamic_index_in_dim(value, 1 - mine, dim, keepdims=False)
    received = flip(send.astype(jnp.bfloat16), axis, bit)
    return (keep.astype(jnp.float32) + received.astype(jnp.float32)).astype(jnp.bfloat16)


def halve_start(value, dim, axis, bit):
    mine = (lax.axis_index(axis) // bit) % 2
    keep = lax.dynamic_index_in_dim(value, mine, dim, keepdims=False)
    send = lax.dynamic_index_in_dim(value, 1 - mine, dim, keepdims=False)
    return keep, flip(send, axis, bit)


def halve_end(pair):
    return (pair[0].astype(jnp.float32) + pair[1].astype(jnp.float32)).astype(jnp.bfloat16)


def double(value, axis, bit):
    mine = (lax.axis_index(axis) // bit) % 2
    other = flip(value, axis, bit)
    return jnp.where(mine == 0, jnp.stack([value, other]), jnp.stack([other, value]))


def bits_of(size):
    bits = []
    bit = 1
    while bit < size:
        bits.append(bit)
        bit *= 2
    return bits


def with_partner(own):
    return jnp.concatenate([own, flip(own, "team", 1)], axis=0)


def feed_grads_kernel(core_ref, own_ref, got_ref, up_ref, down_ref, *, spots):
    unit = own_ref.shape[2]
    half = len(spots) // 2

    def write(piece_ref, places):
        for index, spot in enumerate(places):
            where = slice(spot * unit, (spot + 1) * unit)
            up_ref[:, where] = jnp.transpose(piece_ref[index, 0].astype(jnp.float32))
            down_ref[where, :] = piece_ref[index, 1].astype(jnp.float32)

    def both(core):
        write(own_ref, spots[core * half : (core + 1) * half])
        write(got_ref, spots[(1 - core) * half : (2 - core) * half])

    for core in range(2):
        pl.when(core_ref[0] == core)(functools.partial(both, core))


def feed_grads_out(core, own, got, copies):
    count, _, unit, depth = own.shape
    merge = max(1, 128 // unit)
    if merge > 1:
        own, got = (
            jnp.transpose(
                one.reshape(count // merge, merge, 2, unit, depth), (0, 2, 1, 3, 4)
            ).reshape(count // merge, 2, merge * unit, depth)
            for one in (own, got)
        )
    count, _, unit, depth = own.shape
    each = copies // merge
    spots = []
    for step in range(2 * count):
        half, side, place = place_in_group(step, each)
        spots.append((side * 2 + half) * each + place)
    take = depth // 4
    piece = pl.BlockSpec((count, 2, unit, take), lambda step, core: (0, 0, 0, step))
    return pl.pallas_call(
        functools.partial(feed_grads_kernel, spots=spots),
        grid_spec=pltpu.PrefetchScalarGridSpec(
            num_scalar_prefetch=1,
            grid=(4,),
            in_specs=[piece, piece],
            out_specs=[
                pl.BlockSpec((take, 2 * count * unit), lambda step, core: (step, 0)),
                pl.BlockSpec((2 * count * unit, take), lambda step, core: (0, step)),
            ],
        ),
        out_shape=[
            jax.ShapeDtypeStruct((depth, 2 * count * unit), jnp.float32),
            jax.ShapeDtypeStruct((2 * count * unit, depth), jnp.float32),
        ],
        compiler_params=pltpu.CompilerParams(dimension_semantics=("arbitrary",)),
        cost_estimate=LIGHT,
        name="feed_grads_out",
    )(core, own, got)


def attention_grads_kernel(core_ref, own_ref, got_ref, qkv_ref, out_ref, *, spots):
    group = own_ref.shape[0]
    rows, width = qkv_ref.shape[1] // group, qkv_ref.shape[2]
    few = out_ref.shape[0] // group

    def place_all(piece_ref, core):
        for item in range(group):
            spot = spots[core * group + item] - core * group
            for slot in range(3):
                qkv_ref[slot, spot * rows : (spot + 1) * rows, :] = piece_ref[
                    item, slot * rows : (slot + 1) * rows, :
                ].astype(jnp.float32)
            for place in range(out_ref.shape[1] // width):
                start = 3 * rows + place * few
                out_ref[
                    spot * few : (spot + 1) * few, place * width : (place + 1) * width
                ] = piece_ref[item, start : start + few, :].astype(jnp.float32)

    step = pl.program_id(0)
    for core in range(2):
        mine = (step == core) & (core_ref[0] == core)
        other = (step == core) & (core_ref[0] != core)
        pl.when(mine)(functools.partial(place_all, own_ref, core))
        pl.when(other)(functools.partial(place_all, got_ref, core))


def attention_grads_out(core, own, got, depth, head_width):
    half = own.shape[0]
    copies = half // 2
    spots = []
    for step in range(2 * half):
        side_core, side, place = place_in_group(step, copies)
        spots.append((side_core * 2 + side) * copies + place)
    whole = pl.BlockSpec(own.shape, lambda step, core: (0, 0, 0))
    return pl.pallas_call(
        functools.partial(attention_grads_kernel, spots=spots),
        grid_spec=pltpu.PrefetchScalarGridSpec(
            num_scalar_prefetch=1,
            grid=(2,),
            in_specs=[whole, whole],
            out_specs=[
                pl.BlockSpec((3, depth // 2, head_width), lambda step, core: (0, step, 0)),
                pl.BlockSpec((head_width // 2, depth), lambda step, core: (step, 0)),
            ],
        ),
        out_shape=[
            jax.ShapeDtypeStruct((3, depth, head_width), jnp.float32),
            jax.ShapeDtypeStruct((head_width, depth), jnp.float32),
        ],
        compiler_params=pltpu.CompilerParams(dimension_semantics=("arbitrary",)),
        cost_estimate=LIGHT,
        name="attention_grads_out",
    )(core, own, got)


def qkv_grad_kernel(core_ref, rows_ref, grad_a, grad_b, send_ref, keep_ref):
    width = grad_a.shape[1]
    both = [dot_tn(rows_ref[...], grad[...]).astype(jnp.bfloat16) for grad in (grad_a, grad_b)]

    @pl.when(pl.program_id(0) == 0)
    def _():
        send_ref[:, 0:width] = both[0]
        send_ref[:, width:] = both[1]

    @pl.when(pl.program_id(0) == 1)
    def _():
        keep_ref[:, 0:width] = both[0]
        keep_ref[:, width:] = both[1]


def qkv_weight_grad(core, rows, grads):
    length, depth = rows.shape
    width = grads[0].shape[1]
    half = depth // 2
    whole = pl.BlockSpec((length, width), lambda step, core: (0, 0))
    out = pl.BlockSpec((half, 2 * width), lambda step, core: (0, 0))
    return pl.pallas_call(
        qkv_grad_kernel,
        grid_spec=pltpu.PrefetchScalarGridSpec(
            num_scalar_prefetch=1,
            grid=(2,),
            in_specs=[
                pl.BlockSpec((length, half), lambda step, core: (0, 1 - core[0] ^ step)),
                whole, whole,
            ],
            out_specs=[out, out],
        ),
        out_shape=[jax.ShapeDtypeStruct((half, 2 * width), jnp.bfloat16)] * 2,
        compiler_params=pltpu.CompilerParams(
            dimension_semantics=("arbitrary",), vmem_limit_bytes=40 * 1024 * 1024
        ),
        cost_estimate=SMALL,
        name="qkv_weight_grad",
    )(core, rows, *grads)


def branch_kernel(*refs, count):
    pieces = refs[:count]
    weight_ref, token_ref, line_ref, hidden_ref, second_ref, left_ref = refs[count:]
    left = jnp.concatenate([piece[...] for piece in pieces], axis=1)
    left_ref[...] = left
    hidden = token_ref[...].astype(jnp.float32) + dot_nn(left, weight_ref[...])
    unit, _ = normalize(hidden)
    hidden_ref[...] = hidden
    second_ref[...] = (unit * line_ref[0:1, :] + line_ref[1:2, :]).astype(jnp.bfloat16)


def branch_and_norm(pieces, weights, tokens, lines):
    rows, depth = tokens.shape
    return pl.pallas_call(
        functools.partial(branch_kernel, count=len(pieces)),
        out_shape=[
            jax.ShapeDtypeStruct((rows, depth), jnp.float32),
            jax.ShapeDtypeStruct((rows, depth), jnp.bfloat16),
            jax.ShapeDtypeStruct((rows, weights.shape[0]), jnp.bfloat16),
        ],
        compiler_params=pltpu.CompilerParams(vmem_limit_bytes=32 * 1024 * 1024),
        cost_estimate=LIGHT,
        name="branch_and_norm",
    )(*pieces, weights, tokens, lines)


def row_grads_kernel(
    own_ref, core_ref, across_ref, grad_ref, hidden_ref, weight_ref, line_ref,
    total_ref, branch_ref, *refs,
):
    block_refs, sum_ref = refs[:-1], refs[-1]
    second = (
        own_ref[...].astype(jnp.float32) + core_ref[...].astype(jnp.float32)
        + across_ref[...].astype(jnp.float32)
    )
    grad = grad_ref[...].astype(jnp.float32)
    unit, inverse = normalize(hidden_ref[...])
    total = grad + normalize_backward(second, line_ref[0:1, :], unit, inverse)
    branch = total.astype(jnp.bfloat16)
    total_ref[...] = total
    branch_ref[...] = branch
    width = block_refs[0].shape[1]
    for index, block_ref in enumerate(block_refs):
        block_ref[...] = dot_nt(
            branch, weight_ref[index * width : (index + 1) * width, :]
        ).astype(jnp.bfloat16)
    sums = [jnp.sum(one, axis=0, keepdims=True) for one in (second * unit, second, grad)]
    lines = jnp.concatenate(sums + [jnp.zeros((5, sums[0].shape[1]), jnp.float32)])

    sum_ref[...] = lines


def row_grads(backs, grad, hidden, weights, lines, parts):
    rows, depth = hidden.shape
    width = weights.shape[0] // parts
    return pl.pallas_call(
        row_grads_kernel,
        out_shape=[
            jax.ShapeDtypeStruct((rows, depth), jnp.float32),
            jax.ShapeDtypeStruct((rows, depth), jnp.bfloat16),
        ]
        + [jax.ShapeDtypeStruct((rows, width), jnp.bfloat16)] * parts
        + [jax.ShapeDtypeStruct((8, depth), jnp.float32)],
        compiler_params=pltpu.CompilerParams(vmem_limit_bytes=40 * 1024 * 1024),
        cost_estimate=LIGHT,
        name="row_grads",
    )(*backs, grad, hidden, weights, lines)


def out_grad_kernel(core_ref, left_ref, right_ref, keep_ref, send_ref):
    parts, half, _ = keep_ref.shape

    def columns(core):
        return jnp.concatenate(
            [
                left_ref[:, pl.ds(pl.multiple_of((2 * part + core) * half, 128), half)]
                for part in range(parts)
            ],
            axis=1,
        )

    for out_ref, core in ((keep_ref, core_ref[0]), (send_ref, 1 - core_ref[0])):
        grad = dot_tn(columns(core), right_ref[...]).astype(jnp.bfloat16)
        for part in range(parts):
            out_ref[part] = grad[part * half : (part + 1) * half]


def out_weight_grad(core, own_rows, grads, parts):
    rows, depth = grads.shape
    half = own_rows.shape[1] // parts // 2
    whole = pl.BlockSpec((rows, depth), lambda step, core: (0, 0))
    out = pl.BlockSpec((parts, half, depth), lambda step, core: (0, 0, 0))
    return pl.pallas_call(
        out_grad_kernel,
        grid_spec=pltpu.PrefetchScalarGridSpec(
            num_scalar_prefetch=1,
            grid=(1,),
            in_specs=[
                pl.BlockSpec(own_rows.shape, lambda step, core: (0, 0)), whole,
            ],
            out_specs=[out, out],
        ),
        out_shape=[jax.ShapeDtypeStruct((parts, half, depth), jnp.bfloat16)] * 2,
        compiler_params=pltpu.CompilerParams(dimension_semantics=("arbitrary",)),
        cost_estimate=COVER,
        name="out_weight_grad",
    )(core, own_rows, grads)


def normalize(inputs):
    center = inputs - jnp.mean(inputs, axis=-1, keepdims=True)
    spread = jnp.mean(center * center, axis=-1, keepdims=True)
    inverse = lax.rsqrt(spread + EPSILON)
    return center * inverse, inverse


def normalize_backward(grad, gain, unit, inverse):
    scaled_grad = grad * gain
    middle = jnp.mean(scaled_grad, axis=-1, keepdims=True)
    along = jnp.mean(scaled_grad * unit, axis=-1, keepdims=True)
    return (scaled_grad - middle - unit * along) * inverse


def dot_tn(left, right):
    return lax.dot_general(
        left, right, (((0,), (0,)), ((), ())), preferred_element_type=jnp.float32
    )


def copies_of(value, size):
    halves = [value[None]]
    for bit in bits_of(size):
        value = halves[0] if len(halves) == 1 else jnp.concatenate(halves)
        halves = [value, flip(value, "copy", bit)]
    return halves


def untangle(value, axis, index, size):
    for bit in bits_of(size):
        shape = value.shape
        split = value.reshape(
            shape[:axis] + (size // (2 * bit), 2, bit) + shape[axis + 1 :]
        )
        split = jnp.where((index // bit) % 2 == 1, jnp.flip(split, axis + 1), split)
        value = split.reshape(shape)
    return value


def orders(copies):
    first = [("copy", bit) for bit in bits_of(copies)] + [("team", 2)]
    return first, first[::-1] if copies == 2 else first


def spread_group(value, step, copies):
    choices = [order[step] for order in orders(copies)]
    moves = []
    for place in range(copies * TEAM):
        axis, bit = choices[place % 2]
        moves.append((place, place ^ (bit if axis == "team" else bit * TEAM)))
    got = lax.ppermute(value, ("copy", "team"), moves)
    mine = [(lax.axis_index(axis) // bit) % 2 for axis, bit in choices]
    mine = jnp.where(lax.axis_index("team") % 2 == 0, mine[0], mine[1])
    return jnp.where(mine == 0, jnp.stack([value, got]), jnp.stack([got, value]))


def place_in_group(step, copies):
    core, index = step // (2 * copies), step % (2 * copies)
    if copies != 2:
        return core, index // copies, index % copies
    outer, inner = index // 2, index % 2
    return core, outer + core * (inner - outer), inner + core * (outer - inner)


def exchange(blocks):
    return [blocks[0]] + [flip(blocks[k], "mp", k) for k in range(1, len(blocks))]


def cotangent_kernel(grad_a, grad_b, weight_a, weight_b, normed_ref, line_ref, out_ref, sum_ref):
    grad = sum(
        dot_nt(grad_ref[...], jnp.concatenate([weight_ref[slot] for slot in range(3)], axis=1))
        for grad_ref, weight_ref in ((grad_a, weight_a), (grad_b, weight_b))
    )
    unit = (normed_ref[...].astype(jnp.float32) - line_ref[0:1, :]) * line_ref[1:2, :]
    out_ref[...] = grad.astype(jnp.bfloat16)
    rows, depth = grad.shape
    both = jnp.concatenate(
        [
            jnp.sum((grad * unit).reshape(rows // 8, 8, depth), axis=0),
            jnp.sum(grad.reshape(rows // 8, 8, depth), axis=0),
        ],
        axis=0,
    )

    @pl.when(pl.program_id(0) == 0)
    def _():
        sum_ref[...] = both

    @pl.when(pl.program_id(0) > 0)
    def _():
        sum_ref[...] += both


def input_cotangent(grads, weights, normed, lines):
    length, width = grads[0].shape
    depth = weights.shape[1]
    row = pl.BlockSpec((BLK, width), lambda step: (step, 0))
    part_a = pl.BlockSpec((3, depth, width // 3), lambda step: (0, 0, 0))
    part_b = pl.BlockSpec((3, depth, width // 3), lambda step: (0, 0, 1))
    return pl.pallas_call(
        cotangent_kernel,
        grid=(length // BLK,),
        in_specs=[
            row, row, part_a, part_b,
            pl.BlockSpec((BLK, depth), lambda step: (step, 0)),
            pl.BlockSpec((2, depth), lambda step: (0, 0)),
        ],
        out_specs=[
            pl.BlockSpec((BLK, depth), lambda step: (step, 0)),
            pl.BlockSpec((16, depth), lambda step: (0, 0)),
        ],
        out_shape=[
            jax.ShapeDtypeStruct((length, depth), jnp.bfloat16),
            jax.ShapeDtypeStruct((16, depth), jnp.float32),
        ],
        compiler_params=pltpu.CompilerParams(dimension_semantics=("arbitrary",)),
        cost_estimate=SMALL,
        name="input_cotangent",
    )(*grads, weights, weights, normed, lines)


def feed_kernel(*refs, unit, count):
    weight_refs = refs[:count]
    (
        bias_ref, second_ref, grad_ref,
        act_ref, pre_ref, back_own, back_other, out_own, out_other, sum_ref,
    ) = refs[count:]
    w_up, w_down = (
        jnp.concatenate(
            [
                ref[:, start : start + unit, :].reshape(ref.shape[0] * unit, ref.shape[2])
                for ref in weight_refs
            ]
        )
        for start in (0, unit)
    )
    pre = dot_nt(second_ref[...], w_up) + bias_ref[...]
    grad_act = dot_nt(grad_ref[...], w_down)
    cdf = 0.5 + 0.5 * lax.erf(pre * 0.7071067811865476)
    pdf = jnp.exp(pre * pre * -0.5) * 0.3989422804014327
    active = (pre * cdf).astype(jnp.bfloat16)
    grad_pre = ((cdf + pre * pdf) * grad_act).astype(jnp.bfloat16)
    act_ref[...] = active
    pre_ref[...] = grad_pre
    line = jnp.sum(grad_pre.astype(jnp.float32), axis=0, keepdims=True)
    back = dot_nn(grad_pre, w_up).astype(jnp.bfloat16)
    out = dot_nn(active, w_down).astype(jnp.bfloat16)

    step = pl.program_id(0)
    middle = pl.num_programs(0) // 2

    @pl.when(step < middle)
    def _():
        back_own[...] = back
        out_own[...] = out

    @pl.when(step >= middle)
    def _():
        back_other[...] = back
        out_other[...] = out

    @pl.when(step == 0)
    def _():
        sum_ref[...] = line

    @pl.when(step > 0)
    def _():
        sum_ref[...] += line


def feed_forward(weights, bias_row, second, grad, unit):
    depth = weights[0].shape[2]
    rows = second.shape[0]
    width = unit * sum(one.shape[0] for one in weights)
    steps = FEED_STEPS
    take = rows // steps
    middle = steps // 2
    row = pl.BlockSpec((take, depth), lambda step: (step, 0))
    near = pl.BlockSpec((take, depth), lambda step: (jnp.minimum(step, middle - 1), 0))
    far = pl.BlockSpec((take, depth), lambda step: (jnp.maximum(step - middle, 0), 0))
    wide = pl.BlockSpec((take, width), lambda step: (step, 0))
    line = pl.BlockSpec((1, width), lambda step: (0, 0))
    part = jax.ShapeDtypeStruct((rows // 2, depth), jnp.bfloat16)
    return pl.pallas_call(
        functools.partial(feed_kernel, unit=unit, count=len(weights)),
        grid=(steps,),
        in_specs=[pl.BlockSpec(each.shape, lambda step: (0, 0, 0)) for each in weights]
        + [line, row, row],
        out_specs=[wide, wide, near, far, near, far, line],
        out_shape=[
            jax.ShapeDtypeStruct((rows, width), jnp.bfloat16),
            jax.ShapeDtypeStruct((rows, width), jnp.bfloat16),
            part, part, part, part,
            jax.ShapeDtypeStruct((1, width), jnp.float32),
        ],
        compiler_params=pltpu.CompilerParams(
            dimension_semantics=("arbitrary",), vmem_limit_bytes=48 * 1024 * 1024
        ),
        cost_estimate=LIGHT,
        name="feed_forward",
    )(*weights, bias_row, second, grad)


def weight_grad_kernel(
    part_ref, act_a, act_b, pre_a, pre_b, second_a, second_b, grad_a, grad_b, *out_refs
):
    _, places, _, unit, _ = out_refs[0].shape
    up = dot_tn(pre_a[...], second_a[...]) + dot_tn(pre_b[...], second_b[...])
    down = dot_tn(act_a[...], grad_a[...]) + dot_tn(act_b[...], grad_b[...])
    for index, out_ref in enumerate(out_refs):
        for place in range(places):
            start = (index * places + place) * unit
            out_ref[0, place, 0] = up[start : start + unit].astype(jnp.bfloat16)
            out_ref[0, place, 1] = down[start : start + unit].astype(jnp.bfloat16)


def weight_grads(part, acts, pres, seconds, grads, parts, copies):
    rows, width = acts[0].shape
    depth = seconds[0].shape[1]
    unit = width // (parts * copies)
    count = 2 if copies > 1 else 1
    places = copies // count
    column = pl.BlockSpec((rows, width // parts), lambda step, part: (0, step))
    whole = pl.BlockSpec((rows, depth), lambda step, part: (0, 0))
    out = pl.BlockSpec(
        (1, places, 2, unit, depth), lambda step, part: (part[0] ^ step, 0, 0, 0, 0)
    )
    return pl.pallas_call(
        weight_grad_kernel,
        grid_spec=pltpu.PrefetchScalarGridSpec(
            num_scalar_prefetch=1,
            grid=(parts,),
            in_specs=[column] * 4 + [whole] * 4,
            out_specs=[out] * count,
        ),
        out_shape=[jax.ShapeDtypeStruct((parts, places, 2, unit, depth), jnp.bfloat16)] * count,
        compiler_params=pltpu.CompilerParams(
            dimension_semantics=("arbitrary",), vmem_limit_bytes=56 * 1024 * 1024
        ),
        cost_estimate=HEAVY,
        name="weight_grads",
    )(part, *acts, *pres, *seconds, *grads)


def fold_copies(halves, got):
    if len(halves) == 1:
        return halves[0]
    value = halve_end((halves[0], got))
    while value.shape[1] > 1:
        half = value.shape[1] // 2
        value = halve_end((value[:, :half], flip(value[:, half:], "copy", half)))
    return value


def sync(*values):
    return lax.optimization_barrier(values)


def body(
    tokens, seg_ids, bucket_of, ln1_gain, ln1_bias, w_qkv, rel_table, w_out,
    ln2_gain, ln2_bias, w_up, up_bias, w_down, down_bias, out_grad,
):
    low = jnp.bfloat16
    wide = jnp.float32
    copies = lax.axis_size("copy")
    parts = lax.axis_size("mp")
    copy = lax.axis_index("copy")
    member = lax.axis_index("team")
    part = lax.axis_index("mp")
    core = member % 2
    rows, depth = tokens.shape
    head_width = w_out.shape[0]
    pair_width = head_width // 2
    pairs = 2
    team_units = w_up.shape[1] // TEAM
    unit = team_units // copies
    out_rows = head_width // (2 * copies)
    seg_row = seg_ids[0]
    to_right = [(i, i + 1) for i in range(parts - 1)]
    to_left = [(i + 1, i) for i in range(parts - 1)]

    def relay(right, left, step):
        return (
            lax.ppermute(right, "mp", to_right[step - 1 :]),
            lax.ppermute(left, "mp", to_left[: parts - step]),
        )

    def corner_of(right1, left1, right3, left3):
        return jnp.where(
            (part == 0) | (part == parts - 1), right3 + left3, jnp.where(part == 1, left1, right1)
        )

    x_part = tokens.astype(wide)
    unit1, inverse1 = normalize(x_part)
    normed = lax.all_gather(
        (unit1 * ln1_gain + ln1_bias).astype(low), "mp", axis=0, tiled=True
    )
    def own_units(place):
        first = member * team_units + (copy ^ place) * unit
        return jnp.concatenate(
            [
                jnp.transpose(lax.dynamic_slice_in_dim(w_up, first, unit, 1)),
                lax.dynamic_slice_in_dim(w_down, first, unit, 0),
            ]
        )

    own_slot = jnp.stack([own_units(place) for place in range(copies)])
    out_own = lax.dynamic_slice_in_dim(w_out, (copy * 2 + core) * out_rows, out_rows, 0)
    own_biases = [
        lax.dynamic_slice_in_dim(up_bias, member * team_units + (copy ^ place) * unit, unit, 0)
        for place in range(copies)
    ]
    high = lax.reduce_precision(own_biases[0], 8, 7)
    middle = lax.reduce_precision(own_biases[0] - high, 8, 7)
    bias_lines = jnp.stack([high, middle, own_biases[0] - high - middle]).astype(low)
    bias_lines = jnp.pad(bias_lines, ((0, 5), (0, depth - unit)))
    piece = jnp.concatenate([own_slot[0], out_own, bias_lines])
    w_right1, w_left1 = relay(piece, piece, 1)
    w_right2, w_left2 = relay(w_right1, w_left1, 2)
    beside = copies_of(jnp.where(part % 2 == 0, w_left1, w_right1), copies)
    grad_across = flip(out_grad, "team", 2)
    grad_near = with_partner(out_grad)
    grad_far = with_partner(grad_across)
    hot, by_distance = distance_bias(rel_table, bucket_of)
    forward_bias, backward_bias = near_tables(by_distance)
    cut = jnp.sum((seg_row == seg_row[0]).astype(jnp.int32)).reshape(1)
    normed = after(
        normed, grad_near, grad_far, own_slot, forward_bias, backward_bias, cut,
        w_right2, w_left2, beside[1],
    )

    def whole_out(halves):
        mine = jnp.concatenate([half[:, 2 * unit : 2 * unit + out_rows] for half in halves])
        mine = untangle(mine, 0, copy, copies)
        other = flip(mine, "team", 1)
        return jnp.where(
            core == 0, jnp.stack([mine, other], axis=1), jnp.stack([other, mine], axis=1)
        ).reshape(head_width, depth)

    w_right2, w_left2 = after(w_right2, normed), after(w_left2, normed)
    w_right3, w_left3 = relay(w_right2, w_left2, 3)
    across = copies_of(w_right2 + w_left2, copies)
    *results, = attention_forward(cut, after(normed, across[0]), w_qkv, forward_bias)
    projected, attended, logs = results[0:2], results[2], results[3:5]
    w_right3, w_left3, across[1], attended = sync(w_right3, w_left3, across[1], attended)
    corner = copies_of(corner_of(w_right1, w_left1, w_right3, w_left3), copies)
    stack = attended.reshape(parts, rows, head_width)
    moved = exchange(
        [lax.dynamic_index_in_dim(stack, part ^ k, 0, keepdims=False) for k in range(parts)]
    )
    w_out_full = jnp.concatenate(
        [w_out] + [whole_out(halves) for halves in (beside, across, corner)]
    )
    weights = [own_slot] + beside + across + corner
    bias_row = jnp.concatenate(
        own_biases
        + [
            jnp.sum(half[:, -8:-5, :unit].astype(wide), axis=1).reshape(-1)
            for half in weights[1:]
        ]
    )[None]

    hidden_in, second, own_rows = branch_and_norm(
        moved, w_out_full, tokens, jnp.stack([ln2_gain, ln2_bias])
    )
    second_across = flip(second, "team", 2)
    second_near = with_partner(second)
    act_near, pre_near, back_own, back_core, feed_own, feed_core, sums_near = feed_forward(
        weights, bias_row, second_near, grad_near, unit
    )
    second_across = after(second_across, back_own)
    back_core = flip(back_core, "team", 1)
    second_far = with_partner(second_across)
    act_far, pre_far, back_side, back_corner, feed_side, feed_corner, sums_far = feed_forward(
        weights, bias_row, second_far, grad_far, unit
    )
    onward = (
        back_side.astype(wide) + flip(back_corner, "team", 1).astype(wide)
    ).astype(low)
    back_across = flip(onward, "team", 2)
    feed_stack = jnp.stack([after(feed_corner, onward), feed_core])
    feed_beside = flip(feed_stack, "team", 1)
    ff_grads = weight_grads(
        part.reshape(1), (act_near, after(act_far, onward, feed_stack)), (pre_near, pre_far),
        (second_near, second_far), (grad_near, grad_far), parts, copies,
    )
    ff_got = flip(ff_grads[-1], "copy", max(1, copies // 2)) if copies > 1 else ff_grads[0]
    back_across = after(back_across, ff_grads[0])
    grad_hidden, grad_branch, *grad_rows = row_grads(
        (back_own, back_core, back_across), out_grad, hidden_in, w_out_full, ln2_gain[None], parts
    )
    row_sums = grad_rows.pop()
    received = exchange(grad_rows)
    wout_keep, wout_send = out_weight_grad(core.reshape(1), own_rows, grad_branch, parts)
    received[0] = after(received[0], wout_keep)
    wout_got = flip(wout_send, "team", 1)
    results = sync(wout_got, feed_beside, ff_got, *received)
    wout_got, feed_beside, ff_got = results[:3]
    received = results[3:]
    wout_grad = halve_end((wout_keep, wout_got)).reshape(parts, 2, copies, -1, depth)
    wout_pair = halve_start(wout_grad, 1, "team", 2)
    ff_value = fold_copies(ff_grads, ff_got).reshape(parts, 2 * unit, depth)
    ff_piece = lax.psum_scatter(ff_value, "mp", scatter_dimension=0, tiled=False)
    feed_sum = (feed_side.astype(wide) + feed_beside[0].astype(wide)).astype(low)
    feed_across = flip(feed_sum, "team", 2)
    natural = jnp.zeros((parts, rows, head_width), low)
    for k in range(parts):
        natural = lax.dynamic_update_index_in_dim(natural, received[k], part ^ k, 0)
    grad_att = after(natural.reshape(parts * rows, head_width), wout_pair[0], feed_sum, ff_value)
    first_grads, last_grads, table_sums = attention_backward(
        cut, projected, grad_att, attended, logs, backward_bias
    )
    first_grads, last_grads, wout_last, feed_across = sync(
        first_grads, last_grads, wout_pair[1], feed_across
    )
    dqkv = [first_grads, last_grads]
    wout_grad = halve_end((wout_pair[0], wout_last))
    for bit in reversed(bits_of(copies)):
        wout_grad = wout_grad.reshape((parts, 2, -1) + wout_grad.shape[2:])
        wout_pair = halve_start(wout_grad, 1, "copy", bit)
        if bit > 1:
            wout_grad = halve_end(wout_pair)
    wout_keep, wout_last = wout_pair
    qkv_send, qkv_keep = qkv_weight_grad(
        core.reshape(1), normed, [after(dqkv[0], wout_keep), dqkv[1]]
    )
    wout_last, qkv_keep, qkv_send = sync(wout_last, qkv_keep, qkv_send)
    qkv_got = flip(qkv_send, "team", 1)
    wout_grad = halve_end((wout_keep, wout_last)).reshape(parts, -1, depth)
    dqkv[0], wout_grad = sync(dqkv[0], wout_grad)
    wout_got = flip(wout_grad[2:], "mp", 2)
    running, line_sums = input_cotangent(
        dqkv, w_qkv, normed,
        jnp.stack([after(ln1_bias, dqkv[0]), 1.0 / ln1_gain]),
    )
    grad_first = lax.psum_scatter(running, "mp", scatter_dimension=0, tiled=True).astype(wide)
    qkv_got, running, ff_piece = sync(qkv_got, running, ff_piece)
    qkv_grad = halve_end((qkv_keep, qkv_got))
    table_sums = after(table_sums, running)
    table_line = table_gradient(
        hot, table_sums[: table_sums.shape[0] // 2], table_sums[table_sums.shape[0] // 2 :]
    ).reshape(1, -1)
    table_all = lax.dynamic_update_slice_in_dim(
        jnp.zeros((parts, table_line.shape[1]), wide), table_line, part, 0
    )
    sums = (after(sums_near, running) + sums_far).reshape(parts, copies, unit)
    sums = untangle(untangle(sums, 0, part, parts), 1, copy, copies)
    up_sums = lax.dynamic_update_slice_in_dim(
        jnp.zeros((parts, TEAM * team_units), wide), sums.reshape(parts, team_units),
        member * team_units, 1,
    )
    early_lines = jnp.concatenate([row_sums[0:3].reshape(-1), up_sums.reshape(-1)])
    small = jnp.concatenate(
        [
            jnp.sum(line_sums[0:8], axis=0), jnp.sum(line_sums[8:16], axis=0),
            early_lines, table_all.reshape(-1),
        ]
    )
    small = jnp.pad(small, (0, -small.shape[0] % 1024)).reshape(-1, 1024)

    qkv_pair = halve_start(qkv_grad.reshape(2, copies, -1, qkv_grad.shape[1]), 0, "team", 2)
    ff_all = spread_group(ff_piece, 0, copies)
    small_got = flip(small, "team", 1)
    feed_own = feed_own.astype(wide) + feed_beside[1].astype(wide) + feed_across.astype(wide)
    layer_out = (hidden_in + feed_own + down_bias).astype(low)
    qkv_last, ff_all, small_got, layer_out, wout_got = sync(
        qkv_pair[1], ff_all, small_got, layer_out, wout_got
    )
    wout_grad = (wout_grad[:2].astype(wide) + wout_got.astype(wide)).astype(low)
    qkv_grad = halve_end((qkv_pair[0], qkv_last))
    small = small + small_got

    for bit in reversed(bits_of(copies)):
        qkv_grad = halve(qkv_grad.reshape((2, -1) + qkv_grad.shape[1:]), 0, "copy", bit)
    for step in range(1, len(orders(copies)[0])):
        ff_all = spread_group(ff_all, step, copies)
    wout_got = flip(wout_grad[1:], "mp", 1)
    small = small + flip(small, "mp", 1)
    wout_grad = (wout_grad[:1].astype(wide) + wout_got.astype(wide)).astype(low)
    wout_grad = wout_grad.reshape(-1, depth)
    qkv_grad = qkv_grad.reshape(-1, 3 * head_width)
    columns = [
        jnp.concatenate(
            [
                qkv_grad[:, (3 * pair + slot) * pair_width : (3 * pair + slot + 1) * pair_width]
                for pair in range(pairs)
            ],
            axis=1,
        )
        for slot in range(3)
    ] + [wout_grad[:, start : start + head_width] for start in range(0, depth, head_width)]
    flat, ff_all, small = sync(jnp.concatenate(columns), ff_all, small)

    ff_got = flip(ff_all, "team", 1)
    flat = spread_group(flat, 0, copies)
    small = small + flip(small, "mp", 2)
    flat, small, ff_got = sync(flat, small, ff_got)

    for step in range(1, len(orders(copies)[0])):
        flat = spread_group(flat, step, copies)
    small = small + flip(small, "team", 2)
    grad_up, grad_down = feed_grads_out(
        core.reshape(1), ff_all.reshape(2 * copies, 2, unit, depth),
        ff_got.reshape(2 * copies, 2, unit, depth), copies,
    )
    flat, small, grad_up, grad_down = sync(flat, small, grad_up, grad_down)

    flat_got = flip(flat, "team", 1)
    for bit in bits_of(copies):
        small = small + flip(small, "copy", bit)
    flat_got, small, grad_first = sync(flat_got, small, grad_first)
    grad_qkv, grad_wout = attention_grads_out(
        core.reshape(1), flat.reshape(2 * copies, -1, head_width),
        flat_got.reshape(2 * copies, -1, head_width), depth, head_width,
    )

    small = small.reshape(-1)
    lines = [small[index * depth : (index + 1) * depth] for index in range(5)]
    start = 5 * depth
    count = TEAM * team_units
    up_sums = small[start : start + parts * count].reshape(parts, count)
    grad_up_bias = lax.dynamic_index_in_dim(up_sums, part, 0, keepdims=False)
    start = start + parts * count
    count = rel_table.size
    table_all = small[start : start + parts * count].reshape(parts, count)
    grad_table = lax.dynamic_index_in_dim(table_all, part, 0, keepdims=False).reshape(
        rel_table.shape
    )

    grad_first = after(grad_first, grad_qkv, grad_wout)
    unit1, inverse1 = normalize(after(tokens, grad_first).astype(wide))
    grad_first_norm = normalize_backward(grad_first, ln1_gain, unit1, inverse1)
    grad_tokens = (grad_hidden + grad_first_norm).astype(low)
    return (
        layer_out, grad_tokens, lines[0], lines[1], grad_qkv, grad_table, grad_wout,
        lines[2], lines[3], grad_up, grad_up_bias, grad_down, lines[4],
    )


def solution(mesh):
    groups, parts = mesh.shape["dp"], mesh.shape["mp"]
    split = Mesh(
        mesh.devices.reshape(groups // TEAM, TEAM, parts), ("copy", "team", "mp")
    )
    every = ("copy", "team", "mp")
    return jax.shard_map(
        body,
        mesh=split,
        in_specs=(
            P(every, None), P(("copy", "team"), None), P(), P(), P(), P(None, None, "mp"),
            P(None, "mp"), P("mp", None), P(), P(), P(None, "mp"), P("mp"), P("mp", None), P(),
            P(every, None),
        ),
        out_specs=(
            P(every, None), P(every, None), P(), P(), P(None, None, "mp"), P(None, "mp"),
            P("mp", None), P(), P(), P(None, "mp"), P("mp"), P("mp", None), P(),
        ),
        check_vma=False,
    )
```

```python
import functools

import jax
import jax.numpy as jnp
from jax import lax
from jax.experimental import pallas as pl
from jax.experimental.pallas import tpu as pltpu
from jax.sharding import Mesh, PartitionSpec as P

EPSILON = 1e-05
HIGHEST_PRECISION = lax.Precision.HIGHEST
LIGHT = pl.CostEstimate(flops=1, bytes_accessed=1, transcendentals=0)
MIDDLE = pl.CostEstimate(flops=2 * 10**10, bytes_accessed=1, transcendentals=0)
SMALL = pl.CostEstimate(flops=1, bytes_accessed=1, transcendentals=0)
COVER = pl.CostEstimate(flops=1, bytes_accessed=1, transcendentals=0)
HEAVY = pl.CostEstimate(flops=10**11, bytes_accessed=1, transcendentals=0)
FEED_STEPS = 2
BLK = 256
HEAD_LANES = 64
NEAR = 128


def head_mask(rows, width, head, axis):
    place = lax.broadcasted_iota(jnp.int32, (rows, width), axis)
    return (place >= head * HEAD_LANES) & (place < (head + 1) * HEAD_LANES)


def one_head(value, head):
    keep = head_mask(value.shape[0], value.shape[1], head, 1)
    return jnp.where(keep, value, jnp.zeros_like(value))


def scaled(queries):
    return queries * jnp.asarray(HEAD_LANES ** -0.5, queries.dtype)


def dot_nt(left, right):
    return lax.dot_general(
        left, right, (((1,), (1,)), ((), ())), preferred_element_type=jnp.float32
    )


def dot_nn(left, right):
    return lax.dot_general(
        left, right, (((1,), (0,)), ((), ())), preferred_element_type=jnp.float32
    )


def attention_forward_kernel(
    cut_ref, rows_ref, weight_ref, bias_ref,
    qkv_a, qkv_b, out_ref, lse_a, lse_b, tile_ref, masked_v, score_ref,
):
    heads = masked_v.shape[0]
    width = out_ref.shape[1] // 2
    block = pl.program_id(0)
    cut = cut_ref[0]
    qkv_refs, lse_refs = (qkv_a, qkv_b), (lse_a, lse_b)

    @pl.when(block == 0)
    def _():
        weights = [
            jnp.concatenate(
                [weight_ref[slot, :, pair * width : (pair + 1) * width] for slot in range(3)],
                axis=1,
            )
            for pair in range(2)
        ]

        def one_chunk(chunk, carry):
            spot = pl.ds(pl.multiple_of(chunk * BLK, BLK), BLK)
            for pair in range(2):
                qkv_refs[pair][spot, :] = dot_nn(rows_ref[spot, :], weights[pair]).astype(
                    jnp.bfloat16
                )
            return carry

        lax.fori_loop(0, rows_ref.shape[0] // BLK, one_chunk, 0)
        for head in range(heads):
            wide = jnp.broadcast_to(bias_ref[head : head + 1, :], (BLK, 2 * BLK))
            tile_ref[head] = pltpu.roll(wide, 0, 1, stride=1, stride_axis=0)
            masked_v[head] = one_head(qkv_refs[head // 2][:, 2 * width :], head % 2)

    row_start = block * BLK
    first = jnp.where(row_start >= cut, cut // BLK, 0)
    rows = row_start + lax.broadcasted_iota(jnp.int32, (BLK, BLK), 0)
    seg_start = jnp.where(rows >= cut, cut, 0)
    columns = lax.broadcasted_iota(jnp.int32, (BLK, BLK), 1)
    own = pl.ds(pl.multiple_of(row_start, BLK), BLK)
    q_heads = [
        one_head(scaled(qkv_refs[head // 2][own, 0:width]), head % 2) for head in range(heads)
    ]

    def scores_of(key_block, tops):
        key_start = pl.multiple_of(key_block * BLK, BLK)
        keys = [ref[pl.ds(key_start, BLK), width : 2 * width] for ref in qkv_refs]
        places = key_start + columns
        allowed = (places <= rows) & (places >= seg_start)
        offset = pl.multiple_of(jnp.maximum(key_block - block + 1, 0) * BLK, BLK)
        near = key_block - block + 1 >= 0
        new_tops = []
        for head in range(heads):
            raw = dot_nt(q_heads[head], keys[head // 2])
            far = bias_ref[head : head + 1, 2 * BLK - 1 : 2 * BLK]
            bias = jnp.where(near, tile_ref[head, :, pl.ds(offset, BLK)], far)
            scores = jnp.where(allowed, raw + bias, -1e30)
            score_ref[head, :, pl.ds(key_start, BLK)] = scores
            top = tops[head]
            for lane in range(0, BLK, 128):
                top = jnp.maximum(top, scores[:, lane : lane + 128])
            new_tops.append(top)
        return tuple(new_tops)

    start = tuple(jnp.full((BLK, 128), -1e30, jnp.float32) for _ in range(heads))
    tops = lax.fori_loop(first, block + 1, scores_of, start)
    tops = [jnp.max(top, axis=1, keepdims=True) for top in tops]

    def weighted(key_block, carry):
        totals, sums = carry
        key_start = pl.multiple_of(key_block * BLK, BLK)
        new_totals, new_sums = [], []
        for pair in range(2):
            pieces, values = [], []
            for head in (2 * pair, 2 * pair + 1):
                soft = jnp.exp(score_ref[head, :, pl.ds(key_start, BLK)] - tops[head])
                part = sums[head]
                for lane in range(0, BLK, 128):
                    part = part + soft[:, lane : lane + 128]
                new_sums.append(part)
                pieces.append(soft.astype(jnp.bfloat16))
                values.append(masked_v[head, pl.ds(key_start, BLK), :])
            new_totals.append(
                totals[pair]
                + dot_nn(jnp.concatenate(pieces, axis=1), jnp.concatenate(values, axis=0))
            )
        return tuple(new_totals), tuple(new_sums)

    totals, sums = lax.fori_loop(
        first,
        block + 1,
        weighted,
        (
            tuple(jnp.zeros((BLK, width), jnp.float32) for _ in range(2)),
            tuple(jnp.zeros((BLK, 128), jnp.float32) for _ in range(heads)),
        ),
    )
    lanes = lax.broadcasted_iota(jnp.int32, (BLK, width), 1)
    for pair in range(2):
        scale = jnp.zeros((BLK, width), jnp.float32)
        logs = jnp.zeros((BLK, width), jnp.float32)
        for place in range(2):
            head = 2 * pair + place
            sum_one = jnp.sum(sums[head], axis=1, keepdims=True)
            scale = jnp.where(lanes // HEAD_LANES == place, 1.0 / sum_one, scale)
            logs = jnp.where(lanes == place, tops[head] + jnp.log(sum_one), logs)
        out_ref[:, pair * width : (pair + 1) * width] = (totals[pair] * scale).astype(jnp.bfloat16)
        lse_refs[pair][...] = jnp.transpose(logs)[0:8, :]


def attention_forward(cut, normed, weights, near_bias):
    length, depth = normed.shape
    width = weights.shape[2] // 2
    heads = 2 * width // HEAD_LANES
    whole = lambda block, cut: (0, 0)
    full = pl.BlockSpec((length, 3 * width), whole)
    row = pl.BlockSpec((BLK, 2 * width), lambda block, cut: (block, 0))
    line = pl.BlockSpec((8, BLK), lambda block, cut: (0, block))
    return pl.pallas_call(
        attention_forward_kernel,
        grid_spec=pltpu.PrefetchScalarGridSpec(
            num_scalar_prefetch=1,
            grid=(length // BLK,),
            in_specs=[
                pl.BlockSpec((length, depth), whole, pipeline_mode=pl.Buffered(1)),
                pl.BlockSpec(
                    weights.shape, lambda block, cut: (0, 0, 0), pipeline_mode=pl.Buffered(1)
                ),
                pl.BlockSpec((8, 2 * BLK), whole),
            ],
            out_specs=[full, full, row, line, line],
            scratch_shapes=[
                pltpu.VMEM((heads, BLK, 2 * BLK), jnp.float32),
                pltpu.VMEM((heads, length, width), jnp.bfloat16),
                pltpu.VMEM((heads, BLK, length), jnp.float32),
            ],
        ),
        out_shape=[jax.ShapeDtypeStruct((length, 3 * width), jnp.bfloat16)] * 2
        + [jax.ShapeDtypeStruct((length, 2 * width), jnp.bfloat16)]
        + [jax.ShapeDtypeStruct((8, length), jnp.float32)] * 2,
        compiler_params=pltpu.CompilerParams(dimension_semantics=("arbitrary",)),
        cost_estimate=LIGHT,
        name="attention_forward",
    )(cut, normed, weights, near_bias)


def attention_backward_kernel(
    cut_ref, qkv_a, qkv_b, grad_ref, att_ref, lse_a, lse_b, bias_ref,
    dqkv_a, dqkv_b, table_ref,
    tile_ref, q_masked, grad_masked, delta_ref, dq_sum, near_sum, far_sum,
):
    heads = q_masked.shape[0]
    block = pl.program_id(0)
    n_blocks = pl.num_programs(0)
    length = grad_ref.shape[0]
    width = att_ref.shape[1] // 2
    cut = cut_ref[0]
    qkv_refs, lse_refs, out_refs = (qkv_a, qkv_b), (lse_a, lse_b), (dqkv_a, dqkv_b)

    @pl.when(block == 0)
    def _():
        row = lax.broadcasted_iota(jnp.int32, (16, width), 0)
        lane = lax.broadcasted_iota(jnp.int32, (16, width), 1)
        pick = jnp.where(lane // HEAD_LANES == row, 1.0, 0.0).astype(jnp.bfloat16)
        for pair in range(2):
            lanes = slice(pair * width, (pair + 1) * width)
            grad_pair = grad_ref[:, lanes]
            product = grad_pair.astype(jnp.float32) * att_ref[:, lanes].astype(jnp.float32)
            high = product.astype(jnp.bfloat16)
            rest = (product - high.astype(jnp.float32)).astype(jnp.bfloat16)
            delta_ref[pair] = (dot_nt(pick, high) + dot_nt(pick, rest))[0:8, :]
            queries = scaled(qkv_refs[pair][:, 0:width])
            for place in range(2):
                head = 2 * pair + place
                q_masked[head] = one_head(queries, place)
                grad_masked[head] = one_head(grad_pair, place)
        for head in range(heads):
            wide = jnp.broadcast_to(bias_ref[head : head + 1, :], (BLK, 2 * BLK))
            tile_ref[head] = pltpu.roll(wide, 0, 1, stride=1, stride_axis=0)
        dq_sum[...] = jnp.zeros_like(dq_sum)
        near_sum[...] = jnp.zeros_like(near_sum)
        far_sum[...] = jnp.zeros_like(far_sum)

    key_start = pl.multiple_of(block * BLK, BLK)
    keys = [ref[pl.ds(key_start, BLK), width : 2 * width] for ref in qkv_refs]
    values = [ref[pl.ds(key_start, BLK), 2 * width :] for ref in qkv_refs]
    keys_t = [jnp.transpose(one) for one in keys]
    places = key_start + lax.broadcasted_iota(jnp.int32, (BLK, BLK), 0)
    columns = lax.broadcasted_iota(jnp.int32, (BLK, BLK), 1)
    last = jnp.where(key_start + BLK <= cut, (cut + BLK - 1) // BLK, n_blocks)

    def one_block(query_block, carry):
        row_start = pl.multiple_of(query_block * BLK, BLK)
        rows = row_start + columns
        allowed = (places <= rows) & (places >= jnp.where(rows >= cut, cut, 0))
        distance = query_block - block
        near = distance <= 1
        offset = pl.multiple_of(jnp.minimum(distance, 1) * BLK, BLK)
        results = []
        for pair in range(2):
            soft_pieces, grad_pieces, q_pieces, out_pieces = [], [], [], []
            for place in range(2):
                head = 2 * pair + place
                q_head = q_masked[head, pl.ds(row_start, BLK), :]
                grad_head = grad_masked[head, pl.ds(row_start, BLK), :]
                far = bias_ref[head : head + 1, BLK - 1 : BLK]
                bias = jnp.where(near, tile_ref[head, :, pl.ds(offset, BLK)], far)
                scores = dot_nt(keys[pair], q_head) + bias
                log_total = lse_refs[pair][place : place + 1, pl.ds(row_start, BLK)]
                soft = jnp.exp(jnp.where(allowed, scores - log_total, -1e30))
                grad_soft = dot_nt(values[pair], grad_head)
                delta = delta_ref[pair, place : place + 1, pl.ds(row_start, BLK)]
                grad_scores = soft * (grad_soft - delta)
                grad_low = grad_scores.astype(jnp.bfloat16)

                @pl.when(near)
                def _():
                    near_sum[head, :, pl.ds(offset, BLK)] += grad_scores

                @pl.when(jnp.logical_not(near))
                def _():
                    far_sum[head] += jnp.sum(
                        grad_scores.reshape(BLK // 8, 8, BLK), axis=0
                    )

                own = slice(place * HEAD_LANES, (place + 1) * HEAD_LANES)
                spot = slice(head * HEAD_LANES, (head + 1) * HEAD_LANES)
                dq_sum[spot, pl.ds(row_start, BLK)] += dot_nn(keys_t[pair][own, :], grad_low)
                soft_pieces.append(soft.astype(jnp.bfloat16))
                grad_pieces.append(grad_low)
                q_pieces.append(q_head)
                out_pieces.append(grad_head)
            dk, dv = carry[pair]
            dv = dv + dot_nn(
                jnp.concatenate(soft_pieces, axis=1), jnp.concatenate(out_pieces, axis=0)
            )
            dk = dk + dot_nn(
                jnp.concatenate(grad_pieces, axis=1), jnp.concatenate(q_pieces, axis=0)
            )
            results.append((dk, dv))
        return tuple(results)

    empty = jnp.zeros((BLK, width), jnp.float32)
    results = lax.fori_loop(block, last, one_block, ((empty, empty), (empty, empty)))
    for pair in range(2):
        dk, dv = results[pair]
        out_refs[pair][pl.ds(key_start, BLK), width : 2 * width] = dk.astype(jnp.bfloat16)
        out_refs[pair][pl.ds(key_start, BLK), 2 * width :] = dv.astype(jnp.bfloat16)

    @pl.when(block == n_blocks - 1)
    def _():
        for query_block in range(length // BLK):
            spot = slice(query_block * BLK, (query_block + 1) * BLK)
            turned = (jnp.transpose(dq_sum[:, spot]) * (HEAD_LANES ** -0.5)).astype(jnp.bfloat16)
            for pair in range(2):
                out_refs[pair][spot, 0:width] = turned[:, pair * width : (pair + 1) * width]
        for head in range(heads):
            lined = jnp.zeros((8, 2 * BLK), jnp.float32)
            for group in range(BLK // 8):
                piece = near_sum[head, group * 8 : group * 8 + 8, :]
                shift = (2 * BLK - group * 8) % (2 * BLK)
                lined = lined + (pltpu.roll(piece, shift, 1) if shift else piece)
            total = lined[0:1, :]
            for row in range(1, 8):
                total = total + pltpu.roll(lined, 2 * BLK - row, 1)[row : row + 1, :]
            table_ref[head : head + 1, :] = total
            rest = jnp.sum(far_sum[head], axis=0, keepdims=True)
            table_ref[heads + head : heads + head + 1, :] = jnp.concatenate(
                [rest, jnp.zeros_like(rest)], axis=1
            )


def attention_backward(cut, projected, grad_att, attended, logs, near_bias):
    length, width = attended.shape[0], attended.shape[1] // 2
    heads = 2 * width // HEAD_LANES
    whole = lambda block, cut: (0, 0)
    full = lambda columns: pl.BlockSpec((length, columns), whole)
    lse = pl.BlockSpec((8, length), whole)
    return pl.pallas_call(
        attention_backward_kernel,
        grid_spec=pltpu.PrefetchScalarGridSpec(
            num_scalar_prefetch=1,
            grid=(length // BLK,),
            in_specs=[
                full(3 * width), full(3 * width), full(2 * width), full(2 * width),
                lse, lse, pl.BlockSpec((8, 2 * BLK), whole),
            ],
            out_specs=[
                full(3 * width), full(3 * width), pl.BlockSpec((8, 2 * BLK), whole),
            ],
            scratch_shapes=[
                pltpu.VMEM((heads, BLK, 2 * BLK), jnp.float32),
                pltpu.VMEM((heads, length, width), jnp.bfloat16),
                pltpu.VMEM((heads, length, width), jnp.bfloat16),
                pltpu.VMEM((2, 8, length), jnp.float32),
                pltpu.VMEM((2 * width, length), jnp.float32),
                pltpu.VMEM((heads, BLK, 2 * BLK), jnp.float32),
                pltpu.VMEM((heads, 8, BLK), jnp.float32),
            ],
        ),
        out_shape=[
            jax.ShapeDtypeStruct((length, 3 * width), jnp.bfloat16),
            jax.ShapeDtypeStruct((length, 3 * width), jnp.bfloat16),
            jax.ShapeDtypeStruct((8, 2 * BLK), jnp.float32),
        ],
        compiler_params=pltpu.CompilerParams(dimension_semantics=("arbitrary",)),
        cost_estimate=MIDDLE,
        name="attention_backward",
    )(cut, *projected, grad_att, attended, *logs, near_bias)


def distance_bias(rel_table, bucket_of):
    hot = (
        bucket_of[:, None] == jnp.arange(rel_table.shape[0], dtype=jnp.int32)[None, :]
    ).astype(jnp.float32)
    by_distance = jnp.einsum(
        "dn,nh->hd", hot, rel_table, precision=HIGHEST_PRECISION,
        preferred_element_type=jnp.float32,
    )
    return hot, by_distance


def near_tables(by_distance):
    heads, reach = by_distance.shape
    far = by_distance[:, reach - 1 :]
    forward = jnp.concatenate(
        [
            jnp.broadcast_to(far, (heads, BLK - reach + 1)),
            by_distance[:, ::-1],
            jnp.broadcast_to(far, (heads, BLK - 1)),
        ],
        axis=1,
    )
    backward = jnp.concatenate(
        [by_distance, jnp.broadcast_to(far, (heads, 2 * BLK - reach))], axis=1
    )
    rows = ((0, 8 - heads), (0, 0))
    return jnp.pad(forward, rows), jnp.pad(backward, rows)


def table_gradient(hot, near_sums, far_sums):
    reach = hot.shape[0]
    near = near_sums[:, : reach - 1]
    far = jnp.sum(near_sums[:, reach - 1 :], axis=1) + jnp.sum(far_sums, axis=1)
    by_distance = jnp.concatenate([near, far[:, None]], axis=1)
    return jnp.einsum(
        "dn,hd->nh", hot, by_distance, precision=HIGHEST_PRECISION,
        preferred_element_type=jnp.float32,
    )


TEAM = 4


def after(value, *gates):
    return lax.optimization_barrier((value,) + gates)[0]


def flip(value, axis, bit):
    size = lax.axis_size(axis)
    return lax.ppermute(value, axis, [(i, i ^ bit) for i in range(size)])


def halve(value, dim, axis, bit):
    mine = (lax.axis_index(axis) // bit) % 2
    keep = lax.dynamic_index_in_dim(value, mine, dim, keepdims=False)
    send = lax.dynamic_index_in_dim(value, 1 - mine, dim, keepdims=False)
    received = flip(send.astype(jnp.bfloat16), axis, bit)
    return (keep.astype(jnp.float32) + received.astype(jnp.float32)).astype(jnp.bfloat16)


def halve_start(value, dim, axis, bit):
    mine = (lax.axis_index(axis) // bit) % 2
    keep = lax.dynamic_index_in_dim(value, mine, dim, keepdims=False)
    send = lax.dynamic_index_in_dim(value, 1 - mine, dim, keepdims=False)
    return keep, flip(send, axis, bit)


def halve_end(pair):
    return (pair[0].astype(jnp.float32) + pair[1].astype(jnp.float32)).astype(jnp.bfloat16)


def double(value, axis, bit):
    mine = (lax.axis_index(axis) // bit) % 2
    other = flip(value, axis, bit)
    return jnp.where(mine == 0, jnp.stack([value, other]), jnp.stack([other, value]))


def bits_of(size):
    bits = []
    bit = 1
    while bit < size:
        bits.append(bit)
        bit *= 2
    return bits


def with_partner(own):
    return jnp.concatenate([own, flip(own, "team", 1)], axis=0)


def feed_grads_kernel(core_ref, own_ref, got_ref, up_ref, down_ref, *, spots):
    unit = own_ref.shape[2]
    half = len(spots) // 2

    def write(piece_ref, places):
        for index, spot in enumerate(places):
            where = slice(spot * unit, (spot + 1) * unit)
            up_ref[:, where] = jnp.transpose(piece_ref[index, 0].astype(jnp.float32))
            down_ref[where, :] = piece_ref[index, 1].astype(jnp.float32)

    def both(core):
        write(own_ref, spots[core * half : (core + 1) * half])
        write(got_ref, spots[(1 - core) * half : (2 - core) * half])

    for core in range(2):
        pl.when(core_ref[0] == core)(functools.partial(both, core))


def feed_grads_out(core, own, got, copies):
    count, _, unit, depth = own.shape
    merge = max(1, 128 // unit)
    if merge > 1:
        own, got = (
            jnp.transpose(
                one.reshape(count // merge, merge, 2, unit, depth), (0, 2, 1, 3, 4)
            ).reshape(count // merge, 2, merge * unit, depth)
            for one in (own, got)
        )
    count, _, unit, depth = own.shape
    each = copies // merge
    spots = []
    for step in range(2 * count):
        half, side, place = place_in_group(step, each)
        spots.append((side * 2 + half) * each + place)
    take = depth // 4
    piece = pl.BlockSpec((count, 2, unit, take), lambda step, core: (0, 0, 0, step))
    return pl.pallas_call(
        functools.partial(feed_grads_kernel, spots=spots),
        grid_spec=pltpu.PrefetchScalarGridSpec(
            num_scalar_prefetch=1,
            grid=(4,),
            in_specs=[piece, piece],
            out_specs=[
                pl.BlockSpec((take, 2 * count * unit), lambda step, core: (step, 0)),
                pl.BlockSpec((2 * count * unit, take), lambda step, core: (0, step)),
            ],
        ),
        out_shape=[
            jax.ShapeDtypeStruct((depth, 2 * count * unit), jnp.float32),
            jax.ShapeDtypeStruct((2 * count * unit, depth), jnp.float32),
        ],
        compiler_params=pltpu.CompilerParams(dimension_semantics=("arbitrary",)),
        cost_estimate=LIGHT,
        name="feed_grads_out",
    )(core, own, got)


def attention_grads_kernel(core_ref, own_ref, got_ref, qkv_ref, out_ref, *, spots):
    group = own_ref.shape[0]
    rows, width = qkv_ref.shape[1] // group, qkv_ref.shape[2]
    few = out_ref.shape[0] // group

    def place_all(piece_ref, core):
        for item in range(group):
            spot = spots[core * group + item] - core * group
            for slot in range(3):
                qkv_ref[slot, spot * rows : (spot + 1) * rows, :] = piece_ref[
                    item, slot * rows : (slot + 1) * rows, :
                ].astype(jnp.float32)
            for place in range(out_ref.shape[1] // width):
                start = 3 * rows + place * few
                out_ref[
                    spot * few : (spot + 1) * few, place * width : (place + 1) * width
                ] = piece_ref[item, start : start + few, :].astype(jnp.float32)

    step = pl.program_id(0)
    for core in range(2):
        mine = (step == core) & (core_ref[0] == core)
        other = (step == core) & (core_ref[0] != core)
        pl.when(mine)(functools.partial(place_all, own_ref, core))
        pl.when(other)(functools.partial(place_all, got_ref, core))


def attention_grads_out(core, own, got, depth, head_width):
    half = own.shape[0]
    copies = half // 2
    spots = []
    for step in range(2 * half):
        side_core, side, place = place_in_group(step, copies)
        spots.append((side_core * 2 + side) * copies + place)
    whole = pl.BlockSpec(own.shape, lambda step, core: (0, 0, 0))
    return pl.pallas_call(
        functools.partial(attention_grads_kernel, spots=spots),
        grid_spec=pltpu.PrefetchScalarGridSpec(
            num_scalar_prefetch=1,
            grid=(2,),
            in_specs=[whole, whole],
            out_specs=[
                pl.BlockSpec((3, depth // 2, head_width), lambda step, core: (0, step, 0)),
                pl.BlockSpec((head_width // 2, depth), lambda step, core: (step, 0)),
            ],
        ),
        out_shape=[
            jax.ShapeDtypeStruct((3, depth, head_width), jnp.float32),
            jax.ShapeDtypeStruct((head_width, depth), jnp.float32),
        ],
        compiler_params=pltpu.CompilerParams(dimension_semantics=("arbitrary",)),
        cost_estimate=HEAVY,
        name="attention_grads_out",
    )(core, own, got)


def qkv_grad_kernel(core_ref, rows_ref, grad_a, grad_b, send_ref, keep_ref):
    width = grad_a.shape[1]
    both = [dot_tn(rows_ref[...], grad[...]).astype(jnp.bfloat16) for grad in (grad_a, grad_b)]

    @pl.when(pl.program_id(0) == 0)
    def _():
        send_ref[:, 0:width] = both[0]
        send_ref[:, width:] = both[1]

    @pl.when(pl.program_id(0) == 1)
    def _():
        keep_ref[:, 0:width] = both[0]
        keep_ref[:, width:] = both[1]


def qkv_weight_grad(core, rows, grads):
    length, depth = rows.shape
    width = grads[0].shape[1]
    half = depth // 2
    whole = pl.BlockSpec((length, width), lambda step, core: (0, 0))
    out = pl.BlockSpec((half, 2 * width), lambda step, core: (0, 0))
    return pl.pallas_call(
        qkv_grad_kernel,
        grid_spec=pltpu.PrefetchScalarGridSpec(
            num_scalar_prefetch=1,
            grid=(2,),
            in_specs=[
                pl.BlockSpec((length, half), lambda step, core: (0, 1 - core[0] ^ step)),
                whole, whole,
            ],
            out_specs=[out, out],
        ),
        out_shape=[jax.ShapeDtypeStruct((half, 2 * width), jnp.bfloat16)] * 2,
        compiler_params=pltpu.CompilerParams(dimension_semantics=("arbitrary",)),
        cost_estimate=SMALL,
        name="qkv_weight_grad",
    )(core, rows, *grads)


def first_norm_kernel(token_ref, line_ref, out_ref):
    unit, _ = normalize(token_ref[...].astype(jnp.float32))
    out_ref[...] = (unit * line_ref[0:1, :] + line_ref[1:2, :]).astype(jnp.bfloat16)


def first_norm(tokens, lines):
    return pl.pallas_call(
        first_norm_kernel,
        out_shape=jax.ShapeDtypeStruct(tokens.shape, jnp.bfloat16),
        cost_estimate=LIGHT,
        name="first_norm",
    )(tokens, lines)


def token_grads_kernel(grad_ref, hidden_ref, token_ref, line_ref, out_ref):
    unit, inverse = normalize(token_ref[...].astype(jnp.float32))
    grad = normalize_backward(grad_ref[...].astype(jnp.float32), line_ref[...], unit, inverse)
    out_ref[...] = (hidden_ref[...] + grad).astype(jnp.bfloat16)


def token_grads(grad, hidden, tokens, line):
    return pl.pallas_call(
        token_grads_kernel,
        out_shape=jax.ShapeDtypeStruct(tokens.shape, jnp.bfloat16),
        compiler_params=pltpu.CompilerParams(vmem_limit_bytes=32 * 1024 * 1024),
        cost_estimate=LIGHT,
        name="token_grads",
    )(grad, hidden, tokens, line)


def branch_kernel(*refs, count):
    pieces = refs[:count]
    weight_ref, token_ref, line_ref, hidden_ref, second_ref, left_ref = refs[count:]
    left = jnp.concatenate([piece[...] for piece in pieces], axis=1)
    left_ref[...] = left
    hidden = token_ref[...].astype(jnp.float32) + dot_nn(left, weight_ref[...])
    unit, _ = normalize(hidden)
    hidden_ref[...] = hidden
    second_ref[...] = (unit * line_ref[0:1, :] + line_ref[1:2, :]).astype(jnp.bfloat16)


def branch_and_norm(pieces, weights, tokens, lines):
    rows, depth = tokens.shape
    return pl.pallas_call(
        functools.partial(branch_kernel, count=len(pieces)),
        out_shape=[
            jax.ShapeDtypeStruct((rows, depth), jnp.float32),
            jax.ShapeDtypeStruct((rows, depth), jnp.bfloat16),
            jax.ShapeDtypeStruct((rows, weights.shape[0]), jnp.bfloat16),
        ],
        compiler_params=pltpu.CompilerParams(vmem_limit_bytes=32 * 1024 * 1024),
        cost_estimate=LIGHT,
        name="branch_and_norm",
    )(*pieces, weights, tokens, lines)


def row_grads_kernel(
    own_ref, core_ref, across_ref, grad_ref, hidden_ref, weight_ref, line_ref,
    total_ref, branch_ref, *refs,
):
    block_refs, sum_ref = refs[:-1], refs[-1]
    second = (
        own_ref[...].astype(jnp.float32) + core_ref[...].astype(jnp.float32)
        + across_ref[...].astype(jnp.float32)
    )
    grad = grad_ref[...].astype(jnp.float32)
    unit, inverse = normalize(hidden_ref[...])
    total = grad + normalize_backward(second, line_ref[0:1, :], unit, inverse)
    branch = total.astype(jnp.bfloat16)
    total_ref[...] = total
    branch_ref[...] = branch
    width = block_refs[0].shape[1]
    for index, block_ref in enumerate(block_refs):
        block_ref[...] = dot_nt(
            branch, weight_ref[index * width : (index + 1) * width, :]
        ).astype(jnp.bfloat16)
    sums = [jnp.sum(one, axis=0, keepdims=True) for one in (second * unit, second, grad)]
    lines = jnp.concatenate(sums + [jnp.zeros((5, sums[0].shape[1]), jnp.float32)])

    sum_ref[...] = lines


def row_grads(backs, grad, hidden, weights, lines, parts):
    rows, depth = hidden.shape
    width = weights.shape[0] // parts
    return pl.pallas_call(
        row_grads_kernel,
        out_shape=[
            jax.ShapeDtypeStruct((rows, depth), jnp.float32),
            jax.ShapeDtypeStruct((rows, depth), jnp.bfloat16),
        ]
        + [jax.ShapeDtypeStruct((rows, width), jnp.bfloat16)] * parts
        + [jax.ShapeDtypeStruct((8, depth), jnp.float32)],
        compiler_params=pltpu.CompilerParams(vmem_limit_bytes=40 * 1024 * 1024),
        cost_estimate=LIGHT,
        name="row_grads",
    )(*backs, grad, hidden, weights, lines)


def out_grad_kernel(core_ref, left_ref, right_ref, keep_ref, send_ref):
    parts, half, _ = keep_ref.shape

    def columns(core):
        return jnp.concatenate(
            [
                left_ref[:, pl.ds(pl.multiple_of((2 * part + core) * half, 128), half)]
                for part in range(parts)
            ],
            axis=1,
        )

    for out_ref, core in ((keep_ref, core_ref[0]), (send_ref, 1 - core_ref[0])):
        grad = dot_tn(columns(core), right_ref[...]).astype(jnp.bfloat16)
        for part in range(parts):
            out_ref[part] = grad[part * half : (part + 1) * half]


def out_weight_grad(core, own_rows, grads, parts):
    rows, depth = grads.shape
    half = own_rows.shape[1] // parts // 2
    whole = pl.BlockSpec((rows, depth), lambda step, core: (0, 0))
    out = pl.BlockSpec((parts, half, depth), lambda step, core: (0, 0, 0))
    return pl.pallas_call(
        out_grad_kernel,
        grid_spec=pltpu.PrefetchScalarGridSpec(
            num_scalar_prefetch=1,
            grid=(1,),
            in_specs=[
                pl.BlockSpec(own_rows.shape, lambda step, core: (0, 0)), whole,
            ],
            out_specs=[out, out],
        ),
        out_shape=[jax.ShapeDtypeStruct((parts, half, depth), jnp.bfloat16)] * 2,
        compiler_params=pltpu.CompilerParams(dimension_semantics=("arbitrary",)),
        cost_estimate=COVER,
        name="out_weight_grad",
    )(core, own_rows, grads)


def normalize(inputs):
    center = inputs - jnp.mean(inputs, axis=-1, keepdims=True)
    spread = jnp.mean(center * center, axis=-1, keepdims=True)
    inverse = lax.rsqrt(spread + EPSILON)
    return center * inverse, inverse


def normalize_backward(grad, gain, unit, inverse):
    scaled_grad = grad * gain
    middle = jnp.mean(scaled_grad, axis=-1, keepdims=True)
    along = jnp.mean(scaled_grad * unit, axis=-1, keepdims=True)
    return (scaled_grad - middle - unit * along) * inverse


def dot_tn(left, right):
    return lax.dot_general(
        left, right, (((0,), (0,)), ((), ())), preferred_element_type=jnp.float32
    )


def copies_of(value, size):
    halves = [value[None]]
    for bit in bits_of(size):
        value = halves[0] if len(halves) == 1 else jnp.concatenate(halves)
        halves = [value, flip(value, "copy", bit)]
    return halves


def untangle(value, axis, index, size):
    for bit in bits_of(size):
        shape = value.shape
        split = value.reshape(
            shape[:axis] + (size // (2 * bit), 2, bit) + shape[axis + 1 :]
        )
        split = jnp.where((index // bit) % 2 == 1, jnp.flip(split, axis + 1), split)
        value = split.reshape(shape)
    return value


def orders(copies):
    first = [("copy", bit) for bit in bits_of(copies)] + [("team", 2)]
    return first, first[::-1] if copies == 2 else first


def spread_end(value, got, mine):
    return jnp.where(mine == 0, jnp.stack([value, got]), jnp.stack([got, value]))


def spread_group(value, step, copies):
    return spread_end(*spread_start(value, step, copies))


def spread_start(value, step, copies):
    choices = [order[step] for order in orders(copies)]
    moves = []
    for place in range(copies * TEAM):
        axis, bit = choices[place % 2]
        moves.append((place, place ^ (bit if axis == "team" else bit * TEAM)))
    got = lax.ppermute(value, ("copy", "team"), moves)
    mine = [(lax.axis_index(axis) // bit) % 2 for axis, bit in choices]
    return value, got, jnp.where(lax.axis_index("team") % 2 == 0, mine[0], mine[1])


def place_in_group(step, copies):
    core, index = step // (2 * copies), step % (2 * copies)
    if copies != 2:
        return core, index // copies, index % copies
    outer, inner = index // 2, index % 2
    return core, outer + core * (inner - outer), inner + core * (outer - inner)


def exchange(blocks):
    return [blocks[0]] + [flip(blocks[k], "mp", k) for k in range(1, len(blocks))]


def cotangent_kernel(grad_a, grad_b, weight_a, weight_b, normed_ref, line_ref, out_ref, sum_ref):
    grad = sum(
        dot_nt(grad_ref[...], jnp.concatenate([weight_ref[slot] for slot in range(3)], axis=1))
        for grad_ref, weight_ref in ((grad_a, weight_a), (grad_b, weight_b))
    )
    unit = (normed_ref[...].astype(jnp.float32) - line_ref[0:1, :]) * line_ref[1:2, :]
    out_ref[...] = grad.astype(jnp.bfloat16)
    rows, depth = grad.shape
    both = jnp.concatenate(
        [
            jnp.sum((grad * unit).reshape(rows // 8, 8, depth), axis=0),
            jnp.sum(grad.reshape(rows // 8, 8, depth), axis=0),
        ],
        axis=0,
    )

    @pl.when(pl.program_id(0) == 0)
    def _():
        sum_ref[...] = both

    @pl.when(pl.program_id(0) > 0)
    def _():
        sum_ref[...] += both


def input_cotangent(grads, weights, normed, lines):
    length, width = grads[0].shape
    depth = weights.shape[1]
    row = pl.BlockSpec((BLK, width), lambda step: (step, 0))
    part_a = pl.BlockSpec((3, depth, width // 3), lambda step: (0, 0, 0))
    part_b = pl.BlockSpec((3, depth, width // 3), lambda step: (0, 0, 1))
    return pl.pallas_call(
        cotangent_kernel,
        grid=(length // BLK,),
        in_specs=[
            row, row, part_a, part_b,
            pl.BlockSpec((BLK, depth), lambda step: (step, 0)),
            pl.BlockSpec((2, depth), lambda step: (0, 0)),
        ],
        out_specs=[
            pl.BlockSpec((BLK, depth), lambda step: (step, 0)),
            pl.BlockSpec((16, depth), lambda step: (0, 0)),
        ],
        out_shape=[
            jax.ShapeDtypeStruct((length, depth), jnp.bfloat16),
            jax.ShapeDtypeStruct((16, depth), jnp.float32),
        ],
        compiler_params=pltpu.CompilerParams(dimension_semantics=("arbitrary",)),
        cost_estimate=SMALL,
        name="input_cotangent",
    )(*grads, weights, weights, normed, lines)


def feed_kernel(*refs, unit, count):
    weight_refs = refs[:count]
    (
        bias_ref, second_ref, grad_ref,
        act_ref, pre_ref, back_own, back_other, out_own, out_other, sum_ref,
    ) = refs[count:]
    w_up, w_down = (
        jnp.concatenate(
            [
                ref[:, start : start + unit, :].reshape(ref.shape[0] * unit, ref.shape[2])
                for ref in weight_refs
            ]
        )
        for start in (0, unit)
    )
    pre = dot_nt(second_ref[...], w_up) + bias_ref[...]
    grad_act = dot_nt(grad_ref[...], w_down)
    cdf = 0.5 + 0.5 * lax.erf(pre * 0.7071067811865476)
    pdf = jnp.exp(pre * pre * -0.5) * 0.3989422804014327
    active = (pre * cdf).astype(jnp.bfloat16)
    grad_pre = ((cdf + pre * pdf) * grad_act).astype(jnp.bfloat16)
    act_ref[...] = active
    pre_ref[...] = grad_pre
    line = jnp.sum(grad_pre.astype(jnp.float32), axis=0, keepdims=True)
    back = dot_nn(grad_pre, w_up).astype(jnp.bfloat16)
    out = dot_nn(active, w_down).astype(jnp.bfloat16)

    step = pl.program_id(0)
    middle = pl.num_programs(0) // 2

    @pl.when(step < middle)
    def _():
        back_own[...] = back
        out_own[...] = out

    @pl.when(step >= middle)
    def _():
        back_other[...] = back
        out_other[...] = out

    @pl.when(step == 0)
    def _():
        sum_ref[...] = line

    @pl.when(step > 0)
    def _():
        sum_ref[...] += line


def feed_forward(weights, bias_row, second, grad, unit):
    depth = weights[0].shape[2]
    rows = second.shape[0]
    width = unit * sum(one.shape[0] for one in weights)
    steps = FEED_STEPS
    take = rows // steps
    middle = steps // 2
    row = pl.BlockSpec((take, depth), lambda step: (step, 0))
    near = pl.BlockSpec((take, depth), lambda step: (jnp.minimum(step, middle - 1), 0))
    far = pl.BlockSpec((take, depth), lambda step: (jnp.maximum(step - middle, 0), 0))
    wide = pl.BlockSpec((take, width), lambda step: (step, 0))
    line = pl.BlockSpec((1, width), lambda step: (0, 0))
    part = jax.ShapeDtypeStruct((rows // 2, depth), jnp.bfloat16)
    return pl.pallas_call(
        functools.partial(feed_kernel, unit=unit, count=len(weights)),
        grid=(steps,),
        in_specs=[pl.BlockSpec(each.shape, lambda step: (0, 0, 0)) for each in weights]
        + [line, row, row],
        out_specs=[wide, wide, near, far, near, far, line],
        out_shape=[
            jax.ShapeDtypeStruct((rows, width), jnp.bfloat16),
            jax.ShapeDtypeStruct((rows, width), jnp.bfloat16),
            part, part, part, part,
            jax.ShapeDtypeStruct((1, width), jnp.float32),
        ],
        compiler_params=pltpu.CompilerParams(
            dimension_semantics=("arbitrary",), vmem_limit_bytes=48 * 1024 * 1024
        ),
        cost_estimate=LIGHT,
        name="feed_forward",
    )(*weights, bias_row, second, grad)


def weight_grad_kernel(
    part_ref, act_a, act_b, pre_a, pre_b, second_a, second_b, grad_a, grad_b, *out_refs
):
    _, places, _, unit, _ = out_refs[0].shape
    up = dot_tn(pre_a[...], second_a[...]) + dot_tn(pre_b[...], second_b[...])
    down = dot_tn(act_a[...], grad_a[...]) + dot_tn(act_b[...], grad_b[...])
    for index, out_ref in enumerate(out_refs):
        for place in range(places):
            start = (index * places + place) * unit
            out_ref[0, place, 0] = up[start : start + unit].astype(jnp.bfloat16)
            out_ref[0, place, 1] = down[start : start + unit].astype(jnp.bfloat16)


def weight_grads(part, acts, pres, seconds, grads, parts, copies):
    rows, width = acts[0].shape
    depth = seconds[0].shape[1]
    unit = width // (parts * copies)
    count = 2 if copies > 1 else 1
    places = copies // count
    column = pl.BlockSpec((rows, width // parts), lambda step, part: (0, step))
    whole = pl.BlockSpec((rows, depth), lambda step, part: (0, 0))
    out = pl.BlockSpec(
        (1, places, 2, unit, depth), lambda step, part: (part[0] ^ step, 0, 0, 0, 0)
    )
    return pl.pallas_call(
        weight_grad_kernel,
        grid_spec=pltpu.PrefetchScalarGridSpec(
            num_scalar_prefetch=1,
            grid=(parts,),
            in_specs=[column] * 4 + [whole] * 4,
            out_specs=[out] * count,
        ),
        out_shape=[jax.ShapeDtypeStruct((parts, places, 2, unit, depth), jnp.bfloat16)] * count,
        compiler_params=pltpu.CompilerParams(
            dimension_semantics=("arbitrary",), vmem_limit_bytes=56 * 1024 * 1024
        ),
        cost_estimate=HEAVY,
        name="weight_grads",
    )(part, *acts, *pres, *seconds, *grads)


def fold_copies(halves, got):
    if len(halves) == 1:
        return halves[0]
    value = halve_end((halves[0], got))
    while value.shape[1] > 1:
        half = value.shape[1] // 2
        value = halve_end((value[:, :half], flip(value[:, half:], "copy", half)))
    return value


def sync(*values):
    return lax.optimization_barrier(values)


def body(
    tokens, seg_ids, bucket_of, ln1_gain, ln1_bias, w_qkv, rel_table, w_out,
    ln2_gain, ln2_bias, w_up, up_bias, w_down, down_bias, out_grad,
):
    low = jnp.bfloat16
    wide = jnp.float32
    copies = lax.axis_size("copy")
    parts = lax.axis_size("mp")
    copy = lax.axis_index("copy")
    member = lax.axis_index("team")
    part = lax.axis_index("mp")
    core = member % 2
    rows, depth = tokens.shape
    head_width = w_out.shape[0]
    pair_width = head_width // 2
    pairs = 2
    team_units = w_up.shape[1] // TEAM
    unit = team_units // copies
    out_rows = head_width // (2 * copies)
    seg_row = seg_ids[0]
    to_right = [(i, i + 1) for i in range(parts - 1)]
    to_left = [(i + 1, i) for i in range(parts - 1)]

    def relay(right, left, step):
        return (
            lax.ppermute(right, "mp", to_right[step - 1 :]),
            lax.ppermute(left, "mp", to_left[: parts - step]),
        )

    def corner_of(right1, left1, right3, left3):
        return jnp.where(
            (part == 0) | (part == parts - 1), right3 + left3, jnp.where(part == 1, left1, right1)
        )

    normed = lax.all_gather(
        first_norm(tokens, jnp.stack([ln1_gain, ln1_bias])), "mp", axis=0, tiled=True
    )

    def own_units(place):
        first = member * team_units + (copy ^ place) * unit
        return jnp.concatenate(
            [
                jnp.transpose(lax.dynamic_slice_in_dim(w_up, first, unit, 1)),
                lax.dynamic_slice_in_dim(w_down, first, unit, 0),
            ]
        )

    own_slot = jnp.stack([own_units(place) for place in range(copies)])
    out_own = lax.dynamic_slice_in_dim(w_out, (copy * 2 + core) * out_rows, out_rows, 0)
    own_biases = [
        lax.dynamic_slice_in_dim(up_bias, member * team_units + (copy ^ place) * unit, unit, 0)
        for place in range(copies)
    ]
    high = lax.reduce_precision(own_biases[0], 8, 7)
    middle = lax.reduce_precision(own_biases[0] - high, 8, 7)
    bias_lines = jnp.stack([high, middle, own_biases[0] - high - middle]).astype(low)
    bias_lines = jnp.pad(bias_lines, ((0, 5), (0, depth - unit)))
    piece = jnp.concatenate([own_slot[0], out_own, bias_lines])
    w_right1, w_left1 = relay(piece, piece, 1)
    w_right2, w_left2 = relay(w_right1, w_left1, 2)
    beside = copies_of(jnp.where(part % 2 == 0, w_left1, w_right1), copies)
    grad_across = flip(out_grad, "team", 2)
    grad_near = with_partner(out_grad)
    grad_far = with_partner(grad_across)
    hot, by_distance = distance_bias(rel_table, bucket_of)
    forward_bias, backward_bias = near_tables(by_distance)
    cut = jnp.sum((seg_row == seg_row[0]).astype(jnp.int32)).reshape(1)
    normed = after(
        normed, grad_near, grad_far, own_slot, forward_bias, backward_bias, cut,
        w_right2, w_left2, beside[1],
    )

    def whole_out(halves):
        mine = jnp.concatenate([half[:, 2 * unit : 2 * unit + out_rows] for half in halves])
        mine = untangle(mine, 0, copy, copies)
        other = flip(mine, "team", 1)
        return jnp.where(
            core == 0, jnp.stack([mine, other], axis=1), jnp.stack([other, mine], axis=1)
        ).reshape(head_width, depth)

    w_right2, w_left2 = after(w_right2, normed), after(w_left2, normed)
    w_right3, w_left3 = relay(w_right2, w_left2, 3)
    across = copies_of(w_right2 + w_left2, copies)
    *results, = attention_forward(cut, after(normed, across[0]), w_qkv, forward_bias)
    projected, attended, logs = results[0:2], results[2], results[3:5]
    w_right3, w_left3, across[1], attended = sync(w_right3, w_left3, across[1], attended)
    corner = copies_of(corner_of(w_right1, w_left1, w_right3, w_left3), copies)
    stack = attended.reshape(parts, rows, head_width)
    moved = exchange(
        [lax.dynamic_index_in_dim(stack, part ^ k, 0, keepdims=False) for k in range(parts)]
    )
    w_out_full = jnp.concatenate(
        [w_out] + [whole_out(halves) for halves in (beside, across, corner)]
    )
    weights = [own_slot] + beside + across + corner
    bias_row = jnp.concatenate(
        own_biases
        + [
            jnp.sum(half[:, -8:-5, :unit].astype(wide), axis=1).reshape(-1)
            for half in weights[1:]
        ]
    )[None]

    hidden_in, second, own_rows = branch_and_norm(
        moved, w_out_full, tokens, jnp.stack([ln2_gain, ln2_bias])
    )
    second_across = flip(second, "team", 2)
    second_near = with_partner(second)
    act_near, pre_near, back_own, back_core, feed_own, feed_core, sums_near = feed_forward(
        weights, bias_row, second_near, grad_near, unit
    )
    second_across = after(second_across, back_own)
    back_core = flip(back_core, "team", 1)
    second_far = with_partner(second_across)
    act_far, pre_far, back_side, back_corner, feed_side, feed_corner, sums_far = feed_forward(
        weights, bias_row, second_far, grad_far, unit
    )
    onward = (
        back_side.astype(wide) + flip(back_corner, "team", 1).astype(wide)
    ).astype(low)
    back_across = flip(onward, "team", 2)
    feed_stack = jnp.stack([after(feed_corner, onward), feed_core])
    feed_beside = flip(feed_stack, "team", 1)
    ff_grads = weight_grads(
        part.reshape(1), (act_near, after(act_far, onward, feed_stack)), (pre_near, pre_far),
        (second_near, second_far), (grad_near, grad_far), parts, copies,
    )
    ff_got = flip(ff_grads[-1], "copy", max(1, copies // 2)) if copies > 1 else ff_grads[0]
    back_across = after(back_across, ff_grads[0])
    grad_hidden, grad_branch, *grad_rows = row_grads(
        (back_own, back_core, back_across), out_grad, hidden_in, w_out_full, ln2_gain[None], parts
    )
    row_sums = grad_rows.pop()
    received = exchange(grad_rows)
    grad_branch, feed_beside, *received = sync(grad_branch, feed_beside, *received)
    wout_keep, wout_send = out_weight_grad(core.reshape(1), own_rows, grad_branch, parts)
    wout_got = flip(wout_send, "team", 1)
    feed_sum = (feed_side.astype(wide) + feed_beside[0].astype(wide)).astype(low)
    natural = jnp.zeros((parts, rows, head_width), low)
    for k in range(parts):
        natural = lax.dynamic_update_index_in_dim(natural, received[k], part ^ k, 0)
    wout_grad = halve_end((wout_keep, wout_got)).reshape(parts, 2, copies, -1, depth)
    side_bit = (member // 2) % 2
    wout_keep = lax.dynamic_index_in_dim(wout_grad, side_bit, 1, keepdims=False)
    wout_send = lax.dynamic_index_in_dim(wout_grad, 1 - side_bit, 1, keepdims=False)
    ff_got, natural, feed_sum, wout_keep, wout_send = sync(
        ff_got, natural, feed_sum, wout_keep, wout_send
    )
    ff_value = fold_copies(ff_grads, ff_got).reshape(parts, 2 * unit, depth)
    ff_piece = lax.psum_scatter(ff_value, "mp", scatter_dimension=0, tiled=False)
    wout_pair = (wout_keep, flip(wout_send, "team", 2))
    feed_across = flip(feed_sum, "team", 2)
    grad_att = natural.reshape(parts * rows, head_width)
    first_grads, last_grads, table_sums = attention_backward(
        cut, projected, grad_att, attended, logs, backward_bias
    )
    first_grads, last_grads, wout_last, feed_across = sync(
        first_grads, last_grads, wout_pair[1], feed_across
    )
    dqkv = [first_grads, last_grads]
    wout_grad = halve_end((wout_pair[0], wout_last))
    for bit in reversed(bits_of(copies)):
        wout_grad = wout_grad.reshape((parts, 2, -1) + wout_grad.shape[2:])
        wout_pair = halve_start(wout_grad, 1, "copy", bit)
        if bit > 1:
            wout_grad = halve_end(wout_pair)
    wout_keep, wout_last = wout_pair
    qkv_send, qkv_keep = qkv_weight_grad(
        core.reshape(1), normed, [after(dqkv[0], wout_keep), dqkv[1]]
    )
    qkv_keep, qkv_send, dqkv[0] = sync(qkv_keep, qkv_send, dqkv[0])
    qkv_got = flip(qkv_send, "team", 1)
    running, line_sums = input_cotangent(
        dqkv, w_qkv, normed,
        jnp.stack([after(ln1_bias, dqkv[0]), 1.0 / ln1_gain]),
    )
    grad_first = lax.psum_scatter(running, "mp", scatter_dimension=0, tiled=True)
    qkv_got, running, ff_piece, wout_last = sync(qkv_got, running, ff_piece, wout_last)
    wout_grad = halve_end((wout_keep, wout_last)).reshape(parts, -1, depth)
    wout_blocks = exchange([wout_grad[k] for k in range(parts)])
    qkv_grad = halve_end((qkv_keep, qkv_got))
    table_sums = after(table_sums, running)
    table_line = table_gradient(
        hot, table_sums[: table_sums.shape[0] // 2], table_sums[table_sums.shape[0] // 2 :]
    ).reshape(1, -1)
    table_all = lax.dynamic_update_slice_in_dim(
        jnp.zeros((parts, table_line.shape[1]), wide), table_line, part, 0
    )
    sums = (after(sums_near, running) + sums_far).reshape(parts, copies, unit)
    sums = untangle(untangle(sums, 0, part, parts), 1, copy, copies)
    up_sums = lax.dynamic_update_slice_in_dim(
        jnp.zeros((parts, TEAM * team_units), wide), sums.reshape(parts, team_units),
        member * team_units, 1,
    )
    early_lines = jnp.concatenate([row_sums[0:3].reshape(-1), up_sums.reshape(-1)])
    small = jnp.concatenate(
        [
            jnp.sum(line_sums[0:8], axis=0), jnp.sum(line_sums[8:16], axis=0),
            early_lines, table_all.reshape(-1),
        ]
    )
    small = jnp.pad(small, (0, -small.shape[0] % 1024)).reshape(-1, 1024)

    qkv_pair = halve_start(qkv_grad.reshape(2, copies, -1, qkv_grad.shape[1]), 0, "team", 2)
    ff_all = spread_group(ff_piece, 0, copies)
    small = small + flip(small, "team", 1)
    small_got = flip(small, "team", 2)
    feed_own = feed_own.astype(wide) + feed_beside[1].astype(wide) + feed_across.astype(wide)
    layer_out = (hidden_in + feed_own + down_bias).astype(low)
    qkv_last, ff_all, small_got, layer_out = sync(qkv_pair[1], ff_all, small_got, layer_out)
    qkv_grad = halve_end((qkv_pair[0], qkv_last))
    small = small + small_got

    for bit in reversed(bits_of(copies)):
        qkv_pair = halve_start(qkv_grad.reshape((2, -1) + qkv_grad.shape[1:]), 0, "copy", bit)
        if bit > 1:
            qkv_grad = halve_end(qkv_pair)
    if copies == 1:
        qkv_pair = (qkv_grad, jnp.zeros_like(qkv_grad))
    for step in range(1, len(orders(copies)[0]) - 1):
        ff_all = spread_group(ff_all, step, copies)
    ff_own, ff_got, ff_mine = spread_start(ff_all, len(orders(copies)[0]) - 1, copies)
    for bit in bits_of(copies)[1:]:
        small = small + flip(small, "copy", bit)
    small_got = flip(small, "copy", 1) if copies > 1 else jnp.zeros_like(small)
    results = sync(qkv_pair[1], small_got, small, ff_got, *wout_blocks)
    qkv_last, small_got, small, ff_got = results[:4]
    ff_all = spread_end(ff_own, ff_got, ff_mine)
    small = small + small_got
    qkv_grad = halve_end((qkv_pair[0], qkv_last))
    wout_grad = sum(one.astype(wide) for one in results[4:]).astype(low)
    qkv_grad = qkv_grad.reshape(-1, 3 * head_width)
    columns = [
        jnp.concatenate(
            [
                qkv_grad[:, (3 * pair + slot) * pair_width : (3 * pair + slot + 1) * pair_width]
                for pair in range(pairs)
            ],
            axis=1,
        )
        for slot in range(3)
    ] + [wout_grad[:, start : start + head_width] for start in range(0, depth, head_width)]
    flat = jnp.concatenate(columns)
    ff_got = flip(ff_all, "team", 1)
    flat = spread_group(flat, 0, copies)
    flat, ff_got = sync(flat, ff_got)

    for step in range(1, len(orders(copies)[0])):
        flat = spread_group(flat, step, copies)
    grad_up, grad_down = feed_grads_out(
        core.reshape(1), ff_all.reshape(2 * copies, 2, unit, depth),
        ff_got.reshape(2 * copies, 2, unit, depth), copies,
    )
    flat, grad_up, grad_down = sync(flat, grad_up, grad_down)

    flat, small, grad_first = sync(flat, small, grad_first)
    flat_got = flip(flat, "team", 1)
    small_got = flip(small, "mp", 1)
    flat_got, small_got = sync(flat_got, small_got)
    small = small + small_got
    small_got = flip(small, "mp", 2)
    grad_qkv, grad_wout = attention_grads_out(
        core.reshape(1), flat.reshape(2 * copies, -1, head_width),
        flat_got.reshape(2 * copies, -1, head_width), depth, head_width,
    )

    grad_tokens = token_grads(grad_first, grad_hidden, tokens, ln1_gain[None])
    small_got, grad_qkv, grad_wout, grad_tokens = sync(
        small_got, grad_qkv, grad_wout, grad_tokens
    )
    small = small + small_got
    small = small.reshape(-1)
    lines = [small[index * depth : (index + 1) * depth] for index in range(5)]
    start = 5 * depth
    count = TEAM * team_units
    up_sums = small[start : start + parts * count].reshape(parts, count)
    grad_up_bias = lax.dynamic_index_in_dim(up_sums, part, 0, keepdims=False)
    start = start + parts * count
    count = rel_table.size
    table_all = small[start : start + parts * count].reshape(parts, count)
    grad_table = lax.dynamic_index_in_dim(table_all, part, 0, keepdims=False).reshape(
        rel_table.shape
    )

    return (
        layer_out, grad_tokens, lines[0], lines[1], grad_qkv, grad_table, grad_wout,
        lines[2], lines[3], grad_up, grad_up_bias, grad_down, lines[4],
    )


def solution(mesh):
    groups, parts = mesh.shape["dp"], mesh.shape["mp"]
    split = Mesh(
        mesh.devices.reshape(groups // TEAM, TEAM, parts), ("copy", "team", "mp")
    )
    every = ("copy", "team", "mp")
    return jax.shard_map(
        body,
        mesh=split,
        in_specs=(
            P(every, None), P(("copy", "team"), None), P(), P(), P(), P(None, None, "mp"),
            P(None, "mp"), P("mp", None), P(), P(), P(None, "mp"), P("mp"), P("mp", None), P(),
            P(every, None),
        ),
        out_specs=(
            P(every, None), P(every, None), P(), P(), P(None, None, "mp"), P(None, "mp"),
            P("mp", None), P(), P(), P(None, "mp"), P("mp"), P("mp", None), P(),
        ),
        check_vma=False,
    )
```

```python
import functools

import jax
import jax.numpy as jnp
from jax import lax
from jax.experimental import pallas as pl
from jax.experimental.pallas import tpu as pltpu
from jax.sharding import Mesh, PartitionSpec as P

EPSILON = 1e-05
HIGHEST_PRECISION = lax.Precision.HIGHEST
LIGHT = pl.CostEstimate(flops=1, bytes_accessed=1, transcendentals=0)
MIDDLE = pl.CostEstimate(flops=2 * 10**10, bytes_accessed=1, transcendentals=0)
SMALL = pl.CostEstimate(flops=1, bytes_accessed=1, transcendentals=0)
COVER = pl.CostEstimate(flops=1, bytes_accessed=1, transcendentals=0)
HEAVY = pl.CostEstimate(flops=10**11, bytes_accessed=1, transcendentals=0)
FEED_STEPS = 2
BLK = 256
HEAD_LANES = 64
NEAR = 128


def head_mask(rows, width, head, axis):
    place = lax.broadcasted_iota(jnp.int32, (rows, width), axis)
    return (place >= head * HEAD_LANES) & (place < (head + 1) * HEAD_LANES)


def one_head(value, head):
    keep = head_mask(value.shape[0], value.shape[1], head, 1)
    return jnp.where(keep, value, jnp.zeros_like(value))


def scaled(queries):
    return queries * jnp.asarray(HEAD_LANES ** -0.5, queries.dtype)


def dot_nt(left, right):
    return lax.dot_general(
        left, right, (((1,), (1,)), ((), ())), preferred_element_type=jnp.float32
    )


def dot_nn(left, right):
    return lax.dot_general(
        left, right, (((1,), (0,)), ((), ())), preferred_element_type=jnp.float32
    )


def attention_forward_kernel(
    cut_ref, rows_ref, weight_ref, bias_ref,
    qkv_a, qkv_b, out_ref, lse_a, lse_b, tile_ref, masked_v, score_ref,
):
    heads = masked_v.shape[0]
    width = out_ref.shape[1] // 2
    block = pl.program_id(0)
    cut = cut_ref[0]
    qkv_refs, lse_refs = (qkv_a, qkv_b), (lse_a, lse_b)

    @pl.when(block == 0)
    def _():
        weights = [
            jnp.concatenate(
                [weight_ref[slot, :, pair * width : (pair + 1) * width] for slot in range(3)],
                axis=1,
            )
            for pair in range(2)
        ]

        def one_chunk(chunk, carry):
            spot = pl.ds(pl.multiple_of(chunk * BLK, BLK), BLK)
            for pair in range(2):
                qkv_refs[pair][spot, :] = dot_nn(rows_ref[spot, :], weights[pair]).astype(
                    jnp.bfloat16
                )
            return carry

        lax.fori_loop(0, rows_ref.shape[0] // BLK, one_chunk, 0)
        for head in range(heads):
            wide = jnp.broadcast_to(bias_ref[head : head + 1, :], (BLK, 2 * BLK))
            tile_ref[head, :, 0 : 2 * BLK] = pltpu.roll(wide, 0, 1, stride=1, stride_axis=0)
            tile_ref[head, :, 2 * BLK :] = wide[:, 2 * BLK - 1 :] + jnp.zeros(
                (BLK, BLK), jnp.float32
            )
            masked_v[head] = one_head(qkv_refs[head // 2][:, 2 * width :], head % 2)

    row_start = block * BLK
    first = jnp.where(row_start >= cut, cut // BLK, 0)
    rows = row_start + lax.broadcasted_iota(jnp.int32, (BLK, BLK), 0)
    seg_start = jnp.where(rows >= cut, cut, 0)
    columns = lax.broadcasted_iota(jnp.int32, (BLK, BLK), 1)
    own = pl.ds(pl.multiple_of(row_start, BLK), BLK)
    q_heads = [
        one_head(scaled(qkv_refs[head // 2][own, 0:width]), head % 2) for head in range(heads)
    ]

    def scores_of(key_block, tops):
        key_start = pl.multiple_of(key_block * BLK, BLK)
        keys = [ref[pl.ds(key_start, BLK), width : 2 * width] for ref in qkv_refs]
        places = key_start + columns
        allowed = (places <= rows) & (places >= seg_start)
        order = key_block - block + 1
        offset = pl.multiple_of(jnp.where(order >= 0, order, 2) * BLK, BLK)
        new_tops = []
        for head in range(heads):
            raw = dot_nt(q_heads[head], keys[head // 2])
            bias = tile_ref[head, :, pl.ds(offset, BLK)]
            scores = jnp.where(allowed, raw + bias, -1e30)
            score_ref[head, :, pl.ds(key_start, BLK)] = scores
            top = tops[head]
            for lane in range(0, BLK, 128):
                top = jnp.maximum(top, scores[:, lane : lane + 128])
            new_tops.append(top)
        return tuple(new_tops)

    start = tuple(jnp.full((BLK, 128), -1e30, jnp.float32) for _ in range(heads))
    tops = lax.fori_loop(first, block + 1, scores_of, start)
    tops = [jnp.max(top, axis=1, keepdims=True) for top in tops]

    def weighted(key_block, carry):
        totals, sums = carry
        key_start = pl.multiple_of(key_block * BLK, BLK)
        new_totals, new_sums = [], []
        for pair in range(2):
            pieces, values = [], []
            for head in (2 * pair, 2 * pair + 1):
                soft = jnp.exp(score_ref[head, :, pl.ds(key_start, BLK)] - tops[head])
                part = sums[head]
                for lane in range(0, BLK, 128):
                    part = part + soft[:, lane : lane + 128]
                new_sums.append(part)
                pieces.append(soft.astype(jnp.bfloat16))
                values.append(masked_v[head, pl.ds(key_start, BLK), :])
            new_totals.append(
                totals[pair]
                + dot_nn(jnp.concatenate(pieces, axis=1), jnp.concatenate(values, axis=0))
            )
        return tuple(new_totals), tuple(new_sums)

    totals, sums = lax.fori_loop(
        first,
        block + 1,
        weighted,
        (
            tuple(jnp.zeros((BLK, width), jnp.float32) for _ in range(2)),
            tuple(jnp.zeros((BLK, 128), jnp.float32) for _ in range(heads)),
        ),
    )
    lanes = lax.broadcasted_iota(jnp.int32, (BLK, width), 1)
    for pair in range(2):
        scale = jnp.zeros((BLK, width), jnp.float32)
        logs = jnp.zeros((BLK, width), jnp.float32)
        for place in range(2):
            head = 2 * pair + place
            sum_one = jnp.sum(sums[head], axis=1, keepdims=True)
            scale = jnp.where(lanes // HEAD_LANES == place, 1.0 / sum_one, scale)
            logs = jnp.where(lanes == place, tops[head] + jnp.log(sum_one), logs)
        out_ref[:, pair * width : (pair + 1) * width] = (totals[pair] * scale).astype(jnp.bfloat16)
        lse_refs[pair][...] = jnp.transpose(logs)[0:8, :]


def attention_forward(cut, normed, weights, near_bias):
    length, depth = normed.shape
    width = weights.shape[2] // 2
    heads = 2 * width // HEAD_LANES
    whole = lambda block, cut: (0, 0)
    full = pl.BlockSpec((length, 3 * width), whole)
    row = pl.BlockSpec((BLK, 2 * width), lambda block, cut: (block, 0))
    line = pl.BlockSpec((8, BLK), lambda block, cut: (0, block))
    return pl.pallas_call(
        attention_forward_kernel,
        grid_spec=pltpu.PrefetchScalarGridSpec(
            num_scalar_prefetch=1,
            grid=(length // BLK,),
            in_specs=[
                pl.BlockSpec((length, depth), whole, pipeline_mode=pl.Buffered(1)),
                pl.BlockSpec(
                    weights.shape, lambda block, cut: (0, 0, 0), pipeline_mode=pl.Buffered(1)
                ),
                pl.BlockSpec((8, 2 * BLK), whole),
            ],
            out_specs=[full, full, row, line, line],
            scratch_shapes=[
                pltpu.VMEM((heads, BLK, 3 * BLK), jnp.float32),
                pltpu.VMEM((heads, length, width), jnp.bfloat16),
                pltpu.VMEM((heads, BLK, length), jnp.float32),
            ],
        ),
        out_shape=[jax.ShapeDtypeStruct((length, 3 * width), jnp.bfloat16)] * 2
        + [jax.ShapeDtypeStruct((length, 2 * width), jnp.bfloat16)]
        + [jax.ShapeDtypeStruct((8, length), jnp.float32)] * 2,
        compiler_params=pltpu.CompilerParams(dimension_semantics=("arbitrary",)),
        cost_estimate=LIGHT,
        name="attention_forward",
    )(cut, normed, weights, near_bias)


def attention_backward_kernel(
    cut_ref, qkv_a, qkv_b, grad_ref, att_ref, lse_a, lse_b, bias_ref,
    dqkv_a, dqkv_b, table_ref,
    tile_ref, q_masked, grad_masked, delta_ref, dq_sum, near_sum,
):
    heads = q_masked.shape[0]
    block = pl.program_id(0)
    n_blocks = pl.num_programs(0)
    length = grad_ref.shape[0]
    width = att_ref.shape[1] // 2
    cut = cut_ref[0]
    qkv_refs, lse_refs, out_refs = (qkv_a, qkv_b), (lse_a, lse_b), (dqkv_a, dqkv_b)

    @pl.when(block == 0)
    def _():
        row = lax.broadcasted_iota(jnp.int32, (16, width), 0)
        lane = lax.broadcasted_iota(jnp.int32, (16, width), 1)
        pick = jnp.where(lane // HEAD_LANES == row, 1.0, 0.0).astype(jnp.bfloat16)
        for pair in range(2):
            lanes = slice(pair * width, (pair + 1) * width)
            grad_pair = grad_ref[:, lanes]
            product = grad_pair.astype(jnp.float32) * att_ref[:, lanes].astype(jnp.float32)
            high = product.astype(jnp.bfloat16)
            rest = (product - high.astype(jnp.float32)).astype(jnp.bfloat16)
            delta_ref[pair] = (dot_nt(pick, high) + dot_nt(pick, rest))[0:8, :]
            queries = scaled(qkv_refs[pair][:, 0:width])
            for place in range(2):
                head = 2 * pair + place
                q_masked[head] = one_head(queries, place)
                grad_masked[head] = one_head(grad_pair, place)
        for head in range(heads):
            wide = jnp.broadcast_to(bias_ref[head : head + 1, :], (BLK, 2 * BLK))
            tile_ref[head, :, 0 : 2 * BLK] = pltpu.roll(wide, 0, 1, stride=1, stride_axis=0)
            tile_ref[head, :, 2 * BLK :] = wide[:, BLK - 1 : BLK] + jnp.zeros(
                (BLK, BLK), jnp.float32
            )
        dq_sum[...] = jnp.zeros_like(dq_sum)
        near_sum[...] = jnp.zeros_like(near_sum)

    key_start = pl.multiple_of(block * BLK, BLK)
    keys = [ref[pl.ds(key_start, BLK), width : 2 * width] for ref in qkv_refs]
    values = [ref[pl.ds(key_start, BLK), 2 * width :] for ref in qkv_refs]
    keys_t = [jnp.transpose(one) for one in keys]
    places = key_start + lax.broadcasted_iota(jnp.int32, (BLK, BLK), 0)
    columns = lax.broadcasted_iota(jnp.int32, (BLK, BLK), 1)
    last = jnp.where(key_start + BLK <= cut, (cut + BLK - 1) // BLK, n_blocks)

    def one_block(query_block, carry):
        row_start = pl.multiple_of(query_block * BLK, BLK)
        rows = row_start + columns
        allowed = (places <= rows) & (places >= jnp.where(rows >= cut, cut, 0))
        distance = query_block - block
        offset = pl.multiple_of(jnp.minimum(distance, 2) * BLK, BLK)
        results = []
        for pair in range(2):
            soft_pieces, grad_pieces, q_pieces, out_pieces = [], [], [], []
            for place in range(2):
                head = 2 * pair + place
                q_head = q_masked[head, pl.ds(row_start, BLK), :]
                grad_head = grad_masked[head, pl.ds(row_start, BLK), :]
                bias = tile_ref[head, :, pl.ds(offset, BLK)]
                scores = dot_nt(keys[pair], q_head) + bias
                log_total = lse_refs[pair][place : place + 1, pl.ds(row_start, BLK)]
                soft = jnp.exp(jnp.where(allowed, scores - log_total, -1e30))
                grad_soft = dot_nt(values[pair], grad_head)
                delta = delta_ref[pair, place : place + 1, pl.ds(row_start, BLK)]
                grad_scores = soft * (grad_soft - delta)
                grad_low = grad_scores.astype(jnp.bfloat16)

                near_sum[head, :, pl.ds(offset, BLK)] += grad_scores
                own = slice(place * HEAD_LANES, (place + 1) * HEAD_LANES)
                spot = slice(head * HEAD_LANES, (head + 1) * HEAD_LANES)
                dq_sum[spot, pl.ds(row_start, BLK)] += dot_nn(keys_t[pair][own, :], grad_low)
                soft_pieces.append(soft.astype(jnp.bfloat16))
                grad_pieces.append(grad_low)
                q_pieces.append(q_head)
                out_pieces.append(grad_head)
            dk, dv = carry[pair]
            dv = dv + dot_nn(
                jnp.concatenate(soft_pieces, axis=1), jnp.concatenate(out_pieces, axis=0)
            )
            dk = dk + dot_nn(
                jnp.concatenate(grad_pieces, axis=1), jnp.concatenate(q_pieces, axis=0)
            )
            results.append((dk, dv))
        return tuple(results)

    empty = jnp.zeros((BLK, width), jnp.float32)
    results = lax.fori_loop(block, last, one_block, ((empty, empty), (empty, empty)))
    for pair in range(2):
        dk, dv = results[pair]
        out_refs[pair][pl.ds(key_start, BLK), width : 2 * width] = dk.astype(jnp.bfloat16)
        out_refs[pair][pl.ds(key_start, BLK), 2 * width :] = dv.astype(jnp.bfloat16)

    @pl.when(block == n_blocks - 1)
    def _():
        for query_block in range(length // BLK):
            spot = slice(query_block * BLK, (query_block + 1) * BLK)
            turned = (jnp.transpose(dq_sum[:, spot]) * (HEAD_LANES ** -0.5)).astype(jnp.bfloat16)
            for pair in range(2):
                out_refs[pair][spot, 0:width] = turned[:, pair * width : (pair + 1) * width]
        for head in range(heads):
            lined = jnp.zeros((8, 2 * BLK), jnp.float32)
            for group in range(BLK // 8):
                piece = near_sum[head, group * 8 : group * 8 + 8, 0 : 2 * BLK]
                shift = (2 * BLK - group * 8) % (2 * BLK)
                lined = lined + (pltpu.roll(piece, shift, 1) if shift else piece)
            total = lined[0:1, :]
            for row in range(1, 8):
                total = total + pltpu.roll(lined, 2 * BLK - row, 1)[row : row + 1, :]
            table_ref[head : head + 1, :] = total
            rest = jnp.sum(near_sum[head, :, 2 * BLK :], axis=0, keepdims=True)
            table_ref[heads + head : heads + head + 1, :] = jnp.concatenate(
                [rest, jnp.zeros_like(rest)], axis=1
            )


def attention_backward(cut, projected, grad_att, attended, logs, near_bias):
    length, width = attended.shape[0], attended.shape[1] // 2
    heads = 2 * width // HEAD_LANES
    whole = lambda block, cut: (0, 0)
    full = lambda columns: pl.BlockSpec((length, columns), whole)
    lse = pl.BlockSpec((8, length), whole)
    return pl.pallas_call(
        attention_backward_kernel,
        grid_spec=pltpu.PrefetchScalarGridSpec(
            num_scalar_prefetch=1,
            grid=(length // BLK,),
            in_specs=[
                full(3 * width), full(3 * width), full(2 * width), full(2 * width),
                lse, lse, pl.BlockSpec((8, 2 * BLK), whole),
            ],
            out_specs=[
                full(3 * width), full(3 * width), pl.BlockSpec((8, 2 * BLK), whole),
            ],
            scratch_shapes=[
                pltpu.VMEM((heads, BLK, 3 * BLK), jnp.float32),
                pltpu.VMEM((heads, length, width), jnp.bfloat16),
                pltpu.VMEM((heads, length, width), jnp.bfloat16),
                pltpu.VMEM((2, 8, length), jnp.float32),
                pltpu.VMEM((2 * width, length), jnp.float32),
                pltpu.VMEM((heads, BLK, 3 * BLK), jnp.float32),
            ],
        ),
        out_shape=[
            jax.ShapeDtypeStruct((length, 3 * width), jnp.bfloat16),
            jax.ShapeDtypeStruct((length, 3 * width), jnp.bfloat16),
            jax.ShapeDtypeStruct((8, 2 * BLK), jnp.float32),
        ],
        compiler_params=pltpu.CompilerParams(dimension_semantics=("arbitrary",)),
        cost_estimate=MIDDLE,
        name="attention_backward",
    )(cut, *projected, grad_att, attended, *logs, near_bias)


def distance_bias(rel_table, bucket_of):
    hot = (
        bucket_of[:, None] == jnp.arange(rel_table.shape[0], dtype=jnp.int32)[None, :]
    ).astype(jnp.float32)
    by_distance = jnp.einsum(
        "dn,nh->hd", hot, rel_table, precision=HIGHEST_PRECISION,
        preferred_element_type=jnp.float32,
    )
    return hot, by_distance


def near_tables(by_distance):
    heads, reach = by_distance.shape
    far = by_distance[:, reach - 1 :]
    forward = jnp.concatenate(
        [
            jnp.broadcast_to(far, (heads, BLK - reach + 1)),
            by_distance[:, ::-1],
            jnp.broadcast_to(far, (heads, BLK - 1)),
        ],
        axis=1,
    )
    backward = jnp.concatenate(
        [by_distance, jnp.broadcast_to(far, (heads, 2 * BLK - reach))], axis=1
    )
    rows = ((0, 8 - heads), (0, 0))
    return jnp.pad(forward, rows), jnp.pad(backward, rows)


def table_gradient(hot, near_sums, far_sums):
    reach = hot.shape[0]
    near = near_sums[:, : reach - 1]
    far = jnp.sum(near_sums[:, reach - 1 :], axis=1) + jnp.sum(far_sums, axis=1)
    by_distance = jnp.concatenate([near, far[:, None]], axis=1)
    return jnp.einsum(
        "dn,hd->nh", hot, by_distance, precision=HIGHEST_PRECISION,
        preferred_element_type=jnp.float32,
    )


TEAM = 4


def after(value, *gates):
    return lax.optimization_barrier((value,) + gates)[0]


def flip(value, axis, bit):
    size = lax.axis_size(axis)
    return lax.ppermute(value, axis, [(i, i ^ bit) for i in range(size)])


def halve(value, dim, axis, bit):
    mine = (lax.axis_index(axis) // bit) % 2
    keep = lax.dynamic_index_in_dim(value, mine, dim, keepdims=False)
    send = lax.dynamic_index_in_dim(value, 1 - mine, dim, keepdims=False)
    received = flip(send.astype(jnp.bfloat16), axis, bit)
    return (keep.astype(jnp.float32) + received.astype(jnp.float32)).astype(jnp.bfloat16)


def halve_start(value, dim, axis, bit):
    mine = (lax.axis_index(axis) // bit) % 2
    keep = lax.dynamic_index_in_dim(value, mine, dim, keepdims=False)
    send = lax.dynamic_index_in_dim(value, 1 - mine, dim, keepdims=False)
    return keep, flip(send, axis, bit)


def halve_end(pair):
    return (pair[0].astype(jnp.float32) + pair[1].astype(jnp.float32)).astype(jnp.bfloat16)


def double(value, axis, bit):
    mine = (lax.axis_index(axis) // bit) % 2
    other = flip(value, axis, bit)
    return jnp.where(mine == 0, jnp.stack([value, other]), jnp.stack([other, value]))


def bits_of(size):
    bits = []
    bit = 1
    while bit < size:
        bits.append(bit)
        bit *= 2
    return bits


def with_partner(own):
    return jnp.concatenate([own, flip(own, "team", 1)], axis=0)


def feed_grads_kernel(core_ref, own_ref, got_ref, up_ref, down_ref, *, spots):
    unit = own_ref.shape[2]
    half = len(spots) // 2

    def write(piece_ref, places):
        for index, spot in enumerate(places):
            where = slice(spot * unit, (spot + 1) * unit)
            up_ref[:, where] = jnp.transpose(piece_ref[index, 0].astype(jnp.float32))
            down_ref[where, :] = piece_ref[index, 1].astype(jnp.float32)

    def both(core):
        write(own_ref, spots[core * half : (core + 1) * half])
        write(got_ref, spots[(1 - core) * half : (2 - core) * half])

    for core in range(2):
        pl.when(core_ref[0] == core)(functools.partial(both, core))


def feed_grads_out(core, own, got, copies):
    count, _, unit, depth = own.shape
    merge = max(1, 128 // unit)
    if merge > 1:
        own, got = (
            jnp.transpose(
                one.reshape(count // merge, merge, 2, unit, depth), (0, 2, 1, 3, 4)
            ).reshape(count // merge, 2, merge * unit, depth)
            for one in (own, got)
        )
    count, _, unit, depth = own.shape
    each = copies // merge
    spots = []
    for step in range(2 * count):
        half, side, place = place_in_group(step, each)
        spots.append((side * 2 + half) * each + place)
    take = depth // 4
    piece = pl.BlockSpec((count, 2, unit, take), lambda step, core: (0, 0, 0, step))
    return pl.pallas_call(
        functools.partial(feed_grads_kernel, spots=spots),
        grid_spec=pltpu.PrefetchScalarGridSpec(
            num_scalar_prefetch=1,
            grid=(4,),
            in_specs=[piece, piece],
            out_specs=[
                pl.BlockSpec((take, 2 * count * unit), lambda step, core: (step, 0)),
                pl.BlockSpec((2 * count * unit, take), lambda step, core: (0, step)),
            ],
        ),
        out_shape=[
            jax.ShapeDtypeStruct((depth, 2 * count * unit), jnp.float32),
            jax.ShapeDtypeStruct((2 * count * unit, depth), jnp.float32),
        ],
        compiler_params=pltpu.CompilerParams(dimension_semantics=("arbitrary",)),
        cost_estimate=LIGHT,
        name="feed_grads_out",
    )(core, own, got)


def attention_grads_kernel(core_ref, own_ref, got_ref, qkv_ref, out_ref, *, spots):
    group = own_ref.shape[0]
    rows, width = qkv_ref.shape[1] // group, qkv_ref.shape[2]
    few = out_ref.shape[0] // group

    def place_all(piece_ref, core):
        for item in range(group):
            spot = spots[core * group + item] - core * group
            for slot in range(3):
                qkv_ref[slot, spot * rows : (spot + 1) * rows, :] = piece_ref[
                    item, slot * rows : (slot + 1) * rows, :
                ].astype(jnp.float32)
            for place in range(out_ref.shape[1] // width):
                start = 3 * rows + place * few
                out_ref[
                    spot * few : (spot + 1) * few, place * width : (place + 1) * width
                ] = piece_ref[item, start : start + few, :].astype(jnp.float32)

    step = pl.program_id(0)
    for core in range(2):
        mine = (step == core) & (core_ref[0] == core)
        other = (step == core) & (core_ref[0] != core)
        pl.when(mine)(functools.partial(place_all, own_ref, core))
        pl.when(other)(functools.partial(place_all, got_ref, core))


def attention_grads_out(core, own, got, depth, head_width):
    half = own.shape[0]
    copies = half // 2
    spots = []
    for step in range(2 * half):
        side_core, side, place = place_in_group(step, copies)
        spots.append((side_core * 2 + side) * copies + place)
    whole = pl.BlockSpec(own.shape, lambda step, core: (0, 0, 0))
    return pl.pallas_call(
        functools.partial(attention_grads_kernel, spots=spots),
        grid_spec=pltpu.PrefetchScalarGridSpec(
            num_scalar_prefetch=1,
            grid=(2,),
            in_specs=[whole, whole],
            out_specs=[
                pl.BlockSpec((3, depth // 2, head_width), lambda step, core: (0, step, 0)),
                pl.BlockSpec((head_width // 2, depth), lambda step, core: (step, 0)),
            ],
        ),
        out_shape=[
            jax.ShapeDtypeStruct((3, depth, head_width), jnp.float32),
            jax.ShapeDtypeStruct((head_width, depth), jnp.float32),
        ],
        compiler_params=pltpu.CompilerParams(dimension_semantics=("arbitrary",)),
        cost_estimate=HEAVY,
        name="attention_grads_out",
    )(core, own, got)


def qkv_grad_kernel(core_ref, rows_ref, grad_a, grad_b, send_ref, keep_ref):
    width = grad_a.shape[1]
    both = [dot_tn(rows_ref[...], grad[...]).astype(jnp.bfloat16) for grad in (grad_a, grad_b)]

    @pl.when(pl.program_id(0) == 0)
    def _():
        send_ref[:, 0:width] = both[0]
        send_ref[:, width:] = both[1]

    @pl.when(pl.program_id(0) == 1)
    def _():
        keep_ref[:, 0:width] = both[0]
        keep_ref[:, width:] = both[1]


def qkv_weight_grad(core, rows, grads):
    length, depth = rows.shape
    width = grads[0].shape[1]
    half = depth // 2
    whole = pl.BlockSpec((length, width), lambda step, core: (0, 0))
    out = pl.BlockSpec((half, 2 * width), lambda step, core: (0, 0))
    return pl.pallas_call(
        qkv_grad_kernel,
        grid_spec=pltpu.PrefetchScalarGridSpec(
            num_scalar_prefetch=1,
            grid=(2,),
            in_specs=[
                pl.BlockSpec((length, half), lambda step, core: (0, 1 - core[0] ^ step)),
                whole, whole,
            ],
            out_specs=[out, out],
        ),
        out_shape=[jax.ShapeDtypeStruct((half, 2 * width), jnp.bfloat16)] * 2,
        compiler_params=pltpu.CompilerParams(dimension_semantics=("arbitrary",)),
        cost_estimate=SMALL,
        name="qkv_weight_grad",
    )(core, rows, *grads)


def first_norm_kernel(token_ref, line_ref, out_ref):
    unit, _ = normalize(token_ref[...].astype(jnp.float32))
    out_ref[...] = (unit * line_ref[0:1, :] + line_ref[1:2, :]).astype(jnp.bfloat16)


def first_norm(tokens, lines):
    return pl.pallas_call(
        first_norm_kernel,
        out_shape=jax.ShapeDtypeStruct(tokens.shape, jnp.bfloat16),
        cost_estimate=LIGHT,
        name="first_norm",
    )(tokens, lines)


def token_grads_kernel(grad_ref, hidden_ref, token_ref, line_ref, out_ref):
    unit, inverse = normalize(token_ref[...].astype(jnp.float32))
    grad = normalize_backward(grad_ref[...].astype(jnp.float32), line_ref[...], unit, inverse)
    out_ref[...] = (hidden_ref[...] + grad).astype(jnp.bfloat16)


def token_grads(grad, hidden, tokens, line):
    return pl.pallas_call(
        token_grads_kernel,
        out_shape=jax.ShapeDtypeStruct(tokens.shape, jnp.bfloat16),
        compiler_params=pltpu.CompilerParams(vmem_limit_bytes=32 * 1024 * 1024),
        cost_estimate=LIGHT,
        name="token_grads",
    )(grad, hidden, tokens, line)


def branch_kernel(*refs, count):
    pieces = refs[:count]
    weight_ref, token_ref, line_ref, hidden_ref, second_ref, left_ref = refs[count:]
    left = jnp.concatenate([piece[...] for piece in pieces], axis=1)
    left_ref[...] = left
    hidden = token_ref[...].astype(jnp.float32) + dot_nn(left, weight_ref[...])
    unit, _ = normalize(hidden)
    hidden_ref[...] = hidden
    second_ref[...] = (unit * line_ref[0:1, :] + line_ref[1:2, :]).astype(jnp.bfloat16)


def branch_and_norm(pieces, weights, tokens, lines):
    rows, depth = tokens.shape
    return pl.pallas_call(
        functools.partial(branch_kernel, count=len(pieces)),
        out_shape=[
            jax.ShapeDtypeStruct((rows, depth), jnp.float32),
            jax.ShapeDtypeStruct((rows, depth), jnp.bfloat16),
            jax.ShapeDtypeStruct((rows, weights.shape[0]), jnp.bfloat16),
        ],
        compiler_params=pltpu.CompilerParams(vmem_limit_bytes=32 * 1024 * 1024),
        cost_estimate=LIGHT,
        name="branch_and_norm",
    )(*pieces, weights, tokens, lines)


def row_grads_kernel(
    own_ref, core_ref, across_ref, grad_ref, hidden_ref, weight_ref, line_ref,
    total_ref, branch_ref, *refs,
):
    block_refs, sum_ref = refs[:-1], refs[-1]
    second = (
        own_ref[...].astype(jnp.float32) + core_ref[...].astype(jnp.float32)
        + across_ref[...].astype(jnp.float32)
    )
    grad = grad_ref[...].astype(jnp.float32)
    unit, inverse = normalize(hidden_ref[...])
    total = grad + normalize_backward(second, line_ref[0:1, :], unit, inverse)
    branch = total.astype(jnp.bfloat16)
    total_ref[...] = total
    branch_ref[...] = branch
    width = block_refs[0].shape[1]
    for index, block_ref in enumerate(block_refs):
        block_ref[...] = dot_nt(
            branch, weight_ref[index * width : (index + 1) * width, :]
        ).astype(jnp.bfloat16)
    sums = [jnp.sum(one, axis=0, keepdims=True) for one in (second * unit, second, grad)]
    lines = jnp.concatenate(sums + [jnp.zeros((5, sums[0].shape[1]), jnp.float32)])

    sum_ref[...] = lines


def row_grads(backs, grad, hidden, weights, lines, parts):
    rows, depth = hidden.shape
    width = weights.shape[0] // parts
    return pl.pallas_call(
        row_grads_kernel,
        out_shape=[
            jax.ShapeDtypeStruct((rows, depth), jnp.float32),
            jax.ShapeDtypeStruct((rows, depth), jnp.bfloat16),
        ]
        + [jax.ShapeDtypeStruct((rows, width), jnp.bfloat16)] * parts
        + [jax.ShapeDtypeStruct((8, depth), jnp.float32)],
        compiler_params=pltpu.CompilerParams(vmem_limit_bytes=40 * 1024 * 1024),
        cost_estimate=LIGHT,
        name="row_grads",
    )(*backs, grad, hidden, weights, lines)


def out_grad_kernel(core_ref, left_ref, right_ref, keep_ref, send_ref):
    parts, half, _ = keep_ref.shape

    def columns(core):
        return jnp.concatenate(
            [
                left_ref[:, pl.ds(pl.multiple_of((2 * part + core) * half, 128), half)]
                for part in range(parts)
            ],
            axis=1,
        )

    for out_ref, core in ((keep_ref, core_ref[0]), (send_ref, 1 - core_ref[0])):
        grad = dot_tn(columns(core), right_ref[...]).astype(jnp.bfloat16)
        for part in range(parts):
            out_ref[part] = grad[part * half : (part + 1) * half]


def out_weight_grad(core, own_rows, grads, parts):
    rows, depth = grads.shape
    half = own_rows.shape[1] // parts // 2
    whole = pl.BlockSpec((rows, depth), lambda step, core: (0, 0))
    out = pl.BlockSpec((parts, half, depth), lambda step, core: (0, 0, 0))
    return pl.pallas_call(
        out_grad_kernel,
        grid_spec=pltpu.PrefetchScalarGridSpec(
            num_scalar_prefetch=1,
            grid=(1,),
            in_specs=[
                pl.BlockSpec(own_rows.shape, lambda step, core: (0, 0)), whole,
            ],
            out_specs=[out, out],
        ),
        out_shape=[jax.ShapeDtypeStruct((parts, half, depth), jnp.bfloat16)] * 2,
        compiler_params=pltpu.CompilerParams(dimension_semantics=("arbitrary",)),
        cost_estimate=COVER,
        name="out_weight_grad",
    )(core, own_rows, grads)


def normalize(inputs):
    center = inputs - jnp.mean(inputs, axis=-1, keepdims=True)
    spread = jnp.mean(center * center, axis=-1, keepdims=True)
    inverse = lax.rsqrt(spread + EPSILON)
    return center * inverse, inverse


def normalize_backward(grad, gain, unit, inverse):
    scaled_grad = grad * gain
    middle = jnp.mean(scaled_grad, axis=-1, keepdims=True)
    along = jnp.mean(scaled_grad * unit, axis=-1, keepdims=True)
    return (scaled_grad - middle - unit * along) * inverse


def dot_tn(left, right):
    return lax.dot_general(
        left, right, (((0,), (0,)), ((), ())), preferred_element_type=jnp.float32
    )


def copies_of(value, size):
    halves = [value[None]]
    for bit in bits_of(size):
        value = halves[0] if len(halves) == 1 else jnp.concatenate(halves)
        halves = [value, flip(value, "copy", bit)]
    return halves


def untangle(value, axis, index, size):
    for bit in bits_of(size):
        shape = value.shape
        split = value.reshape(
            shape[:axis] + (size // (2 * bit), 2, bit) + shape[axis + 1 :]
        )
        split = jnp.where((index // bit) % 2 == 1, jnp.flip(split, axis + 1), split)
        value = split.reshape(shape)
    return value


def orders(copies):
    first = [("copy", bit) for bit in bits_of(copies)] + [("team", 2)]
    return first, first[::-1] if copies == 2 else first


def spread_end(value, got, mine):
    return jnp.where(mine == 0, jnp.stack([value, got]), jnp.stack([got, value]))


def spread_group(value, step, copies):
    return spread_end(*spread_start(value, step, copies))


def spread_start(value, step, copies):
    choices = [order[step] for order in orders(copies)]
    moves = []
    for place in range(copies * TEAM):
        axis, bit = choices[place % 2]
        moves.append((place, place ^ (bit if axis == "team" else bit * TEAM)))
    got = lax.ppermute(value, ("copy", "team"), moves)
    mine = [(lax.axis_index(axis) // bit) % 2 for axis, bit in choices]
    return value, got, jnp.where(lax.axis_index("team") % 2 == 0, mine[0], mine[1])


def place_in_group(step, copies):
    core, index = step // (2 * copies), step % (2 * copies)
    if copies != 2:
        return core, index // copies, index % copies
    outer, inner = index // 2, index % 2
    return core, outer + core * (inner - outer), inner + core * (outer - inner)


def exchange(blocks):
    return [blocks[0]] + [flip(blocks[k], "mp", k) for k in range(1, len(blocks))]


def cotangent_kernel(grad_a, grad_b, weight_a, weight_b, normed_ref, line_ref, out_ref, sum_ref):
    grad = sum(
        dot_nt(grad_ref[...], jnp.concatenate([weight_ref[slot] for slot in range(3)], axis=1))
        for grad_ref, weight_ref in ((grad_a, weight_a), (grad_b, weight_b))
    )
    unit = (normed_ref[...].astype(jnp.float32) - line_ref[0:1, :]) * line_ref[1:2, :]
    out_ref[...] = grad.astype(jnp.bfloat16)
    rows, depth = grad.shape
    both = jnp.concatenate(
        [
            jnp.sum((grad * unit).reshape(rows // 8, 8, depth), axis=0),
            jnp.sum(grad.reshape(rows // 8, 8, depth), axis=0),
        ],
        axis=0,
    )

    @pl.when(pl.program_id(0) == 0)
    def _():
        sum_ref[...] = both

    @pl.when(pl.program_id(0) > 0)
    def _():
        sum_ref[...] += both


def input_cotangent(grads, weights, normed, lines):
    length, width = grads[0].shape
    depth = weights.shape[1]
    row = pl.BlockSpec((BLK, width), lambda step: (step, 0))
    part_a = pl.BlockSpec((3, depth, width // 3), lambda step: (0, 0, 0))
    part_b = pl.BlockSpec((3, depth, width // 3), lambda step: (0, 0, 1))
    return pl.pallas_call(
        cotangent_kernel,
        grid=(length // BLK,),
        in_specs=[
            row, row, part_a, part_b,
            pl.BlockSpec((BLK, depth), lambda step: (step, 0)),
            pl.BlockSpec((2, depth), lambda step: (0, 0)),
        ],
        out_specs=[
            pl.BlockSpec((BLK, depth), lambda step: (step, 0)),
            pl.BlockSpec((16, depth), lambda step: (0, 0)),
        ],
        out_shape=[
            jax.ShapeDtypeStruct((length, depth), jnp.bfloat16),
            jax.ShapeDtypeStruct((16, depth), jnp.float32),
        ],
        compiler_params=pltpu.CompilerParams(dimension_semantics=("arbitrary",)),
        cost_estimate=SMALL,
        name="input_cotangent",
    )(*grads, weights, weights, normed, lines)


def feed_kernel(*refs, unit, count):
    weight_refs = refs[:count]
    (
        bias_ref, second_ref, grad_ref,
        act_ref, pre_ref, back_own, back_other, out_own, out_other, sum_ref,
    ) = refs[count:]
    w_up, w_down = (
        jnp.concatenate(
            [
                ref[:, start : start + unit, :].reshape(ref.shape[0] * unit, ref.shape[2])
                for ref in weight_refs
            ]
        )
        for start in (0, unit)
    )
    pre = dot_nt(second_ref[...], w_up) + bias_ref[...]
    grad_act = dot_nt(grad_ref[...], w_down)
    cdf = 0.5 + 0.5 * lax.erf(pre * 0.7071067811865476)
    pdf = jnp.exp(pre * pre * -0.5) * 0.3989422804014327
    active = (pre * cdf).astype(jnp.bfloat16)
    grad_pre = ((cdf + pre * pdf) * grad_act).astype(jnp.bfloat16)
    act_ref[...] = active
    pre_ref[...] = grad_pre
    line = jnp.sum(grad_pre.astype(jnp.float32), axis=0, keepdims=True)
    back = dot_nn(grad_pre, w_up).astype(jnp.bfloat16)
    out = dot_nn(active, w_down).astype(jnp.bfloat16)

    step = pl.program_id(0)
    middle = pl.num_programs(0) // 2

    @pl.when(step < middle)
    def _():
        back_own[...] = back
        out_own[...] = out

    @pl.when(step >= middle)
    def _():
        back_other[...] = back
        out_other[...] = out

    @pl.when(step == 0)
    def _():
        sum_ref[...] = line

    @pl.when(step > 0)
    def _():
        sum_ref[...] += line


def feed_forward(weights, bias_row, second, grad, unit):
    depth = weights[0].shape[2]
    rows = second.shape[0]
    width = unit * sum(one.shape[0] for one in weights)
    steps = FEED_STEPS
    take = rows // steps
    middle = steps // 2
    row = pl.BlockSpec((take, depth), lambda step: (step, 0))
    near = pl.BlockSpec((take, depth), lambda step: (jnp.minimum(step, middle - 1), 0))
    far = pl.BlockSpec((take, depth), lambda step: (jnp.maximum(step - middle, 0), 0))
    wide = pl.BlockSpec((take, width), lambda step: (step, 0))
    line = pl.BlockSpec((1, width), lambda step: (0, 0))
    part = jax.ShapeDtypeStruct((rows // 2, depth), jnp.bfloat16)
    return pl.pallas_call(
        functools.partial(feed_kernel, unit=unit, count=len(weights)),
        grid=(steps,),
        in_specs=[pl.BlockSpec(each.shape, lambda step: (0, 0, 0)) for each in weights]
        + [line, row, row],
        out_specs=[wide, wide, near, far, near, far, line],
        out_shape=[
            jax.ShapeDtypeStruct((rows, width), jnp.bfloat16),
            jax.ShapeDtypeStruct((rows, width), jnp.bfloat16),
            part, part, part, part,
            jax.ShapeDtypeStruct((1, width), jnp.float32),
        ],
        compiler_params=pltpu.CompilerParams(
            dimension_semantics=("arbitrary",), vmem_limit_bytes=48 * 1024 * 1024
        ),
        cost_estimate=LIGHT,
        name="feed_forward",
    )(*weights, bias_row, second, grad)


def weight_grad_kernel(
    part_ref, act_a, act_b, pre_a, pre_b, second_a, second_b, grad_a, grad_b, *out_refs
):
    _, places, _, unit, _ = out_refs[0].shape
    up = dot_tn(pre_a[...], second_a[...]) + dot_tn(pre_b[...], second_b[...])
    down = dot_tn(act_a[...], grad_a[...]) + dot_tn(act_b[...], grad_b[...])
    for index, out_ref in enumerate(out_refs):
        for place in range(places):
            start = (index * places + place) * unit
            out_ref[0, place, 0] = up[start : start + unit].astype(jnp.bfloat16)
            out_ref[0, place, 1] = down[start : start + unit].astype(jnp.bfloat16)


def weight_grads(part, acts, pres, seconds, grads, parts, copies):
    rows, width = acts[0].shape
    depth = seconds[0].shape[1]
    unit = width // (parts * copies)
    count = 2 if copies > 1 else 1
    places = copies // count
    column = pl.BlockSpec((rows, width // parts), lambda step, part: (0, step))
    whole = pl.BlockSpec((rows, depth), lambda step, part: (0, 0))
    out = pl.BlockSpec(
        (1, places, 2, unit, depth), lambda step, part: (part[0] ^ step, 0, 0, 0, 0)
    )
    return pl.pallas_call(
        weight_grad_kernel,
        grid_spec=pltpu.PrefetchScalarGridSpec(
            num_scalar_prefetch=1,
            grid=(parts,),
            in_specs=[column] * 4 + [whole] * 4,
            out_specs=[out] * count,
        ),
        out_shape=[jax.ShapeDtypeStruct((parts, places, 2, unit, depth), jnp.bfloat16)] * count,
        compiler_params=pltpu.CompilerParams(
            dimension_semantics=("arbitrary",), vmem_limit_bytes=56 * 1024 * 1024
        ),
        cost_estimate=HEAVY,
        name="weight_grads",
    )(part, *acts, *pres, *seconds, *grads)


def fold_copies(halves, got):
    if len(halves) == 1:
        return halves[0]
    value = halve_end((halves[0], got))
    while value.shape[1] > 1:
        half = value.shape[1] // 2
        value = halve_end((value[:, :half], flip(value[:, half:], "copy", half)))
    return value


def sync(*values):
    return lax.optimization_barrier(values)


def body(
    tokens, seg_ids, bucket_of, ln1_gain, ln1_bias, w_qkv, rel_table, w_out,
    ln2_gain, ln2_bias, w_up, up_bias, w_down, down_bias, out_grad,
):
    low = jnp.bfloat16
    wide = jnp.float32
    copies = lax.axis_size("copy")
    parts = lax.axis_size("mp")
    copy = lax.axis_index("copy")
    member = lax.axis_index("team")
    part = lax.axis_index("mp")
    core = member % 2
    rows, depth = tokens.shape
    head_width = w_out.shape[0]
    pair_width = head_width // 2
    pairs = 2
    team_units = w_up.shape[1] // TEAM
    unit = team_units // copies
    out_rows = head_width // (2 * copies)
    seg_row = seg_ids[0]
    to_right = [(i, i + 1) for i in range(parts - 1)]
    to_left = [(i + 1, i) for i in range(parts - 1)]

    def relay(right, left, step):
        return (
            lax.ppermute(right, "mp", to_right[step - 1 :]),
            lax.ppermute(left, "mp", to_left[: parts - step]),
        )

    def corner_of(right1, left1, right3, left3):
        return jnp.where(
            (part == 0) | (part == parts - 1), right3 + left3, jnp.where(part == 1, left1, right1)
        )

    normed = lax.all_gather(
        first_norm(tokens, jnp.stack([ln1_gain, ln1_bias])), "mp", axis=0, tiled=True
    )

    def own_units(place):
        first = member * team_units + (copy ^ place) * unit
        return jnp.concatenate(
            [
                jnp.transpose(lax.dynamic_slice_in_dim(w_up, first, unit, 1)),
                lax.dynamic_slice_in_dim(w_down, first, unit, 0),
            ]
        )

    own_slot = jnp.stack([own_units(place) for place in range(copies)])
    out_own = lax.dynamic_slice_in_dim(w_out, (copy * 2 + core) * out_rows, out_rows, 0)
    own_biases = [
        lax.dynamic_slice_in_dim(up_bias, member * team_units + (copy ^ place) * unit, unit, 0)
        for place in range(copies)
    ]
    high = lax.reduce_precision(own_biases[0], 8, 7)
    middle = lax.reduce_precision(own_biases[0] - high, 8, 7)
    bias_lines = jnp.stack([high, middle, own_biases[0] - high - middle]).astype(low)
    bias_lines = jnp.pad(bias_lines, ((0, 5), (0, depth - unit)))
    piece = jnp.concatenate([own_slot[0], out_own, bias_lines])
    w_right1, w_left1 = relay(piece, piece, 1)
    w_right2, w_left2 = relay(w_right1, w_left1, 2)
    beside = copies_of(jnp.where(part % 2 == 0, w_left1, w_right1), copies)
    grad_across = flip(out_grad, "team", 2)
    grad_near = with_partner(out_grad)
    grad_far = with_partner(grad_across)
    hot, by_distance = distance_bias(rel_table, bucket_of)
    forward_bias, backward_bias = near_tables(by_distance)
    cut = jnp.sum((seg_row == seg_row[0]).astype(jnp.int32)).reshape(1)
    normed = after(
        normed, grad_near, grad_far, own_slot, forward_bias, backward_bias, cut,
        w_right2, w_left2, beside[1],
    )

    def whole_out(halves):
        mine = jnp.concatenate([half[:, 2 * unit : 2 * unit + out_rows] for half in halves])
        mine = untangle(mine, 0, copy, copies)
        other = flip(mine, "team", 1)
        return jnp.where(
            core == 0, jnp.stack([mine, other], axis=1), jnp.stack([other, mine], axis=1)
        ).reshape(head_width, depth)

    w_right2, w_left2 = after(w_right2, normed), after(w_left2, normed)
    w_right3, w_left3 = relay(w_right2, w_left2, 3)
    across = copies_of(w_right2 + w_left2, copies)
    *results, = attention_forward(cut, after(normed, across[0]), w_qkv, forward_bias)
    projected, attended, logs = results[0:2], results[2], results[3:5]
    w_right3, w_left3, across[1], attended = sync(w_right3, w_left3, across[1], attended)
    corner = copies_of(corner_of(w_right1, w_left1, w_right3, w_left3), copies)
    stack = attended.reshape(parts, rows, head_width)
    moved = exchange(
        [lax.dynamic_index_in_dim(stack, part ^ k, 0, keepdims=False) for k in range(parts)]
    )
    w_out_full = jnp.concatenate(
        [w_out] + [whole_out(halves) for halves in (beside, across, corner)]
    )
    weights = [own_slot] + beside + across + corner
    bias_row = jnp.concatenate(
        own_biases
        + [
            jnp.sum(half[:, -8:-5, :unit].astype(wide), axis=1).reshape(-1)
            for half in weights[1:]
        ]
    )[None]

    hidden_in, second, own_rows = branch_and_norm(
        moved, w_out_full, tokens, jnp.stack([ln2_gain, ln2_bias])
    )
    second_across = flip(second, "team", 2)
    second_near = with_partner(second)
    act_near, pre_near, back_own, back_core, feed_own, feed_core, sums_near = feed_forward(
        weights, bias_row, second_near, grad_near, unit
    )
    second_across = after(second_across, back_own)
    back_core = flip(back_core, "team", 1)
    second_far = with_partner(second_across)
    act_far, pre_far, back_side, back_corner, feed_side, feed_corner, sums_far = feed_forward(
        weights, bias_row, second_far, grad_far, unit
    )
    onward = (
        back_side.astype(wide) + flip(back_corner, "team", 1).astype(wide)
    ).astype(low)
    back_across = flip(onward, "team", 2)
    feed_stack = jnp.stack([after(feed_corner, onward), feed_core])
    feed_beside = flip(feed_stack, "team", 1)
    ff_grads = weight_grads(
        part.reshape(1), (act_near, after(act_far, onward, feed_stack)), (pre_near, pre_far),
        (second_near, second_far), (grad_near, grad_far), parts, copies,
    )
    ff_got = flip(ff_grads[-1], "copy", max(1, copies // 2)) if copies > 1 else ff_grads[0]
    back_across = after(back_across, ff_grads[0])
    grad_hidden, grad_branch, *grad_rows = row_grads(
        (back_own, back_core, back_across), out_grad, hidden_in, w_out_full, ln2_gain[None], parts
    )
    row_sums = grad_rows.pop()
    received = exchange(grad_rows)
    grad_branch, feed_beside, *received = sync(grad_branch, feed_beside, *received)
    wout_keep, wout_send = out_weight_grad(core.reshape(1), own_rows, grad_branch, parts)
    wout_got = flip(wout_send, "team", 1)
    feed_sum = (feed_side.astype(wide) + feed_beside[0].astype(wide)).astype(low)
    natural = jnp.zeros((parts, rows, head_width), low)
    for k in range(parts):
        natural = lax.dynamic_update_index_in_dim(natural, received[k], part ^ k, 0)
    wout_grad = halve_end((wout_keep, wout_got)).reshape(parts, 2, copies, -1, depth)
    side_bit = (member // 2) % 2
    wout_keep = lax.dynamic_index_in_dim(wout_grad, side_bit, 1, keepdims=False)
    wout_send = lax.dynamic_index_in_dim(wout_grad, 1 - side_bit, 1, keepdims=False)
    ff_got, natural, feed_sum, wout_keep, wout_send = sync(
        ff_got, natural, feed_sum, wout_keep, wout_send
    )
    ff_value = fold_copies(ff_grads, ff_got).reshape(parts, 2 * unit, depth)
    ff_piece = lax.psum_scatter(ff_value, "mp", scatter_dimension=0, tiled=False)
    wout_pair = (wout_keep, flip(wout_send, "team", 2))
    feed_across = flip(feed_sum, "team", 2)
    grad_att = natural.reshape(parts * rows, head_width)
    first_grads, last_grads, table_sums = attention_backward(
        cut, projected, grad_att, attended, logs, backward_bias
    )
    first_grads, last_grads, wout_last, feed_across = sync(
        first_grads, last_grads, wout_pair[1], feed_across
    )
    dqkv = [first_grads, last_grads]
    wout_grad = halve_end((wout_pair[0], wout_last))
    for bit in reversed(bits_of(copies)):
        wout_grad = wout_grad.reshape((parts, 2, -1) + wout_grad.shape[2:])
        wout_pair = halve_start(wout_grad, 1, "copy", bit)
        if bit > 1:
            wout_grad = halve_end(wout_pair)
    wout_keep, wout_last = wout_pair
    qkv_send, qkv_keep = qkv_weight_grad(
        core.reshape(1), normed, [after(dqkv[0], wout_keep), dqkv[1]]
    )
    qkv_keep, qkv_send, dqkv[0] = sync(qkv_keep, qkv_send, dqkv[0])
    qkv_got = flip(qkv_send, "team", 1)
    running, line_sums = input_cotangent(
        dqkv, w_qkv, normed,
        jnp.stack([after(ln1_bias, dqkv[0]), 1.0 / ln1_gain]),
    )
    grad_first = lax.psum_scatter(running, "mp", scatter_dimension=0, tiled=True)
    qkv_got, running, ff_piece, wout_last = sync(qkv_got, running, ff_piece, wout_last)
    wout_grad = halve_end((wout_keep, wout_last)).reshape(parts, -1, depth)
    wout_blocks = exchange([wout_grad[k] for k in range(parts)])
    qkv_grad = halve_end((qkv_keep, qkv_got))
    table_sums = after(table_sums, running)
    table_line = table_gradient(
        hot, table_sums[: table_sums.shape[0] // 2], table_sums[table_sums.shape[0] // 2 :]
    ).reshape(1, -1)
    table_all = lax.dynamic_update_slice_in_dim(
        jnp.zeros((parts, table_line.shape[1]), wide), table_line, part, 0
    )
    sums = (after(sums_near, running) + sums_far).reshape(parts, copies, unit)
    sums = untangle(untangle(sums, 0, part, parts), 1, copy, copies)
    up_sums = lax.dynamic_update_slice_in_dim(
        jnp.zeros((parts, TEAM * team_units), wide), sums.reshape(parts, team_units),
        member * team_units, 1,
    )
    early_lines = jnp.concatenate([row_sums[0:3].reshape(-1), up_sums.reshape(-1)])
    small = jnp.concatenate(
        [
            jnp.sum(line_sums[0:8], axis=0), jnp.sum(line_sums[8:16], axis=0),
            early_lines, table_all.reshape(-1),
        ]
    )
    small = jnp.pad(small, (0, -small.shape[0] % 1024)).reshape(-1, 1024)

    qkv_pair = halve_start(qkv_grad.reshape(2, copies, -1, qkv_grad.shape[1]), 0, "team", 2)
    ff_all = spread_group(ff_piece, 0, copies)
    small = small + flip(small, "team", 1)
    small_got = flip(small, "team", 2)
    feed_own = feed_own.astype(wide) + feed_beside[1].astype(wide) + feed_across.astype(wide)
    layer_out = (hidden_in + feed_own + down_bias).astype(low)
    qkv_last, ff_all, small_got, layer_out = sync(qkv_pair[1], ff_all, small_got, layer_out)
    qkv_grad = halve_end((qkv_pair[0], qkv_last))
    small = small + small_got

    for bit in reversed(bits_of(copies)):
        qkv_pair = halve_start(qkv_grad.reshape((2, -1) + qkv_grad.shape[1:]), 0, "copy", bit)
        if bit > 1:
            qkv_grad = halve_end(qkv_pair)
    if copies == 1:
        qkv_pair = (qkv_grad, jnp.zeros_like(qkv_grad))
    for step in range(1, len(orders(copies)[0]) - 1):
        ff_all = spread_group(ff_all, step, copies)
    ff_own, ff_got, ff_mine = spread_start(ff_all, len(orders(copies)[0]) - 1, copies)
    for bit in bits_of(copies)[1:]:
        small = small + flip(small, "copy", bit)
    small_got = flip(small, "copy", 1) if copies > 1 else jnp.zeros_like(small)
    results = sync(qkv_pair[1], small_got, small, ff_got, *wout_blocks)
    qkv_last, small_got, small, ff_got = results[:4]
    ff_all = spread_end(ff_own, ff_got, ff_mine)
    small = small + small_got
    qkv_grad = halve_end((qkv_pair[0], qkv_last))
    wout_grad = sum(one.astype(wide) for one in results[4:]).astype(low)
    qkv_grad = qkv_grad.reshape(-1, 3 * head_width)
    columns = [
        jnp.concatenate(
            [
                qkv_grad[:, (3 * pair + slot) * pair_width : (3 * pair + slot + 1) * pair_width]
                for pair in range(pairs)
            ],
            axis=1,
        )
        for slot in range(3)
    ] + [wout_grad[:, start : start + head_width] for start in range(0, depth, head_width)]
    flat = jnp.concatenate(columns)
    ff_got = flip(ff_all, "team", 1)
    flat = spread_group(flat, 0, copies)
    flat, ff_got = sync(flat, ff_got)

    for step in range(1, len(orders(copies)[0])):
        flat = spread_group(flat, step, copies)
    grad_up, grad_down = feed_grads_out(
        core.reshape(1), ff_all.reshape(2 * copies, 2, unit, depth),
        ff_got.reshape(2 * copies, 2, unit, depth), copies,
    )
    flat, grad_up, grad_down = sync(flat, grad_up, grad_down)

    flat, small, grad_first = sync(flat, small, grad_first)
    flat_got = flip(flat, "team", 1)
    small_got = flip(small, "mp", 1)
    flat_got, small_got = sync(flat_got, small_got)
    small = small + small_got
    small_got = flip(small, "mp", 2)
    grad_qkv, grad_wout = attention_grads_out(
        core.reshape(1), flat.reshape(2 * copies, -1, head_width),
        flat_got.reshape(2 * copies, -1, head_width), depth, head_width,
    )

    grad_tokens = token_grads(grad_first, grad_hidden, tokens, ln1_gain[None])
    small_got, grad_qkv, grad_wout, grad_tokens = sync(
        small_got, grad_qkv, grad_wout, grad_tokens
    )
    small = small + small_got
    small = small.reshape(-1)
    lines = [small[index * depth : (index + 1) * depth] for index in range(5)]
    start = 5 * depth
    count = TEAM * team_units
    up_sums = small[start : start + parts * count].reshape(parts, count)
    grad_up_bias = lax.dynamic_index_in_dim(up_sums, part, 0, keepdims=False)
    start = start + parts * count
    count = rel_table.size
    table_all = small[start : start + parts * count].reshape(parts, count)
    grad_table = lax.dynamic_index_in_dim(table_all, part, 0, keepdims=False).reshape(
        rel_table.shape
    )

    return (
        layer_out, grad_tokens, lines[0], lines[1], grad_qkv, grad_table, grad_wout,
        lines[2], lines[3], grad_up, grad_up_bias, grad_down, lines[4],
    )


def solution(mesh):
    groups, parts = mesh.shape["dp"], mesh.shape["mp"]
    split = Mesh(
        mesh.devices.reshape(groups // TEAM, TEAM, parts), ("copy", "team", "mp")
    )
    every = ("copy", "team", "mp")
    return jax.shard_map(
        body,
        mesh=split,
        in_specs=(
            P(every, None), P(("copy", "team"), None), P(), P(), P(), P(None, None, "mp"),
            P(None, "mp"), P("mp", None), P(), P(), P(None, "mp"), P("mp"), P("mp", None), P(),
            P(every, None),
        ),
        out_specs=(
            P(every, None), P(every, None), P(), P(), P(None, None, "mp"), P(None, "mp"),
            P("mp", None), P(), P(), P(None, "mp"), P("mp"), P("mp", None), P(),
        ),
        check_vma=False,
    )
```

```python
import functools

import jax
import jax.numpy as jnp
from jax import lax
from jax.experimental import pallas as pl
from jax.experimental.pallas import tpu as pltpu
from jax.sharding import Mesh, PartitionSpec as P

EPSILON = 1e-05
HIGHEST_PRECISION = lax.Precision.HIGHEST
LIGHT = pl.CostEstimate(flops=1, bytes_accessed=1, transcendentals=0)
MIDDLE = pl.CostEstimate(flops=2 * 10**10, bytes_accessed=1, transcendentals=0)
SMALL = pl.CostEstimate(flops=1, bytes_accessed=1, transcendentals=0)
COVER = pl.CostEstimate(flops=1, bytes_accessed=1, transcendentals=0)
HEAVY = pl.CostEstimate(flops=10**11, bytes_accessed=1, transcendentals=0)
FEED_STEPS = 2
BLK = 256
HEAD_LANES = 64
NEAR = 128


def head_mask(rows, width, head, axis):
    place = lax.broadcasted_iota(jnp.int32, (rows, width), axis)
    return (place >= head * HEAD_LANES) & (place < (head + 1) * HEAD_LANES)


def one_head(value, head):
    keep = head_mask(value.shape[0], value.shape[1], head, 1)
    return jnp.where(keep, value, jnp.zeros_like(value))


def scaled(queries):
    return queries * jnp.asarray(HEAD_LANES ** -0.5, queries.dtype)


def dot_nt(left, right):
    return lax.dot_general(
        left, right, (((1,), (1,)), ((), ())), preferred_element_type=jnp.float32
    )


def dot_nn(left, right):
    return lax.dot_general(
        left, right, (((1,), (0,)), ((), ())), preferred_element_type=jnp.float32
    )


def attention_forward_kernel(
    cut_ref, rows_ref, weight_ref, bias_ref,
    qkv_a, qkv_b, out_ref, lse_a, lse_b, tile_ref, masked_v, score_ref,
):
    heads = masked_v.shape[0]
    width = out_ref.shape[1] // 2
    block = pl.program_id(0)
    cut = cut_ref[0]
    qkv_refs, lse_refs = (qkv_a, qkv_b), (lse_a, lse_b)

    @pl.when(block == 0)
    def _():
        weights = [
            jnp.concatenate(
                [weight_ref[slot, :, pair * width : (pair + 1) * width] for slot in range(3)],
                axis=1,
            )
            for pair in range(2)
        ]

        def one_chunk(chunk, carry):
            spot = pl.ds(pl.multiple_of(chunk * BLK, BLK), BLK)
            for pair in range(2):
                qkv_refs[pair][spot, :] = dot_nn(rows_ref[spot, :], weights[pair]).astype(
                    jnp.bfloat16
                )
            return carry

        lax.fori_loop(0, rows_ref.shape[0] // BLK, one_chunk, 0)
        for head in range(heads):
            wide = jnp.broadcast_to(bias_ref[head : head + 1, :], (BLK, 2 * BLK))
            tile_ref[head, :, 0 : 2 * BLK] = pltpu.roll(wide, 0, 1, stride=1, stride_axis=0)
            tile_ref[head, :, 2 * BLK :] = wide[:, 2 * BLK - 1 :] + jnp.zeros(
                (BLK, BLK), jnp.float32
            )
            masked_v[head] = one_head(qkv_refs[head // 2][:, 2 * width :], head % 2)

    row_start = block * BLK
    first = jnp.where(row_start >= cut, cut // BLK, 0)
    rows = row_start + lax.broadcasted_iota(jnp.int32, (BLK, BLK), 0)
    seg_start = jnp.where(rows >= cut, cut, 0)
    columns = lax.broadcasted_iota(jnp.int32, (BLK, BLK), 1)
    own = pl.ds(pl.multiple_of(row_start, BLK), BLK)
    q_heads = [
        one_head(scaled(qkv_refs[head // 2][own, 0:width]), head % 2) for head in range(heads)
    ]

    def scores_of(key_block, tops):
        key_start = pl.multiple_of(key_block * BLK, BLK)
        keys = [ref[pl.ds(key_start, BLK), width : 2 * width] for ref in qkv_refs]
        places = key_start + columns
        allowed = (places <= rows) & (places >= seg_start)
        order = key_block - block + 1
        offset = pl.multiple_of(jnp.where(order >= 0, order, 2) * BLK, BLK)
        new_tops = []
        for head in range(heads):
            raw = dot_nt(q_heads[head], keys[head // 2])
            bias = tile_ref[head, :, pl.ds(offset, BLK)]
            scores = jnp.where(allowed, raw + bias, -1e30)
            score_ref[head, :, pl.ds(key_start, BLK)] = scores
            top = tops[head]
            for lane in range(0, BLK, 128):
                top = jnp.maximum(top, scores[:, lane : lane + 128])
            new_tops.append(top)
        return tuple(new_tops)

    start = tuple(jnp.full((BLK, 128), -1e30, jnp.float32) for _ in range(heads))
    tops = lax.fori_loop(first, block + 1, scores_of, start)
    tops = [jnp.max(top, axis=1, keepdims=True) for top in tops]

    def weighted(key_block, carry):
        totals, sums = carry
        key_start = pl.multiple_of(key_block * BLK, BLK)
        new_totals, new_sums = [], []
        for pair in range(2):
            pieces, values = [], []
            for head in (2 * pair, 2 * pair + 1):
                soft = jnp.exp(score_ref[head, :, pl.ds(key_start, BLK)] - tops[head])
                part = sums[head]
                for lane in range(0, BLK, 128):
                    part = part + soft[:, lane : lane + 128]
                new_sums.append(part)
                pieces.append(soft.astype(jnp.bfloat16))
                values.append(masked_v[head, pl.ds(key_start, BLK), :])
            new_totals.append(
                totals[pair]
                + dot_nn(jnp.concatenate(pieces, axis=1), jnp.concatenate(values, axis=0))
            )
        return tuple(new_totals), tuple(new_sums)

    totals, sums = lax.fori_loop(
        first,
        block + 1,
        weighted,
        (
            tuple(jnp.zeros((BLK, width), jnp.float32) for _ in range(2)),
            tuple(jnp.zeros((BLK, 128), jnp.float32) for _ in range(heads)),
        ),
    )
    lanes = lax.broadcasted_iota(jnp.int32, (BLK, width), 1)
    for pair in range(2):
        scale = jnp.zeros((BLK, width), jnp.float32)
        logs = jnp.zeros((BLK, width), jnp.float32)
        for place in range(2):
            head = 2 * pair + place
            sum_one = jnp.sum(sums[head], axis=1, keepdims=True)
            scale = jnp.where(lanes // HEAD_LANES == place, 1.0 / sum_one, scale)
            logs = jnp.where(lanes == place, tops[head] + jnp.log(sum_one), logs)
        out_ref[:, pair * width : (pair + 1) * width] = (totals[pair] * scale).astype(jnp.bfloat16)
        lse_refs[pair][...] = jnp.transpose(logs)[0:8, :]


def attention_forward(cut, normed, weights, near_bias):
    length, depth = normed.shape
    width = weights.shape[2] // 2
    heads = 2 * width // HEAD_LANES
    whole = lambda block, cut: (0, 0)
    full = pl.BlockSpec((length, 3 * width), whole)
    row = pl.BlockSpec((BLK, 2 * width), lambda block, cut: (block, 0))
    line = pl.BlockSpec((8, BLK), lambda block, cut: (0, block))
    return pl.pallas_call(
        attention_forward_kernel,
        grid_spec=pltpu.PrefetchScalarGridSpec(
            num_scalar_prefetch=1,
            grid=(length // BLK,),
            in_specs=[
                pl.BlockSpec((length, depth), whole, pipeline_mode=pl.Buffered(1)),
                pl.BlockSpec(
                    weights.shape, lambda block, cut: (0, 0, 0), pipeline_mode=pl.Buffered(1)
                ),
                pl.BlockSpec((8, 2 * BLK), whole),
            ],
            out_specs=[full, full, row, line, line],
            scratch_shapes=[
                pltpu.VMEM((heads, BLK, 3 * BLK), jnp.float32),
                pltpu.VMEM((heads, length, width), jnp.bfloat16),
                pltpu.VMEM((heads, BLK, length), jnp.float32),
            ],
        ),
        out_shape=[jax.ShapeDtypeStruct((length, 3 * width), jnp.bfloat16)] * 2
        + [jax.ShapeDtypeStruct((length, 2 * width), jnp.bfloat16)]
        + [jax.ShapeDtypeStruct((8, length), jnp.float32)] * 2,
        compiler_params=pltpu.CompilerParams(
            dimension_semantics=("arbitrary",), vmem_limit_bytes=54 * 1024 * 1024
        ),
        cost_estimate=LIGHT,
        name="attention_forward",
    )(cut, normed, weights, near_bias)


def attention_backward_kernel(
    cut_ref, qkv_a, qkv_b, grad_ref, att_ref, lse_a, lse_b, bias_ref,
    dqkv_a, dqkv_b, table_ref,
    tile_ref, q_masked, grad_masked, delta_ref, dq_sum, near_sum,
):
    heads = q_masked.shape[0]
    block = pl.program_id(0)
    n_blocks = pl.num_programs(0)
    length = grad_ref.shape[0]
    width = att_ref.shape[1] // 2
    cut = cut_ref[0]
    qkv_refs, lse_refs, out_refs = (qkv_a, qkv_b), (lse_a, lse_b), (dqkv_a, dqkv_b)

    @pl.when(block == 0)
    def _():
        row = lax.broadcasted_iota(jnp.int32, (16, width), 0)
        lane = lax.broadcasted_iota(jnp.int32, (16, width), 1)
        pick = jnp.where(lane // HEAD_LANES == row, 1.0, 0.0).astype(jnp.bfloat16)
        for pair in range(2):
            lanes = slice(pair * width, (pair + 1) * width)
            grad_pair = grad_ref[:, lanes]
            product = grad_pair.astype(jnp.float32) * att_ref[:, lanes].astype(jnp.float32)
            high = product.astype(jnp.bfloat16)
            rest = (product - high.astype(jnp.float32)).astype(jnp.bfloat16)
            delta_ref[pair] = (dot_nt(pick, high) + dot_nt(pick, rest))[0:8, :]
            queries = scaled(qkv_refs[pair][:, 0:width])
            for place in range(2):
                head = 2 * pair + place
                q_masked[head] = one_head(queries, place)
                grad_masked[head] = one_head(grad_pair, place)
        for head in range(heads):
            wide = jnp.broadcast_to(bias_ref[head : head + 1, :], (BLK, 2 * BLK))
            tile_ref[head, :, 0 : 2 * BLK] = pltpu.roll(wide, 0, 1, stride=1, stride_axis=0)
            tile_ref[head, :, 2 * BLK :] = wide[:, BLK - 1 : BLK] + jnp.zeros(
                (BLK, BLK), jnp.float32
            )
        dq_sum[...] = jnp.zeros_like(dq_sum)
        near_sum[...] = jnp.zeros_like(near_sum)

    key_start = pl.multiple_of(block * BLK, BLK)
    keys = [ref[pl.ds(key_start, BLK), width : 2 * width] for ref in qkv_refs]
    values = [ref[pl.ds(key_start, BLK), 2 * width :] for ref in qkv_refs]
    keys_t = [jnp.transpose(one) for one in keys]
    places = key_start + lax.broadcasted_iota(jnp.int32, (BLK, BLK), 0)
    columns = lax.broadcasted_iota(jnp.int32, (BLK, BLK), 1)
    last = jnp.where(key_start + BLK <= cut, (cut + BLK - 1) // BLK, n_blocks)

    def one_block(query_block, carry):
        row_start = pl.multiple_of(query_block * BLK, BLK)
        rows = row_start + columns
        allowed = (places <= rows) & (places >= jnp.where(rows >= cut, cut, 0))
        distance = query_block - block
        offset = pl.multiple_of(jnp.minimum(distance, 2) * BLK, BLK)
        results = []
        for pair in range(2):
            soft_pieces, grad_pieces, q_pieces, out_pieces = [], [], [], []
            for place in range(2):
                head = 2 * pair + place
                q_head = q_masked[head, pl.ds(row_start, BLK), :]
                grad_head = grad_masked[head, pl.ds(row_start, BLK), :]
                bias = tile_ref[head, :, pl.ds(offset, BLK)]
                scores = dot_nt(keys[pair], q_head) + bias
                log_total = lse_refs[pair][place : place + 1, pl.ds(row_start, BLK)]
                soft = jnp.exp(jnp.where(allowed, scores - log_total, -1e30))
                grad_soft = dot_nt(values[pair], grad_head)
                delta = delta_ref[pair, place : place + 1, pl.ds(row_start, BLK)]
                grad_scores = soft * (grad_soft - delta)
                grad_low = grad_scores.astype(jnp.bfloat16)

                near_sum[head, :, pl.ds(offset, BLK)] += grad_scores
                own = slice(place * HEAD_LANES, (place + 1) * HEAD_LANES)
                spot = slice(head * HEAD_LANES, (head + 1) * HEAD_LANES)
                dq_sum[spot, pl.ds(row_start, BLK)] += dot_nn(keys_t[pair][own, :], grad_low)
                soft_pieces.append(soft.astype(jnp.bfloat16))
                grad_pieces.append(grad_low)
                q_pieces.append(q_head)
                out_pieces.append(grad_head)
            dk, dv = carry[pair]
            dv = dv + dot_nn(
                jnp.concatenate(soft_pieces, axis=1), jnp.concatenate(out_pieces, axis=0)
            )
            dk = dk + dot_nn(
                jnp.concatenate(grad_pieces, axis=1), jnp.concatenate(q_pieces, axis=0)
            )
            results.append((dk, dv))
        return tuple(results)

    empty = jnp.zeros((BLK, width), jnp.float32)
    results = lax.fori_loop(block, last, one_block, ((empty, empty), (empty, empty)))
    for pair in range(2):
        dk, dv = results[pair]
        out_refs[pair][pl.ds(key_start, BLK), width : 2 * width] = dk.astype(jnp.bfloat16)
        out_refs[pair][pl.ds(key_start, BLK), 2 * width :] = dv.astype(jnp.bfloat16)

    @pl.when(block == n_blocks - 1)
    def _():
        for query_block in range(length // BLK):
            spot = slice(query_block * BLK, (query_block + 1) * BLK)
            turned = (jnp.transpose(dq_sum[:, spot]) * (HEAD_LANES ** -0.5)).astype(jnp.bfloat16)
            for pair in range(2):
                out_refs[pair][spot, 0:width] = turned[:, pair * width : (pair + 1) * width]
        for head in range(heads):
            lined = jnp.zeros((8, 2 * BLK), jnp.float32)
            for group in range(BLK // 8):
                piece = near_sum[head, group * 8 : group * 8 + 8, 0 : 2 * BLK]
                shift = (2 * BLK - group * 8) % (2 * BLK)
                lined = lined + (pltpu.roll(piece, shift, 1) if shift else piece)
            total = lined[0:1, :]
            for row in range(1, 8):
                total = total + pltpu.roll(lined, 2 * BLK - row, 1)[row : row + 1, :]
            table_ref[head : head + 1, :] = total
            rest = jnp.sum(near_sum[head, :, 2 * BLK :], axis=0, keepdims=True)
            table_ref[heads + head : heads + head + 1, :] = jnp.concatenate(
                [rest, jnp.zeros_like(rest)], axis=1
            )


def attention_backward(cut, projected, grad_att, attended, logs, near_bias):
    length, width = attended.shape[0], attended.shape[1] // 2
    heads = 2 * width // HEAD_LANES
    whole = lambda block, cut: (0, 0)
    full = lambda columns: pl.BlockSpec((length, columns), whole)
    lse = pl.BlockSpec((8, length), whole)
    return pl.pallas_call(
        attention_backward_kernel,
        grid_spec=pltpu.PrefetchScalarGridSpec(
            num_scalar_prefetch=1,
            grid=(length // BLK,),
            in_specs=[
                full(3 * width), full(3 * width), full(2 * width), full(2 * width),
                lse, lse, pl.BlockSpec((8, 2 * BLK), whole),
            ],
            out_specs=[
                full(3 * width), full(3 * width), pl.BlockSpec((8, 2 * BLK), whole),
            ],
            scratch_shapes=[
                pltpu.VMEM((heads, BLK, 3 * BLK), jnp.float32),
                pltpu.VMEM((heads, length, width), jnp.bfloat16),
                pltpu.VMEM((heads, length, width), jnp.bfloat16),
                pltpu.VMEM((2, 8, length), jnp.float32),
                pltpu.VMEM((2 * width, length), jnp.float32),
                pltpu.VMEM((heads, BLK, 3 * BLK), jnp.float32),
            ],
        ),
        out_shape=[
            jax.ShapeDtypeStruct((length, 3 * width), jnp.bfloat16),
            jax.ShapeDtypeStruct((length, 3 * width), jnp.bfloat16),
            jax.ShapeDtypeStruct((8, 2 * BLK), jnp.float32),
        ],
        compiler_params=pltpu.CompilerParams(dimension_semantics=("arbitrary",)),
        cost_estimate=MIDDLE,
        name="attention_backward",
    )(cut, *projected, grad_att, attended, *logs, near_bias)


def distance_bias(rel_table, bucket_of):
    hot = (
        bucket_of[:, None] == jnp.arange(rel_table.shape[0], dtype=jnp.int32)[None, :]
    ).astype(jnp.float32)
    by_distance = jnp.einsum(
        "dn,nh->hd", hot, rel_table, precision=HIGHEST_PRECISION,
        preferred_element_type=jnp.float32,
    )
    return hot, by_distance


def near_tables(by_distance):
    heads, reach = by_distance.shape
    far = by_distance[:, reach - 1 :]
    forward = jnp.concatenate(
        [
            jnp.broadcast_to(far, (heads, BLK - reach + 1)),
            by_distance[:, ::-1],
            jnp.broadcast_to(far, (heads, BLK - 1)),
        ],
        axis=1,
    )
    backward = jnp.concatenate(
        [by_distance, jnp.broadcast_to(far, (heads, 2 * BLK - reach))], axis=1
    )
    rows = ((0, 8 - heads), (0, 0))
    return jnp.pad(forward, rows), jnp.pad(backward, rows)


def table_gradient(hot, near_sums, far_sums):
    reach = hot.shape[0]
    near = near_sums[:, : reach - 1]
    far = jnp.sum(near_sums[:, reach - 1 :], axis=1) + jnp.sum(far_sums, axis=1)
    by_distance = jnp.concatenate([near, far[:, None]], axis=1)
    return jnp.einsum(
        "dn,hd->nh", hot, by_distance, precision=HIGHEST_PRECISION,
        preferred_element_type=jnp.float32,
    )


TEAM = 4


def after(value, *gates):
    return lax.optimization_barrier((value,) + gates)[0]


def flip(value, axis, bit):
    size = lax.axis_size(axis)
    return lax.ppermute(value, axis, [(i, i ^ bit) for i in range(size)])


def halve(value, dim, axis, bit):
    mine = (lax.axis_index(axis) // bit) % 2
    keep = lax.dynamic_index_in_dim(value, mine, dim, keepdims=False)
    send = lax.dynamic_index_in_dim(value, 1 - mine, dim, keepdims=False)
    received = flip(send.astype(jnp.bfloat16), axis, bit)
    return (keep.astype(jnp.float32) + received.astype(jnp.float32)).astype(jnp.bfloat16)


def halve_start(value, dim, axis, bit):
    mine = (lax.axis_index(axis) // bit) % 2
    keep = lax.dynamic_index_in_dim(value, mine, dim, keepdims=False)
    send = lax.dynamic_index_in_dim(value, 1 - mine, dim, keepdims=False)
    return keep, flip(send, axis, bit)


def halve_end(pair):
    return (pair[0].astype(jnp.float32) + pair[1].astype(jnp.float32)).astype(jnp.bfloat16)


def double(value, axis, bit):
    mine = (lax.axis_index(axis) // bit) % 2
    other = flip(value, axis, bit)
    return jnp.where(mine == 0, jnp.stack([value, other]), jnp.stack([other, value]))


def bits_of(size):
    bits = []
    bit = 1
    while bit < size:
        bits.append(bit)
        bit *= 2
    return bits


def with_partner(own):
    return jnp.concatenate([own, flip(own, "team", 1)], axis=0)


def feed_grads_kernel(core_ref, own_ref, got_ref, up_ref, down_ref, *, spots):
    unit = own_ref.shape[2]
    half = len(spots) // 2

    def write(piece_ref, places):
        for index, spot in enumerate(places):
            where = slice(spot * unit, (spot + 1) * unit)
            up_ref[:, where] = jnp.transpose(piece_ref[index, 0].astype(jnp.float32))
            down_ref[where, :] = piece_ref[index, 1].astype(jnp.float32)

    def both(core):
        write(own_ref, spots[core * half : (core + 1) * half])
        write(got_ref, spots[(1 - core) * half : (2 - core) * half])

    for core in range(2):
        pl.when(core_ref[0] == core)(functools.partial(both, core))


def feed_grads_out(core, own, got, copies):
    count, _, unit, depth = own.shape
    merge = max(1, 128 // unit)
    if merge > 1:
        own, got = (
            jnp.transpose(
                one.reshape(count // merge, merge, 2, unit, depth), (0, 2, 1, 3, 4)
            ).reshape(count // merge, 2, merge * unit, depth)
            for one in (own, got)
        )
    count, _, unit, depth = own.shape
    each = copies // merge
    spots = []
    for step in range(2 * count):
        half, side, place = place_in_group(step, each)
        spots.append((side * 2 + half) * each + place)
    take = depth // 4
    piece = pl.BlockSpec((count, 2, unit, take), lambda step, core: (0, 0, 0, step))
    return pl.pallas_call(
        functools.partial(feed_grads_kernel, spots=spots),
        grid_spec=pltpu.PrefetchScalarGridSpec(
            num_scalar_prefetch=1,
            grid=(4,),
            in_specs=[piece, piece],
            out_specs=[
                pl.BlockSpec((take, 2 * count * unit), lambda step, core: (step, 0)),
                pl.BlockSpec((2 * count * unit, take), lambda step, core: (0, step)),
            ],
        ),
        out_shape=[
            jax.ShapeDtypeStruct((depth, 2 * count * unit), jnp.float32),
            jax.ShapeDtypeStruct((2 * count * unit, depth), jnp.float32),
        ],
        compiler_params=pltpu.CompilerParams(dimension_semantics=("arbitrary",)),
        cost_estimate=LIGHT,
        name="feed_grads_out",
    )(core, own, got)


def attention_grads_kernel(core_ref, own_ref, got_ref, qkv_ref, out_ref, *, spots):
    group = own_ref.shape[0]
    rows, width = qkv_ref.shape[1] // group, qkv_ref.shape[2]
    few = out_ref.shape[0] // group

    def place_all(piece_ref, core):
        for item in range(group):
            spot = spots[core * group + item] - core * group
            for slot in range(3):
                qkv_ref[slot, spot * rows : (spot + 1) * rows, :] = piece_ref[
                    item, slot * rows : (slot + 1) * rows, :
                ].astype(jnp.float32)
            for place in range(out_ref.shape[1] // width):
                start = 3 * rows + place * few
                out_ref[
                    spot * few : (spot + 1) * few, place * width : (place + 1) * width
                ] = piece_ref[item, start : start + few, :].astype(jnp.float32)

    step = pl.program_id(0)
    for core in range(2):
        mine = (step == core) & (core_ref[0] == core)
        other = (step == core) & (core_ref[0] != core)
        pl.when(mine)(functools.partial(place_all, own_ref, core))
        pl.when(other)(functools.partial(place_all, got_ref, core))


def attention_grads_out(core, own, got, depth, head_width):
    half = own.shape[0]
    copies = half // 2
    spots = []
    for step in range(2 * half):
        side_core, side, place = place_in_group(step, copies)
        spots.append((side_core * 2 + side) * copies + place)
    whole = pl.BlockSpec(own.shape, lambda step, core: (0, 0, 0))
    return pl.pallas_call(
        functools.partial(attention_grads_kernel, spots=spots),
        grid_spec=pltpu.PrefetchScalarGridSpec(
            num_scalar_prefetch=1,
            grid=(2,),
            in_specs=[whole, whole],
            out_specs=[
                pl.BlockSpec((3, depth // 2, head_width), lambda step, core: (0, step, 0)),
                pl.BlockSpec((head_width // 2, depth), lambda step, core: (step, 0)),
            ],
        ),
        out_shape=[
            jax.ShapeDtypeStruct((3, depth, head_width), jnp.float32),
            jax.ShapeDtypeStruct((head_width, depth), jnp.float32),
        ],
        compiler_params=pltpu.CompilerParams(dimension_semantics=("arbitrary",)),
        cost_estimate=HEAVY,
        name="attention_grads_out",
    )(core, own, got)


def qkv_grad_kernel(core_ref, rows_ref, grad_a, grad_b, send_ref, keep_ref):
    width = grad_a.shape[1]
    both = [dot_tn(rows_ref[...], grad[...]).astype(jnp.bfloat16) for grad in (grad_a, grad_b)]

    @pl.when(pl.program_id(0) == 0)
    def _():
        send_ref[:, 0:width] = both[0]
        send_ref[:, width:] = both[1]

    @pl.when(pl.program_id(0) == 1)
    def _():
        keep_ref[:, 0:width] = both[0]
        keep_ref[:, width:] = both[1]


def qkv_weight_grad(core, rows, grads):
    length, depth = rows.shape
    width = grads[0].shape[1]
    half = depth // 2
    whole = pl.BlockSpec((length, width), lambda step, core: (0, 0))
    out = pl.BlockSpec((half, 2 * width), lambda step, core: (0, 0))
    return pl.pallas_call(
        qkv_grad_kernel,
        grid_spec=pltpu.PrefetchScalarGridSpec(
            num_scalar_prefetch=1,
            grid=(2,),
            in_specs=[
                pl.BlockSpec((length, half), lambda step, core: (0, 1 - core[0] ^ step)),
                whole, whole,
            ],
            out_specs=[out, out],
        ),
        out_shape=[jax.ShapeDtypeStruct((half, 2 * width), jnp.bfloat16)] * 2,
        compiler_params=pltpu.CompilerParams(dimension_semantics=("arbitrary",)),
        cost_estimate=SMALL,
        name="qkv_weight_grad",
    )(core, rows, *grads)


def first_norm_kernel(token_ref, line_ref, out_ref):
    unit, _ = normalize(token_ref[...].astype(jnp.float32))
    out_ref[...] = (unit * line_ref[0:1, :] + line_ref[1:2, :]).astype(jnp.bfloat16)


def first_norm(tokens, lines):
    return pl.pallas_call(
        first_norm_kernel,
        out_shape=jax.ShapeDtypeStruct(tokens.shape, jnp.bfloat16),
        cost_estimate=LIGHT,
        name="first_norm",
    )(tokens, lines)


def token_grads_kernel(grad_ref, hidden_ref, token_ref, line_ref, out_ref):
    unit, inverse = normalize(token_ref[...].astype(jnp.float32))
    grad = normalize_backward(grad_ref[...].astype(jnp.float32), line_ref[...], unit, inverse)
    out_ref[...] = (hidden_ref[...] + grad).astype(jnp.bfloat16)


def token_grads(grad, hidden, tokens, line):
    return pl.pallas_call(
        token_grads_kernel,
        out_shape=jax.ShapeDtypeStruct(tokens.shape, jnp.bfloat16),
        compiler_params=pltpu.CompilerParams(vmem_limit_bytes=32 * 1024 * 1024),
        cost_estimate=LIGHT,
        name="token_grads",
    )(grad, hidden, tokens, line)


def branch_kernel(*refs, count):
    pieces = refs[:count]
    weight_ref, token_ref, line_ref, hidden_ref, second_ref, left_ref = refs[count:]
    left = jnp.concatenate([piece[...] for piece in pieces], axis=1)
    left_ref[...] = left
    hidden = token_ref[...].astype(jnp.float32) + dot_nn(left, weight_ref[...])
    unit, _ = normalize(hidden)
    hidden_ref[...] = hidden
    second_ref[...] = (unit * line_ref[0:1, :] + line_ref[1:2, :]).astype(jnp.bfloat16)


def branch_and_norm(pieces, weights, tokens, lines):
    rows, depth = tokens.shape
    return pl.pallas_call(
        functools.partial(branch_kernel, count=len(pieces)),
        out_shape=[
            jax.ShapeDtypeStruct((rows, depth), jnp.float32),
            jax.ShapeDtypeStruct((rows, depth), jnp.bfloat16),
            jax.ShapeDtypeStruct((rows, weights.shape[0]), jnp.bfloat16),
        ],
        compiler_params=pltpu.CompilerParams(vmem_limit_bytes=32 * 1024 * 1024),
        cost_estimate=LIGHT,
        name="branch_and_norm",
    )(*pieces, weights, tokens, lines)


def row_grads_kernel(
    own_ref, core_ref, across_ref, grad_ref, hidden_ref, weight_ref, line_ref,
    total_ref, branch_ref, *refs,
):
    block_refs, sum_ref = refs[:-1], refs[-1]
    second = (
        own_ref[...].astype(jnp.float32) + core_ref[...].astype(jnp.float32)
        + across_ref[...].astype(jnp.float32)
    )
    grad = grad_ref[...].astype(jnp.float32)
    unit, inverse = normalize(hidden_ref[...])
    total = grad + normalize_backward(second, line_ref[0:1, :], unit, inverse)
    branch = total.astype(jnp.bfloat16)
    total_ref[...] = total
    branch_ref[...] = branch
    width = block_refs[0].shape[1]
    for index, block_ref in enumerate(block_refs):
        block_ref[...] = dot_nt(
            branch, weight_ref[index * width : (index + 1) * width, :]
        ).astype(jnp.bfloat16)
    sums = [jnp.sum(one, axis=0, keepdims=True) for one in (second * unit, second, grad)]
    lines = jnp.concatenate(sums + [jnp.zeros((5, sums[0].shape[1]), jnp.float32)])

    sum_ref[...] = lines


def row_grads(backs, grad, hidden, weights, lines, parts):
    rows, depth = hidden.shape
    width = weights.shape[0] // parts
    return pl.pallas_call(
        row_grads_kernel,
        out_shape=[
            jax.ShapeDtypeStruct((rows, depth), jnp.float32),
            jax.ShapeDtypeStruct((rows, depth), jnp.bfloat16),
        ]
        + [jax.ShapeDtypeStruct((rows, width), jnp.bfloat16)] * parts
        + [jax.ShapeDtypeStruct((8, depth), jnp.float32)],
        compiler_params=pltpu.CompilerParams(vmem_limit_bytes=40 * 1024 * 1024),
        cost_estimate=LIGHT,
        name="row_grads",
    )(*backs, grad, hidden, weights, lines)


def out_grad_kernel(core_ref, left_ref, right_ref, keep_ref, send_ref):
    parts, half, _ = keep_ref.shape

    def columns(core):
        return jnp.concatenate(
            [
                left_ref[:, pl.ds(pl.multiple_of((2 * part + core) * half, 128), half)]
                for part in range(parts)
            ],
            axis=1,
        )

    for out_ref, core in ((keep_ref, core_ref[0]), (send_ref, 1 - core_ref[0])):
        grad = dot_tn(columns(core), right_ref[...]).astype(jnp.bfloat16)
        for part in range(parts):
            out_ref[part] = grad[part * half : (part + 1) * half]


def out_weight_grad(core, own_rows, grads, parts):
    rows, depth = grads.shape
    half = own_rows.shape[1] // parts // 2
    whole = pl.BlockSpec((rows, depth), lambda step, core: (0, 0))
    out = pl.BlockSpec((parts, half, depth), lambda step, core: (0, 0, 0))
    return pl.pallas_call(
        out_grad_kernel,
        grid_spec=pltpu.PrefetchScalarGridSpec(
            num_scalar_prefetch=1,
            grid=(1,),
            in_specs=[
                pl.BlockSpec(own_rows.shape, lambda step, core: (0, 0)), whole,
            ],
            out_specs=[out, out],
        ),
        out_shape=[jax.ShapeDtypeStruct((parts, half, depth), jnp.bfloat16)] * 2,
        compiler_params=pltpu.CompilerParams(dimension_semantics=("arbitrary",)),
        cost_estimate=COVER,
        name="out_weight_grad",
    )(core, own_rows, grads)


def normalize(inputs):
    center = inputs - jnp.mean(inputs, axis=-1, keepdims=True)
    spread = jnp.mean(center * center, axis=-1, keepdims=True)
    inverse = lax.rsqrt(spread + EPSILON)
    return center * inverse, inverse


def normalize_backward(grad, gain, unit, inverse):
    scaled_grad = grad * gain
    middle = jnp.mean(scaled_grad, axis=-1, keepdims=True)
    along = jnp.mean(scaled_grad * unit, axis=-1, keepdims=True)
    return (scaled_grad - middle - unit * along) * inverse


def dot_tn(left, right):
    return lax.dot_general(
        left, right, (((0,), (0,)), ((), ())), preferred_element_type=jnp.float32
    )


def copies_of(value, size):
    halves = [value[None]]
    for bit in bits_of(size):
        value = halves[0] if len(halves) == 1 else jnp.concatenate(halves)
        halves = [value, flip(value, "copy", bit)]
    return halves


def untangle(value, axis, index, size):
    for bit in bits_of(size):
        shape = value.shape
        split = value.reshape(
            shape[:axis] + (size // (2 * bit), 2, bit) + shape[axis + 1 :]
        )
        split = jnp.where((index // bit) % 2 == 1, jnp.flip(split, axis + 1), split)
        value = split.reshape(shape)
    return value


def orders(copies):
    first = [("copy", bit) for bit in bits_of(copies)] + [("team", 2)]
    return first, first[::-1] if copies == 2 else first


def spread_end(value, got, mine):
    return jnp.where(mine == 0, jnp.stack([value, got]), jnp.stack([got, value]))


def spread_group(value, step, copies):
    return spread_end(*spread_start(value, step, copies))


def spread_start(value, step, copies):
    choices = [order[step] for order in orders(copies)]
    moves = []
    for place in range(copies * TEAM):
        axis, bit = choices[place % 2]
        moves.append((place, place ^ (bit if axis == "team" else bit * TEAM)))
    got = lax.ppermute(value, ("copy", "team"), moves)
    mine = [(lax.axis_index(axis) // bit) % 2 for axis, bit in choices]
    return value, got, jnp.where(lax.axis_index("team") % 2 == 0, mine[0], mine[1])


def place_in_group(step, copies):
    core, index = step // (2 * copies), step % (2 * copies)
    if copies != 2:
        return core, index // copies, index % copies
    outer, inner = index // 2, index % 2
    return core, outer + core * (inner - outer), inner + core * (outer - inner)


def exchange(blocks):
    return [blocks[0]] + [flip(blocks[k], "mp", k) for k in range(1, len(blocks))]


def cotangent_kernel(grad_a, grad_b, weight_a, weight_b, normed_ref, line_ref, out_ref, sum_ref):
    grad = sum(
        dot_nt(grad_ref[...], jnp.concatenate([weight_ref[slot] for slot in range(3)], axis=1))
        for grad_ref, weight_ref in ((grad_a, weight_a), (grad_b, weight_b))
    )
    unit = (normed_ref[...].astype(jnp.float32) - line_ref[0:1, :]) * line_ref[1:2, :]
    out_ref[...] = grad.astype(jnp.bfloat16)
    rows, depth = grad.shape
    both = jnp.concatenate(
        [
            jnp.sum((grad * unit).reshape(rows // 8, 8, depth), axis=0),
            jnp.sum(grad.reshape(rows // 8, 8, depth), axis=0),
        ],
        axis=0,
    )

    @pl.when(pl.program_id(0) == 0)
    def _():
        sum_ref[...] = both

    @pl.when(pl.program_id(0) > 0)
    def _():
        sum_ref[...] += both


def input_cotangent(grads, weights, normed, lines):
    length, width = grads[0].shape
    depth = weights.shape[1]
    row = pl.BlockSpec((BLK, width), lambda step: (step, 0))
    part_a = pl.BlockSpec((3, depth, width // 3), lambda step: (0, 0, 0))
    part_b = pl.BlockSpec((3, depth, width // 3), lambda step: (0, 0, 1))
    return pl.pallas_call(
        cotangent_kernel,
        grid=(length // BLK,),
        in_specs=[
            row, row, part_a, part_b,
            pl.BlockSpec((BLK, depth), lambda step: (step, 0)),
            pl.BlockSpec((2, depth), lambda step: (0, 0)),
        ],
        out_specs=[
            pl.BlockSpec((BLK, depth), lambda step: (step, 0)),
            pl.BlockSpec((16, depth), lambda step: (0, 0)),
        ],
        out_shape=[
            jax.ShapeDtypeStruct((length, depth), jnp.bfloat16),
            jax.ShapeDtypeStruct((16, depth), jnp.float32),
        ],
        compiler_params=pltpu.CompilerParams(dimension_semantics=("arbitrary",)),
        cost_estimate=SMALL,
        name="input_cotangent",
    )(*grads, weights, weights, normed, lines)


def feed_kernel(*refs, unit, count):
    weight_refs = refs[:count]
    (
        bias_ref, second_ref, grad_ref,
        act_ref, pre_ref, back_own, back_other, out_own, out_other, sum_ref,
    ) = refs[count:]
    w_up, w_down = (
        jnp.concatenate(
            [
                ref[:, start : start + unit, :].reshape(ref.shape[0] * unit, ref.shape[2])
                for ref in weight_refs
            ]
        )
        for start in (0, unit)
    )
    pre = dot_nt(second_ref[...], w_up) + bias_ref[...]
    grad_act = dot_nt(grad_ref[...], w_down)
    cdf = 0.5 + 0.5 * lax.erf(pre * 0.7071067811865476)
    pdf = jnp.exp(pre * pre * -0.5) * 0.3989422804014327
    active = (pre * cdf).astype(jnp.bfloat16)
    grad_pre = ((cdf + pre * pdf) * grad_act).astype(jnp.bfloat16)
    act_ref[...] = active
    pre_ref[...] = grad_pre
    line = jnp.sum(grad_pre.astype(jnp.float32), axis=0, keepdims=True)
    back = dot_nn(grad_pre, w_up).astype(jnp.bfloat16)
    out = dot_nn(active, w_down).astype(jnp.bfloat16)

    step = pl.program_id(0)
    middle = pl.num_programs(0) // 2

    @pl.when(step < middle)
    def _():
        back_own[...] = back
        out_own[...] = out

    @pl.when(step >= middle)
    def _():
        back_other[...] = back
        out_other[...] = out

    @pl.when(step == 0)
    def _():
        sum_ref[...] = line

    @pl.when(step > 0)
    def _():
        sum_ref[...] += line


def feed_forward(weights, bias_row, second, grad, unit):
    depth = weights[0].shape[2]
    rows = second.shape[0]
    width = unit * sum(one.shape[0] for one in weights)
    steps = FEED_STEPS
    take = rows // steps
    middle = steps // 2
    row = pl.BlockSpec((take, depth), lambda step: (step, 0))
    near = pl.BlockSpec((take, depth), lambda step: (jnp.minimum(step, middle - 1), 0))
    far = pl.BlockSpec((take, depth), lambda step: (jnp.maximum(step - middle, 0), 0))
    wide = pl.BlockSpec((take, width), lambda step: (step, 0))
    line = pl.BlockSpec((1, width), lambda step: (0, 0))
    part = jax.ShapeDtypeStruct((rows // 2, depth), jnp.bfloat16)
    return pl.pallas_call(
        functools.partial(feed_kernel, unit=unit, count=len(weights)),
        grid=(steps,),
        in_specs=[pl.BlockSpec(each.shape, lambda step: (0, 0, 0)) for each in weights]
        + [line, row, row],
        out_specs=[wide, wide, near, far, near, far, line],
        out_shape=[
            jax.ShapeDtypeStruct((rows, width), jnp.bfloat16),
            jax.ShapeDtypeStruct((rows, width), jnp.bfloat16),
            part, part, part, part,
            jax.ShapeDtypeStruct((1, width), jnp.float32),
        ],
        compiler_params=pltpu.CompilerParams(
            dimension_semantics=("arbitrary",), vmem_limit_bytes=48 * 1024 * 1024
        ),
        cost_estimate=LIGHT,
        name="feed_forward",
    )(*weights, bias_row, second, grad)


def weight_grad_kernel(
    part_ref, act_a, act_b, pre_a, pre_b, second_a, second_b, grad_a, grad_b, *out_refs
):
    _, places, _, unit, _ = out_refs[0].shape
    up = dot_tn(pre_a[...], second_a[...]) + dot_tn(pre_b[...], second_b[...])
    down = dot_tn(act_a[...], grad_a[...]) + dot_tn(act_b[...], grad_b[...])
    for index, out_ref in enumerate(out_refs):
        for place in range(places):
            start = (index * places + place) * unit
            out_ref[0, place, 0] = up[start : start + unit].astype(jnp.bfloat16)
            out_ref[0, place, 1] = down[start : start + unit].astype(jnp.bfloat16)


def weight_grads(part, acts, pres, seconds, grads, parts, copies):
    rows, width = acts[0].shape
    depth = seconds[0].shape[1]
    unit = width // (parts * copies)
    count = 2 if copies > 1 else 1
    places = copies // count
    column = pl.BlockSpec((rows, width // parts), lambda step, part: (0, step))
    whole = pl.BlockSpec((rows, depth), lambda step, part: (0, 0))
    out = pl.BlockSpec(
        (1, places, 2, unit, depth), lambda step, part: (part[0] ^ step, 0, 0, 0, 0)
    )
    return pl.pallas_call(
        weight_grad_kernel,
        grid_spec=pltpu.PrefetchScalarGridSpec(
            num_scalar_prefetch=1,
            grid=(parts,),
            in_specs=[column] * 4 + [whole] * 4,
            out_specs=[out] * count,
        ),
        out_shape=[jax.ShapeDtypeStruct((parts, places, 2, unit, depth), jnp.bfloat16)] * count,
        compiler_params=pltpu.CompilerParams(
            dimension_semantics=("arbitrary",), vmem_limit_bytes=56 * 1024 * 1024
        ),
        cost_estimate=HEAVY,
        name="weight_grads",
    )(part, *acts, *pres, *seconds, *grads)


def fold_copies(halves, got):
    if len(halves) == 1:
        return halves[0]
    value = halve_end((halves[0], got))
    while value.shape[1] > 1:
        half = value.shape[1] // 2
        value = halve_end((value[:, :half], flip(value[:, half:], "copy", half)))
    return value


def sync(*values):
    return lax.optimization_barrier(values)


def body(
    tokens, seg_ids, bucket_of, ln1_gain, ln1_bias, w_qkv, rel_table, w_out,
    ln2_gain, ln2_bias, w_up, up_bias, w_down, down_bias, out_grad,
):
    low = jnp.bfloat16
    wide = jnp.float32
    copies = lax.axis_size("copy")
    parts = lax.axis_size("mp")
    copy = lax.axis_index("copy")
    member = lax.axis_index("team")
    part = lax.axis_index("mp")
    core = member % 2
    rows, depth = tokens.shape
    head_width = w_out.shape[0]
    pair_width = head_width // 2
    pairs = 2
    team_units = w_up.shape[1] // TEAM
    unit = team_units // copies
    out_rows = head_width // (2 * copies)
    seg_row = seg_ids[0]
    to_right = [(i, i + 1) for i in range(parts - 1)]
    to_left = [(i + 1, i) for i in range(parts - 1)]

    def relay(right, left, step):
        return (
            lax.ppermute(right, "mp", to_right[step - 1 :]),
            lax.ppermute(left, "mp", to_left[: parts - step]),
        )

    def corner_of(right1, left1, right3, left3):
        return jnp.where(
            (part == 0) | (part == parts - 1), right3 + left3, jnp.where(part == 1, left1, right1)
        )

    normed = lax.all_gather(
        first_norm(tokens, jnp.stack([ln1_gain, ln1_bias])), "mp", axis=0, tiled=True
    )

    def own_units(place):
        first = member * team_units + (copy ^ place) * unit
        return jnp.concatenate(
            [
                jnp.transpose(lax.dynamic_slice_in_dim(w_up, first, unit, 1)),
                lax.dynamic_slice_in_dim(w_down, first, unit, 0),
            ]
        )

    own_slot = jnp.stack([own_units(place) for place in range(copies)])
    out_own = lax.dynamic_slice_in_dim(w_out, (copy * 2 + core) * out_rows, out_rows, 0)
    own_biases = [
        lax.dynamic_slice_in_dim(up_bias, member * team_units + (copy ^ place) * unit, unit, 0)
        for place in range(copies)
    ]
    high = lax.reduce_precision(own_biases[0], 8, 7)
    middle = lax.reduce_precision(own_biases[0] - high, 8, 7)
    bias_lines = jnp.stack([high, middle, own_biases[0] - high - middle]).astype(low)
    bias_lines = jnp.pad(bias_lines, ((0, 5), (0, depth - unit)))
    piece = jnp.concatenate([own_slot[0], out_own, bias_lines])
    w_right1, w_left1 = relay(piece, piece, 1)
    w_right2, w_left2 = relay(w_right1, w_left1, 2)
    beside = copies_of(jnp.where(part % 2 == 0, w_left1, w_right1), copies)
    grad_across = flip(out_grad, "team", 2)
    grad_near = with_partner(out_grad)
    grad_far = with_partner(grad_across)
    hot, by_distance = distance_bias(rel_table, bucket_of)
    forward_bias, backward_bias = near_tables(by_distance)
    cut = jnp.sum((seg_row == seg_row[0]).astype(jnp.int32)).reshape(1)
    normed = after(
        normed, grad_near, grad_far, own_slot, forward_bias, backward_bias, cut,
        w_right2, w_left2, beside[1],
    )

    def whole_out(halves):
        mine = jnp.concatenate([half[:, 2 * unit : 2 * unit + out_rows] for half in halves])
        mine = untangle(mine, 0, copy, copies)
        other = flip(mine, "team", 1)
        return jnp.where(
            core == 0, jnp.stack([mine, other], axis=1), jnp.stack([other, mine], axis=1)
        ).reshape(head_width, depth)

    w_right2, w_left2 = after(w_right2, normed), after(w_left2, normed)
    w_right3, w_left3 = relay(w_right2, w_left2, 3)
    across = copies_of(w_right2 + w_left2, copies)
    *results, = attention_forward(cut, after(normed, across[0]), w_qkv, forward_bias)
    projected, attended, logs = results[0:2], results[2], results[3:5]
    w_right3, w_left3, across[1], attended = sync(w_right3, w_left3, across[1], attended)
    corner = copies_of(corner_of(w_right1, w_left1, w_right3, w_left3), copies)
    stack = attended.reshape(parts, rows, head_width)
    moved = exchange(
        [lax.dynamic_index_in_dim(stack, part ^ k, 0, keepdims=False) for k in range(parts)]
    )
    w_out_full = jnp.concatenate(
        [w_out] + [whole_out(halves) for halves in (beside, across, corner)]
    )
    weights = [own_slot] + beside + across + corner
    bias_row = jnp.concatenate(
        own_biases
        + [
            jnp.sum(half[:, -8:-5, :unit].astype(wide), axis=1).reshape(-1)
            for half in weights[1:]
        ]
    )[None]

    hidden_in, second, own_rows = branch_and_norm(
        moved, w_out_full, tokens, jnp.stack([ln2_gain, ln2_bias])
    )
    second_across = flip(second, "team", 2)
    second_near = with_partner(second)
    act_near, pre_near, back_own, back_core, feed_own, feed_core, sums_near = feed_forward(
        weights, bias_row, second_near, grad_near, unit
    )
    second_across = after(second_across, back_own)
    back_core = flip(back_core, "team", 1)
    second_far = with_partner(second_across)
    act_far, pre_far, back_side, back_corner, feed_side, feed_corner, sums_far = feed_forward(
        weights, bias_row, second_far, grad_far, unit
    )
    onward = (
        back_side.astype(wide) + flip(back_corner, "team", 1).astype(wide)
    ).astype(low)
    back_across = flip(onward, "team", 2)
    feed_stack = jnp.stack([after(feed_corner, onward), feed_core])
    feed_beside = flip(feed_stack, "team", 1)
    ff_grads = weight_grads(
        part.reshape(1), (act_near, after(act_far, onward, feed_stack)), (pre_near, pre_far),
        (second_near, second_far), (grad_near, grad_far), parts, copies,
    )
    ff_got = flip(ff_grads[-1], "copy", max(1, copies // 2)) if copies > 1 else ff_grads[0]
    back_across = after(back_across, ff_grads[0])
    grad_hidden, grad_branch, *grad_rows = row_grads(
        (back_own, back_core, back_across), out_grad, hidden_in, w_out_full, ln2_gain[None], parts
    )
    row_sums = grad_rows.pop()
    received = exchange(grad_rows)
    grad_branch, feed_beside, *received = sync(grad_branch, feed_beside, *received)
    wout_keep, wout_send = out_weight_grad(core.reshape(1), own_rows, grad_branch, parts)
    wout_got = flip(wout_send, "team", 1)
    feed_sum = (feed_side.astype(wide) + feed_beside[0].astype(wide)).astype(low)
    natural = jnp.zeros((parts, rows, head_width), low)
    for k in range(parts):
        natural = lax.dynamic_update_index_in_dim(natural, received[k], part ^ k, 0)
    wout_grad = halve_end((wout_keep, wout_got)).reshape(parts, 2, copies, -1, depth)
    side_bit = (member // 2) % 2
    wout_keep = lax.dynamic_index_in_dim(wout_grad, side_bit, 1, keepdims=False)
    wout_send = lax.dynamic_index_in_dim(wout_grad, 1 - side_bit, 1, keepdims=False)
    ff_got, natural, feed_sum, wout_keep, wout_send = sync(
        ff_got, natural, feed_sum, wout_keep, wout_send
    )
    ff_value = fold_copies(ff_grads, ff_got).reshape(parts, 2 * unit, depth)
    ff_piece = lax.psum_scatter(ff_value, "mp", scatter_dimension=0, tiled=False)
    wout_pair = (wout_keep, flip(wout_send, "team", 2))
    feed_across = flip(feed_sum, "team", 2)
    grad_att = natural.reshape(parts * rows, head_width)
    first_grads, last_grads, table_sums = attention_backward(
        cut, projected, grad_att, attended, logs, backward_bias
    )
    first_grads, last_grads, wout_last, feed_across = sync(
        first_grads, last_grads, wout_pair[1], feed_across
    )
    dqkv = [first_grads, last_grads]
    wout_grad = halve_end((wout_pair[0], wout_last))
    for bit in reversed(bits_of(copies)):
        wout_grad = wout_grad.reshape((parts, 2, -1) + wout_grad.shape[2:])
        wout_pair = halve_start(wout_grad, 1, "copy", bit)
        if bit > 1:
            wout_grad = halve_end(wout_pair)
    wout_keep, wout_last = wout_pair
    qkv_send, qkv_keep = qkv_weight_grad(
        core.reshape(1), normed, [after(dqkv[0], wout_keep), dqkv[1]]
    )
    qkv_keep, qkv_send, dqkv[0] = sync(qkv_keep, qkv_send, dqkv[0])
    qkv_got = flip(qkv_send, "team", 1)
    running, line_sums = input_cotangent(
        dqkv, w_qkv, normed,
        jnp.stack([after(ln1_bias, dqkv[0]), 1.0 / ln1_gain]),
    )
    grad_first = lax.psum_scatter(running, "mp", scatter_dimension=0, tiled=True)
    qkv_got, running, ff_piece, wout_last = sync(qkv_got, running, ff_piece, wout_last)
    wout_grad = halve_end((wout_keep, wout_last)).reshape(parts, -1, depth)
    wout_blocks = exchange([wout_grad[k] for k in range(parts)])
    qkv_grad = halve_end((qkv_keep, qkv_got))
    table_sums = after(table_sums, running)
    table_line = table_gradient(
        hot, table_sums[: table_sums.shape[0] // 2], table_sums[table_sums.shape[0] // 2 :]
    ).reshape(1, -1)
    table_all = lax.dynamic_update_slice_in_dim(
        jnp.zeros((parts, table_line.shape[1]), wide), table_line, part, 0
    )
    sums = (after(sums_near, running) + sums_far).reshape(parts, copies, unit)
    sums = untangle(untangle(sums, 0, part, parts), 1, copy, copies)
    up_sums = lax.dynamic_update_slice_in_dim(
        jnp.zeros((parts, TEAM * team_units), wide), sums.reshape(parts, team_units),
        member * team_units, 1,
    )
    early_lines = jnp.concatenate([row_sums[0:3].reshape(-1), up_sums.reshape(-1)])
    small = jnp.concatenate(
        [
            jnp.sum(line_sums[0:8], axis=0), jnp.sum(line_sums[8:16], axis=0),
            early_lines, table_all.reshape(-1),
        ]
    )
    small = jnp.pad(small, (0, -small.shape[0] % 1024)).reshape(-1, 1024)

    qkv_pair = halve_start(qkv_grad.reshape(2, copies, -1, qkv_grad.shape[1]), 0, "team", 2)
    ff_all = spread_group(ff_piece, 0, copies)
    small = small + flip(small, "team", 1)
    small_got = flip(small, "team", 2)
    feed_own = feed_own.astype(wide) + feed_beside[1].astype(wide) + feed_across.astype(wide)
    layer_out = (hidden_in + feed_own + down_bias).astype(low)
    qkv_last, ff_all, small_got, layer_out = sync(qkv_pair[1], ff_all, small_got, layer_out)
    qkv_grad = halve_end((qkv_pair[0], qkv_last))
    small = small + small_got

    for bit in reversed(bits_of(copies)):
        qkv_pair = halve_start(qkv_grad.reshape((2, -1) + qkv_grad.shape[1:]), 0, "copy", bit)
        if bit > 1:
            qkv_grad = halve_end(qkv_pair)
    if copies == 1:
        qkv_pair = (qkv_grad, jnp.zeros_like(qkv_grad))
    for step in range(1, len(orders(copies)[0]) - 1):
        ff_all = spread_group(ff_all, step, copies)
    ff_own, ff_got, ff_mine = spread_start(ff_all, len(orders(copies)[0]) - 1, copies)
    for bit in bits_of(copies)[1:]:
        small = small + flip(small, "copy", bit)
    small_got = flip(small, "copy", 1) if copies > 1 else jnp.zeros_like(small)
    results = sync(qkv_pair[1], small_got, small, ff_got, *wout_blocks)
    qkv_last, small_got, small, ff_got = results[:4]
    ff_all = spread_end(ff_own, ff_got, ff_mine)
    small = small + small_got
    qkv_grad = halve_end((qkv_pair[0], qkv_last))
    wout_grad = sum(one.astype(wide) for one in results[4:]).astype(low)
    qkv_grad = qkv_grad.reshape(-1, 3 * head_width)
    columns = [
        jnp.concatenate(
            [
                qkv_grad[:, (3 * pair + slot) * pair_width : (3 * pair + slot + 1) * pair_width]
                for pair in range(pairs)
            ],
            axis=1,
        )
        for slot in range(3)
    ] + [wout_grad[:, start : start + head_width] for start in range(0, depth, head_width)]
    flat = jnp.concatenate(columns)
    ff_got = flip(ff_all, "team", 1)
    flat = spread_group(flat, 0, copies)
    flat, ff_got = sync(flat, ff_got)

    for step in range(1, len(orders(copies)[0])):
        flat = spread_group(flat, step, copies)
    grad_up, grad_down = feed_grads_out(
        core.reshape(1), ff_all.reshape(2 * copies, 2, unit, depth),
        ff_got.reshape(2 * copies, 2, unit, depth), copies,
    )
    flat, grad_up, grad_down = sync(flat, grad_up, grad_down)

    flat, small, grad_first = sync(flat, small, grad_first)
    flat_got = flip(flat, "team", 1)
    small_got = flip(small, "mp", 1)
    flat_got, small_got = sync(flat_got, small_got)
    small = small + small_got
    small_got = flip(small, "mp", 2)
    grad_qkv, grad_wout = attention_grads_out(
        core.reshape(1), flat.reshape(2 * copies, -1, head_width),
        flat_got.reshape(2 * copies, -1, head_width), depth, head_width,
    )

    grad_tokens = token_grads(grad_first, grad_hidden, tokens, ln1_gain[None])
    small_got, grad_qkv, grad_wout, grad_tokens = sync(
        small_got, grad_qkv, grad_wout, grad_tokens
    )
    small = small + small_got
    small = small.reshape(-1)
    lines = [small[index * depth : (index + 1) * depth] for index in range(5)]
    start = 5 * depth
    count = TEAM * team_units
    up_sums = small[start : start + parts * count].reshape(parts, count)
    grad_up_bias = lax.dynamic_index_in_dim(up_sums, part, 0, keepdims=False)
    start = start + parts * count
    count = rel_table.size
    table_all = small[start : start + parts * count].reshape(parts, count)
    grad_table = lax.dynamic_index_in_dim(table_all, part, 0, keepdims=False).reshape(
        rel_table.shape
    )

    return (
        layer_out, grad_tokens, lines[0], lines[1], grad_qkv, grad_table, grad_wout,
        lines[2], lines[3], grad_up, grad_up_bias, grad_down, lines[4],
    )


def solution(mesh):
    groups, parts = mesh.shape["dp"], mesh.shape["mp"]
    split = Mesh(
        mesh.devices.reshape(groups // TEAM, TEAM, parts), ("copy", "team", "mp")
    )
    every = ("copy", "team", "mp")
    return jax.shard_map(
        body,
        mesh=split,
        in_specs=(
            P(every, None), P(("copy", "team"), None), P(), P(), P(), P(None, None, "mp"),
            P(None, "mp"), P("mp", None), P(), P(), P(None, "mp"), P("mp"), P("mp", None), P(),
            P(every, None),
        ),
        out_specs=(
            P(every, None), P(every, None), P(), P(), P(None, None, "mp"), P(None, "mp"),
            P("mp", None), P(), P(), P(None, "mp"), P("mp"), P("mp", None), P(),
        ),
        check_vma=False,
    )
```

```python
import functools

import jax
import jax.numpy as jnp
from jax import lax
from jax.experimental import pallas as pl
from jax.experimental.pallas import tpu as pltpu
from jax.sharding import Mesh, PartitionSpec as P

EPSILON = 1e-05
HIGHEST_PRECISION = lax.Precision.HIGHEST
LIGHT = pl.CostEstimate(flops=1, bytes_accessed=1, transcendentals=0)
MIDDLE = pl.CostEstimate(flops=2 * 10**10, bytes_accessed=1, transcendentals=0)
SMALL = pl.CostEstimate(flops=1, bytes_accessed=1, transcendentals=0)
COVER = pl.CostEstimate(flops=1, bytes_accessed=1, transcendentals=0)
HEAVY = pl.CostEstimate(flops=10**11, bytes_accessed=1, transcendentals=0)
FEED_STEPS = 2
BLK = 256
HEAD_LANES = 64
NEAR = 128


def head_mask(rows, width, head, axis):
    place = lax.broadcasted_iota(jnp.int32, (rows, width), axis)
    return (place >= head * HEAD_LANES) & (place < (head + 1) * HEAD_LANES)


def one_head(value, head):
    keep = head_mask(value.shape[0], value.shape[1], head, 1)
    return jnp.where(keep, value, jnp.zeros_like(value))


def scaled(queries):
    return queries * jnp.asarray(HEAD_LANES ** -0.5, queries.dtype)


def dot_nt(left, right):
    return lax.dot_general(
        left, right, (((1,), (1,)), ((), ())), preferred_element_type=jnp.float32
    )


def dot_nn(left, right):
    return lax.dot_general(
        left, right, (((1,), (0,)), ((), ())), preferred_element_type=jnp.float32
    )


def attention_forward_kernel(
    cut_ref, rows_ref, weight_ref, bias_ref,
    qkv_a, qkv_b, out_ref, lse_a, lse_b, tile_ref, masked_v, score_ref,
):
    heads = masked_v.shape[0]
    width = out_ref.shape[1] // 2
    block = pl.program_id(0)
    cut = cut_ref[0]
    qkv_refs, lse_refs = (qkv_a, qkv_b), (lse_a, lse_b)

    @pl.when(block == 0)
    def _():
        weights = [
            jnp.concatenate(
                [weight_ref[slot, :, pair * width : (pair + 1) * width] for slot in range(3)],
                axis=1,
            )
            for pair in range(2)
        ]

        def one_chunk(chunk, carry):
            spot = pl.ds(pl.multiple_of(chunk * BLK, BLK), BLK)
            for pair in range(2):
                qkv_refs[pair][spot, :] = dot_nn(rows_ref[spot, :], weights[pair]).astype(
                    jnp.bfloat16
                )
            return carry

        lax.fori_loop(0, rows_ref.shape[0] // BLK, one_chunk, 0)
        for head in range(heads):
            wide = jnp.broadcast_to(bias_ref[head : head + 1, :], (BLK, 2 * BLK))
            tile_ref[head, :, 0 : 2 * BLK] = pltpu.roll(wide, 0, 1, stride=1, stride_axis=0)
            tile_ref[head, :, 2 * BLK :] = wide[:, 2 * BLK - 1 :] + jnp.zeros(
                (BLK, BLK), jnp.float32
            )
            masked_v[head] = one_head(qkv_refs[head // 2][:, 2 * width :], head % 2)

    row_start = block * BLK
    first = jnp.where(row_start >= cut, cut // BLK, 0)
    rows = row_start + lax.broadcasted_iota(jnp.int32, (BLK, BLK), 0)
    seg_start = jnp.where(rows >= cut, cut, 0)
    columns = lax.broadcasted_iota(jnp.int32, (BLK, BLK), 1)
    own = pl.ds(pl.multiple_of(row_start, BLK), BLK)
    q_heads = [
        one_head(scaled(qkv_refs[head // 2][own, 0:width]), head % 2) for head in range(heads)
    ]

    def scores_of(key_block, tops):
        key_start = pl.multiple_of(key_block * BLK, BLK)
        keys = [ref[pl.ds(key_start, BLK), width : 2 * width] for ref in qkv_refs]
        places = key_start + columns
        allowed = (places <= rows) & (places >= seg_start)
        order = key_block - block + 1
        offset = pl.multiple_of(jnp.where(order >= 0, order, 2) * BLK, BLK)
        new_tops = []
        for head in range(heads):
            raw = dot_nt(q_heads[head], keys[head // 2])
            bias = tile_ref[head, :, pl.ds(offset, BLK)]
            scores = jnp.where(allowed, raw + bias, -1e30)
            score_ref[head, :, pl.ds(key_start, BLK)] = scores
            top = tops[head]
            for lane in range(0, BLK, 128):
                top = jnp.maximum(top, scores[:, lane : lane + 128])
            new_tops.append(top)
        return tuple(new_tops)

    start = tuple(jnp.full((BLK, 128), -1e30, jnp.float32) for _ in range(heads))
    tops = lax.fori_loop(first, block + 1, scores_of, start)
    tops = [jnp.max(top, axis=1, keepdims=True) for top in tops]

    def weighted(key_block, carry):
        totals, sums = carry
        key_start = pl.multiple_of(key_block * BLK, BLK)
        new_totals, new_sums = [], []
        for pair in range(2):
            pieces, values = [], []
            for head in (2 * pair, 2 * pair + 1):
                soft = jnp.exp(score_ref[head, :, pl.ds(key_start, BLK)] - tops[head])
                part = sums[head]
                for lane in range(0, BLK, 128):
                    part = part + soft[:, lane : lane + 128]
                new_sums.append(part)
                pieces.append(soft.astype(jnp.bfloat16))
                values.append(masked_v[head, pl.ds(key_start, BLK), :])
            new_totals.append(
                totals[pair]
                + dot_nn(jnp.concatenate(pieces, axis=1), jnp.concatenate(values, axis=0))
            )
        return tuple(new_totals), tuple(new_sums)

    totals, sums = lax.fori_loop(
        first,
        block + 1,
        weighted,
        (
            tuple(jnp.zeros((BLK, width), jnp.float32) for _ in range(2)),
            tuple(jnp.zeros((BLK, 128), jnp.float32) for _ in range(heads)),
        ),
    )
    lanes = lax.broadcasted_iota(jnp.int32, (BLK, width), 1)
    for pair in range(2):
        scale = jnp.zeros((BLK, width), jnp.float32)
        logs = jnp.zeros((BLK, width), jnp.float32)
        for place in range(2):
            head = 2 * pair + place
            sum_one = jnp.sum(sums[head], axis=1, keepdims=True)
            scale = jnp.where(lanes // HEAD_LANES == place, 1.0 / sum_one, scale)
            logs = jnp.where(lanes == place, tops[head] + jnp.log(sum_one), logs)
        out_ref[:, pair * width : (pair + 1) * width] = (totals[pair] * scale).astype(jnp.bfloat16)
        lse_refs[pair][...] = jnp.transpose(logs)[0:8, :]


def attention_forward(cut, normed, weights, near_bias):
    length, depth = normed.shape
    width = weights.shape[2] // 2
    heads = 2 * width // HEAD_LANES
    whole = lambda block, cut: (0, 0)
    full = pl.BlockSpec((length, 3 * width), whole)
    row = pl.BlockSpec((BLK, 2 * width), lambda block, cut: (block, 0))
    line = pl.BlockSpec((8, BLK), lambda block, cut: (0, block))
    return pl.pallas_call(
        attention_forward_kernel,
        grid_spec=pltpu.PrefetchScalarGridSpec(
            num_scalar_prefetch=1,
            grid=(length // BLK,),
            in_specs=[
                pl.BlockSpec((length, depth), whole, pipeline_mode=pl.Buffered(1)),
                pl.BlockSpec(
                    weights.shape, lambda block, cut: (0, 0, 0), pipeline_mode=pl.Buffered(1)
                ),
                pl.BlockSpec((8, 2 * BLK), whole),
            ],
            out_specs=[full, full, row, line, line],
            scratch_shapes=[
                pltpu.VMEM((heads, BLK, 3 * BLK), jnp.float32),
                pltpu.VMEM((heads, length, width), jnp.bfloat16),
                pltpu.VMEM((heads, BLK, length), jnp.float32),
            ],
        ),
        out_shape=[jax.ShapeDtypeStruct((length, 3 * width), jnp.bfloat16)] * 2
        + [jax.ShapeDtypeStruct((length, 2 * width), jnp.bfloat16)]
        + [jax.ShapeDtypeStruct((8, length), jnp.float32)] * 2,
        compiler_params=pltpu.CompilerParams(
            dimension_semantics=("arbitrary",), vmem_limit_bytes=54 * 1024 * 1024
        ),
        cost_estimate=LIGHT,
        name="attention_forward",
    )(cut, normed, weights, near_bias)


def attention_backward_kernel(
    cut_ref, qkv_a, qkv_b, grad_ref, att_ref, lse_a, lse_b, bias_ref,
    dqkv_a, dqkv_b, table_ref,
    tile_ref, q_masked, grad_masked, delta_ref, dq_sum, near_sum,
):
    heads = q_masked.shape[0]
    block = pl.program_id(0)
    n_blocks = pl.num_programs(0)
    length = grad_ref.shape[0]
    width = att_ref.shape[1] // 2
    cut = cut_ref[0]
    qkv_refs, lse_refs, out_refs = (qkv_a, qkv_b), (lse_a, lse_b), (dqkv_a, dqkv_b)

    @pl.when(block == 0)
    def _():
        row = lax.broadcasted_iota(jnp.int32, (16, width), 0)
        lane = lax.broadcasted_iota(jnp.int32, (16, width), 1)
        pick = jnp.where(lane // HEAD_LANES == row, 1.0, 0.0).astype(jnp.bfloat16)
        for pair in range(2):
            lanes = slice(pair * width, (pair + 1) * width)
            grad_pair = grad_ref[:, lanes]
            product = grad_pair.astype(jnp.float32) * att_ref[:, lanes].astype(jnp.float32)
            high = product.astype(jnp.bfloat16)
            rest = (product - high.astype(jnp.float32)).astype(jnp.bfloat16)
            delta_ref[pair] = (dot_nt(pick, high) + dot_nt(pick, rest))[0:8, :]
            queries = scaled(qkv_refs[pair][:, 0:width])
            for place in range(2):
                head = 2 * pair + place
                q_masked[head] = one_head(queries, place)
                grad_masked[head] = one_head(grad_pair, place)
        for head in range(heads):
            wide = jnp.broadcast_to(bias_ref[head : head + 1, :], (BLK, 2 * BLK))
            tile_ref[head, :, 0 : 2 * BLK] = pltpu.roll(wide, 0, 1, stride=1, stride_axis=0)
            tile_ref[head, :, 2 * BLK :] = wide[:, BLK - 1 : BLK] + jnp.zeros(
                (BLK, BLK), jnp.float32
            )
        dq_sum[...] = jnp.zeros_like(dq_sum)
        near_sum[...] = jnp.zeros_like(near_sum)

    key_start = pl.multiple_of(block * BLK, BLK)
    keys = [ref[pl.ds(key_start, BLK), width : 2 * width] for ref in qkv_refs]
    values = [ref[pl.ds(key_start, BLK), 2 * width :] for ref in qkv_refs]
    keys_t = [jnp.transpose(one) for one in keys]
    places = key_start + lax.broadcasted_iota(jnp.int32, (BLK, BLK), 0)
    columns = lax.broadcasted_iota(jnp.int32, (BLK, BLK), 1)
    last = jnp.where(key_start + BLK <= cut, (cut + BLK - 1) // BLK, n_blocks)

    def one_block(query_block, carry):
        row_start = pl.multiple_of(query_block * BLK, BLK)
        rows = row_start + columns
        allowed = (places <= rows) & (places >= jnp.where(rows >= cut, cut, 0))
        distance = query_block - block
        offset = pl.multiple_of(jnp.minimum(distance, 2) * BLK, BLK)
        results = []
        for pair in range(2):
            soft_pieces, grad_pieces, q_pieces, out_pieces = [], [], [], []
            for place in range(2):
                head = 2 * pair + place
                q_head = q_masked[head, pl.ds(row_start, BLK), :]
                grad_head = grad_masked[head, pl.ds(row_start, BLK), :]
                bias = tile_ref[head, :, pl.ds(offset, BLK)]
                scores = dot_nt(keys[pair], q_head) + bias
                log_total = lse_refs[pair][place : place + 1, pl.ds(row_start, BLK)]
                soft = jnp.exp(jnp.where(allowed, scores - log_total, -1e30))
                grad_soft = dot_nt(values[pair], grad_head)
                delta = delta_ref[pair, place : place + 1, pl.ds(row_start, BLK)]
                grad_scores = soft * (grad_soft - delta)
                grad_low = grad_scores.astype(jnp.bfloat16)

                near_sum[head, :, pl.ds(offset, BLK)] += grad_scores
                own = slice(place * HEAD_LANES, (place + 1) * HEAD_LANES)
                spot = slice(head * HEAD_LANES, (head + 1) * HEAD_LANES)
                dq_sum[spot, pl.ds(row_start, BLK)] += dot_nn(keys_t[pair][own, :], grad_low)
                soft_pieces.append(soft.astype(jnp.bfloat16))
                grad_pieces.append(grad_low)
                q_pieces.append(q_head)
                out_pieces.append(grad_head)
            dk, dv = carry[pair]
            dv = dv + dot_nn(
                jnp.concatenate(soft_pieces, axis=1), jnp.concatenate(out_pieces, axis=0)
            )
            dk = dk + dot_nn(
                jnp.concatenate(grad_pieces, axis=1), jnp.concatenate(q_pieces, axis=0)
            )
            results.append((dk, dv))
        return tuple(results)

    empty = jnp.zeros((BLK, width), jnp.float32)
    results = lax.fori_loop(block, last, one_block, ((empty, empty), (empty, empty)))
    for pair in range(2):
        dk, dv = results[pair]
        out_refs[pair][pl.ds(key_start, BLK), width : 2 * width] = dk.astype(jnp.bfloat16)
        out_refs[pair][pl.ds(key_start, BLK), 2 * width :] = dv.astype(jnp.bfloat16)

    @pl.when(block == n_blocks - 1)
    def _():
        for query_block in range(length // BLK):
            spot = slice(query_block * BLK, (query_block + 1) * BLK)
            turned = (jnp.transpose(dq_sum[:, spot]) * (HEAD_LANES ** -0.5)).astype(jnp.bfloat16)
            for pair in range(2):
                out_refs[pair][spot, 0:width] = turned[:, pair * width : (pair + 1) * width]
        for head in range(heads):
            lined = jnp.zeros((8, 2 * BLK), jnp.float32)
            for group in range(BLK // 8):
                piece = near_sum[head, group * 8 : group * 8 + 8, 0 : 2 * BLK]
                shift = (2 * BLK - group * 8) % (2 * BLK)
                lined = lined + (pltpu.roll(piece, shift, 1) if shift else piece)
            total = lined[0:1, :]
            for row in range(1, 8):
                total = total + pltpu.roll(lined, 2 * BLK - row, 1)[row : row + 1, :]
            table_ref[head : head + 1, :] = total
            rest = jnp.sum(near_sum[head, :, 2 * BLK :], axis=0, keepdims=True)
            table_ref[heads + head : heads + head + 1, :] = jnp.concatenate(
                [rest, jnp.zeros_like(rest)], axis=1
            )


def attention_backward(cut, projected, grad_att, attended, logs, near_bias):
    length, width = attended.shape[0], attended.shape[1] // 2
    heads = 2 * width // HEAD_LANES
    whole = lambda block, cut: (0, 0)
    full = lambda columns: pl.BlockSpec((length, columns), whole)
    lse = pl.BlockSpec((8, length), whole)
    return pl.pallas_call(
        attention_backward_kernel,
        grid_spec=pltpu.PrefetchScalarGridSpec(
            num_scalar_prefetch=1,
            grid=(length // BLK,),
            in_specs=[
                full(3 * width), full(3 * width), full(2 * width), full(2 * width),
                lse, lse, pl.BlockSpec((8, 2 * BLK), whole),
            ],
            out_specs=[
                full(3 * width), full(3 * width), pl.BlockSpec((8, 2 * BLK), whole),
            ],
            scratch_shapes=[
                pltpu.VMEM((heads, BLK, 3 * BLK), jnp.float32),
                pltpu.VMEM((heads, length, width), jnp.bfloat16),
                pltpu.VMEM((heads, length, width), jnp.bfloat16),
                pltpu.VMEM((2, 8, length), jnp.float32),
                pltpu.VMEM((2 * width, length), jnp.float32),
                pltpu.VMEM((heads, BLK, 3 * BLK), jnp.float32),
            ],
        ),
        out_shape=[
            jax.ShapeDtypeStruct((length, 3 * width), jnp.bfloat16),
            jax.ShapeDtypeStruct((length, 3 * width), jnp.bfloat16),
            jax.ShapeDtypeStruct((8, 2 * BLK), jnp.float32),
        ],
        compiler_params=pltpu.CompilerParams(dimension_semantics=("arbitrary",)),
        cost_estimate=MIDDLE,
        name="attention_backward",
    )(cut, *projected, grad_att, attended, *logs, near_bias)


def distance_bias(rel_table, bucket_of):
    hot = (
        bucket_of[:, None] == jnp.arange(rel_table.shape[0], dtype=jnp.int32)[None, :]
    ).astype(jnp.float32)
    by_distance = jnp.einsum(
        "dn,nh->hd", hot, rel_table, precision=HIGHEST_PRECISION,
        preferred_element_type=jnp.float32,
    )
    return hot, by_distance


def near_tables(by_distance):
    heads, reach = by_distance.shape
    far = by_distance[:, reach - 1 :]
    forward = jnp.concatenate(
        [
            jnp.broadcast_to(far, (heads, BLK - reach + 1)),
            by_distance[:, ::-1],
            jnp.broadcast_to(far, (heads, BLK - 1)),
        ],
        axis=1,
    )
    backward = jnp.concatenate(
        [by_distance, jnp.broadcast_to(far, (heads, 2 * BLK - reach))], axis=1
    )
    rows = ((0, 8 - heads), (0, 0))
    return jnp.pad(forward, rows), jnp.pad(backward, rows)


def table_gradient(hot, near_sums, far_sums):
    reach = hot.shape[0]
    near = near_sums[:, : reach - 1]
    far = jnp.sum(near_sums[:, reach - 1 :], axis=1) + jnp.sum(far_sums, axis=1)
    by_distance = jnp.concatenate([near, far[:, None]], axis=1)
    return jnp.einsum(
        "dn,hd->nh", hot, by_distance, precision=HIGHEST_PRECISION,
        preferred_element_type=jnp.float32,
    )


TEAM = 4


def after(value, *gates):
    return lax.optimization_barrier((value,) + gates)[0]


def flip(value, axis, bit):
    size = lax.axis_size(axis)
    return lax.ppermute(value, axis, [(i, i ^ bit) for i in range(size)])


def halve(value, dim, axis, bit):
    mine = (lax.axis_index(axis) // bit) % 2
    keep = lax.dynamic_index_in_dim(value, mine, dim, keepdims=False)
    send = lax.dynamic_index_in_dim(value, 1 - mine, dim, keepdims=False)
    received = flip(send.astype(jnp.bfloat16), axis, bit)
    return (keep.astype(jnp.float32) + received.astype(jnp.float32)).astype(jnp.bfloat16)


def halve_start(value, dim, axis, bit):
    mine = (lax.axis_index(axis) // bit) % 2
    keep = lax.dynamic_index_in_dim(value, mine, dim, keepdims=False)
    send = lax.dynamic_index_in_dim(value, 1 - mine, dim, keepdims=False)
    return keep, flip(send, axis, bit)


def halve_end(pair):
    return (pair[0].astype(jnp.float32) + pair[1].astype(jnp.float32)).astype(jnp.bfloat16)


def double(value, axis, bit):
    mine = (lax.axis_index(axis) // bit) % 2
    other = flip(value, axis, bit)
    return jnp.where(mine == 0, jnp.stack([value, other]), jnp.stack([other, value]))


def bits_of(size):
    bits = []
    bit = 1
    while bit < size:
        bits.append(bit)
        bit *= 2
    return bits


def with_partner(own):
    return jnp.concatenate([own, flip(own, "team", 1)], axis=0)


def feed_grads_kernel(core_ref, own_ref, got_ref, up_ref, down_ref, *, spots):
    unit = own_ref.shape[2]
    half = len(spots) // 2

    def write(piece_ref, places):
        for index, spot in enumerate(places):
            where = slice(spot * unit, (spot + 1) * unit)
            up_ref[:, where] = jnp.transpose(piece_ref[index, 0].astype(jnp.float32))
            down_ref[where, :] = piece_ref[index, 1].astype(jnp.float32)

    def both(core):
        write(own_ref, spots[core * half : (core + 1) * half])
        write(got_ref, spots[(1 - core) * half : (2 - core) * half])

    for core in range(2):
        pl.when(core_ref[0] == core)(functools.partial(both, core))


def feed_grads_out(core, own, got, copies):
    count, _, unit, depth = own.shape
    merge = max(1, 128 // unit)
    if merge > 1:
        own, got = (
            jnp.transpose(
                one.reshape(count // merge, merge, 2, unit, depth), (0, 2, 1, 3, 4)
            ).reshape(count // merge, 2, merge * unit, depth)
            for one in (own, got)
        )
    count, _, unit, depth = own.shape
    each = copies // merge
    spots = []
    for step in range(2 * count):
        half, side, place = place_in_group(step, each)
        spots.append((side * 2 + half) * each + place)
    take = depth // 4
    piece = pl.BlockSpec((count, 2, unit, take), lambda step, core: (0, 0, 0, step))
    return pl.pallas_call(
        functools.partial(feed_grads_kernel, spots=spots),
        grid_spec=pltpu.PrefetchScalarGridSpec(
            num_scalar_prefetch=1,
            grid=(4,),
            in_specs=[piece, piece],
            out_specs=[
                pl.BlockSpec((take, 2 * count * unit), lambda step, core: (step, 0)),
                pl.BlockSpec((2 * count * unit, take), lambda step, core: (0, step)),
            ],
        ),
        out_shape=[
            jax.ShapeDtypeStruct((depth, 2 * count * unit), jnp.float32),
            jax.ShapeDtypeStruct((2 * count * unit, depth), jnp.float32),
        ],
        compiler_params=pltpu.CompilerParams(dimension_semantics=("arbitrary",)),
        cost_estimate=LIGHT,
        name="feed_grads_out",
    )(core, own, got)


def attention_grads_kernel(core_ref, own_ref, got_ref, qkv_ref, out_ref, *, spots):
    group = own_ref.shape[0]
    rows, width = qkv_ref.shape[1] // group, qkv_ref.shape[2]
    few = out_ref.shape[0] // group

    def place_all(piece_ref, core):
        for item in range(group):
            spot = spots[core * group + item] - core * group
            for slot in range(3):
                qkv_ref[slot, spot * rows : (spot + 1) * rows, :] = piece_ref[
                    item, slot * rows : (slot + 1) * rows, :
                ].astype(jnp.float32)
            for place in range(out_ref.shape[1] // width):
                start = 3 * rows + place * few
                out_ref[
                    spot * few : (spot + 1) * few, place * width : (place + 1) * width
                ] = piece_ref[item, start : start + few, :].astype(jnp.float32)

    step = pl.program_id(0)
    for core in range(2):
        mine = (step == core) & (core_ref[0] == core)
        other = (step == core) & (core_ref[0] != core)
        pl.when(mine)(functools.partial(place_all, own_ref, core))
        pl.when(other)(functools.partial(place_all, got_ref, core))


def attention_grads_out(core, own, got, depth, head_width):
    half = own.shape[0]
    copies = half // 2
    spots = []
    for step in range(2 * half):
        side_core, side, place = place_in_group(step, copies)
        spots.append((side_core * 2 + side) * copies + place)
    whole = pl.BlockSpec(own.shape, lambda step, core: (0, 0, 0))
    return pl.pallas_call(
        functools.partial(attention_grads_kernel, spots=spots),
        grid_spec=pltpu.PrefetchScalarGridSpec(
            num_scalar_prefetch=1,
            grid=(2,),
            in_specs=[whole, whole],
            out_specs=[
                pl.BlockSpec((3, depth // 2, head_width), lambda step, core: (0, step, 0)),
                pl.BlockSpec((head_width // 2, depth), lambda step, core: (step, 0)),
            ],
        ),
        out_shape=[
            jax.ShapeDtypeStruct((3, depth, head_width), jnp.float32),
            jax.ShapeDtypeStruct((head_width, depth), jnp.float32),
        ],
        compiler_params=pltpu.CompilerParams(dimension_semantics=("arbitrary",)),
        cost_estimate=HEAVY,
        name="attention_grads_out",
    )(core, own, got)


def qkv_grad_kernel(core_ref, rows_ref, grad_a, grad_b, send_ref, keep_ref):
    width = grad_a.shape[1]
    both = [dot_tn(rows_ref[...], grad[...]).astype(jnp.bfloat16) for grad in (grad_a, grad_b)]

    @pl.when(pl.program_id(0) == 0)
    def _():
        send_ref[:, 0:width] = both[0]
        send_ref[:, width:] = both[1]

    @pl.when(pl.program_id(0) == 1)
    def _():
        keep_ref[:, 0:width] = both[0]
        keep_ref[:, width:] = both[1]


def qkv_weight_grad(core, rows, grads):
    length, depth = rows.shape
    width = grads[0].shape[1]
    half = depth // 2
    whole = pl.BlockSpec((length, width), lambda step, core: (0, 0))
    out = pl.BlockSpec((half, 2 * width), lambda step, core: (0, 0))
    return pl.pallas_call(
        qkv_grad_kernel,
        grid_spec=pltpu.PrefetchScalarGridSpec(
            num_scalar_prefetch=1,
            grid=(2,),
            in_specs=[
                pl.BlockSpec((length, half), lambda step, core: (0, 1 - core[0] ^ step)),
                whole, whole,
            ],
            out_specs=[out, out],
        ),
        out_shape=[jax.ShapeDtypeStruct((half, 2 * width), jnp.bfloat16)] * 2,
        compiler_params=pltpu.CompilerParams(dimension_semantics=("arbitrary",)),
        cost_estimate=SMALL,
        name="qkv_weight_grad",
    )(core, rows, *grads)


def first_norm_kernel(token_ref, line_ref, out_ref):
    unit, _ = normalize(token_ref[...].astype(jnp.float32))
    out_ref[...] = (unit * line_ref[0:1, :] + line_ref[1:2, :]).astype(jnp.bfloat16)


def first_norm(tokens, lines):
    return pl.pallas_call(
        first_norm_kernel,
        out_shape=jax.ShapeDtypeStruct(tokens.shape, jnp.bfloat16),
        cost_estimate=LIGHT,
        name="first_norm",
    )(tokens, lines)


def token_grads_kernel(grad_ref, hidden_ref, token_ref, line_ref, out_ref):
    unit, inverse = normalize(token_ref[...].astype(jnp.float32))
    grad = normalize_backward(grad_ref[...].astype(jnp.float32), line_ref[...], unit, inverse)
    out_ref[...] = (hidden_ref[...] + grad).astype(jnp.bfloat16)


def token_grads(grad, hidden, tokens, line):
    return pl.pallas_call(
        token_grads_kernel,
        out_shape=jax.ShapeDtypeStruct(tokens.shape, jnp.bfloat16),
        compiler_params=pltpu.CompilerParams(vmem_limit_bytes=32 * 1024 * 1024),
        cost_estimate=LIGHT,
        name="token_grads",
    )(grad, hidden, tokens, line)


def branch_kernel(*refs, count):
    pieces = refs[:count]
    weight_ref, token_ref, line_ref, hidden_ref, second_ref, left_ref = refs[count:]
    left = jnp.concatenate([piece[...] for piece in pieces], axis=1)
    left_ref[...] = left
    hidden = token_ref[...].astype(jnp.float32) + dot_nn(left, weight_ref[...])
    unit, _ = normalize(hidden)
    hidden_ref[...] = hidden
    second_ref[...] = (unit * line_ref[0:1, :] + line_ref[1:2, :]).astype(jnp.bfloat16)


def branch_and_norm(pieces, weights, tokens, lines):
    rows, depth = tokens.shape
    return pl.pallas_call(
        functools.partial(branch_kernel, count=len(pieces)),
        out_shape=[
            jax.ShapeDtypeStruct((rows, depth), jnp.float32),
            jax.ShapeDtypeStruct((rows, depth), jnp.bfloat16),
            jax.ShapeDtypeStruct((rows, weights.shape[0]), jnp.bfloat16),
        ],
        compiler_params=pltpu.CompilerParams(vmem_limit_bytes=32 * 1024 * 1024),
        cost_estimate=LIGHT,
        name="branch_and_norm",
    )(*pieces, weights, tokens, lines)


def row_grads_kernel(
    own_ref, core_ref, across_ref, grad_ref, hidden_ref, weight_ref, line_ref,
    total_ref, branch_ref, *refs,
):
    block_refs, sum_ref = refs[:-1], refs[-1]
    second = (
        own_ref[...].astype(jnp.float32) + core_ref[...].astype(jnp.float32)
        + across_ref[...].astype(jnp.float32)
    )
    grad = grad_ref[...].astype(jnp.float32)
    unit, inverse = normalize(hidden_ref[...])
    total = grad + normalize_backward(second, line_ref[0:1, :], unit, inverse)
    branch = total.astype(jnp.bfloat16)
    total_ref[...] = total
    branch_ref[...] = branch
    width = block_refs[0].shape[1]
    for index, block_ref in enumerate(block_refs):
        block_ref[...] = dot_nt(
            branch, weight_ref[index * width : (index + 1) * width, :]
        ).astype(jnp.bfloat16)
    sums = [jnp.sum(one, axis=0, keepdims=True) for one in (second * unit, second, grad)]
    lines = jnp.concatenate(sums + [jnp.zeros((5, sums[0].shape[1]), jnp.float32)])

    sum_ref[...] = lines


def row_grads(backs, grad, hidden, weights, lines, parts):
    rows, depth = hidden.shape
    width = weights.shape[0] // parts
    return pl.pallas_call(
        row_grads_kernel,
        out_shape=[
            jax.ShapeDtypeStruct((rows, depth), jnp.float32),
            jax.ShapeDtypeStruct((rows, depth), jnp.bfloat16),
        ]
        + [jax.ShapeDtypeStruct((rows, width), jnp.bfloat16)] * parts
        + [jax.ShapeDtypeStruct((8, depth), jnp.float32)],
        compiler_params=pltpu.CompilerParams(vmem_limit_bytes=40 * 1024 * 1024),
        cost_estimate=LIGHT,
        name="row_grads",
    )(*backs, grad, hidden, weights, lines)


def out_grad_kernel(core_ref, left_ref, right_ref, keep_ref, send_ref):
    parts, half, _ = keep_ref.shape

    def columns(core):
        return jnp.concatenate(
            [
                left_ref[:, pl.ds(pl.multiple_of((2 * part + core) * half, 128), half)]
                for part in range(parts)
            ],
            axis=1,
        )

    for out_ref, core in ((keep_ref, core_ref[0]), (send_ref, 1 - core_ref[0])):
        grad = dot_tn(columns(core), right_ref[...]).astype(jnp.bfloat16)
        for part in range(parts):
            out_ref[part] = grad[part * half : (part + 1) * half]


def out_weight_grad(core, own_rows, grads, parts):
    rows, depth = grads.shape
    half = own_rows.shape[1] // parts // 2
    whole = pl.BlockSpec((rows, depth), lambda step, core: (0, 0))
    out = pl.BlockSpec((parts, half, depth), lambda step, core: (0, 0, 0))
    return pl.pallas_call(
        out_grad_kernel,
        grid_spec=pltpu.PrefetchScalarGridSpec(
            num_scalar_prefetch=1,
            grid=(1,),
            in_specs=[
                pl.BlockSpec(own_rows.shape, lambda step, core: (0, 0)), whole,
            ],
            out_specs=[out, out],
        ),
        out_shape=[jax.ShapeDtypeStruct((parts, half, depth), jnp.bfloat16)] * 2,
        compiler_params=pltpu.CompilerParams(dimension_semantics=("arbitrary",)),
        cost_estimate=COVER,
        name="out_weight_grad",
    )(core, own_rows, grads)


def normalize(inputs):
    center = inputs - jnp.mean(inputs, axis=-1, keepdims=True)
    spread = jnp.mean(center * center, axis=-1, keepdims=True)
    inverse = lax.rsqrt(spread + EPSILON)
    return center * inverse, inverse


def normalize_backward(grad, gain, unit, inverse):
    scaled_grad = grad * gain
    middle = jnp.mean(scaled_grad, axis=-1, keepdims=True)
    along = jnp.mean(scaled_grad * unit, axis=-1, keepdims=True)
    return (scaled_grad - middle - unit * along) * inverse


def dot_tn(left, right):
    return lax.dot_general(
        left, right, (((0,), (0,)), ((), ())), preferred_element_type=jnp.float32
    )


def copies_of(value, size):
    halves = [value[None]]
    for bit in bits_of(size):
        value = halves[0] if len(halves) == 1 else jnp.concatenate(halves)
        halves = [value, flip(value, "copy", bit)]
    return halves


def untangle(value, axis, index, size):
    for bit in bits_of(size):
        shape = value.shape
        split = value.reshape(
            shape[:axis] + (size // (2 * bit), 2, bit) + shape[axis + 1 :]
        )
        split = jnp.where((index // bit) % 2 == 1, jnp.flip(split, axis + 1), split)
        value = split.reshape(shape)
    return value


def orders(copies):
    first = [("copy", bit) for bit in bits_of(copies)] + [("team", 2)]
    return first, first[::-1] if copies == 2 else first


def spread_end(value, got, mine):
    return jnp.where(mine == 0, jnp.stack([value, got]), jnp.stack([got, value]))


def spread_group(value, step, copies):
    return spread_end(*spread_start(value, step, copies))


def spread_start(value, step, copies):
    choices = [order[step] for order in orders(copies)]
    moves = []
    for place in range(copies * TEAM):
        axis, bit = choices[place % 2]
        moves.append((place, place ^ (bit if axis == "team" else bit * TEAM)))
    got = lax.ppermute(value, ("copy", "team"), moves)
    mine = [(lax.axis_index(axis) // bit) % 2 for axis, bit in choices]
    return value, got, jnp.where(lax.axis_index("team") % 2 == 0, mine[0], mine[1])


def place_in_group(step, copies):
    core, index = step // (2 * copies), step % (2 * copies)
    if copies != 2:
        return core, index // copies, index % copies
    outer, inner = index // 2, index % 2
    return core, outer + core * (inner - outer), inner + core * (outer - inner)


def exchange(blocks):
    return [blocks[0]] + [flip(blocks[k], "mp", k) for k in range(1, len(blocks))]


def cotangent_kernel(grad_a, grad_b, weight_a, weight_b, normed_ref, line_ref, out_ref, sum_ref):
    grad = sum(
        dot_nt(grad_ref[...], jnp.concatenate([weight_ref[slot] for slot in range(3)], axis=1))
        for grad_ref, weight_ref in ((grad_a, weight_a), (grad_b, weight_b))
    )
    unit = (normed_ref[...].astype(jnp.float32) - line_ref[0:1, :]) * line_ref[1:2, :]
    out_ref[...] = grad.astype(jnp.bfloat16)
    rows, depth = grad.shape
    both = jnp.concatenate(
        [
            jnp.sum((grad * unit).reshape(rows // 8, 8, depth), axis=0),
            jnp.sum(grad.reshape(rows // 8, 8, depth), axis=0),
        ],
        axis=0,
    )

    @pl.when(pl.program_id(0) == 0)
    def _():
        sum_ref[...] = both

    @pl.when(pl.program_id(0) > 0)
    def _():
        sum_ref[...] += both


def input_cotangent(grads, weights, normed, lines):
    length, width = grads[0].shape
    depth = weights.shape[1]
    row = pl.BlockSpec((BLK, width), lambda step: (step, 0))
    part_a = pl.BlockSpec((3, depth, width // 3), lambda step: (0, 0, 0))
    part_b = pl.BlockSpec((3, depth, width // 3), lambda step: (0, 0, 1))
    return pl.pallas_call(
        cotangent_kernel,
        grid=(length // BLK,),
        in_specs=[
            row, row, part_a, part_b,
            pl.BlockSpec((BLK, depth), lambda step: (step, 0)),
            pl.BlockSpec((2, depth), lambda step: (0, 0)),
        ],
        out_specs=[
            pl.BlockSpec((BLK, depth), lambda step: (step, 0)),
            pl.BlockSpec((16, depth), lambda step: (0, 0)),
        ],
        out_shape=[
            jax.ShapeDtypeStruct((length, depth), jnp.bfloat16),
            jax.ShapeDtypeStruct((16, depth), jnp.float32),
        ],
        compiler_params=pltpu.CompilerParams(dimension_semantics=("arbitrary",)),
        cost_estimate=SMALL,
        name="input_cotangent",
    )(*grads, weights, weights, normed, lines)


def feed_kernel(*refs, unit, count):
    weight_refs = refs[:count]
    (
        bias_ref, second_ref, grad_ref,
        act_ref, pre_ref, back_own, back_other, out_own, out_other, sum_ref,
    ) = refs[count:]
    w_up, w_down = (
        jnp.concatenate(
            [
                ref[:, start : start + unit, :].reshape(ref.shape[0] * unit, ref.shape[2])
                for ref in weight_refs
            ]
        )
        for start in (0, unit)
    )
    pre = dot_nt(second_ref[...], w_up) + bias_ref[...]
    grad_act = dot_nt(grad_ref[...], w_down)
    cdf = 0.5 + 0.5 * lax.erf(pre * 0.7071067811865476)
    pdf = jnp.exp(pre * pre * -0.5) * 0.3989422804014327
    active = (pre * cdf).astype(jnp.bfloat16)
    grad_pre = ((cdf + pre * pdf) * grad_act).astype(jnp.bfloat16)
    act_ref[...] = active
    pre_ref[...] = grad_pre
    line = jnp.sum(grad_pre.astype(jnp.float32), axis=0, keepdims=True)
    back = dot_nn(grad_pre, w_up).astype(jnp.bfloat16)
    out = dot_nn(active, w_down).astype(jnp.bfloat16)

    step = pl.program_id(0)
    middle = pl.num_programs(0) // 2

    @pl.when(step < middle)
    def _():
        back_own[...] = back
        out_own[...] = out

    @pl.when(step >= middle)
    def _():
        back_other[...] = back
        out_other[...] = out

    @pl.when(step == 0)
    def _():
        sum_ref[...] = line

    @pl.when(step > 0)
    def _():
        sum_ref[...] += line


def feed_forward(weights, bias_row, second, grad, unit):
    depth = weights[0].shape[2]
    rows = second.shape[0]
    width = unit * sum(one.shape[0] for one in weights)
    steps = FEED_STEPS
    take = rows // steps
    middle = steps // 2
    row = pl.BlockSpec((take, depth), lambda step: (step, 0))
    near = pl.BlockSpec((take, depth), lambda step: (jnp.minimum(step, middle - 1), 0))
    far = pl.BlockSpec((take, depth), lambda step: (jnp.maximum(step - middle, 0), 0))
    wide = pl.BlockSpec((take, width), lambda step: (step, 0))
    line = pl.BlockSpec((1, width), lambda step: (0, 0))
    part = jax.ShapeDtypeStruct((rows // 2, depth), jnp.bfloat16)
    return pl.pallas_call(
        functools.partial(feed_kernel, unit=unit, count=len(weights)),
        grid=(steps,),
        in_specs=[pl.BlockSpec(each.shape, lambda step: (0, 0, 0)) for each in weights]
        + [line, row, row],
        out_specs=[wide, wide, near, far, near, far, line],
        out_shape=[
            jax.ShapeDtypeStruct((rows, width), jnp.bfloat16),
            jax.ShapeDtypeStruct((rows, width), jnp.bfloat16),
            part, part, part, part,
            jax.ShapeDtypeStruct((1, width), jnp.float32),
        ],
        compiler_params=pltpu.CompilerParams(
            dimension_semantics=("arbitrary",), vmem_limit_bytes=54 * 1024 * 1024
        ),
        cost_estimate=LIGHT,
        name="feed_forward",
    )(*weights, bias_row, second, grad)


def weight_grad_kernel(
    part_ref, act_a, act_b, pre_a, pre_b, second_a, second_b, grad_a, grad_b, *out_refs
):
    _, places, _, unit, _ = out_refs[0].shape
    up = dot_tn(pre_a[...], second_a[...]) + dot_tn(pre_b[...], second_b[...])
    down = dot_tn(act_a[...], grad_a[...]) + dot_tn(act_b[...], grad_b[...])
    for index, out_ref in enumerate(out_refs):
        for place in range(places):
            start = (index * places + place) * unit
            out_ref[0, place, 0] = up[start : start + unit].astype(jnp.bfloat16)
            out_ref[0, place, 1] = down[start : start + unit].astype(jnp.bfloat16)


def weight_grads(part, acts, pres, seconds, grads, parts, copies):
    rows, width = acts[0].shape
    depth = seconds[0].shape[1]
    unit = width // (parts * copies)
    count = 2 if copies > 1 else 1
    places = copies // count
    column = pl.BlockSpec((rows, width // parts), lambda step, part: (0, step))
    whole = pl.BlockSpec((rows, depth), lambda step, part: (0, 0))
    out = pl.BlockSpec(
        (1, places, 2, unit, depth), lambda step, part: (part[0] ^ step, 0, 0, 0, 0)
    )
    return pl.pallas_call(
        weight_grad_kernel,
        grid_spec=pltpu.PrefetchScalarGridSpec(
            num_scalar_prefetch=1,
            grid=(parts,),
            in_specs=[column] * 4 + [whole] * 4,
            out_specs=[out] * count,
        ),
        out_shape=[jax.ShapeDtypeStruct((parts, places, 2, unit, depth), jnp.bfloat16)] * count,
        compiler_params=pltpu.CompilerParams(
            dimension_semantics=("arbitrary",), vmem_limit_bytes=56 * 1024 * 1024
        ),
        cost_estimate=HEAVY,
        name="weight_grads",
    )(part, *acts, *pres, *seconds, *grads)


def fold_copies(halves, got):
    if len(halves) == 1:
        return halves[0]
    value = halve_end((halves[0], got))
    while value.shape[1] > 1:
        half = value.shape[1] // 2
        value = halve_end((value[:, :half], flip(value[:, half:], "copy", half)))
    return value


def sync(*values):
    return lax.optimization_barrier(values)


def body(
    tokens, seg_ids, bucket_of, ln1_gain, ln1_bias, w_qkv, rel_table, w_out,
    ln2_gain, ln2_bias, w_up, up_bias, w_down, down_bias, out_grad,
):
    low = jnp.bfloat16
    wide = jnp.float32
    copies = lax.axis_size("copy")
    parts = lax.axis_size("mp")
    copy = lax.axis_index("copy")
    member = lax.axis_index("team")
    part = lax.axis_index("mp")
    core = member % 2
    rows, depth = tokens.shape
    head_width = w_out.shape[0]
    pair_width = head_width // 2
    pairs = 2
    team_units = w_up.shape[1] // TEAM
    unit = team_units // copies
    out_rows = head_width // (2 * copies)
    seg_row = seg_ids[0]
    to_right = [(i, i + 1) for i in range(parts - 1)]
    to_left = [(i + 1, i) for i in range(parts - 1)]

    def relay(right, left, step):
        return (
            lax.ppermute(right, "mp", to_right[step - 1 :]),
            lax.ppermute(left, "mp", to_left[: parts - step]),
        )

    def corner_of(right1, left1, right3, left3):
        return jnp.where(
            (part == 0) | (part == parts - 1), right3 + left3, jnp.where(part == 1, left1, right1)
        )

    normed = lax.all_gather(
        first_norm(tokens, jnp.stack([ln1_gain, ln1_bias])), "mp", axis=0, tiled=True
    )

    def own_units(place):
        first = member * team_units + (copy ^ place) * unit
        return jnp.concatenate(
            [
                jnp.transpose(lax.dynamic_slice_in_dim(w_up, first, unit, 1)),
                lax.dynamic_slice_in_dim(w_down, first, unit, 0),
            ]
        )

    own_slot = jnp.stack([own_units(place) for place in range(copies)])
    out_own = lax.dynamic_slice_in_dim(w_out, (copy * 2 + core) * out_rows, out_rows, 0)
    own_biases = [
        lax.dynamic_slice_in_dim(up_bias, member * team_units + (copy ^ place) * unit, unit, 0)
        for place in range(copies)
    ]
    high = lax.reduce_precision(own_biases[0], 8, 7)
    middle = lax.reduce_precision(own_biases[0] - high, 8, 7)
    bias_lines = jnp.stack([high, middle, own_biases[0] - high - middle]).astype(low)
    bias_lines = jnp.pad(bias_lines, ((0, 5), (0, depth - unit)))
    piece = jnp.concatenate([own_slot[0], out_own, bias_lines])
    w_right1, w_left1 = relay(piece, piece, 1)
    w_right2, w_left2 = relay(w_right1, w_left1, 2)
    beside = copies_of(jnp.where(part % 2 == 0, w_left1, w_right1), copies)
    grad_across = flip(out_grad, "team", 2)
    grad_near = with_partner(out_grad)
    grad_far = with_partner(grad_across)
    hot, by_distance = distance_bias(rel_table, bucket_of)
    forward_bias, backward_bias = near_tables(by_distance)
    cut = jnp.sum((seg_row == seg_row[0]).astype(jnp.int32)).reshape(1)
    normed = after(
        normed, grad_near, grad_far, own_slot, forward_bias, backward_bias, cut,
        w_right2, w_left2, beside[1],
    )

    def whole_out(halves):
        mine = jnp.concatenate([half[:, 2 * unit : 2 * unit + out_rows] for half in halves])
        mine = untangle(mine, 0, copy, copies)
        other = flip(mine, "team", 1)
        return jnp.where(
            core == 0, jnp.stack([mine, other], axis=1), jnp.stack([other, mine], axis=1)
        ).reshape(head_width, depth)

    w_right2, w_left2 = after(w_right2, normed), after(w_left2, normed)
    w_right3, w_left3 = relay(w_right2, w_left2, 3)
    across = copies_of(w_right2 + w_left2, copies)
    *results, = attention_forward(cut, after(normed, across[0]), w_qkv, forward_bias)
    projected, attended, logs = results[0:2], results[2], results[3:5]
    w_right3, w_left3, across[1], attended = sync(w_right3, w_left3, across[1], attended)
    corner = copies_of(corner_of(w_right1, w_left1, w_right3, w_left3), copies)
    stack = attended.reshape(parts, rows, head_width)
    moved = exchange(
        [lax.dynamic_index_in_dim(stack, part ^ k, 0, keepdims=False) for k in range(parts)]
    )
    w_out_full = jnp.concatenate(
        [w_out] + [whole_out(halves) for halves in (beside, across, corner)]
    )
    weights = [own_slot] + beside + across + corner
    bias_row = jnp.concatenate(
        own_biases
        + [
            jnp.sum(half[:, -8:-5, :unit].astype(wide), axis=1).reshape(-1)
            for half in weights[1:]
        ]
    )[None]

    hidden_in, second, own_rows = branch_and_norm(
        moved, w_out_full, tokens, jnp.stack([ln2_gain, ln2_bias])
    )
    second_across = flip(second, "team", 2)
    second_near = with_partner(second)
    act_near, pre_near, back_own, back_core, feed_own, feed_core, sums_near = feed_forward(
        weights, bias_row, second_near, grad_near, unit
    )
    second_across = after(second_across, back_own)
    back_core = flip(back_core, "team", 1)
    second_far = with_partner(second_across)
    act_far, pre_far, back_side, back_corner, feed_side, feed_corner, sums_far = feed_forward(
        weights, bias_row, second_far, grad_far, unit
    )
    onward = (
        back_side.astype(wide) + flip(back_corner, "team", 1).astype(wide)
    ).astype(low)
    back_across = flip(onward, "team", 2)
    feed_stack = jnp.stack([after(feed_corner, onward), feed_core])
    feed_beside = flip(feed_stack, "team", 1)
    ff_grads = weight_grads(
        part.reshape(1), (act_near, after(act_far, onward, feed_stack)), (pre_near, pre_far),
        (second_near, second_far), (grad_near, grad_far), parts, copies,
    )
    ff_got = flip(ff_grads[-1], "copy", max(1, copies // 2)) if copies > 1 else ff_grads[0]
    back_across = after(back_across, ff_grads[0])
    grad_hidden, grad_branch, *grad_rows = row_grads(
        (back_own, back_core, back_across), out_grad, hidden_in, w_out_full, ln2_gain[None], parts
    )
    row_sums = grad_rows.pop()
    received = exchange(grad_rows)
    grad_branch, feed_beside, *received = sync(grad_branch, feed_beside, *received)
    wout_keep, wout_send = out_weight_grad(core.reshape(1), own_rows, grad_branch, parts)
    wout_got = flip(wout_send, "team", 1)
    feed_sum = (feed_side.astype(wide) + feed_beside[0].astype(wide)).astype(low)
    natural = jnp.zeros((parts, rows, head_width), low)
    for k in range(parts):
        natural = lax.dynamic_update_index_in_dim(natural, received[k], part ^ k, 0)
    wout_grad = halve_end((wout_keep, wout_got)).reshape(parts, 2, copies, -1, depth)
    side_bit = (member // 2) % 2
    wout_keep = lax.dynamic_index_in_dim(wout_grad, side_bit, 1, keepdims=False)
    wout_send = lax.dynamic_index_in_dim(wout_grad, 1 - side_bit, 1, keepdims=False)
    ff_got, natural, feed_sum, wout_keep, wout_send = sync(
        ff_got, natural, feed_sum, wout_keep, wout_send
    )
    ff_value = fold_copies(ff_grads, ff_got).reshape(parts, 2 * unit, depth)
    ff_piece = lax.psum_scatter(ff_value, "mp", scatter_dimension=0, tiled=False)
    wout_pair = (wout_keep, flip(wout_send, "team", 2))
    feed_across = flip(feed_sum, "team", 2)
    grad_att = natural.reshape(parts * rows, head_width)
    first_grads, last_grads, table_sums = attention_backward(
        cut, projected, grad_att, attended, logs, backward_bias
    )
    first_grads, last_grads, wout_last, feed_across = sync(
        first_grads, last_grads, wout_pair[1], feed_across
    )
    dqkv = [first_grads, last_grads]
    wout_grad = halve_end((wout_pair[0], wout_last))
    for bit in reversed(bits_of(copies)):
        wout_grad = wout_grad.reshape((parts, 2, -1) + wout_grad.shape[2:])
        wout_pair = halve_start(wout_grad, 1, "copy", bit)
        if bit > 1:
            wout_grad = halve_end(wout_pair)
    wout_keep, wout_last = wout_pair
    qkv_send, qkv_keep = qkv_weight_grad(
        core.reshape(1), normed, [after(dqkv[0], wout_keep), dqkv[1]]
    )
    qkv_keep, qkv_send, dqkv[0] = sync(qkv_keep, qkv_send, dqkv[0])
    qkv_got = flip(qkv_send, "team", 1)
    running, line_sums = input_cotangent(
        dqkv, w_qkv, normed,
        jnp.stack([after(ln1_bias, dqkv[0]), 1.0 / ln1_gain]),
    )
    grad_first = lax.psum_scatter(running, "mp", scatter_dimension=0, tiled=True)
    qkv_got, running, ff_piece, wout_last = sync(qkv_got, running, ff_piece, wout_last)
    wout_grad = halve_end((wout_keep, wout_last)).reshape(parts, -1, depth)
    wout_blocks = exchange([wout_grad[k] for k in range(parts)])
    qkv_grad = halve_end((qkv_keep, qkv_got))
    table_sums = after(table_sums, running)
    table_line = table_gradient(
        hot, table_sums[: table_sums.shape[0] // 2], table_sums[table_sums.shape[0] // 2 :]
    ).reshape(1, -1)
    table_all = lax.dynamic_update_slice_in_dim(
        jnp.zeros((parts, table_line.shape[1]), wide), table_line, part, 0
    )
    sums = (after(sums_near, running) + sums_far).reshape(parts, copies, unit)
    sums = untangle(untangle(sums, 0, part, parts), 1, copy, copies)
    up_sums = lax.dynamic_update_slice_in_dim(
        jnp.zeros((parts, TEAM * team_units), wide), sums.reshape(parts, team_units),
        member * team_units, 1,
    )
    early_lines = jnp.concatenate([row_sums[0:3].reshape(-1), up_sums.reshape(-1)])
    small = jnp.concatenate(
        [
            jnp.sum(line_sums[0:8], axis=0), jnp.sum(line_sums[8:16], axis=0),
            early_lines, table_all.reshape(-1),
        ]
    )
    small = jnp.pad(small, (0, -small.shape[0] % 1024)).reshape(-1, 1024)

    qkv_pair = halve_start(qkv_grad.reshape(2, copies, -1, qkv_grad.shape[1]), 0, "team", 2)
    ff_all = spread_group(ff_piece, 0, copies)
    small = small + flip(small, "team", 1)
    small_got = flip(small, "team", 2)
    feed_own = feed_own.astype(wide) + feed_beside[1].astype(wide) + feed_across.astype(wide)
    layer_out = (hidden_in + feed_own + down_bias).astype(low)
    qkv_last, ff_all, small_got, layer_out = sync(qkv_pair[1], ff_all, small_got, layer_out)
    qkv_grad = halve_end((qkv_pair[0], qkv_last))
    small = small + small_got

    for bit in reversed(bits_of(copies)):
        qkv_pair = halve_start(qkv_grad.reshape((2, -1) + qkv_grad.shape[1:]), 0, "copy", bit)
        if bit > 1:
            qkv_grad = halve_end(qkv_pair)
    if copies == 1:
        qkv_pair = (qkv_grad, jnp.zeros_like(qkv_grad))
    for step in range(1, len(orders(copies)[0]) - 1):
        ff_all = spread_group(ff_all, step, copies)
    ff_own, ff_got, ff_mine = spread_start(ff_all, len(orders(copies)[0]) - 1, copies)
    for bit in bits_of(copies)[1:]:
        small = small + flip(small, "copy", bit)
    small_got = flip(small, "copy", 1) if copies > 1 else jnp.zeros_like(small)
    results = sync(qkv_pair[1], small_got, small, ff_got, *wout_blocks)
    qkv_last, small_got, small, ff_got = results[:4]
    ff_all = spread_end(ff_own, ff_got, ff_mine)
    small = small + small_got
    qkv_grad = halve_end((qkv_pair[0], qkv_last))
    wout_grad = sum(one.astype(wide) for one in results[4:]).astype(low)
    qkv_grad = qkv_grad.reshape(-1, 3 * head_width)
    columns = [
        jnp.concatenate(
            [
                qkv_grad[:, (3 * pair + slot) * pair_width : (3 * pair + slot + 1) * pair_width]
                for pair in range(pairs)
            ],
            axis=1,
        )
        for slot in range(3)
    ] + [wout_grad[:, start : start + head_width] for start in range(0, depth, head_width)]
    flat = jnp.concatenate(columns)
    ff_got = flip(ff_all, "team", 1)
    flat = spread_group(flat, 0, copies)
    flat, ff_got = sync(flat, ff_got)

    for step in range(1, len(orders(copies)[0])):
        flat = spread_group(flat, step, copies)
    grad_up, grad_down = feed_grads_out(
        core.reshape(1), ff_all.reshape(2 * copies, 2, unit, depth),
        ff_got.reshape(2 * copies, 2, unit, depth), copies,
    )
    flat, grad_up, grad_down = sync(flat, grad_up, grad_down)

    flat, small, grad_first = sync(flat, small, grad_first)
    flat_got = flip(flat, "team", 1)
    small_got = flip(small, "mp", 1)
    flat_got, small_got = sync(flat_got, small_got)
    small = small + small_got
    small_got = flip(small, "mp", 2)
    grad_qkv, grad_wout = attention_grads_out(
        core.reshape(1), flat.reshape(2 * copies, -1, head_width),
        flat_got.reshape(2 * copies, -1, head_width), depth, head_width,
    )

    grad_tokens = token_grads(grad_first, grad_hidden, tokens, ln1_gain[None])
    small_got, grad_qkv, grad_wout, grad_tokens = sync(
        small_got, grad_qkv, grad_wout, grad_tokens
    )
    small = small + small_got
    small = small.reshape(-1)
    lines = [small[index * depth : (index + 1) * depth] for index in range(5)]
    start = 5 * depth
    count = TEAM * team_units
    up_sums = small[start : start + parts * count].reshape(parts, count)
    grad_up_bias = lax.dynamic_index_in_dim(up_sums, part, 0, keepdims=False)
    start = start + parts * count
    count = rel_table.size
    table_all = small[start : start + parts * count].reshape(parts, count)
    grad_table = lax.dynamic_index_in_dim(table_all, part, 0, keepdims=False).reshape(
        rel_table.shape
    )

    return (
        layer_out, grad_tokens, lines[0], lines[1], grad_qkv, grad_table, grad_wout,
        lines[2], lines[3], grad_up, grad_up_bias, grad_down, lines[4],
    )


def solution(mesh):
    groups, parts = mesh.shape["dp"], mesh.shape["mp"]
    split = Mesh(
        mesh.devices.reshape(groups // TEAM, TEAM, parts), ("copy", "team", "mp")
    )
    every = ("copy", "team", "mp")
    return jax.shard_map(
        body,
        mesh=split,
        in_specs=(
            P(every, None), P(("copy", "team"), None), P(), P(), P(), P(None, None, "mp"),
            P(None, "mp"), P("mp", None), P(), P(), P(None, "mp"), P("mp"), P("mp", None), P(),
            P(every, None),
        ),
        out_specs=(
            P(every, None), P(every, None), P(), P(), P(None, None, "mp"), P(None, "mp"),
            P("mp", None), P(), P(), P(None, "mp"), P("mp"), P("mp", None), P(),
        ),
        check_vma=False,
    )
```
